32 devices in a mesh: dp: 8 (over y, x, core), seq: 4 (over z).
Axes of the slice: x: 2, y: 2, z: 4, core: 2. Of those that a mesh axis runs over, the one named last changes fastest.
Arguments:
- hidden_in: bfloat16 [16, 1024, 768], P('dp', 'seq'), may hold values from -6 to 6
- segment_ids: int32 [16, 1024], P('dp'), may hold values from 0 to 7, never falling along the last dimension, each value on 1 to 512 neighbouring positions
- query_weight: bfloat16 [768, 768], P('dp'), may hold values from -0.21875 to 0.21875
- query_bias: bfloat16 [768], P('dp'), may hold values from -3 to 3
- key_weight: bfloat16 [768, 768], P('dp'), may hold values from -0.21875 to 0.21875
- value_weight: bfloat16 [768, 768], P('dp'), may hold values from -0.21875 to 0.21875
- value_bias: bfloat16 [768], P('dp'), may hold values from -3 to 3
- out_weight: bfloat16 [768, 768], P('dp'), may hold values from -0.875 to 0.875
- out_bias: bfloat16 [768], P('dp'), may hold values from -3 to 3
- first_gain: bfloat16 [768], P('dp'), may hold values from 0.5 to 1.5
- first_shift: bfloat16 [768], P('dp'), may hold values from -3 to 3
- up_weight: bfloat16 [768, 3072], P('dp'), may hold values from -0.21875 to 0.21875
- up_bias: bfloat16 [3072], P('dp'), may hold values from -3 to 3
- down_weight: bfloat16 [3072, 768], P('dp'), may hold values from -0.109375 to 0.109375
- down_bias: bfloat16 [768], P('dp'), may hold values from -3 to 3
- second_gain: bfloat16 [768], P('dp'), may hold values from 0.5 to 1.5
- second_shift: bfloat16 [768], P('dp'), may hold values from -3 to 3
- cotangent: bfloat16 [16, 1024, 768], P('dp', 'seq'), may hold values from -6 to 6
Outputs:
- layer_out: bfloat16 [16, 1024, 768], P('dp', 'seq')
- input_gradient: float32 [16, 1024, 768], P('dp', 'seq')
- query_weight_grad: float32 [768, 768], P(('dp', 'seq'))
- query_bias_grad: float32 [768], P(('dp', 'seq'))
- key_weight_grad: float32 [768, 768], P(('dp', 'seq'))
- value_weight_grad: float32 [768, 768], P(('dp', 'seq'))
- value_bias_grad: float32 [768], P(('dp', 'seq'))
- out_weight_grad: float32 [768, 768], P(('dp', 'seq'))
- out_bias_grad: float32 [768], P(('dp', 'seq'))
- first_gain_grad: float32 [768], P(('dp', 'seq'))
- first_shift_grad: float32 [768], P(('dp', 'seq'))
- up_weight_grad: float32 [768, 3072], P(('dp', 'seq'))
- up_bias_grad: float32 [3072], P(('dp', 'seq'))
- down_weight_grad: float32 [3072, 768], P(('dp', 'seq'))
- down_bias_grad: float32 [768], P(('dp', 'seq'))
- second_gain_grad: float32 [768], P(('dp', 'seq'))
- second_shift_grad: float32 [768], P(('dp', 'seq'))
The draws below stay inside these ranges and needn't reach their ends.
All inputs are finite; a program needn't handle non-finite values.
Results may differ from the reference program's by a relative error of at most 0.013.
Values may be sent and summed in bfloat16 or wider, within the bound.
No kernel may reach another device: no remote copies, remote signals or barrier semaphores. Data moves between devices by JAX's collectives and lax.ppermute only.
A program may use at most 128 MiB of HBM per device.

```python
import math
import jax
import jax.numpy as jnp
import numpy as np
from jax import lax

D = 768
HEADS = 12
HEAD_DIM = 64
FF = 3072
SEQ_LEN = 1024
SEQS = 16


def levels(stream_key, shape, split, smallest, top_value):
    level, own = 1.0, jax.random.fold_in(stream_key, 6)
    for position, shards_of in split:
        heights = jnp.exp(jax.random.uniform(jax.random.fold_in(own, position), (shards_of,), jnp.float32, smallest / len(split), top_value / len(split)))
        level = level * jnp.repeat(heights, shape[position] // shards_of).reshape([-1 if axis == position else 1 for axis in range(len(shape))])
    return level


def profile(number_of, total, limit, lean):
    loads = [(1 << 20) // math.isqrt(grade ** lean) + 1 for grade in range(2, number_of + 1)]
    rest, holding = total - limit - (number_of - 1), [1] * (number_of - 1)
    while rest > 0:
        candidates = [i for i in range(number_of - 1) if holding[i] < limit]
        mass, remaining = sum([loads[i] for i in candidates]), rest
        for i in candidates:
            more = min(limit - holding[i], max(1, remaining * loads[i] // mass), rest)
            holding[i] = holding[i] + more
            rest = rest - more
    return np.array([limit] + holding)


def uneven_parts(own_key, count, total, most, skew):
    if count == 2:
        one = jax.random.randint(own_key, (), max(1, total - most), min(most, total - 1) + 1)
        return jnp.stack([one, total - one])
    tallies = jnp.asarray(profile(count, total, most, skew), jnp.int32)
    twos = (count - 1) // 2
    donor, sink = tallies[1:1 + 2 * twos:2], tallies[2:2 + 2 * twos:2]
    margin = jnp.minimum(donor - 1, most - sink)
    passed = jax.random.randint(jax.random.fold_in(own_key, 1), (twos,), 0, 1 << 20) % (margin + 1)
    tallies = tallies.at[1:1 + 2 * twos:2].set(donor - passed).at[2:2 + 2 * twos:2].set(sink + passed)
    return tallies[jax.random.permutation(jax.random.fold_in(own_key, 2), count)]


def normal_values(own_key, shape, scale, most, pieces=(), dtype=jnp.bfloat16):
    entries = scale * jax.random.normal(own_key, shape, jnp.float32)
    if pieces:
        entries = entries * levels(own_key, shape, pieces, -0.22, 0.18)
    return jnp.clip(entries, -most, most).astype(dtype)


def setup_inputs(seed: int = 0) -> dict:
    key_list = jax.random.split(jax.random.key(seed), 19)
    hidden_in = normal_values(key_list[0], (SEQS, SEQ_LEN, D), 1.0, 6.0, ((0, 8), (1, 4)))
    segment_ids = jax.vmap(lambda own: jnp.searchsorted(jnp.cumsum(uneven_parts(own, max(4, SEQ_LEN // 128), SEQ_LEN, SEQ_LEN // 2, 2)), jnp.arange(SEQ_LEN), side="right"))(jax.random.split(key_list[1], SEQS)).reshape((SEQS, SEQ_LEN)).astype(jnp.int32)
    query_weight = normal_values(key_list[2], (D, D), D ** -0.5, 0.21875, ((0, 8),))
    query_bias = normal_values(key_list[3], (D,), 0.5, 3.0, ((0, 8),))
    key_weight = normal_values(key_list[4], (D, D), D ** -0.5, 0.21875, ((0, 8),))
    value_weight = normal_values(key_list[5], (D, D), D ** -0.5, 0.21875, ((0, 8),))
    value_bias = normal_values(key_list[6], (D,), 0.5, 3.0, ((0, 8),))
    out_weight = normal_values(key_list[7], (D, D), (D // 16) ** -0.5, 0.875, ((0, 8),))
    out_bias = normal_values(key_list[8], (D,), 0.5, 3.0, ((0, 8),))
    first_gain = jnp.clip(1.0 + 0.1 * jax.random.normal(key_list[9], (D,), jnp.float32), 0.5, 1.5).astype(jnp.bfloat16)
    first_shift = normal_values(key_list[10], (D,), 0.5, 3.0, ((0, 8),))
    up_weight = normal_values(key_list[11], (D, FF), D ** -0.5, 0.21875, ((0, 8),))
    up_bias = normal_values(key_list[12], (FF,), 0.5, 3.0, ((0, 8),))
    down_weight = normal_values(key_list[13], (FF, D), FF ** -0.5, 0.109375, ((0, 8),))
    down_bias = normal_values(key_list[14], (D,), 0.5, 3.0, ((0, 8),))
    second_gain = jnp.clip(1.0 + 0.1 * jax.random.normal(key_list[15], (D,), jnp.float32), 0.5, 1.5).astype(jnp.bfloat16)
    second_shift = normal_values(key_list[16], (D,), 0.5, 3.0, ((0, 8),))
    cotangent = normal_values(key_list[17], (SEQS, SEQ_LEN, D), 1.0, 6.0, ((0, 8), (1, 4)))
    return dict(hidden_in=hidden_in, segment_ids=segment_ids, query_weight=query_weight, query_bias=query_bias, key_weight=key_weight, value_weight=value_weight, value_bias=value_bias, out_weight=out_weight, out_bias=out_bias, first_gain=first_gain, first_shift=first_shift, up_weight=up_weight, up_bias=up_bias, down_weight=down_weight, down_bias=down_bias, second_gain=second_gain, second_shift=second_shift, cotangent=cotangent)


@jax.custom_vjp
def low(v):
    return lax.optimization_barrier(v.astype(jnp.bfloat16)).astype(jnp.float32)

@jax.custom_vjp
def low_back(v):
    return v

def low_keep(v):
    return (low(v), None)

def low_pass(kept, grad):
    return (grad,)

def back_keep(v):
    return (v, None)

def back_low(kept, grad):
    return (low(grad),)
low.defvjp(low_keep, low_pass)
low_back.defvjp(back_keep, back_low)
epsilon = 1e-12

def norm_layer(value, gain, shift):
    center = value - lax.optimization_barrier(jnp.mean(value, axis=-1, keepdims=True))
    spread = lax.optimization_barrier(jnp.mean(center * center, axis=-1, keepdims=True))
    return center * lax.rsqrt(spread + epsilon) * gain + shift

def attend(query, keys, values, segment):
    length = query.shape[0]
    block = min(512, length)
    count = length // block
    highest = lax.Precision.HIGHEST
    query_blocks = query.reshape(count, block, HEADS, HEAD_DIM)
    segment_blocks = segment.reshape(count, block)

    def one_block(pair):
        query_part, segment_part = pair
        scores = jnp.einsum('qhd,khd->hqk', query_part, keys, precision=highest) * HEAD_DIM ** (-0.5)
        scores = jnp.where(segment_part[None, :, None] == segment[None, None, :], scores, -1e+30)
        scores = low_back(scores)
        top = lax.optimization_barrier(jnp.max(scores, axis=-1, keepdims=True))
        expo = jnp.exp(scores - top)
        probs = expo / lax.optimization_barrier(jnp.sum(expo, axis=-1, keepdims=True))
        return jnp.einsum('hqk,khd->qhd', low(probs), values, precision=highest)
    result = lax.map(jax.checkpoint(one_block), (query_blocks, segment_blocks))
    return result.reshape(length, HEADS * HEAD_DIM)

def forward(params, hidden, segment):
    query_weight, query_bias, key_weight, value_weight, value_bias, out_weight, out_bias, first_gain, first_shift, up_weight, up_bias, down_weight, down_bias, second_gain, second_shift = params
    highest = lax.Precision.HIGHEST
    length = hidden.shape[0]
    query = low_back(low(jnp.dot(hidden, query_weight, precision=highest) + query_bias))
    keys = low_back(low(jnp.dot(hidden, key_weight, precision=highest)))
    values = low_back(low(jnp.dot(hidden, value_weight, precision=highest) + value_bias))
    attended = attend(query.reshape(length, HEADS, HEAD_DIM), keys.reshape(length, HEADS, HEAD_DIM), values.reshape(length, HEADS, HEAD_DIM), segment)
    attended = low_back(low(attended))
    branch = low_back(jnp.dot(attended, out_weight, precision=highest) + out_bias)
    first = norm_layer(hidden + branch, first_gain, first_shift)
    inner = low_back(jnp.dot(low(first), up_weight, precision=highest) + up_bias)
    active = low(jax.nn.gelu(inner, approximate=False))
    second = low_back(jnp.dot(active, down_weight, precision=highest) + down_bias)
    return norm_layer(first + second, second_gain, second_shift)

def add_trees(left, right):
    return jax.tree.map(jnp.add, left, right)

def reference(hidden_in, segment_ids, query_weight, query_bias, key_weight, value_weight, value_bias, out_weight, out_bias, first_gain, first_shift, up_weight, up_bias, down_weight, down_bias, second_gain, second_shift, cotangent):
    params = tuple((weight.astype(jnp.float32) for weight in (query_weight, query_bias, key_weight, value_weight, value_bias, out_weight, out_bias, first_gain, first_shift, up_weight, up_bias, down_weight, down_bias, second_gain, second_shift)))

    def one_sequence(totals, item):
        hidden, segment, upstream = item

        def run(weights, tokens):
            return forward(weights, tokens, segment)
        output, pullback = jax.vjp(run, params, hidden.astype(jnp.float32))
        weight_grads, hidden_grad = pullback(upstream.astype(jnp.float32))
        return (add_trees(totals, weight_grads), (output.astype(jnp.bfloat16), hidden_grad))
    zeros = tuple((jnp.zeros(weight.shape, jnp.float32) for weight in params))
    totals, (outputs, hidden_grads) = lax.scan(one_sequence, zeros, (hidden_in, segment_ids, cotangent))
    return (outputs, hidden_grads, totals[0], totals[1], totals[2], totals[3], totals[4], totals[5], totals[6], totals[7], totals[8], totals[9], totals[10], totals[11], totals[12], totals[13], totals[14])
```

```python
import functools
import math

import jax
import jax.numpy as jnp
from jax import lax
from jax.experimental import pallas as pl
from jax.experimental.pallas import tpu as pltpu
from jax.sharding import PartitionSpec as P

HEAD_DIM = 64
LANES = 128
CHUNK = 128
NEGATIVE = -1e30


def nt(left, right):
    return lax.dot_general(left, right, (((1,), (1,)), ((), ())), preferred_element_type=jnp.float32)


def nn(left, right):
    return lax.dot_general(left, right, (((1,), (0,)), ((), ())), preferred_element_type=jnp.float32)


def head_parts(block):
    lane = lax.broadcasted_iota(jnp.int32, block.shape, 1)
    zero = jnp.zeros_like(block)
    return (jnp.where(lane < HEAD_DIM, block, zero), jnp.where(lane < HEAD_DIM, zero, block))


def same_document(column_tile, row):
    width = row.shape[1]
    column = jnp.concatenate([column_tile] * (width // LANES), axis=1)
    return column == jnp.broadcast_to(row, column.shape)


def forward_body(qblock, bounds, q_ref, k_ref, v_ref, ko_ref, vo_ref, sq_ref, sk_ref, so_ref, o_ref, lse_ref, vt):
    half = k_ref.shape[0]
    tokens = q_ref.shape[0]
    chunks = half // CHUNK
    for j in range(chunks):
        rows = slice(j * CHUNK, (j + 1) * CHUNK)
        vt[j] = v_ref[rows, :].T
        vt[chunks + j] = vo_ref[rows, :].T
    for b in range(tokens // qblock):
        span = slice(b * qblock, (b + 1) * qblock)
        parts = head_parts(q_ref[span, :] * jnp.bfloat16(HEAD_DIM**-0.5))
        row = sq_ref[:, span]

        def one(j, carry, keys, segs, first):
            start = pl.multiple_of(j * CHUNK, CHUNK)
            key = keys[pl.ds(start, CHUNK), :]
            mask = same_document(segs[pl.ds(start, CHUNK), :], row)
            vals = vt[first + j]
            out = []
            for h in range(2):
                top, total, acc = carry[h]
                score = jnp.where(mask, nt(key, parts[h]), NEGATIVE)
                new_top = jnp.maximum(top, jnp.max(score, axis=0, keepdims=True))
                expo = jnp.exp(score - new_top)
                scale = jnp.exp(top - new_top)
                total = total * scale + jnp.sum(expo, axis=0, keepdims=True)
                acc = acc * scale + nn(vals[h * HEAD_DIM : (h + 1) * HEAD_DIM, :], expo.astype(jnp.bfloat16))
                out.append((new_top, total, acc))
            return tuple(out)

        init = (
            jnp.full((1, qblock), NEGATIVE, jnp.float32),
            jnp.zeros((1, qblock), jnp.float32),
            jnp.zeros((HEAD_DIM, qblock), jnp.float32),
        )
        carry = (init, init)
        carry = lax.fori_loop(
            bounds[4 * b], bounds[4 * b + 1], functools.partial(one, keys=k_ref, segs=sk_ref, first=0), carry
        )
        carry = lax.fori_loop(
            bounds[4 * b + 2], bounds[4 * b + 3], functools.partial(one, keys=ko_ref, segs=so_ref, first=chunks), carry
        )
        result = jnp.concatenate([acc / total for _, total, acc in carry], axis=0)
        o_ref[span, :] = result.T.astype(jnp.bfloat16)
        for h in range(2):
            lse_ref[0, h : h + 1, span] = carry[h][0] + jnp.log(carry[h][1])


def backward_body(
    qblock, bounds, q_ref, k_ref, v_ref, ko_ref, vo_ref, o_ref, do_ref, lse_ref, sq_ref, sk_ref, so_ref,
    dq_ref, dk_ref, dv_ref, dko_ref, dvo_ref, kt, dko, dvo,
):
    half = k_ref.shape[0]
    tokens = q_ref.shape[0]
    chunks = half // CHUNK
    for j in range(chunks):
        rows = slice(j * CHUNK, (j + 1) * CHUNK)
        kt[j] = k_ref[rows, :].T
        kt[chunks + j] = ko_ref[rows, :].T
    for ref in (dk_ref, dv_ref, dko, dvo):
        ref[...] = jnp.zeros_like(ref)
    for b in range(tokens // qblock):
        span = slice(b * qblock, (b + 1) * qblock)
        parts = head_parts(q_ref[span, :] * jnp.bfloat16(HEAD_DIM**-0.5))
        dparts = head_parts(do_ref[span, :])
        both = jnp.concatenate(parts, axis=0)
        dboth = jnp.concatenate(dparts, axis=0)
        row = sq_ref[:, span]
        product = (do_ref[span, :].astype(jnp.float32) * o_ref[span, :].astype(jnp.float32)).T
        delta = [jnp.sum(product[h * HEAD_DIM : (h + 1) * HEAD_DIM], axis=0, keepdims=True) for h in range(2)]
        lse = [lse_ref[0, h : h + 1, span] for h in range(2)]

        def one(j, carry, keys, vals, segs, first, dkeys, dvals):
            start = pl.multiple_of(j * CHUNK, CHUNK)
            key = keys[pl.ds(start, CHUNK), :]
            val = vals[pl.ds(start, CHUNK), :]
            mask = same_document(segs[pl.ds(start, CHUNK), :], row)
            keyt = kt[first + j]
            probs, grads, out = [], [], []
            for h in range(2):
                score = jnp.where(mask, nt(key, parts[h]), NEGATIVE)
                prob = jnp.exp(score - lse[h])
                grad = (prob * (nt(val, dparts[h]) - delta[h])).astype(jnp.bfloat16)
                probs.append(prob.astype(jnp.bfloat16))
                grads.append(grad)
                out.append(carry[h] + nn(keyt[h * HEAD_DIM : (h + 1) * HEAD_DIM, :], grad))
            dvals[pl.ds(start, CHUNK), :] += nn(jnp.concatenate(probs, axis=1), dboth)
            dkeys[pl.ds(start, CHUNK), :] += nn(jnp.concatenate(grads, axis=1), both)
            return tuple(out)

        zero = jnp.zeros((HEAD_DIM, qblock), jnp.float32)
        carry = (zero, zero)
        carry = lax.fori_loop(
            bounds[4 * b], bounds[4 * b + 1],
            functools.partial(one, keys=k_ref, vals=v_ref, segs=sk_ref, first=0, dkeys=dk_ref, dvals=dv_ref), carry,
        )
        carry = lax.fori_loop(
            bounds[4 * b + 2], bounds[4 * b + 3],
            functools.partial(one, keys=ko_ref, vals=vo_ref, segs=so_ref, first=chunks, dkeys=dko, dvals=dvo), carry,
        )
        dq_ref[span, :] = (jnp.concatenate(carry, axis=0).T * HEAD_DIM**-0.5).astype(jnp.bfloat16)
    dko_ref[...] = dko[...].astype(jnp.bfloat16)
    dvo_ref[...] = dvo[...].astype(jnp.bfloat16)


def chunk_bounds(own, other, qblock):
    rows = own.reshape(-1, qblock)
    low, high = rows[:, 0], rows[:, -1]
    found = []
    for part in (own, other):
        tiles = part.reshape(-1, CHUNK)
        live = (tiles[None, :, 0] <= high[:, None]) & (tiles[None, :, -1] >= low[:, None])
        first = jnp.argmax(live, axis=1).astype(jnp.int32)
        found += [first, first + jnp.sum(live, axis=1).astype(jnp.int32)]
    return jnp.stack(found, axis=1).reshape(-1)


def tile_column(segment):
    return jnp.broadcast_to(segment[:, None], (segment.shape[0], LANES))


def attention_specs(tokens, half):
    col = lambda hp, *_: (0, hp)
    whole = lambda hp, *_: (0, 0)
    q = pl.BlockSpec((tokens, LANES), col)
    k = pl.BlockSpec((half, LANES), col)
    seg = [
        pl.BlockSpec((1, tokens), whole),
        pl.BlockSpec((half, LANES), whole),
        pl.BlockSpec((half, LANES), whole),
    ]
    lse = pl.BlockSpec((1, 8, tokens), lambda hp, *_: (hp, 0, 0))
    return q, k, seg, lse


def attend_forward(query, keys, values, keys_other, values_other, own, other, bounds, qblock):
    tokens, width = query.shape
    half = keys.shape[0]
    pairs = width // LANES
    q, k, seg, lse = attention_specs(tokens, half)
    area = tokens * half * 2
    return pl.pallas_call(
        functools.partial(forward_body, qblock),
        grid_spec=pltpu.PrefetchScalarGridSpec(
            num_scalar_prefetch=1,
            grid=(pairs,),
            in_specs=[q, k, k, k, k] + seg,
            out_specs=[q, lse],
            scratch_shapes=[pltpu.VMEM((2 * half // CHUNK, LANES, CHUNK), jnp.bfloat16)],
        ),
        out_shape=[
            jax.ShapeDtypeStruct((tokens, width), jnp.bfloat16),
            jax.ShapeDtypeStruct((pairs, 8, tokens), jnp.float32),
        ],
        cost_estimate=pl.CostEstimate(flops=8 * area * width, transcendentals=area * width // 64, bytes_accessed=6 * tokens * width * 2),
        compiler_params=pltpu.CompilerParams(vmem_limit_bytes=24 << 20),
        name="attend_forward",
    )(bounds, query, keys, values, keys_other, values_other, own[None, :], tile_column(own), tile_column(other))


def attend_back(query, keys, values, keys_other, values_other, attended, grad, lse_rows, own, other, bounds, qblock):
    tokens, width = query.shape
    half = keys.shape[0]
    pairs = width // LANES
    q, k, seg, lse = attention_specs(tokens, half)
    area = tokens * half * 2
    shape = lambda rows, dtype: jax.ShapeDtypeStruct((rows, width), dtype)
    return pl.pallas_call(
        functools.partial(backward_body, qblock),
        grid_spec=pltpu.PrefetchScalarGridSpec(
            num_scalar_prefetch=1,
            grid=(pairs,),
            in_specs=[q, k, k, k, k, q, q, lse] + seg,
            out_specs=[q, k, k, k, k],
            scratch_shapes=[
                pltpu.VMEM((2 * half // CHUNK, LANES, CHUNK), jnp.bfloat16),
                pltpu.VMEM((half, LANES), jnp.float32),
                pltpu.VMEM((half, LANES), jnp.float32),
            ],
        ),
        out_shape=[
            shape(tokens, jnp.bfloat16),
            shape(half, jnp.float32),
            shape(half, jnp.float32),
            shape(half, jnp.bfloat16),
            shape(half, jnp.bfloat16),
        ],
        cost_estimate=pl.CostEstimate(flops=20 * area * width, transcendentals=area * width // 64, bytes_accessed=14 * tokens * width * 2),
        compiler_params=pltpu.CompilerParams(vmem_limit_bytes=24 << 20),
        name="attend_back",
    )(
        bounds, query, keys, values, keys_other, values_other, attended, grad, lse_rows,
        own[None, :], tile_column(own), tile_column(other),
    )


AXES = ("dp", "seq")
epsilon = 1e-12


def bit_count(size):
    return size.bit_length() - 1


def swap_dp(value, bit):
    size = lax.axis_size("dp")
    return lax.ppermute(value, "dp", [(i, i ^ (1 << bit)) for i in range(size)])


def swap_seq(value, bit):
    size = lax.axis_size("seq")
    return lax.ppermute(value, "seq", [(i, i ^ (1 << bit)) for i in range(size)])


def times_left(left, right):
    return lax.dot_general(left, right, (((0,), (0,)), ((), ())), preferred_element_type=jnp.float32)


def column_sum(matrix):
    return jnp.sum(matrix.astype(jnp.float32), axis=0)


def norm_parts(value):
    center = value - jnp.mean(value, axis=-1, keepdims=True)
    spread = jnp.mean(center * center, axis=-1, keepdims=True)
    scale = lax.rsqrt(spread + epsilon)
    return (center * scale, scale)


def norm_back(upstream, normal, scale, gain):
    scaled = upstream * gain
    return scale * (
        scaled
        - jnp.mean(scaled, axis=-1, keepdims=True)
        - normal * jnp.mean(scaled * normal, axis=-1, keepdims=True)
    )


def spread_pairs(first):
    dps, seqs = lax.axis_size("dp"), lax.axis_size("seq")
    pairs = []
    for dp in range(dps):
        for seq in range(seqs):
            piece = first ^ (seq & 1)
            to_dp = (dp & ~1) | (seq >> 1)
            to_seq = 2 * (dp & 1) + piece
            pairs.append((dp * seqs + seq, to_dp * seqs + to_seq))
    return pairs


def to_sequences(local):
    odd = (lax.axis_index("seq") & 1) == 1
    got = []
    for first in range(2):
        piece = jnp.where(odd, local[1 - first], local[first])
        got.append(lax.ppermute(piece, AXES, spread_pairs(first)))
    return jnp.where(odd, jnp.concatenate(got[::-1]), jnp.concatenate(got))


def from_sequences(tokens):
    odd = (lax.axis_index("seq") & 1) == 1
    half = tokens.shape[0] // 2
    got = []
    for first in range(2):
        piece = jnp.where(odd, tokens[(1 - first) * half : (2 - first) * half], tokens[first * half : (first + 1) * half])
        got.append(lax.ppermute(piece, AXES, [(b, a) for a, b in spread_pairs(first)]))
    return jnp.where(odd, jnp.stack(got[::-1]), jnp.stack(got))


def gather_rows(part, order):
    me = lax.axis_index("dp")
    slots = part[None]
    for bit in order:
        slots = jnp.concatenate([slots, swap_dp(slots, bit)], axis=0)
    other = swap_dp(slots, 0)
    pieces = []
    for shard in range(lax.axis_size("dp")):
        relative = me ^ shard
        slot = jnp.int32(0)
        for place, bit in enumerate(order):
            slot = slot | (((relative >> bit) & 1) << place)
        mine = lax.dynamic_index_in_dim(slots, slot, 0, keepdims=False)
        theirs = lax.dynamic_index_in_dim(other, slot, 0, keepdims=False)
        pieces.append(jnp.where((relative & 1) == 0, mine, theirs))
    return jnp.concatenate(pieces, axis=-2)


def scatter_sum(total, order):
    dps, seqs = lax.axis_size("dp"), lax.axis_size("seq")
    nd, ns = bit_count(dps), bit_count(seqs)
    rows, cols = total.shape
    view = total.reshape((2,) * (nd + ns) + (rows // (dps * seqs), cols))
    left = [("dp", b) for b in reversed(range(nd))] + [("seq", b) for b in reversed(range(ns))]
    parts = [view]
    for step in order:
        axis, bit = step
        where = left.index(step)
        mine = (lax.axis_index(axis) >> bit) & 1
        send = sum(
            lax.dynamic_index_in_dim(p, 1 - mine, where, keepdims=False).astype(jnp.float32) for p in parts
        ).astype(jnp.bfloat16)
        keep = [lax.dynamic_index_in_dim(p, mine, where, keepdims=False) for p in parts]
        swap = swap_dp if axis == "dp" else swap_seq
        parts = keep + [swap(send, bit)]
        left.remove(step)
    return sum(p.astype(jnp.float32) for p in parts)


def orders():
    nd, ns = bit_count(lax.axis_size("dp")), bit_count(lax.axis_size("seq"))
    seq = [("seq", b) for b in range(ns)]
    up = [("dp", b) for b in range(1, nd)]
    down = up[::-1]
    core = [("dp", 0)]
    return core + up + seq, core + down + seq, core + seq + up


def per_device(
    hidden_in, segment_ids, query_weight, query_bias, key_weight, value_weight, value_bias, out_weight, out_bias,
    first_gain, first_shift, up_weight, up_bias, down_weight, down_bias, second_gain, second_shift, cotangent,
):
    dps, seqs = lax.axis_size("dp"), lax.axis_size("seq")
    width = query_weight.shape[1]
    bits = list(range(1, bit_count(dps)))
    tokens = to_sequences(hidden_in)
    wq, wk, wv = gather_rows(jnp.stack([query_weight, key_weight, value_weight]), bits)
    vectors = [query_bias, value_bias, out_bias, first_gain, first_shift, down_bias, second_gain, second_shift]
    rows = query_bias.shape[0]
    packed = jnp.concatenate(vectors + [up_bias]).reshape(-1, rows)
    packed = lax.all_gather(packed, "dp", axis=0)
    q_add, v_add, out_add, gain_one, shift_one, down_add, gain_two, shift_two = [
        packed[:, i].reshape(-1).astype(jnp.float32) for i in range(8)
    ]
    up_add = packed[:, 8:].reshape(-1).astype(jnp.float32)

    core = lax.axis_index("dp") & 1
    place = lax.axis_index("seq")
    segments = jnp.where(core == (place >> 1), segment_ids, swap_dp(segment_ids, 0))
    segment = lax.dynamic_index_in_dim(segments, place & 1, 0, keepdims=False)
    half = segment.shape[0] // 2
    own = lax.dynamic_slice_in_dim(segment, core * half, half)
    other = lax.dynamic_slice_in_dim(segment, (1 - core) * half, half)
    qblock = 256
    bounds = chunk_bounds(own, other, qblock)

    keys = nn(tokens, wk).astype(jnp.bfloat16)
    values = (nn(tokens, wv) + v_add).astype(jnp.bfloat16)
    keys_other = swap_dp(keys, 0)
    values_other = swap_dp(values, 0)
    query = (nn(tokens, wq) + q_add).astype(jnp.bfloat16)
    wo = gather_rows(out_weight, bits)
    wu = gather_rows(up_weight, bits)
    wd = gather_rows(down_weight, bits[::-1])
    upstream = to_sequences(cotangent).astype(jnp.float32)

    attended, lse = attend_forward(query, keys, values, keys_other, values_other, own, other, bounds, qblock)
    residual = tokens.astype(jnp.float32) + (nn(attended, wo) + out_add)
    normal_one, scale_one = norm_parts(residual)
    first = normal_one * gain_one + shift_one
    first_low = first.astype(jnp.bfloat16)
    inner = nn(first_low, wu) + up_add
    cumulative = 0.5 * (1.0 + lax.erf(inner * math.sqrt(0.5)))
    active = (inner * cumulative).astype(jnp.bfloat16)
    second = nn(active, wd) + down_add
    normal_two, scale_two = norm_parts(first + second)
    layer_out = from_sequences((normal_two * gain_two + shift_two).astype(jnp.bfloat16))

    sum_two_grad = norm_back(upstream, normal_two, scale_two, gain_two)
    second_grad = sum_two_grad.astype(jnp.bfloat16)
    order_x, order_y, order_z = orders()
    down_grad = scatter_sum(times_left(active, second_grad).astype(jnp.bfloat16), order_x)
    density = jnp.exp(-0.5 * inner * inner) * (1.0 / math.sqrt(2.0 * math.pi))
    inner_grad = (nt(second_grad, wd) * (cumulative + inner * density)).astype(jnp.bfloat16)
    up_grad = scatter_sum(times_left(first_low, inner_grad).astype(jnp.bfloat16), order_y)
    first_grad = sum_two_grad + nt(inner_grad, wu)
    sum_one_grad = norm_back(first_grad, normal_one, scale_one, gain_one)
    branch_grad = sum_one_grad.astype(jnp.bfloat16)
    attended_grad = nt(branch_grad, wo).astype(jnp.bfloat16)
    out_grad = scatter_sum(times_left(attended, branch_grad).astype(jnp.bfloat16), order_z)

    dq, dk, dv, dk_other, dv_other = attend_back(
        query, keys, values, keys_other, values_other, attended, attended_grad, lse, own, other, bounds, qblock
    )
    dk = (dk + swap_dp(dk_other, 0).astype(jnp.float32)).astype(jnp.bfloat16)
    dv = (dv + swap_dp(dv_other, 0).astype(jnp.float32)).astype(jnp.bfloat16)
    input_grad = sum_one_grad + nt(dq, wq) + nt(dk, wk) + nt(dv, wv)
    input_grad = from_sequences(input_grad.astype(jnp.bfloat16)).astype(jnp.float32)

    sums = [
        column_sum(dq), column_sum(dv), column_sum(branch_grad), jnp.sum(first_grad * normal_one, axis=0),
        jnp.sum(first_grad, axis=0), column_sum(second_grad), jnp.sum(upstream * normal_two, axis=0),
        jnp.sum(upstream, axis=0),
    ]
    small = jnp.concatenate([jnp.stack(sums, axis=1), column_sum(inner_grad).reshape(width, -1)], axis=1)
    small = jnp.pad(small, ((0, 0), (0, LANES - small.shape[1])))
    query_grad = scatter_sum(
        jnp.concatenate([times_left(tokens, dq), times_left(tokens, dk), small], axis=1).astype(jnp.bfloat16), order_x
    )
    value_grad = scatter_sum(times_left(tokens, dv).astype(jnp.bfloat16), order_y)
    qb, vb, ob, g1, s1, db, g2, s2 = [query_grad[:, 2 * width + i] for i in range(8)]
    ub = query_grad[:, 2 * width + 8 : 2 * width + 12].reshape(-1)
    return (
        layer_out, input_grad, query_grad[:, :width], qb, query_grad[:, width : 2 * width], value_grad, vb,
        out_grad, ob, g1, s1, up_grad, ub, down_grad, db, g2, s2,
    )


def solution(mesh):
    wide, flat = P("dp", None), P("dp")
    in_specs = (
        P("dp", "seq", None), wide, wide, flat, wide, wide, flat, wide, flat, flat, flat, wide, flat, wide, flat,
        flat, flat, P("dp", "seq", None),
    )
    rows, cells = P(AXES, None), P(AXES)
    out_specs = (
        P("dp", "seq", None), P("dp", "seq", None), rows, cells, rows, rows, cells, rows, cells, cells, cells, rows,
        cells, rows, cells, cells, cells,
    )
    return jax.shard_map(per_device, mesh=mesh, in_specs=in_specs, out_specs=out_specs, check_vma=False)
```

```python
import functools
import math

import jax
import jax.numpy as jnp
from jax import lax
from jax.experimental import pallas as pl
from jax.experimental.pallas import tpu as pltpu
from jax.sharding import PartitionSpec as P

HEAD_DIM = 64
LANES = 128
NEGATIVE = -1e30


def nt(left, right):
    return lax.dot_general(left, right, (((1,), (1,)), ((), ())), preferred_element_type=jnp.float32)


def nn(left, right):
    return lax.dot_general(left, right, (((1,), (0,)), ((), ())), preferred_element_type=jnp.float32)


def head_parts(block):
    lane = lax.broadcasted_iota(jnp.int32, block.shape, 1)
    zero = jnp.zeros_like(block)
    return (jnp.where(lane < HEAD_DIM, block, zero), jnp.where(lane < HEAD_DIM, zero, block))


def same_document(column_tile, row):
    column = jnp.concatenate([column_tile] * (row.shape[1] // LANES), axis=1)
    return column == jnp.broadcast_to(row, column.shape)


def pair_lanes(pair):
    return slice(pair * LANES, (pair + 1) * LANES)


def chunk_of(bounds, block, step, chunks):
    own = bounds[4 * block + 1] - bounds[4 * block]
    return jnp.where(step < own, bounds[4 * block] + step, chunks + bounds[4 * block + 2] + step - own)


def live_chunks(bounds, block):
    return bounds[4 * block + 1] - bounds[4 * block] + bounds[4 * block + 3] - bounds[4 * block + 2]


def forward_body(qblock, chunk, bounds, q_ref, k_ref, v_ref, ko_ref, vo_ref, sq_ref, sk_ref, o_ref, lse_ref, kall, vt):
    half, lanes = k_ref.shape
    chunks, pairs = half // chunk, lanes // LANES
    for j in range(chunks):
        rows = slice(j * chunk, (j + 1) * chunk)
        kall[j] = k_ref[rows, :]
        kall[chunks + j] = ko_ref[rows, :]
        vt[j] = v_ref[rows, :].T
        vt[chunks + j] = vo_ref[rows, :].T
    for b in range(q_ref.shape[0] // qblock):
        span = slice(b * qblock, (b + 1) * qblock)
        parts = []
        for pair in range(pairs):
            parts += head_parts(q_ref[span, pair_lanes(pair)] * jnp.bfloat16(HEAD_DIM**-0.5))
        row = sq_ref[:, span]

        def one(step, carry):
            j = chunk_of(bounds, b, step, chunks)
            mask = same_document(sk_ref[j], row)
            scores = [jnp.where(mask, nt(kall[j, :, pair_lanes(h // 2)], part), NEGATIVE) for h, part in enumerate(parts)]
            out = []
            for h, score in enumerate(scores):
                top, total, acc = carry[h]
                new_top = jnp.maximum(top, jnp.max(score, axis=0, keepdims=True))
                expo = jnp.exp(score - new_top)
                scale = jnp.exp(top - new_top)
                total = total * scale + jnp.sum(expo, axis=0, keepdims=True)
                acc = acc * scale + nn(vt[j, h * HEAD_DIM : (h + 1) * HEAD_DIM, :], expo.astype(jnp.bfloat16))
                out.append((new_top, total, acc))
            return tuple(out)

        init = (
            jnp.full((1, qblock), NEGATIVE, jnp.float32),
            jnp.zeros((1, qblock), jnp.float32),
            jnp.zeros((HEAD_DIM, qblock), jnp.float32),
        )
        carry = lax.fori_loop(0, live_chunks(bounds, b), one, (init,) * len(parts))
        result = jnp.concatenate([acc / total for _, total, acc in carry], axis=0)
        o_ref[span, :] = result.T.astype(jnp.bfloat16)
        for h, (top, total, _) in enumerate(carry):
            lse_ref[0, h : h + 1, span] = top + jnp.log(total)


def backward_body(
    qblock, chunk, bounds, q_ref, k_ref, v_ref, ko_ref, vo_ref, o_ref, do_ref, lse_ref, sq_ref, sk_ref,
    dq_ref, dk_ref, dv_ref, dko_ref, dvo_ref, kall, vall, kt, dkall, dvall,
):
    half, lanes = k_ref.shape
    chunks, pairs = half // chunk, lanes // LANES
    for j in range(chunks):
        rows = slice(j * chunk, (j + 1) * chunk)
        kall[j] = k_ref[rows, :]
        kall[chunks + j] = ko_ref[rows, :]
        vall[j] = v_ref[rows, :]
        vall[chunks + j] = vo_ref[rows, :]
        kt[j] = k_ref[rows, :].T
        kt[chunks + j] = ko_ref[rows, :].T
    dkall[...] = jnp.zeros_like(dkall)
    dvall[...] = jnp.zeros_like(dvall)
    for b in range(q_ref.shape[0] // qblock):
        span = slice(b * qblock, (b + 1) * qblock)
        parts, dparts, delta = [], [], []
        for pair in range(pairs):
            parts.append(head_parts(q_ref[span, pair_lanes(pair)] * jnp.bfloat16(HEAD_DIM**-0.5)))
            dparts.append(head_parts(do_ref[span, pair_lanes(pair)]))
            product = do_ref[span, pair_lanes(pair)].astype(jnp.float32) * o_ref[span, pair_lanes(pair)].astype(jnp.float32)
            product = product.T
            delta += [jnp.sum(product[h * HEAD_DIM : (h + 1) * HEAD_DIM], axis=0, keepdims=True) for h in range(2)]
        both = [jnp.concatenate(p, axis=0) for p in parts]
        dboth = [jnp.concatenate(p, axis=0) for p in dparts]
        row = sq_ref[:, span]
        lse = [lse_ref[0, h : h + 1, span] for h in range(2 * pairs)]

        def one(step, carry):
            j = chunk_of(bounds, b, step, chunks)
            mask = same_document(sk_ref[j], row)
            out = []
            for pair in range(pairs):
                key, val = kall[j, :, pair_lanes(pair)], vall[j, :, pair_lanes(pair)]
                probs, grads = [], []
                for side in range(2):
                    h = 2 * pair + side
                    score = jnp.where(mask, nt(key, parts[pair][side]), NEGATIVE)
                    prob = jnp.exp(score - lse[h])
                    grad = (prob * (nt(val, dparts[pair][side]) - delta[h])).astype(jnp.bfloat16)
                    probs.append(prob.astype(jnp.bfloat16))
                    grads.append(grad)
                    out.append(carry[h] + nn(kt[j, h * HEAD_DIM : (h + 1) * HEAD_DIM, :], grad))
                dvall[j, :, pair_lanes(pair)] += nn(jnp.concatenate(probs, axis=1), dboth[pair])
                dkall[j, :, pair_lanes(pair)] += nn(jnp.concatenate(grads, axis=1), both[pair])
            return tuple(out)

        zero = jnp.zeros((HEAD_DIM, qblock), jnp.float32)
        carry = lax.fori_loop(0, live_chunks(bounds, b), one, (zero,) * (2 * pairs))
        dq_ref[span, :] = (jnp.concatenate(carry, axis=0).T * HEAD_DIM**-0.5).astype(jnp.bfloat16)
    for j in range(chunks):
        rows = slice(j * chunk, (j + 1) * chunk)
        dk_ref[rows, :] = dkall[j]
        dv_ref[rows, :] = dvall[j]
        dko_ref[rows, :] = dkall[chunks + j].astype(jnp.bfloat16)
        dvo_ref[rows, :] = dvall[chunks + j].astype(jnp.bfloat16)


def chunk_bounds(own, other, qblock, chunk):
    rows = own.reshape(-1, qblock)
    low, high = rows[:, 0], rows[:, -1]
    found = []
    for part in (own, other):
        tiles = part.reshape(-1, chunk)
        live = (tiles[None, :, 0] <= high[:, None]) & (tiles[None, :, -1] >= low[:, None])
        first = jnp.argmax(live, axis=1).astype(jnp.int32)
        found += [first, first + jnp.sum(live, axis=1).astype(jnp.int32)]
    return jnp.stack(found, axis=1).reshape(-1)


def segment_tiles(own, other, chunk):
    both = jnp.concatenate([own, other])
    return jnp.broadcast_to(both[:, None], (both.shape[0], LANES)).reshape(-1, chunk, LANES)


def attend_forward(query, keys, values, keys_other, values_other, row, tiles, bounds, qblock, chunk, pairs):
    tokens, width = query.shape
    half = keys.shape[0]
    lanes = pairs * LANES
    steps = width // lanes
    q = pl.BlockSpec((tokens, lanes), lambda i, *_: (0, i))
    k = pl.BlockSpec((half, lanes), lambda i, *_: (0, i))
    lse = pl.BlockSpec((1, 8, tokens), lambda i, *_: (i, 0, 0))
    area = tokens * half * 2
    return pl.pallas_call(
        functools.partial(forward_body, qblock, chunk),
        grid_spec=pltpu.PrefetchScalarGridSpec(
            num_scalar_prefetch=1,
            grid=(steps,),
            in_specs=[q, k, k, k, k, pl.BlockSpec((1, tokens), lambda i, *_: (0, 0)), pl.BlockSpec(tiles.shape, lambda i, *_: (0, 0, 0))],
            out_specs=[q, lse],
            scratch_shapes=[
                pltpu.VMEM((2 * half // chunk, chunk, lanes), jnp.bfloat16),
                pltpu.VMEM((2 * half // chunk, lanes, chunk), jnp.bfloat16),
            ],
        ),
        out_shape=[
            jax.ShapeDtypeStruct((tokens, width), jnp.bfloat16),
            jax.ShapeDtypeStruct((steps, 8, tokens), jnp.float32),
        ],
        cost_estimate=pl.CostEstimate(flops=4 * area * width, transcendentals=area * width // 64, bytes_accessed=6 * tokens * width * 2),
        compiler_params=pltpu.CompilerParams(vmem_limit_bytes=32 << 20),
        name="attend_forward",
    )(bounds, query, keys, values, keys_other, values_other, row, tiles)


def attend_back(query, keys, values, keys_other, values_other, attended, grad, lse_rows, row, tiles, bounds, qblock, chunk, pairs, side):
    tokens, width = query.shape
    half = keys.shape[0]
    lanes = pairs * LANES
    q = pl.BlockSpec((tokens, lanes), lambda i, *_: (0, side))
    k = pl.BlockSpec((half, lanes), lambda i, *_: (0, side))
    lse = pl.BlockSpec((1, 8, tokens), lambda i, *_: (side, 0, 0))
    to_q = pl.BlockSpec((tokens, lanes), lambda i, *_: (0, 0))
    to_k = pl.BlockSpec((half, lanes), lambda i, *_: (0, 0))
    area = tokens * half * 2
    shape = lambda rows, dtype: jax.ShapeDtypeStruct((rows, lanes), dtype)
    n = 2 * half // chunk
    return pl.pallas_call(
        functools.partial(backward_body, qblock, chunk),
        grid_spec=pltpu.PrefetchScalarGridSpec(
            num_scalar_prefetch=1,
            grid=(1,),
            in_specs=[q, k, k, k, k, q, q, lse, pl.BlockSpec((1, tokens), lambda i, *_: (0, 0)), pl.BlockSpec(tiles.shape, lambda i, *_: (0, 0, 0))],
            out_specs=[to_q, to_k, to_k, to_k, to_k],
            scratch_shapes=[
                pltpu.VMEM((n, chunk, lanes), jnp.bfloat16),
                pltpu.VMEM((n, chunk, lanes), jnp.bfloat16),
                pltpu.VMEM((n, lanes, chunk), jnp.bfloat16),
                pltpu.VMEM((n, chunk, lanes), jnp.float32),
                pltpu.VMEM((n, chunk, lanes), jnp.float32),
            ],
        ),
        out_shape=[
            shape(tokens, jnp.bfloat16), shape(half, jnp.float32), shape(half, jnp.float32), shape(half, jnp.bfloat16), shape(half, jnp.bfloat16),
        ],
        cost_estimate=pl.CostEstimate(flops=10 * area * lanes, transcendentals=area * lanes // 64, bytes_accessed=14 * tokens * lanes * 2),
        compiler_params=pltpu.CompilerParams(vmem_limit_bytes=48 << 20),
        name="attend_back",
    )(bounds, query, keys, values, keys_other, values_other, attended, grad, lse_rows, row, tiles)


AXES = ("dp", "seq")
PARTS = 8
epsilon = 1e-12


def after(value, *others):
    return lax.optimization_barrier((value,) + others)[0]


def bit_count(size):
    return size.bit_length() - 1


def swap_dp(value, mask):
    return lax.ppermute(value, "dp", [(i, i ^ mask) for i in range(lax.axis_size("dp"))])


def swap_seq(value, mask):
    return lax.ppermute(value, "seq", [(i, i ^ mask) for i in range(lax.axis_size("seq"))])


def times_left(left, right):
    return lax.dot_general(left, right, (((0,), (0,)), ((), ())), preferred_element_type=jnp.float32)


def column_sum(matrix):
    return jnp.sum(matrix.astype(jnp.float32), axis=0)


def norm_parts(value):
    center = value - jnp.mean(value, axis=-1, keepdims=True)
    spread = jnp.mean(center * center, axis=-1, keepdims=True)
    scale = lax.rsqrt(spread + epsilon)
    return (center * scale, scale)


def norm_back(upstream, normal, scale, gain):
    scaled = upstream * gain
    return scale * (
        scaled
        - jnp.mean(scaled, axis=-1, keepdims=True)
        - normal * jnp.mean(scaled * normal, axis=-1, keepdims=True)
    )


def spread_pairs(first):
    dps, seqs = lax.axis_size("dp"), lax.axis_size("seq")
    pairs = []
    for dp in range(dps):
        for seq in range(seqs):
            piece = first ^ (seq & 1)
            to_dp = (dp & ~1) | (seq >> 1)
            to_seq = 2 * (dp & 1) + piece
            pairs.append((dp * seqs + seq, to_dp * seqs + to_seq))
    return pairs


def to_sequences(local):
    odd = (lax.axis_index("seq") & 1) == 1
    got = []
    for first in range(2):
        piece = jnp.where(odd, local[1 - first], local[first])
        got.append(lax.ppermute(piece, AXES, spread_pairs(first)))
    return jnp.where(odd, jnp.concatenate(got[::-1]), jnp.concatenate(got))


def from_sequences(tokens):
    odd = (lax.axis_index("seq") & 1) == 1
    half = tokens.shape[0] // 2
    got = []
    for first in range(2):
        piece = jnp.where(odd, tokens[(1 - first) * half : (2 - first) * half], tokens[first * half : (first + 1) * half])
        got.append(lax.ppermute(piece, AXES, [(b, a) for a, b in spread_pairs(first)]))
    return jnp.where(odd, jnp.stack(got[::-1]), jnp.stack(got))


class Shards:
    def __init__(self, me, pieces):
        self.me, self.pieces = me, pieces


def whole_shards(part):
    axis = part.ndim - 2
    full = lax.all_gather(part, "dp", axis=axis, tiled=True)
    return Shards(jnp.zeros((1,), jnp.int32), [[p] for p in jnp.split(full, PARTS, axis=axis)])


def my_part():
    return lax.axis_index("dp").astype(jnp.int32)[None]


def direct_shards(part):
    near = [part, swap_dp(part, 2), swap_dp(part, 4), swap_dp(part, 6)]
    pieces = []
    for piece in near:
        pieces += [[piece], [swap_dp(piece, 1)]]
    return Shards(my_part(), pieces)


def start_relay(part):
    return (part, swap_dp(part, 2), swap_dp(part, 4))


def end_relay(own, along_x, along_y):
    rows = own.shape[-2] // 2
    top = swap_dp(lax.slice_in_dim(along_x, 0, rows, axis=own.ndim - 2), 4)
    bottom = swap_dp(lax.slice_in_dim(along_y, rows, 2 * rows, axis=own.ndim - 2), 2)
    pieces = []
    for piece in ([own], [along_x], [along_y], [top, bottom]):
        pieces += [piece, [swap_dp(p, 1) for p in piece]]
    return Shards(my_part(), pieces)


def assemble_body(cuts, counts, me, *refs):
    pieces, outs, sems = refs[: sum(counts)], refs[sum(counts) : -1], refs[-1]
    copies = []
    index = 0
    for place, count in enumerate(counts):
        rows = outs[0].shape[0] // PARTS
        start = (me[0] ^ place) * rows
        for part in range(count):
            ref = pieces[index]
            index += 1
            size = ref.shape[0]
            for out, cut in zip(outs, cuts):
                target = out.at[pl.ds(pl.multiple_of(start + part * size, 16), size), :]
                copy = pltpu.make_async_copy(ref.at[:, cut], target, sems.at[len(copies)])
                copy.start()
                copies.append(copy)
    for copy in copies:
        copy.wait()


def assemble(shards, widths):
    pieces = [p for piece in shards.pieces for p in piece]
    counts = [len(piece) for piece in shards.pieces]
    cuts, start = [], 0
    for width in widths:
        cuts.append(slice(start, start + width))
        start += width
    rows = PARTS * sum(p.shape[0] for p in shards.pieces[0])
    return pl.pallas_call(
        functools.partial(assemble_body, cuts, counts),
        grid_spec=pltpu.PrefetchScalarGridSpec(
            num_scalar_prefetch=1,
            grid=(1,),
            in_specs=[pl.BlockSpec(memory_space=pl.ANY)] * len(pieces),
            out_specs=[pl.BlockSpec(memory_space=pl.ANY)] * len(widths),
            scratch_shapes=[pltpu.SemaphoreType.DMA((len(pieces) * len(widths),))],
        ),
        out_shape=[jax.ShapeDtypeStruct((rows, width), pieces[0].dtype) for width in widths],
        cost_estimate=pl.CostEstimate(flops=0, transcendentals=0, bytes_accessed=4 * rows * sum(widths)),
        name="assemble",
    )(shards.me, *pieces)


def project_body(me, *refs):
    pieces = refs[:PARTS]
    tokens, add, q_ref, k_ref, v_ref, out, held, sems, out_sem = refs[PARTS:]
    width = tokens.shape[1]
    half = width // 2
    rows = width // PARTS
    copies = []
    for place, piece in enumerate(pieces):
        target = pl.ds(pl.multiple_of((me[0] ^ place) * rows, 16), rows)
        for weight in range(3):
            for side in range(2):
                copy = pltpu.make_async_copy(
                    piece.at[weight, :, side * half : (side + 1) * half],
                    held.at[side, target, weight * half : (weight + 1) * half],
                    sems.at[len(copies)],
                )
                copy.start()
                copies.append(copy)
    for copy in copies:
        copy.wait()
    save = pltpu.make_async_copy(held, out, out_sem)
    save.start()
    for weight, ref in ((1, k_ref), (2, v_ref), (0, q_ref)):
        for side in range(2):
            cols = slice(side * half, (side + 1) * half)
            product = nn(tokens[...], held[side, :, weight * half : (weight + 1) * half]) + add[weight : weight + 1, cols]
            ref[:, cols] = product.astype(jnp.bfloat16)
    save.wait()


def project(shards, tokens, add):
    count, width = tokens.shape
    pieces = [p for piece in shards.pieces for p in piece]
    whole = lambda shape: pl.BlockSpec(shape, lambda i, *_: (0,) * len(shape))
    result = jax.ShapeDtypeStruct(tokens.shape, jnp.bfloat16)
    return pl.pallas_call(
        project_body,
        grid_spec=pltpu.PrefetchScalarGridSpec(
            num_scalar_prefetch=1,
            grid=(1,),
            in_specs=[pl.BlockSpec(memory_space=pl.ANY)] * PARTS + [whole(tokens.shape), whole(add.shape)],
            out_specs=[whole(tokens.shape)] * 3 + [pl.BlockSpec(memory_space=pl.ANY)],
            scratch_shapes=[
                pltpu.VMEM((2, width, 3 * width // 2), jnp.bfloat16),
                pltpu.SemaphoreType.DMA((6 * PARTS,)),
                pltpu.SemaphoreType.DMA,
            ],
        ),
        out_shape=[result] * 3 + [jax.ShapeDtypeStruct((2, width, 3 * width // 2), jnp.bfloat16)],
        cost_estimate=pl.CostEstimate(flops=6 * count * width * width, transcendentals=0, bytes_accessed=12 * width * width),
        compiler_params=pltpu.CompilerParams(vmem_limit_bytes=32 << 20),
        name="project",
    )(shards.me, *pieces, tokens, add)


class Reduction:
    def __init__(self, total, order):
        dps, seqs = lax.axis_size("dp"), lax.axis_size("seq")
        nd, ns = bit_count(dps), bit_count(seqs)
        self.left = [("dp", b) for b in reversed(range(nd))] + [("seq", b) for b in reversed(range(ns))]
        self.parts = [total.reshape((2,) * (nd + ns) + (total.shape[0] // (dps * seqs), total.shape[1]))]
        self.order = list(order)

    def send(self):
        axis, bit = step = self.order[0]
        where = self.left.index(step)
        mine = (lax.axis_index(axis) >> bit) & 1
        value = sum(lax.dynamic_index_in_dim(p, 1 - mine, where, keepdims=False).astype(jnp.float32) for p in self.parts)
        self.parts = [lax.dynamic_index_in_dim(p, mine, where, keepdims=False) for p in self.parts]
        self.sent = value.astype(jnp.bfloat16)
        return self.sent

    def move(self, value=None):
        axis, bit = step = self.order.pop(0)
        swap = swap_dp if axis == "dp" else swap_seq
        self.parts.append(swap(self.sent if value is None else value, 1 << bit))
        self.left.remove(step)

    def step(self):
        self.send()
        self.move()

    def finish(self):
        while self.order:
            self.step()
        return sum(p.astype(jnp.float32) for p in self.parts)


def orders():
    nd, ns = bit_count(lax.axis_size("dp")), bit_count(lax.axis_size("seq"))
    seq = [("seq", b) for b in range(ns)]
    up = [("dp", b) for b in range(1, nd)]
    core = [("dp", 0)]
    return core + up + seq, core + up[::-1] + seq


def small_slots(vectors, wide=None):
    devices = lax.axis_size("dp") * lax.axis_size("seq")
    width = vectors[0].shape[0]
    rows = width // devices
    parts = [jnp.stack(vectors).reshape(len(vectors), devices, rows).transpose(1, 0, 2)]
    slot = jnp.pad(parts[0], ((0, 0), (0, 0), (0, LANES - rows)))
    if wide is not None:
        extra = jnp.pad(wide.reshape(devices, 1, -1), ((0, 0), (0, 0), (0, LANES - wide.shape[0] // devices)))
        slot = jnp.concatenate([slot, extra], axis=1)
    return slot


def per_device(
    hidden_in, segment_ids, query_weight, query_bias, key_weight, value_weight, value_bias, out_weight, out_bias,
    first_gain, first_shift, up_weight, up_bias, down_weight, down_bias, second_gain, second_shift, cotangent,
):
    dps, seqs = lax.axis_size("dp"), lax.axis_size("seq")
    direct = dps == PARTS
    width, inner_width = up_weight.shape[1] // 4, up_weight.shape[1]
    rows = query_bias.shape[0]
    qblock = chunk = 256

    qkv_part = jnp.stack([query_weight, key_weight, value_weight])
    qkv_shards = direct_shards(qkv_part) if direct else whole_shards(qkv_part)
    tokens = to_sequences(hidden_in)

    vectors = [query_bias, value_bias, out_bias, first_gain, first_shift, down_bias, second_gain, second_shift]
    line = lax.broadcasted_iota(jnp.int32, (16, up_bias.shape[0]), 0)
    packed = jnp.where(line == 8, up_bias[None, :], jnp.zeros((), jnp.bfloat16))
    for i, vector in enumerate(vectors):
        packed = jnp.where(line == i, jnp.pad(vector, (0, up_bias.shape[0] - rows))[None, :], packed)
    if direct:
        two = jnp.stack([packed, swap_dp(packed, 1)])
        eight = jnp.concatenate([two, swap_dp(two, 2), swap_dp(two, 4), swap_dp(two, 6)])
        packed_all = jnp.take(eight, lax.axis_index("dp") ^ jnp.arange(PARTS), axis=0)
    else:
        packed_all = lax.all_gather(packed, "dp", axis=0)
    packed_all = packed_all.astype(jnp.float32)
    q_add, v_add, out_add, gain_one, shift_one, down_add, gain_two, shift_two = [
        packed_all[:, i, :rows].reshape(-1) for i in range(8)
    ]
    up_add = packed_all[:, 8].reshape(-1)

    core = lax.axis_index("dp") & 1
    place = lax.axis_index("seq")
    segments = jnp.where(core == (place >> 1), segment_ids, swap_dp(segment_ids, 1))
    segment = lax.dynamic_index_in_dim(segments, place & 1, 0, keepdims=False)
    half = segment.shape[0] // 2
    own = lax.dynamic_slice_in_dim(segment, core * half, half)
    other = lax.dynamic_slice_in_dim(segment, (1 - core) * half, half)
    bounds = chunk_bounds(own, other, qblock, chunk)
    row, tiles = own[None, :], segment_tiles(own, other, chunk)

    arrived = [piece[0] for piece in qkv_shards.pieces[2::2]]
    out_weight, up_weight, down_weight, cotangent = lax.optimization_barrier(
        (out_weight, up_weight, down_weight, cotangent, *arrived)
    )[:4]
    out_up = jnp.concatenate([out_weight, up_weight], axis=1)
    if direct:
        out_up_relay = start_relay(out_up)
        down_relay = start_relay(down_weight)
    upstream = to_sequences(cotangent)

    add = jnp.stack([q_add, jnp.zeros_like(q_add), v_add])
    query, keys, values, w_qkv = project(qkv_shards, tokens, jnp.pad(add, ((0, 5), (0, 0))))
    keys_other = swap_dp(keys, 1)
    values_other = swap_dp(values, 1)
    attended, lse = attend_forward(query, keys, values, keys_other, values_other, row, tiles, bounds, qblock, chunk, 3)

    if direct:
        held = lax.optimization_barrier((attended, *out_up_relay))
        attended = held[0]
        wo, wu = assemble(end_relay(*held[1:]), [width, inner_width])
    else:
        wo, wu = assemble(whole_shards(out_up), [width, inner_width])
    residual = tokens.astype(jnp.float32) + (nn(attended, wo) + out_add)
    normal_one, scale_one = norm_parts(residual)
    first = normal_one * gain_one + shift_one
    first_low = first.astype(jnp.bfloat16)
    inner = nn(first_low, wu) + up_add
    cumulative = 0.5 * (1.0 + lax.erf(inner * math.sqrt(0.5)))
    density = jnp.exp(-0.5 * inner * inner) * (1.0 / math.sqrt(2.0 * math.pi))
    active = (inner * cumulative).astype(jnp.bfloat16)
    slope = (cumulative + inner * density).astype(jnp.bfloat16)
    if direct:
        held = lax.optimization_barrier((active, slope, *down_relay))
        active, slope = held[:2]
        (wd,) = assemble(end_relay(*held[2:]), [width])
    else:
        (wd,) = assemble(whole_shards(down_weight), [width])
    second = nn(active, wd) + down_add
    normal_two, scale_two = norm_parts(first + second)
    layer_low = (normal_two * gain_two + shift_two).astype(jnp.bfloat16)

    upstream = upstream.astype(jnp.float32)
    sum_two_grad = norm_back(upstream, normal_two, scale_two, gain_two)
    second_grad = sum_two_grad.astype(jnp.bfloat16)
    order_x, order_y = orders()

    down_total = Reduction(times_left(active, second_grad).astype(jnp.bfloat16), order_x)
    down_total.send()
    second_grad = after(second_grad, down_total.sent)
    down_total.move()
    layer_out = from_sequences(layer_low)
    inner_grad = (nt(second_grad, wd) * slope.astype(jnp.float32)).astype(jnp.bfloat16)
    inner_grad = after(inner_grad, down_total.send())
    down_total.move()
    first_grad = sum_two_grad + nt(inner_grad, wu)
    sum_one_grad = norm_back(first_grad, normal_one, scale_one, gain_one)
    branch_grad = sum_one_grad.astype(jnp.bfloat16)
    attended_grad = nt(branch_grad, wo).astype(jnp.bfloat16)
    sums = [
        column_sum(branch_grad), jnp.sum(first_grad * normal_one, axis=0), jnp.sum(first_grad, axis=0),
        column_sum(second_grad), jnp.sum(upstream * normal_two, axis=0), jnp.sum(upstream, axis=0),
    ]
    slots = small_slots(sums, column_sum(inner_grad))
    share = width // (dps * seqs)
    mixed = jnp.concatenate(
        [times_left(first_low, inner_grad), times_left(attended, branch_grad)], axis=1
    ).astype(jnp.bfloat16)
    up_total = Reduction(mixed, order_y)
    attended_grad = after(attended_grad, up_total.send())
    up_total.move()

    dqs, dvs = [], []
    gradient = sum_one_grad
    qkv_totals = []
    for side in range(2):
        got = attend_back(
            query, keys, values, keys_other, values_other, attended, attended_grad, lse, row, tiles, bounds, qblock, chunk, 3, side
        )
        dk = (got[1] + swap_dp(got[3], 1).astype(jnp.float32)).astype(jnp.bfloat16)
        dv = (got[2] + swap_dp(got[4], 1).astype(jnp.float32)).astype(jnp.bfloat16)
        both = jnp.concatenate([got[0], dk, dv], axis=1)
        total = Reduction(times_left(tokens, both).astype(jnp.bfloat16), order_y if side else order_x)
        qkv_totals.append(total)
        if side == 0:
            attended_grad = after(attended_grad, total.send(), up_total.send(), down_total.send())
            total.move()
            up_total.move()
            down_total.move()
        dqs.append(got[0])
        dvs.append(dv)
        gradient = gradient + nt(both, w_qkv[side])
    input_grad = from_sequences(gradient.astype(jnp.bfloat16)).astype(jnp.float32)
    late = small_slots([jnp.concatenate([column_sum(d) for d in dqs]), jnp.concatenate([column_sum(d) for d in dvs])])
    slots = jnp.concatenate([slots, late], axis=1)
    slots = jnp.pad(slots, ((0, 0), (0, 16 - slots.shape[1]), (0, 0))).astype(jnp.bfloat16)
    small_total = Reduction(slots.reshape(-1, LANES), order_x)

    small = small_total.finish()
    down_grad = down_total.finish()
    mixed_grad = up_total.finish()
    sides = [total.finish() for total in qkv_totals]
    query_grad, key_grad, value_grad = [
        jnp.concatenate([side[:, i * width // 2 : (i + 1) * width // 2] for side in sides], axis=1) for i in range(3)
    ]
    ob, g1, s1, db, g2, s2 = [small[i, :share] for i in range(6)]
    ub = small[6, : inner_width // (dps * seqs)]
    qb, vb = small[7, :share], small[8, :share]
    return (
        layer_out, input_grad, query_grad, qb, key_grad, value_grad, vb, mixed_grad[:, inner_width:], ob, g1, s1,
        mixed_grad[:, :inner_width], ub, down_grad, db, g2, s2,
    )


def solution(mesh):
    wide, flat = P("dp", None), P("dp")
    in_specs = (
        P("dp", "seq", None), wide, wide, flat, wide, wide, flat, wide, flat, flat, flat, wide, flat, wide, flat,
        flat, flat, P("dp", "seq", None),
    )
    rows, cells = P(AXES, None), P(AXES)
    out_specs = (
        P("dp", "seq", None), P("dp", "seq", None), rows, cells, rows, rows, cells, rows, cells, cells, cells, rows,
        cells, rows, cells, cells, cells,
    )
    return jax.shard_map(per_device, mesh=mesh, in_specs=in_specs, out_specs=out_specs, check_vma=False)
```

```python
import functools
import math

import jax
import jax.numpy as jnp
from jax import lax
from jax.experimental import pallas as pl
from jax.experimental.pallas import tpu as pltpu
from jax.sharding import PartitionSpec as P

HEAD_DIM = 64
LANES = 128
NEGATIVE = -1e30


def nt(left, right):
    return lax.dot_general(left, right, (((1,), (1,)), ((), ())), preferred_element_type=jnp.float32)


def nn(left, right):
    return lax.dot_general(left, right, (((1,), (0,)), ((), ())), preferred_element_type=jnp.float32)


def head_parts(block):
    lane = lax.broadcasted_iota(jnp.int32, block.shape, 1)
    zero = jnp.zeros_like(block)
    return (jnp.where(lane < HEAD_DIM, block, zero), jnp.where(lane < HEAD_DIM, zero, block))


def same_document(column_tile, row):
    column = jnp.concatenate([column_tile] * (row.shape[1] // LANES), axis=1)
    return column == jnp.broadcast_to(row, column.shape)


def pair_lanes(pair):
    return slice(pair * LANES, (pair + 1) * LANES)


def chunk_of(bounds, block, step, chunks):
    own = bounds[4 * block + 1] - bounds[4 * block]
    return jnp.where(step < own, bounds[4 * block] + step, chunks + bounds[4 * block + 2] + step - own)


def live_chunks(bounds, block):
    return bounds[4 * block + 1] - bounds[4 * block] + bounds[4 * block + 3] - bounds[4 * block + 2]


def forward_body(qblock, chunk, bounds, q_ref, k_ref, v_ref, ko_ref, vo_ref, sq_ref, sk_ref, o_ref, lse_ref, kall, vt):
    half, lanes = k_ref.shape
    chunks, pairs = half // chunk, lanes // LANES
    for j in range(chunks):
        rows = slice(j * chunk, (j + 1) * chunk)
        kall[j] = k_ref[rows, :]
        kall[chunks + j] = ko_ref[rows, :]
        vt[j] = v_ref[rows, :].T
        vt[chunks + j] = vo_ref[rows, :].T
    for b in range(q_ref.shape[0] // qblock):
        span = slice(b * qblock, (b + 1) * qblock)
        parts = []
        for pair in range(pairs):
            parts += head_parts(q_ref[span, pair_lanes(pair)] * jnp.bfloat16(HEAD_DIM**-0.5))
        row = sq_ref[:, span]

        def one(step, carry):
            j = chunk_of(bounds, b, step, chunks)
            mask = same_document(sk_ref[j], row)
            scores = [jnp.where(mask, nt(kall[j, :, pair_lanes(h // 2)], part), NEGATIVE) for h, part in enumerate(parts)]
            out = []
            for h, score in enumerate(scores):
                top, total, acc = carry[h]
                new_top = jnp.maximum(top, jnp.max(score, axis=0, keepdims=True))
                expo = jnp.exp(score - new_top)
                scale = jnp.exp(top - new_top)
                total = total * scale + jnp.sum(expo, axis=0, keepdims=True)
                acc = acc * scale + nn(vt[j, h * HEAD_DIM : (h + 1) * HEAD_DIM, :], expo.astype(jnp.bfloat16))
                out.append((new_top, total, acc))
            return tuple(out)

        init = (
            jnp.full((1, qblock), NEGATIVE, jnp.float32),
            jnp.zeros((1, qblock), jnp.float32),
            jnp.zeros((HEAD_DIM, qblock), jnp.float32),
        )
        carry = lax.fori_loop(0, live_chunks(bounds, b), one, (init,) * len(parts))
        result = jnp.concatenate([acc / total for _, total, acc in carry], axis=0)
        o_ref[span, :] = result.T.astype(jnp.bfloat16)
        for h, (top, total, _) in enumerate(carry):
            lse_ref[0, h : h + 1, span] = top + jnp.log(total)


def backward_body(
    qblock, chunk, bounds, q_ref, k_ref, v_ref, ko_ref, vo_ref, o_ref, do_ref, lse_ref, sq_ref, sk_ref,
    dq_ref, dk_ref, dv_ref, dko_ref, dvo_ref, kall, vall, kt, dkall, dvall,
):
    half, lanes = k_ref.shape
    chunks, pairs = half // chunk, lanes // LANES
    for j in range(chunks):
        rows = slice(j * chunk, (j + 1) * chunk)
        kall[j] = k_ref[rows, :]
        kall[chunks + j] = ko_ref[rows, :]
        vall[j] = v_ref[rows, :]
        vall[chunks + j] = vo_ref[rows, :]
        kt[j] = k_ref[rows, :].T
        kt[chunks + j] = ko_ref[rows, :].T
    dkall[...] = jnp.zeros_like(dkall)
    dvall[...] = jnp.zeros_like(dvall)
    for b in range(q_ref.shape[0] // qblock):
        span = slice(b * qblock, (b + 1) * qblock)
        parts, dparts, delta = [], [], []
        for pair in range(pairs):
            parts.append(head_parts(q_ref[span, pair_lanes(pair)] * jnp.bfloat16(HEAD_DIM**-0.5)))
            dparts.append(head_parts(do_ref[span, pair_lanes(pair)]))
            product = do_ref[span, pair_lanes(pair)].astype(jnp.float32) * o_ref[span, pair_lanes(pair)].astype(jnp.float32)
            product = product.T
            delta += [jnp.sum(product[h * HEAD_DIM : (h + 1) * HEAD_DIM], axis=0, keepdims=True) for h in range(2)]
        both = [jnp.concatenate(p, axis=0) for p in parts]
        dboth = [jnp.concatenate(p, axis=0) for p in dparts]
        row = sq_ref[:, span]
        lse = [lse_ref[0, h : h + 1, span] for h in range(2 * pairs)]

        def one(step, carry):
            j = chunk_of(bounds, b, step, chunks)
            mask = same_document(sk_ref[j], row)
            out = []
            for pair in range(pairs):
                key, val = kall[j, :, pair_lanes(pair)], vall[j, :, pair_lanes(pair)]
                probs, grads = [], []
                for side in range(2):
                    h = 2 * pair + side
                    score = jnp.where(mask, nt(key, parts[pair][side]), NEGATIVE)
                    prob = jnp.exp(score - lse[h])
                    grad = (prob * (nt(val, dparts[pair][side]) - delta[h])).astype(jnp.bfloat16)
                    probs.append(prob.astype(jnp.bfloat16))
                    grads.append(grad)
                    out.append(carry[h] + nn(kt[j, h * HEAD_DIM : (h + 1) * HEAD_DIM, :], grad))
                dvall[j, :, pair_lanes(pair)] += nn(jnp.concatenate(probs, axis=1), dboth[pair])
                dkall[j, :, pair_lanes(pair)] += nn(jnp.concatenate(grads, axis=1), both[pair])
            return tuple(out)

        zero = jnp.zeros((HEAD_DIM, qblock), jnp.float32)
        carry = lax.fori_loop(0, live_chunks(bounds, b), one, (zero,) * (2 * pairs))
        dq_ref[span, :] = (jnp.concatenate(carry, axis=0).T * HEAD_DIM**-0.5).astype(jnp.bfloat16)
    for j in range(chunks):
        rows = slice(j * chunk, (j + 1) * chunk)
        dk_ref[rows, :] = dkall[j]
        dv_ref[rows, :] = dvall[j]
        dko_ref[rows, :] = dkall[chunks + j].astype(jnp.bfloat16)
        dvo_ref[rows, :] = dvall[chunks + j].astype(jnp.bfloat16)


def chunk_bounds(own, other, qblock, chunk):
    rows = own.reshape(-1, qblock)
    low, high = rows[:, 0], rows[:, -1]
    found = []
    for part in (own, other):
        tiles = part.reshape(-1, chunk)
        live = (tiles[None, :, 0] <= high[:, None]) & (tiles[None, :, -1] >= low[:, None])
        first = jnp.argmax(live, axis=1).astype(jnp.int32)
        found += [first, first + jnp.sum(live, axis=1).astype(jnp.int32)]
    return jnp.stack(found, axis=1).reshape(-1)


def segment_tiles(own, other, chunk):
    both = jnp.concatenate([own, other])
    return jnp.broadcast_to(both[:, None], (both.shape[0], LANES)).reshape(-1, chunk, LANES)


def attend_forward(query, keys, values, keys_other, values_other, row, tiles, bounds, qblock, chunk, pairs):
    tokens, width = query.shape
    half = keys.shape[0]
    lanes = pairs * LANES
    steps = width // lanes
    q = pl.BlockSpec((tokens, lanes), lambda i, *_: (0, i))
    k = pl.BlockSpec((half, lanes), lambda i, *_: (0, i))
    lse = pl.BlockSpec((1, 8, tokens), lambda i, *_: (i, 0, 0))
    area = tokens * half * 2
    return pl.pallas_call(
        functools.partial(forward_body, qblock, chunk),
        grid_spec=pltpu.PrefetchScalarGridSpec(
            num_scalar_prefetch=1,
            grid=(steps,),
            in_specs=[q, k, k, k, k, pl.BlockSpec((1, tokens), lambda i, *_: (0, 0)), pl.BlockSpec(tiles.shape, lambda i, *_: (0, 0, 0))],
            out_specs=[q, lse],
            scratch_shapes=[
                pltpu.VMEM((2 * half // chunk, chunk, lanes), jnp.bfloat16),
                pltpu.VMEM((2 * half // chunk, lanes, chunk), jnp.bfloat16),
            ],
        ),
        out_shape=[
            jax.ShapeDtypeStruct((tokens, width), jnp.bfloat16),
            jax.ShapeDtypeStruct((steps, 8, tokens), jnp.float32),
        ],
        cost_estimate=pl.CostEstimate(flops=4 * area * width, transcendentals=area * width // 64, bytes_accessed=6 * tokens * width * 2),
        compiler_params=pltpu.CompilerParams(vmem_limit_bytes=32 << 20),
        name="attend_forward",
    )(bounds, query, keys, values, keys_other, values_other, row, tiles)


def attend_back(query, keys, values, keys_other, values_other, attended, grad, lse_rows, row, tiles, bounds, qblock, chunk, pairs, side):
    tokens, width = query.shape
    half = keys.shape[0]
    lanes = pairs * LANES
    q = pl.BlockSpec((tokens, lanes), lambda i, *_: (0, side))
    k = pl.BlockSpec((half, lanes), lambda i, *_: (0, side))
    lse = pl.BlockSpec((1, 8, tokens), lambda i, *_: (side, 0, 0))
    to_q = pl.BlockSpec((tokens, lanes), lambda i, *_: (0, 0))
    to_k = pl.BlockSpec((half, lanes), lambda i, *_: (0, 0))
    area = tokens * half * 2
    shape = lambda rows, dtype: jax.ShapeDtypeStruct((rows, lanes), dtype)
    n = 2 * half // chunk
    return pl.pallas_call(
        functools.partial(backward_body, qblock, chunk),
        grid_spec=pltpu.PrefetchScalarGridSpec(
            num_scalar_prefetch=1,
            grid=(1,),
            in_specs=[q, k, k, k, k, q, q, lse, pl.BlockSpec((1, tokens), lambda i, *_: (0, 0)), pl.BlockSpec(tiles.shape, lambda i, *_: (0, 0, 0))],
            out_specs=[to_q, to_k, to_k, to_k, to_k],
            scratch_shapes=[
                pltpu.VMEM((n, chunk, lanes), jnp.bfloat16),
                pltpu.VMEM((n, chunk, lanes), jnp.bfloat16),
                pltpu.VMEM((n, lanes, chunk), jnp.bfloat16),
                pltpu.VMEM((n, chunk, lanes), jnp.float32),
                pltpu.VMEM((n, chunk, lanes), jnp.float32),
            ],
        ),
        out_shape=[
            shape(tokens, jnp.bfloat16), shape(half, jnp.float32), shape(half, jnp.float32), shape(half, jnp.bfloat16), shape(half, jnp.bfloat16),
        ],
        cost_estimate=pl.CostEstimate(flops=10 * area * lanes, transcendentals=area * lanes // 64, bytes_accessed=14 * tokens * lanes * 2),
        compiler_params=pltpu.CompilerParams(vmem_limit_bytes=48 << 20),
        name="attend_back",
    )(bounds, query, keys, values, keys_other, values_other, attended, grad, lse_rows, row, tiles)


AXES = ("dp", "seq")
PARTS = 8
epsilon = 1e-12


def after(value, *others):
    return lax.optimization_barrier((value,) + others)[0]


def bit_count(size):
    return size.bit_length() - 1


def swap_dp(value, mask):
    return lax.ppermute(value, "dp", [(i, i ^ mask) for i in range(lax.axis_size("dp"))])


def swap_seq(value, mask):
    return lax.ppermute(value, "seq", [(i, i ^ mask) for i in range(lax.axis_size("seq"))])


def times_left(left, right):
    return lax.dot_general(left, right, (((0,), (0,)), ((), ())), preferred_element_type=jnp.float32)


def column_sum(matrix):
    return jnp.sum(matrix.astype(jnp.float32), axis=0)


def norm_parts(value):
    center = value - jnp.mean(value, axis=-1, keepdims=True)
    spread = jnp.mean(center * center, axis=-1, keepdims=True)
    scale = lax.rsqrt(spread + epsilon)
    return (center * scale, scale)


def norm_back(upstream, normal, scale, gain):
    scaled = upstream * gain
    return scale * (
        scaled
        - jnp.mean(scaled, axis=-1, keepdims=True)
        - normal * jnp.mean(scaled * normal, axis=-1, keepdims=True)
    )


def spread_pairs(first):
    dps, seqs = lax.axis_size("dp"), lax.axis_size("seq")
    pairs = []
    for dp in range(dps):
        for seq in range(seqs):
            piece = first ^ (seq & 1)
            to_dp = (dp & ~1) | (seq >> 1)
            to_seq = 2 * (dp & 1) + piece
            pairs.append((dp * seqs + seq, to_dp * seqs + to_seq))
    return pairs


def to_sequences(local, order):
    odd = (lax.axis_index("seq") & 1) == 1
    got = []
    pieces = [jnp.where(odd, local[1 - first], local[first]) for first in range(2)]
    order.mark(*pieces)
    for first, piece in enumerate(pieces):
        got.append(lax.ppermute(piece, AXES, spread_pairs(first)))
    return got, odd


def in_order(got, odd, rows):
    return jnp.where(odd, jnp.concatenate([g[:rows] for g in got[::-1]]), jnp.concatenate([g[:rows] for g in got]))


def from_sequences(tokens, order):
    odd = (lax.axis_index("seq") & 1) == 1
    half = tokens.shape[0] // 2
    got = []
    for first in range(2):
        near, far = tokens[first * half : (first + 1) * half], tokens[(1 - first) * half : (2 - first) * half]
        piece = order.mark(jnp.where(order.gate(odd), far, near))
        got.append(lax.ppermute(piece, AXES, [(b, a) for a, b in spread_pairs(first)]))
    return jnp.where(odd, jnp.stack(got[::-1]), jnp.stack(got))


def weight_lines(weights, lines):
    width = weights[0].shape[-1]
    lines = [jnp.pad(v[..., None, :], [(0, 0)] * v.ndim + [(0, width - v.shape[-1])]) for v in lines]
    lines.append(jnp.zeros(lines[0].shape[:-2] + (16 - len(lines), width), jnp.bfloat16))
    return jnp.concatenate(weights + lines, axis=-2)


def shards_of(weights, vectors, order):
    if lax.axis_size("dp") != PARTS:
        gather = lambda v: lax.all_gather(v, "dp", axis=0, tiled=True)
        split = lambda v: gather(v).reshape((PARTS, -1) + v.shape[1:])
        return jnp.zeros((1,), jnp.int32), weight_lines([split(w) for w in weights], [split(v) for v in vectors])
    part = order.mark(weight_lines(order.gate(weights), vectors))
    near = [part, swap_dp(part, 2), swap_dp(part, 4), swap_dp(part, 6)]
    pieces = []
    for piece in near:
        pieces += [piece, swap_dp(piece, 1)]
    return lax.axis_index("dp").astype(jnp.int32)[None], pieces


def project_body(counts, me, *refs):
    devices, rows, wide, vectors = counts
    pieces = refs[: len(refs) - 15]
    tokens, far, q_ref, k_ref, v_ref, ko_ref, vo_ref, out, vec_ref, up_ref, held, small, sems, small_sems, out_sem = refs[len(refs) - 15 :]
    width = tokens.shape[1]
    half = width // 2
    copies = []

    def start(source, target, sem):
        copy = pltpu.make_async_copy(source, target, sem)
        copy.start()
        copies.append(copy)

    for place in range(devices):
        piece = pieces[place] if len(pieces) > 1 else pieces[0].at[place]
        where = me[0] ^ place
        start(piece.at[3 * rows :, :], small.at[where], small_sems.at[place])
        target = pl.ds(where * rows, rows)
        for weight in range(3):
            for side in range(2):
                start(
                    piece.at[weight * rows : (weight + 1) * rows, side * half : (side + 1) * half],
                    held.at[side, target, weight * half : (weight + 1) * half],
                    sems.at[len(copies) - place - 1],
                )
    for copy in copies:
        copy.wait()
    save = pltpu.make_async_copy(held, out, out_sem)
    save.start()
    vec_ref[...] = jnp.concatenate([small[i, :, :rows] for i in range(devices)], axis=1).astype(jnp.float32)
    up_ref[...] = jnp.concatenate([small[i, vectors : vectors + 1, :wide] for i in range(devices)], axis=1).astype(jnp.float32)
    for weight, add, goal, source in ((1, None, k_ref, tokens), (1, None, ko_ref, far), (2, 1, v_ref, tokens), (2, 1, vo_ref, far), (0, 0, q_ref, tokens)):
        for side in range(2):
            cols = slice(side * half, (side + 1) * half)
            product = nn(source[...], held[side, :, weight * half : (weight + 1) * half])
            if add is not None:
                product = product + vec_ref[add : add + 1, cols]
            goal[:, cols] = product.astype(jnp.bfloat16)
    save.wait()


def project(me, pieces, tokens, far, rows, wide, vectors):
    count, width = tokens.shape
    pieces = list(pieces) if isinstance(pieces, list) else [pieces]
    devices = width // rows
    lines = pieces[0].shape[-2] - 3 * rows
    whole = lambda shape: pl.BlockSpec(shape, lambda i, *_: (0,) * len(shape))
    result = jax.ShapeDtypeStruct(tokens.shape, jnp.bfloat16)
    any_space = pl.BlockSpec(memory_space=pl.ANY)
    return pl.pallas_call(
        functools.partial(project_body, (devices, rows, wide, vectors)),
        grid_spec=pltpu.PrefetchScalarGridSpec(
            num_scalar_prefetch=1,
            grid=(1,),
            in_specs=[any_space] * len(pieces) + [whole(tokens.shape)] * 2,
            out_specs=[whole(tokens.shape)] * 5 + [any_space, whole((lines, width)), whole((1, wide * devices))],
            scratch_shapes=[
                pltpu.VMEM((2, width, 3 * width // 2), jnp.bfloat16),
                pltpu.VMEM((devices, lines, width), jnp.bfloat16),
                pltpu.SemaphoreType.DMA((6 * devices,)),
                pltpu.SemaphoreType.DMA((devices,)),
                pltpu.SemaphoreType.DMA,
            ],
        ),
        out_shape=[result] * 5
        + [
            jax.ShapeDtypeStruct((2, width, 3 * width // 2), jnp.bfloat16),
            jax.ShapeDtypeStruct((lines, width), jnp.float32),
            jax.ShapeDtypeStruct((1, wide * devices), jnp.float32),
        ],
        cost_estimate=pl.CostEstimate(flops=10 * count * width * width, transcendentals=0, bytes_accessed=12 * width * width),
        compiler_params=pltpu.CompilerParams(vmem_limit_bytes=32 << 20),
        name="project",
    )(me, *pieces, tokens, far)


class Order:
    def __init__(self):
        self.last = ()

    def gate(self, value):
        return lax.optimization_barrier((value, *self.last))[0] if self.last else value

    def mark(self, *values):
        self.last = values
        return values[0] if len(values) == 1 else values


class Reduction:
    def __init__(self, order, total, steps):
        dps, seqs = lax.axis_size("dp"), lax.axis_size("seq")
        nd, ns = bit_count(dps), bit_count(seqs)
        self.order = order
        self.left = [("dp", b) for b in reversed(range(nd))] + [("seq", b) for b in reversed(range(ns))]
        self.parts = [total.reshape((2,) * (nd + ns) + (total.shape[0] // (dps * seqs), total.shape[1]))]
        self.steps = list(steps)

    def step(self):
        if not self.steps:
            return
        axis, bit = step = self.steps.pop(0)
        where = self.left.index(step)
        mine = self.order.gate((lax.axis_index(axis) >> bit) & 1)
        value = sum(lax.dynamic_index_in_dim(p, 1 - mine, where, keepdims=False).astype(jnp.float32) for p in self.parts)
        self.parts = [lax.dynamic_index_in_dim(p, mine, where, keepdims=False) for p in self.parts]
        value = self.order.mark(value.astype(jnp.bfloat16))
        self.parts.append((swap_dp if axis == "dp" else swap_seq)(value, 1 << bit))
        self.left.remove(step)

    def finish(self):
        while self.steps:
            self.step()
        return sum(p.astype(jnp.float32) for p in self.parts)


def orders():
    nd, ns = bit_count(lax.axis_size("dp")), bit_count(lax.axis_size("seq"))
    seq = [("seq", b) for b in range(ns)]
    up = [("dp", b) for b in range(1, nd)]
    core = [("dp", 0)]
    return core + up + seq, core + up[::-1] + seq


def small_slots(vectors, devices):
    share = vectors[0].shape[0] // devices
    lines = [jnp.pad(v.reshape(devices, 1, -1), ((0, 0), (0, 0), (0, LANES - v.shape[0] // devices))) for v in vectors]
    empty = -len(lines) % share
    lines.append(jnp.zeros((devices, empty, LANES), jnp.float32))
    slots = jnp.concatenate(lines, axis=1).astype(jnp.bfloat16).reshape(devices, -1, share, LANES)
    return jnp.concatenate([slots[:, i] for i in range(slots.shape[1])], axis=-1).reshape(devices * share, -1)


def small_parts(slots, sizes):
    share = slots.shape[0]
    return [slots[j % share, LANES * (j // share) : LANES * (j // share) + size] for j, size in enumerate(sizes)]


def per_device(
    hidden_in, segment_ids, query_weight, query_bias, key_weight, value_weight, value_bias, out_weight, out_bias,
    first_gain, first_shift, up_weight, up_bias, down_weight, down_bias, second_gain, second_shift, cotangent,
):
    dps, seqs = lax.axis_size("dp"), lax.axis_size("seq")
    inner_width, width = up_weight.shape[1], query_weight.shape[1]
    block = hidden_in.shape[1]
    length = segment_ids.shape[1]
    share = width // (dps * seqs)
    qblock = chunk = 256

    ids = segment_ids.astype(jnp.bfloat16).reshape(segment_ids.shape[0], 2, length // 2)
    ids = jnp.pad(ids, ((0, 0), (0, 14), (0, width - length // 2)))
    order = Order()
    got, odd = to_sequences(jnp.concatenate([hidden_in, ids], axis=1), order)

    vectors = [query_bias, value_bias, out_bias, first_gain, first_shift, down_bias, second_gain, second_shift]
    me, pieces = shards_of([query_weight, key_weight, value_weight], vectors + [up_bias], order)

    tokens = in_order(got, odd, block)
    tokens_other = swap_dp(tokens, 1)
    segment = got[0][block : block + 2, : length // 2].astype(jnp.int32)
    core = lax.axis_index("dp") & 1
    half = length // 2
    own = lax.dynamic_index_in_dim(segment, core, 0, keepdims=False)
    other = lax.dynamic_index_in_dim(segment, 1 - core, 0, keepdims=False)
    bounds = chunk_bounds(own, other, qblock, chunk)
    row, tiles = own[None, :], segment_tiles(own, other, chunk)

    weights = lax.all_gather(jnp.concatenate([order.gate(out_weight), up_weight], axis=1), "dp", axis=0, tiled=True)
    wo, wu = weights[:, :width], weights[:, width:]
    wd = lax.all_gather(after(down_weight, tokens), "dp", axis=0, tiled=True)
    got_up, _ = to_sequences(after(cotangent, tokens), order)
    upstream = in_order(got_up, odd, block)

    query, keys, values, keys_other, values_other, w_qkv, vec, up_add = project(
        me, pieces, tokens, tokens_other, width // PARTS, inner_width // PARTS, len(vectors)
    )
    out_add, gain_one, shift_one, down_add, gain_two, shift_two = [vec[i : i + 1] for i in range(2, 8)]
    attended, lse = attend_forward(query, keys, values, keys_other, values_other, row, tiles, bounds, qblock, chunk, 3)

    residual = tokens.astype(jnp.float32) + (nn(attended, wo) + out_add)
    normal_one, scale_one = norm_parts(residual)
    first = normal_one * gain_one + shift_one
    first_low = first.astype(jnp.bfloat16)
    inner = nn(first_low, wu) + up_add
    cumulative = 0.5 * (1.0 + lax.erf(inner * math.sqrt(0.5)))
    density = jnp.exp(-0.5 * inner * inner) * (1.0 / math.sqrt(2.0 * math.pi))
    active = (inner * cumulative).astype(jnp.bfloat16)
    slope = (cumulative + inner * density).astype(jnp.bfloat16)
    second = nn(active, wd) + down_add
    normal_two, scale_two = norm_parts(first + second)
    layer_low = (normal_two * gain_two + shift_two).astype(jnp.bfloat16)

    upstream = upstream.astype(jnp.float32)
    sum_two_grad = norm_back(upstream, normal_two, scale_two, gain_two)
    second_grad = sum_two_grad.astype(jnp.bfloat16)
    steps_x, steps_y = orders()
    order = Order()

    down_total = Reduction(order, times_left(active, second_grad).astype(jnp.bfloat16), steps_x)
    down_total.step()
    inner_grad = nt(order.gate(second_grad), wd) * slope.astype(jnp.float32)
    inner_grad = order.mark(inner_grad.astype(jnp.bfloat16))
    down_total.step()
    up_total = Reduction(order, times_left(first_low, order.gate(inner_grad)).astype(jnp.bfloat16), steps_y)
    up_total.step()
    layer_out = from_sequences(layer_low, order)
    first_grad = sum_two_grad + nt(order.gate(inner_grad), wu)
    sum_one_grad = norm_back(first_grad, normal_one, scale_one, gain_one)
    branch_grad = sum_one_grad.astype(jnp.bfloat16)
    attended_grad = order.mark(nt(branch_grad, wo).astype(jnp.bfloat16))
    up_total.step()
    sums = [
        column_sum(branch_grad), jnp.sum(first_grad * normal_one, axis=0), jnp.sum(first_grad, axis=0),
        column_sum(second_grad), jnp.sum(upstream * normal_two, axis=0), jnp.sum(upstream, axis=0),
    ]
    slots = small_slots(sums + [column_sum(inner_grad)], dps * seqs)
    out_part = times_left(attended, order.gate(branch_grad)).astype(jnp.bfloat16)
    order.mark(slots, out_part)

    def attend(side):
        given = (query, keys, values, keys_other, values_other, attended, order.gate(attended_grad), lse, row, tiles, bounds)
        return order.mark(*attend_back(*given, qblock, chunk, 3, side))

    def exchange(result):
        dq, dk, dv, dk_other, dv_other = result
        dk = (dk + swap_dp(dk_other, 1).astype(jnp.float32)).astype(jnp.bfloat16)
        dv = (dv + swap_dp(dv_other, 1).astype(jnp.float32)).astype(jnp.bfloat16)
        both = jnp.concatenate([dq, dk, dv], axis=1)
        return both, column_sum(dq), column_sum(dv)

    result = attend(0)
    down_total.step()
    first_side, first_query, first_value = exchange(result)
    part = times_left(tokens, first_side).astype(jnp.bfloat16)
    one_total = Reduction(order, jnp.concatenate([part, out_part, slots], axis=1), steps_y)
    one_total.step()
    result = attend(1)
    up_total.step()
    one_total.step()
    second_side, second_query, second_value = exchange(result)
    part = times_left(tokens, second_side).astype(jnp.bfloat16)
    late = [jnp.concatenate([first_query, second_query]), jnp.concatenate([first_value, second_value])]
    two_total = Reduction(order, jnp.concatenate([part, small_slots(late, dps * seqs)], axis=1), steps_x)
    two_total.step()
    down_total.step()
    gradient = sum_one_grad + nt(first_side, w_qkv[0]) + nt(order.gate(second_side), w_qkv[1])
    input_grad = from_sequences(gradient.astype(jnp.bfloat16), order).astype(jnp.float32)
    for total in (two_total, down_total, up_total, one_total, up_total, two_total, two_total, one_total, two_total, one_total):
        total.step()
    down_grad = down_total.finish()
    up_grad = up_total.finish()
    two = two_total.finish()
    one = one_total.finish()
    cut = width // 2
    query_grad, key_grad, value_grad = [
        jnp.concatenate([side[:, i * cut : (i + 1) * cut] for side in (one, two)], axis=1) for i in range(3)
    ]
    ob, g1, s1, db, g2, s2, ub = small_parts(one[:, 3 * cut + width :], [share] * 6 + [inner_width // (dps * seqs)])
    qb, vb = small_parts(two[:, 3 * cut :], [share] * 2)
    return (
        layer_out, input_grad, query_grad, qb, key_grad, value_grad, vb, one[:, 3 * cut : 3 * cut + width], ob, g1, s1,
        up_grad, ub, down_grad, db, g2, s2,
    )


def solution(mesh):
    wide, flat = P("dp", None), P("dp")
    in_specs = (
        P("dp", "seq", None), wide, wide, flat, wide, wide, flat, wide, flat, flat, flat, wide, flat, wide, flat,
        flat, flat, P("dp", "seq", None),
    )
    rows, cells = P(AXES, None), P(AXES)
    out_specs = (
        P("dp", "seq", None), P("dp", "seq", None), rows, cells, rows, rows, cells, rows, cells, cells, cells, rows,
        cells, rows, cells, cells, cells,
    )
    return jax.shard_map(per_device, mesh=mesh, in_specs=in_specs, out_specs=out_specs, check_vma=False)
```

```python
import functools
import math

import jax
import jax.numpy as jnp
from jax import lax
from jax.experimental import pallas as pl
from jax.experimental.pallas import tpu as pltpu
from jax.sharding import PartitionSpec as P

HEAD_DIM = 64
LANES = 128
NEGATIVE = -1e30


def nt(left, right):
    return lax.dot_general(left, right, (((1,), (1,)), ((), ())), preferred_element_type=jnp.float32)


def nn(left, right):
    return lax.dot_general(left, right, (((1,), (0,)), ((), ())), preferred_element_type=jnp.float32)


def head_parts(block):
    lane = lax.broadcasted_iota(jnp.int32, block.shape, 1)
    zero = jnp.zeros_like(block)
    return (jnp.where(lane < HEAD_DIM, block, zero), jnp.where(lane < HEAD_DIM, zero, block))


def same_document(column_tile, row):
    column = jnp.concatenate([column_tile] * (row.shape[1] // LANES), axis=1)
    return column == jnp.broadcast_to(row, column.shape)


def pair_lanes(pair):
    return slice(pair * LANES, (pair + 1) * LANES)


def chunk_of(bounds, block, step, chunks):
    own = bounds[4 * block + 1] - bounds[4 * block]
    return jnp.where(step < own, bounds[4 * block] + step, chunks + bounds[4 * block + 2] + step - own)


def live_chunks(bounds, block):
    return bounds[4 * block + 1] - bounds[4 * block] + bounds[4 * block + 3] - bounds[4 * block + 2]


def forward_body(qblock, chunk, bounds, q_ref, k_ref, v_ref, ko_ref, vo_ref, sq_ref, sk_ref, o_ref, lse_ref, kall, vt):
    half, lanes = k_ref.shape
    chunks, pairs = half // chunk, lanes // LANES
    for j in range(chunks):
        rows = slice(j * chunk, (j + 1) * chunk)
        kall[j] = k_ref[rows, :]
        kall[chunks + j] = ko_ref[rows, :]
        vt[j] = v_ref[rows, :].T
        vt[chunks + j] = vo_ref[rows, :].T
    for b in range(q_ref.shape[0] // qblock):
        span = slice(b * qblock, (b + 1) * qblock)
        parts = []
        for pair in range(pairs):
            parts += head_parts(q_ref[span, pair_lanes(pair)] * jnp.bfloat16(HEAD_DIM**-0.5))
        row = sq_ref[:, span]

        def one(step, carry):
            j = chunk_of(bounds, b, step, chunks)
            mask = same_document(sk_ref[j], row)
            scores = [jnp.where(mask, nt(kall[j, :, pair_lanes(h // 2)], part), NEGATIVE) for h, part in enumerate(parts)]
            out = []
            for h, score in enumerate(scores):
                top, total, acc = carry[h]
                new_top = jnp.maximum(top, jnp.max(score, axis=0, keepdims=True))
                expo = jnp.exp(score - new_top)
                scale = jnp.exp(top - new_top)
                total = total * scale + jnp.sum(expo, axis=0, keepdims=True)
                acc = acc * scale + nn(vt[j, h * HEAD_DIM : (h + 1) * HEAD_DIM, :], expo.astype(jnp.bfloat16))
                out.append((new_top, total, acc))
            return tuple(out)

        init = (
            jnp.full((1, qblock), NEGATIVE, jnp.float32),
            jnp.zeros((1, qblock), jnp.float32),
            jnp.zeros((HEAD_DIM, qblock), jnp.float32),
        )
        carry = lax.fori_loop(0, live_chunks(bounds, b), one, (init,) * len(parts))
        result = jnp.concatenate([acc / total for _, total, acc in carry], axis=0)
        o_ref[span, :] = result.T.astype(jnp.bfloat16)
        for h, (top, total, _) in enumerate(carry):
            lse_ref[0, h : h + 1, span] = top + jnp.log(total)


def backward_body(
    qblock, chunk, bounds, q_ref, k_ref, v_ref, ko_ref, vo_ref, o_ref, do_ref, lse_ref, sq_ref, sk_ref,
    dq_ref, dk_ref, dv_ref, far_ref, kall, vall, kt, dkall, dvall,
):
    half, lanes = k_ref.shape
    chunks, pairs = half // chunk, lanes // LANES
    for j in range(chunks):
        rows = slice(j * chunk, (j + 1) * chunk)
        kall[j] = k_ref[rows, :]
        kall[chunks + j] = ko_ref[rows, :]
        vall[j] = v_ref[rows, :]
        vall[chunks + j] = vo_ref[rows, :]
        kt[j] = k_ref[rows, :].T
        kt[chunks + j] = ko_ref[rows, :].T
    dkall[...] = jnp.zeros_like(dkall)
    dvall[...] = jnp.zeros_like(dvall)
    for b in range(q_ref.shape[0] // qblock):
        span = slice(b * qblock, (b + 1) * qblock)
        parts, dparts, delta = [], [], []
        for pair in range(pairs):
            parts.append(head_parts(q_ref[span, pair_lanes(pair)] * jnp.bfloat16(HEAD_DIM**-0.5)))
            dparts.append(head_parts(do_ref[span, pair_lanes(pair)]))
            product = do_ref[span, pair_lanes(pair)].astype(jnp.float32) * o_ref[span, pair_lanes(pair)].astype(jnp.float32)
            product = product.T
            delta += [jnp.sum(product[h * HEAD_DIM : (h + 1) * HEAD_DIM], axis=0, keepdims=True) for h in range(2)]
        both = [jnp.concatenate(p, axis=0) for p in parts]
        dboth = [jnp.concatenate(p, axis=0) for p in dparts]
        row = sq_ref[:, span]
        lse = [lse_ref[0, h : h + 1, span] for h in range(2 * pairs)]

        def one(step, carry):
            j = chunk_of(bounds, b, step, chunks)
            mask = same_document(sk_ref[j], row)
            out = []
            for pair in range(pairs):
                key, val = kall[j, :, pair_lanes(pair)], vall[j, :, pair_lanes(pair)]
                probs, grads = [], []
                for side in range(2):
                    h = 2 * pair + side
                    score = jnp.where(mask, nt(key, parts[pair][side]), NEGATIVE)
                    prob = jnp.exp(score - lse[h])
                    grad = (prob * (nt(val, dparts[pair][side]) - delta[h])).astype(jnp.bfloat16)
                    probs.append(prob.astype(jnp.bfloat16))
                    grads.append(grad)
                    out.append(carry[h] + nn(kt[j, h * HEAD_DIM : (h + 1) * HEAD_DIM, :], grad))
                dvall[j, :, pair_lanes(pair)] += nn(jnp.concatenate(probs, axis=1), dboth[pair])
                dkall[j, :, pair_lanes(pair)] += nn(jnp.concatenate(grads, axis=1), both[pair])
            return tuple(out)

        zero = jnp.zeros((HEAD_DIM, qblock), jnp.float32)
        carry = lax.fori_loop(0, live_chunks(bounds, b), one, (zero,) * (2 * pairs))
        dq_ref[span, :] = (jnp.concatenate(carry, axis=0).T * HEAD_DIM**-0.5).astype(jnp.bfloat16)
    for j in range(chunks):
        rows = slice(j * chunk, (j + 1) * chunk)
        dk_ref[rows, :] = dkall[j]
        dv_ref[rows, :] = dvall[j]
        far_ref[0, rows, :] = dkall[chunks + j].astype(jnp.bfloat16)
        far_ref[1, rows, :] = dvall[chunks + j].astype(jnp.bfloat16)


def chunk_bounds(own, other, qblock, chunk):
    rows = own.reshape(-1, qblock)
    low, high = rows[:, 0], rows[:, -1]
    found = []
    for part in (own, other):
        tiles = part.reshape(-1, chunk)
        live = (tiles[None, :, 0] <= high[:, None]) & (tiles[None, :, -1] >= low[:, None])
        first = jnp.argmax(live, axis=1).astype(jnp.int32)
        found += [first, first + jnp.sum(live, axis=1).astype(jnp.int32)]
    return jnp.stack(found, axis=1).reshape(-1)


def segment_tiles(own, other, chunk):
    both = jnp.concatenate([own, other])
    return jnp.broadcast_to(both[:, None], (both.shape[0], LANES)).reshape(-1, chunk, LANES)


def attend_forward(query, keys, values, keys_other, values_other, row, tiles, bounds, qblock, chunk, pairs):
    tokens, width = query.shape
    half = keys.shape[0]
    lanes = pairs * LANES
    steps = width // lanes
    q = pl.BlockSpec((tokens, lanes), lambda i, *_: (0, i))
    k = pl.BlockSpec((half, lanes), lambda i, *_: (0, i))
    lse = pl.BlockSpec((1, 8, tokens), lambda i, *_: (i, 0, 0))
    area = tokens * half * 2
    return pl.pallas_call(
        functools.partial(forward_body, qblock, chunk),
        grid_spec=pltpu.PrefetchScalarGridSpec(
            num_scalar_prefetch=1,
            grid=(steps,),
            in_specs=[q, k, k, k, k, pl.BlockSpec((1, tokens), lambda i, *_: (0, 0)), pl.BlockSpec(tiles.shape, lambda i, *_: (0, 0, 0))],
            out_specs=[q, lse],
            scratch_shapes=[
                pltpu.VMEM((2 * half // chunk, chunk, lanes), jnp.bfloat16),
                pltpu.VMEM((2 * half // chunk, lanes, chunk), jnp.bfloat16),
            ],
        ),
        out_shape=[
            jax.ShapeDtypeStruct((tokens, width), jnp.bfloat16),
            jax.ShapeDtypeStruct((steps, 8, tokens), jnp.float32),
        ],
        cost_estimate=pl.CostEstimate(flops=1, transcendentals=0, bytes_accessed=1),
        compiler_params=pltpu.CompilerParams(vmem_limit_bytes=32 << 20),
        name="attend_forward",
    )(bounds, query, keys, values, keys_other, values_other, row, tiles)


def attend_back(query, keys, values, keys_other, values_other, attended, grad, lse_rows, row, tiles, bounds, qblock, chunk, pairs, side):
    tokens, width = query.shape
    half = keys.shape[0]
    lanes = pairs * LANES
    q = pl.BlockSpec((tokens, lanes), lambda i, *_: (0, side))
    k = pl.BlockSpec((half, lanes), lambda i, *_: (0, side))
    lse = pl.BlockSpec((1, 8, tokens), lambda i, *_: (side, 0, 0))
    to_q = pl.BlockSpec((tokens, lanes), lambda i, *_: (0, 0))
    to_k = pl.BlockSpec((half, lanes), lambda i, *_: (0, 0))
    area = tokens * half * 2
    shape = lambda rows, dtype: jax.ShapeDtypeStruct((rows, lanes), dtype)
    n = 2 * half // chunk
    return pl.pallas_call(
        functools.partial(backward_body, qblock, chunk),
        grid_spec=pltpu.PrefetchScalarGridSpec(
            num_scalar_prefetch=1,
            grid=(1,),
            in_specs=[q, k, k, k, k, q, q, lse, pl.BlockSpec((1, tokens), lambda i, *_: (0, 0)), pl.BlockSpec(tiles.shape, lambda i, *_: (0, 0, 0))],
            out_specs=[to_q, to_k, to_k, pl.BlockSpec((2, half, lanes), lambda i, *_: (0, 0, 0))],
            scratch_shapes=[
                pltpu.VMEM((n, chunk, lanes), jnp.bfloat16),
                pltpu.VMEM((n, chunk, lanes), jnp.bfloat16),
                pltpu.VMEM((n, lanes, chunk), jnp.bfloat16),
                pltpu.VMEM((n, chunk, lanes), jnp.float32),
                pltpu.VMEM((n, chunk, lanes), jnp.float32),
            ],
        ),
        out_shape=[
            shape(tokens, jnp.bfloat16), shape(half, jnp.float32), shape(half, jnp.float32), jax.ShapeDtypeStruct((2, half, lanes), jnp.bfloat16),
        ],
        cost_estimate=pl.CostEstimate(flops=1, transcendentals=0, bytes_accessed=1),
        compiler_params=pltpu.CompilerParams(vmem_limit_bytes=48 << 20),
        name="attend_back",
    )(bounds, query, keys, values, keys_other, values_other, attended, grad, lse_rows, row, tiles)


AXES = ("dp", "seq")
PARTS = 8
SHARDS = 6
epsilon = 1e-12


def tn(left, right):
    return lax.dot_general(left, right, (((0,), (0,)), ((), ())), preferred_element_type=jnp.float32)


def norm_parts(value):
    center = value - jnp.mean(value, axis=-1, keepdims=True)
    spread = jnp.mean(center * center, axis=-1, keepdims=True)
    scale = lax.rsqrt(spread + epsilon)
    return (center * scale, scale)


def norm_back(upstream, normal, scale, gain):
    scaled = upstream * gain
    return scale * (
        scaled
        - jnp.mean(scaled, axis=-1, keepdims=True)
        - normal * jnp.mean(scaled * normal, axis=-1, keepdims=True)
    )


def row_sum(matrix):
    return jnp.sum(matrix.astype(jnp.float32), axis=0, keepdims=True)


def parts_of(refs):
    own, own_far, near_x, near_y, near_d, far = refs
    rows = own.shape[0]
    near = [(ref, 0, rows) for ref in (own, own_far, near_x, near_y, near_d)]
    other = [(far, i * rows, rows) for i in range(3)]
    return [near[0], near[1], near[2], other[0], near[3], other[1], near[4], other[2]]


def load_pieces(me, pieces, targets, sems):
    copies = [[] for _ in targets]
    for place, (ref, first, rows) in enumerate(pieces):
        where = pl.ds(pl.multiple_of((me ^ place) * rows, 32), rows)
        for i, (target, columns) in enumerate(targets):
            copy = pltpu.make_async_copy(ref.at[first : first + rows, columns], target.at[where, :], sems.at[i, place])
            copy.start()
            copies[i].append(copy)
    return copies


def wait_all(copies):
    for copy in copies:
        copy.wait()


def step_of(block, size):
    return pl.ds(pl.multiple_of(block * size, size), size)


BLOCK = 256
ROWS = 256


def widen_body(scalars, *refs):
    pieces = parts_of(refs[:SHARDS])
    (attended, tokens, vec, up_add, normal_ref, scale_ref, low_ref, active_ref, slope_ref, wo_out, wu_out, wo, wu, sems, out_sems) = refs[SHARDS:]
    width, wide = wu.shape
    loads = load_pieces(scalars[0], pieces, [(wo, slice(0, width)), (wu, slice(width, width + wide))], sems)
    wait_all(loads[0])

    @pl.loop(0, tokens.shape[0] // ROWS)
    def _(i):
        rows = step_of(i, ROWS)
        branch = nn(attended[rows, :], wo[...]) + vec[2:3, :]
        normal, scale = norm_parts(tokens[rows, :].astype(jnp.float32) + branch)
        first = normal * vec[3:4, :] + vec[4:5, :]
        normal_ref[rows, :] = normal
        scale_ref[rows, :] = jnp.broadcast_to(scale, (ROWS, LANES))
        low_ref[rows, :] = first.astype(jnp.bfloat16)

    wait_all(loads[1])
    saves = [pltpu.make_async_copy(wo, wo_out, out_sems.at[0]), pltpu.make_async_copy(wu, wu_out, out_sems.at[1])]
    for save in saves:
        save.start()

    @pl.loop(0, wide // BLOCK)
    def _(j):
        cols = step_of(j, BLOCK)
        inner = nn(low_ref[...], wu[:, cols]) + up_add[:, cols]
        cumulative = 0.5 * (1.0 + lax.erf(inner * math.sqrt(0.5)))
        density = jnp.exp(-0.5 * inner * inner) * (1.0 / math.sqrt(2.0 * math.pi))
        active_ref[:, cols] = (inner * cumulative).astype(jnp.bfloat16)
        slope_ref[:, cols] = (cumulative + inner * density).astype(jnp.bfloat16)

    wait_all(saves)


def narrow_body(scalars, *refs):
    pieces = parts_of(refs[:SHARDS])
    (active, normal_one, vec, upstream, out_ref, grad_ref, low_ref, sums_ref, send_ref, keep_ref, wd_out, wd, sums, sems, out_sem) = refs[SHARDS:]
    wide, width = wd.shape
    (loads,) = load_pieces(scalars[0], pieces, [(wd, slice(0, width))], sems)
    wait_all(loads)
    save = pltpu.make_async_copy(wd, wd_out, out_sem)
    save.start()
    sums[...] = jnp.zeros_like(sums)

    @pl.loop(0, normal_one.shape[0] // ROWS)
    def _(i):
        rows = step_of(i, ROWS)
        second = nn(active[rows, :], wd[...]) + vec[5:6, :]
        normal, scale = norm_parts(normal_one[rows, :] * vec[3:4, :] + vec[4:5, :] + second)
        out_ref[rows, :] = (normal * vec[6:7, :] + vec[7:8, :]).astype(jnp.bfloat16)
        up = upstream[rows, :].astype(jnp.float32)
        grad = norm_back(up, normal, scale, vec[6:7, :])
        low = grad.astype(jnp.bfloat16)
        grad_ref[rows, :] = grad
        low_ref[rows, :] = low
        sums[0:1, :] += row_sum(low)
        sums[1:2, :] += row_sum(up * normal)
        sums[2:3, :] += row_sum(up)

    sums_ref[...] = sums[...]
    size = wide // PARTS

    @pl.loop(0, PARTS // 2)
    def _(i):
        send_ref[i] = tn(active[:, step_of(2 * i + 1 - scalars[1], size)], low_ref[...]).astype(jnp.bfloat16)
        keep_ref[i] = tn(active[:, step_of(2 * i + scalars[1], size)], low_ref[...]).astype(jnp.bfloat16)

    save.wait()


def turn_parts(core, turned, ordered):
    for i in range(PARTS // 2):
        ordered[0, i] = turned[2 * i + 1 - core]
        ordered[1, i] = turned[2 * i + core]


def inner_back_body(scalars, low, wd, slope, first_low, grad_ref, sums_ref, send_ref, keep_ref, turned, ordered):
    size = first_low.shape[1] // PARTS
    flipped = first_low[...].T
    for i in range(PARTS):
        turned[i] = flipped[i * size : (i + 1) * size, :]
    turn_parts(scalars[1], turned, ordered)
    rows = (PARTS // 2) * size

    @pl.loop(0, slope.shape[1] // BLOCK)
    def _(j):
        cols = step_of(j, BLOCK)
        grad = (nt(low[...], wd[cols, :]) * slope[:, cols].astype(jnp.float32)).astype(jnp.bfloat16)
        grad_ref[:, cols] = grad
        sums_ref[:, cols] = row_sum(grad)
        for side, ref in enumerate((send_ref, keep_ref)):
            left = ordered[side].reshape(rows, low.shape[0])
            ref[:, :, cols] = nn(left, grad).astype(jnp.bfloat16).reshape(PARTS // 2, size, BLOCK)


def outer_back_body(scalars, grad, wu, up_grad, normal_ref, scale_ref, vec, wo, attended, sum_ref, result_ref, sums_ref, send_ref, keep_ref, low, sums, turned):
    width = wo.shape[0]
    sums[...] = jnp.zeros_like(sums)

    @pl.loop(0, grad.shape[0] // ROWS)
    def _(i):
        rows = step_of(i, ROWS)
        first = up_grad[rows, :] + nt(grad[rows, :], wu[...])
        normal = normal_ref[rows, :]
        total = norm_back(first, normal, scale_ref[rows, 0:1], vec[3:4, :])
        branch = total.astype(jnp.bfloat16)
        sum_ref[rows, :] = total
        low[rows, :] = branch
        result_ref[rows, :] = nt(branch, wo[...]).astype(jnp.bfloat16)
        sums[0:1, :] += row_sum(branch)
        sums[1:2, :] += row_sum(first * normal)
        sums[2:3, :] += row_sum(first)

    sums_ref[...] = sums[...]
    size = width // PARTS
    product = tn(attended[...], low[...]).astype(jnp.bfloat16)
    for i in range(PARTS):
        turned[i] = product[i * size : (i + 1) * size, :]
    for i in range(PARTS // 2):
        send_ref[i] = turned[2 * i + 1 - scalars[1]]
        keep_ref[i] = turned[2 * i + scalars[1]]


def whole_call(body, name, scalars, hbm, inputs, outputs, hbm_outputs, scratch, flops):
    shape_of = lambda x: jax.ShapeDtypeStruct(x.shape, x.dtype)
    full = lambda x: pl.BlockSpec(x.shape, lambda i, *_, n=len(x.shape): (0,) * n)
    stay = pl.BlockSpec(memory_space=pl.ANY)
    return pl.pallas_call(
        body,
        grid_spec=pltpu.PrefetchScalarGridSpec(
            num_scalar_prefetch=1,
            grid=(1,),
            in_specs=[stay] * len(hbm) + [full(x) for x in inputs],
            out_specs=[full(x) for x in outputs] + [stay] * len(hbm_outputs),
            scratch_shapes=scratch,
        ),
        out_shape=[shape_of(x) for x in list(outputs) + list(hbm_outputs)],
        cost_estimate=pl.CostEstimate(flops=flops, transcendentals=0, bytes_accessed=1),
        compiler_params=pltpu.CompilerParams(vmem_limit_bytes=56 << 20),
        name=name,
    )(scalars, *hbm, *inputs)


def array(dtype, *shape):
    return jax.ShapeDtypeStruct(shape, dtype)


def widen(scalars, pieces, attended, tokens, vec, up_add):
    count, width = tokens.shape
    wide = up_add.shape[1]
    f32, b16 = jnp.float32, jnp.bfloat16
    return whole_call(
        widen_body, "widen", scalars, pieces, [attended, tokens, vec, up_add],
        [array(f32, count, width), array(f32, count, LANES), array(b16, count, width),
         array(b16, count, wide), array(b16, count, wide)],
        [array(b16, width, width), array(b16, width, wide)],
        [pltpu.VMEM((width, width), b16), pltpu.VMEM((width, wide), b16), pltpu.SemaphoreType.DMA((2, PARTS)),
         pltpu.SemaphoreType.DMA((2,))], 1,
    )


def narrow(scalars, pieces, active, normal, vec, upstream):
    count, wide = active.shape
    width = normal.shape[1]
    f32, b16 = jnp.float32, jnp.bfloat16
    half = array(b16, PARTS // 2, wide // PARTS, width)
    return whole_call(
        narrow_body, "narrow", scalars, pieces, [active, normal, vec, upstream],
        [array(b16, count, width), array(f32, count, width), array(b16, count, width), array(f32, 8, width), half, half],
        [array(b16, wide, width)],
        [pltpu.VMEM((wide, width), b16), pltpu.VMEM((8, width), f32), pltpu.SemaphoreType.DMA((1, PARTS)), pltpu.SemaphoreType.DMA], 1,
    )


def inner_back(scalars, low, wd, slope, first_low):
    count, wide = slope.shape
    width = low.shape[1]
    size = width // PARTS
    f32, b16 = jnp.float32, jnp.bfloat16
    half = array(b16, PARTS // 2, size, wide)
    return whole_call(
        inner_back_body, "inner_back", scalars, [], [low, wd, slope, first_low],
        [array(b16, count, wide), array(f32, 1, wide), half, half], [],
        [pltpu.VMEM((PARTS, size, count), b16), pltpu.VMEM((2, PARTS // 2, size, count), b16)], 1,
    )


def outer_back(scalars, grad, wu, up_grad, normal, scale, vec, wo, attended):
    count, width = normal.shape
    f32, b16 = jnp.float32, jnp.bfloat16
    half = array(b16, PARTS // 2, width // PARTS, width)
    return whole_call(
        outer_back_body, "outer_back", scalars, [], [grad, wu, up_grad, normal, scale, vec, wo, attended],
        [array(f32, count, width), array(b16, count, width), array(f32, 8, width), half, half], [],
        [pltpu.VMEM((count, width), b16), pltpu.VMEM((8, width), f32), pltpu.VMEM((PARTS, width // PARTS, width), b16)], 1,
    )


def split_rows(core, parts, send, keep, cols):
    for i in range(PARTS // 2):
        send[i, :, cols] = parts[2 * i + 1 - core]
        keep[i, :, cols] = parts[2 * i + core]


def sums_to_slots(core, lines, parts, send, keep, first):
    turned = lines[...].T.astype(jnp.bfloat16)
    rows = turned.shape[0] // PARTS
    for i in range(PARTS):
        parts[i] = turned[i * rows : (i + 1) * rows, :]
    split_rows(core, parts, send, keep, slice(first, first + LANES))


def qkv_back_body(side, scalars, dq, dk, dv, far, ordered, weight, gradient, *refs):
    core = scalars[1]
    if side == 0:
        out_send, out_keep, sums_one, sums_two, wide_sums, send, keep, result, sums_ref, both, lines, parts = refs
    else:
        first_sums, send, keep, result, sums_ref, both, lines, parts = refs
    half = dq.shape[1]
    both[:, :half] = dq[...]
    both[:, half : 2 * half] = (dk[...] + far[0].astype(jnp.float32)).astype(jnp.bfloat16)
    both[:, 2 * half :] = (dv[...] + far[1].astype(jnp.float32)).astype(jnp.bfloat16)
    sums_ref[...] = jnp.zeros_like(sums_ref)
    sums_ref[0:1, :] = row_sum(dq[...])
    sums_ref[1:2, :] = row_sum(both[:, 2 * half :])
    rows = ordered.shape[1] * ordered.shape[2]
    for i, ref in enumerate((send, keep)):
        left = ordered[i].reshape(rows, ordered.shape[3])
        product = nn(left, both[...]).astype(jnp.bfloat16)
        ref[:, :, : 3 * half] = product.reshape(ordered.shape[1], ordered.shape[2], 3 * half)
    lines[...] = jnp.zeros_like(lines)
    if side == 0:
        width = out_send.shape[2]
        send[:, :, 3 * half : 3 * half + width] = out_send[...]
        keep[:, :, 3 * half : 3 * half + width] = out_keep[...]
        lines[0:8, :] = sums_one[...]
        lines[8:16, :] = sums_two[...]
        lines[16:24, :] = wide_sums[...]
        sums_to_slots(core, lines, parts, send, keep, 3 * half + width)
    else:
        lines[0:8, :half] = first_sums[...]
        lines[0:8, half:] = sums_ref[...]
        sums_to_slots(core, lines, parts, send, keep, 3 * half)
    result[...] = (gradient[...] + nt(both[...], weight[side])).astype(result.dtype)


def qkv_back(side, scalars, dq, dk, dv, far, ordered, weights, gradient, *more):
    count, half = dq.shape
    width = gradient.shape[1]
    f32, b16 = jnp.float32, jnp.bfloat16
    total = array(b16, PARTS // 2, width // PARTS, 3 * half + LANES + (width if side == 0 else 0))
    return whole_call(
        functools.partial(qkv_back_body, side), "qkv_back", scalars, [], [dq, dk, dv, far, ordered, weights, gradient, *more],
        [total, total, array(b16 if side else f32, count, width), array(f32, 8, half)], [],
        [pltpu.VMEM((count, 3 * half), b16), pltpu.VMEM((LANES, width), f32), pltpu.VMEM((PARTS, width // PARTS, LANES), b16)], 1,
    )


STRIPE = 32


def fold_body(plans, scalars, *refs):
    for item, (outer, inner, bit) in enumerate(plans):
        keep, got = refs[2 * item : 2 * item + 2]
        send, left = refs[2 * (len(plans) + item) : 2 * (len(plans) + item) + 2]
        mine = scalars[bit]
        rows = keep.shape[1]
        stripe = STRIPE if rows % STRIPE == 0 else rows

        @pl.loop(0, rows // stripe)
        def _(k):
            span = step_of(k, stripe) if stripe != rows else slice(None)
            for i in range(outer):
                for j in range(inner):
                    for target, side in ((send, 1 - mine), (left, mine)):
                        place = (2 * i + side) * inner + j
                        value = keep[place, span, :].astype(jnp.float32) + got[place, span, :].astype(jnp.float32)
                        target[i * inner + j, span, :] = value.astype(target.dtype)


def fold(scalars, items):
    outs, plans = [], []
    for keep, got, (outer, inner, bit) in items:
        shape = (keep.shape[0] // 2,) + keep.shape[1:]
        outs += [array(jnp.bfloat16, *shape), array(keep.dtype, *shape)]
        plans.append((outer, inner, bit))
    got = whole_call(
        functools.partial(fold_body, plans), "fold", scalars, [], [x for keep, got, _ in items for x in (keep, got)], outs, [], [], 1
    )
    return [(got[2 * i], got[2 * i + 1]) for i in range(len(items))]


def merge_body(shapes, scalars, *refs):
    send, left = refs[-2:]
    mine = scalars[4]
    low = send.shape[1]
    first = 0
    for item, (rows, wide) in enumerate(shapes):
        keep, got = refs[2 * item : 2 * item + 2]
        for part in range(rows // low):
            span = slice(part * low, (part + 1) * low)
            for high in range(2):
                for target, side in ((send, 1 - mine), (left, mine)):
                    value = keep[2 * high + side, span, :].astype(jnp.float32) + got[2 * high + side, span, :].astype(jnp.float32)
                    target[high, :, first : first + wide] = value.astype(target.dtype)
            first += wide


def merge(scalars, items, low):
    items = [(k.reshape(4, k.shape[-2] // 4, k.shape[-1]), g.reshape(4, g.shape[-2] // 4, g.shape[-1])) for k, g in items]
    shapes = [k.shape[1:] for k, _ in items]
    wide = sum(rows // low * n for rows, n in shapes)
    return whole_call(
        functools.partial(merge_body, shapes), "merge", scalars, [], [x for pair in items for x in pair],
        [array(jnp.bfloat16, 2, low, wide), array(jnp.float32, 2, low, wide)], [], [], 1,
    )


def last_ff_body(scalars, keep, got, down_ref, up_ref):
    low = keep.shape[1]
    width = down_ref.shape[1]
    for part in range(down_ref.shape[0] // low):
        cols = slice(part * width, (part + 1) * width)
        down_ref[part * low : (part + 1) * low, :] = keep[0, :, cols] + got[0, :, cols].astype(jnp.float32)
    cols = slice(4 * width, 4 * width + up_ref.shape[1])
    up_ref[...] = keep[0, :, cols] + got[0, :, cols].astype(jnp.float32)


def last_ff(scalars, keep, got, width):
    low = keep.shape[1]
    return whole_call(
        last_ff_body, "last_ff", scalars, [], [keep, got], [array(jnp.float32, 4 * low, width), array(jnp.float32, low, 4 * width)], [], [], 1
    )


def last_qkv_body(scalars, keep, got, query_ref, key_ref, value_ref, out_ref, small_ref, late_ref, turned):
    low = keep.shape[1]
    width = query_ref.shape[1]
    half = width // 2
    second = 3 * half + width + LANES

    def total(first, size):
        return keep[0, :, first : first + size] + got[0, :, first : first + size].astype(jnp.float32)

    for i, ref in enumerate((query_ref, key_ref, value_ref)):
        ref[:, :half] = total(i * half, half)
        ref[:, half:] = total(second + i * half, half)
    out_ref[...] = total(3 * half, width)
    for ref, first in ((small_ref, 3 * half + width), (late_ref, second + 3 * half)):
        turned[...] = jnp.zeros_like(turned)
        turned[:low, :] = total(first, LANES)
        ref[...] = turned[...].T[: ref.shape[0], :]


def last_qkv(scalars, keep, got, width):
    low = keep.shape[1]
    f32 = jnp.float32
    return whole_call(
        last_qkv_body, "last_qkv", scalars, [], [keep, got],
        [array(f32, low, width)] * 4 + [array(f32, 24, LANES), array(f32, 8, LANES)], [], [pltpu.VMEM((LANES, LANES), f32)], 1,
    )


def after(value, *others):
    return lax.optimization_barrier((value,) + others)[0]


def bit_count(size):
    return size.bit_length() - 1


def swap_dp(value, mask):
    return lax.ppermute(value, "dp", [(i, i ^ mask) for i in range(lax.axis_size("dp"))])


def swap_seq(value, mask):
    return lax.ppermute(value, "seq", [(i, i ^ mask) for i in range(lax.axis_size("seq"))])


def column_sum(matrix):
    return jnp.sum(matrix.astype(jnp.float32), axis=0)


def spread_pairs(first):
    dps, seqs = lax.axis_size("dp"), lax.axis_size("seq")
    pairs = []
    for dp in range(dps):
        for seq in range(seqs):
            piece = first ^ (seq & 1)
            to_dp = (dp & ~1) | (seq >> 1)
            to_seq = 2 * (dp & 1) + piece
            pairs.append((dp * seqs + seq, to_dp * seqs + to_seq))
    return pairs


def to_sequences(local, order):
    odd = (lax.axis_index("seq") & 1) == 1
    got = []
    pieces = [jnp.where(odd, local[1 - first], local[first]) for first in range(2)]
    order.mark(*pieces)
    for first, piece in enumerate(pieces):
        got.append(lax.ppermute(piece, AXES, spread_pairs(first)))
    return got, odd


def in_order(got, odd, rows):
    return jnp.where(odd, jnp.concatenate([g[:rows] for g in got[::-1]]), jnp.concatenate([g[:rows] for g in got]))


def from_sequences(tokens, order):
    odd = (lax.axis_index("seq") & 1) == 1
    half = tokens.shape[0] // 2
    got = []
    for first in range(2):
        near, far = tokens[first * half : (first + 1) * half], tokens[(1 - first) * half : (2 - first) * half]
        piece = order.mark(jnp.where(order.gate(odd), far, near))
        got.append(lax.ppermute(piece, AXES, [(b, a) for a, b in spread_pairs(first)]))
    return got


def both_sequences(order, got):
    odd = order.gate((lax.axis_index("seq") & 1) == 1)
    return jnp.where(odd, jnp.stack(got[::-1]), jnp.stack(got))


def weight_lines(weights, lines):
    width = weights[0].shape[-1]
    lines = [jnp.pad(v[..., None, :], [(0, 0)] * v.ndim + [(0, width - v.shape[-1])]) for v in lines]
    lines.append(jnp.zeros(lines[0].shape[:-2] + (16 - len(lines), width), jnp.bfloat16))
    return jnp.concatenate(weights + lines, axis=-2)


def shards_of(part, ready=None):
    if lax.axis_size("dp") != PARTS:
        p = part if part.ndim == 3 else jnp.stack(jnp.split(lax.all_gather(part, "dp", axis=0, tiled=True), PARTS))
        return [p[0], p[1], p[2], p[4], p[6], jnp.concatenate([p[3], p[5], p[7]])]
    shards = [part, swap_dp(part, 1), swap_dp(part, 2), swap_dp(part, 4), swap_dp(part, 6)]
    return shards if ready is False else last_shards(shards)


def last_shards(shards, *ready):
    if len(shards) == SHARDS:
        return shards
    near = lax.optimization_barrier((*shards[2:], *ready))[:3]
    return shards[:2] + list(near) + [swap_dp(jnp.concatenate(near), 1)]


def projection_shards(weights, vectors):
    if lax.axis_size("dp") == PARTS:
        return shards_of(weight_lines(weights, vectors))
    gather = lambda v: lax.all_gather(v, "dp", axis=0, tiled=True)
    split = lambda v: gather(v).reshape((PARTS, -1) + v.shape[1:])
    return shards_of(weight_lines([split(w) for w in weights], [split(v) for v in vectors]))


def project_body(counts, me, *refs):
    devices, rows, wide, vectors = counts
    pieces = parts_of(refs[:SHARDS])
    tokens, far, q_ref, k_ref, v_ref, ko_ref, vo_ref, vec_ref, up_ref, ordered, out, held, small, turned, sems, small_sems, out_sem = refs[SHARDS:]
    width = tokens.shape[1]
    half = width // 2
    copies = []

    def start(source, target, sem):
        copy = pltpu.make_async_copy(source, target, sem)
        copy.start()
        copies.append(copy)

    for place in range(devices):
        ref, first, size = pieces[place]
        where = me[0] ^ place
        start(ref.at[first + 3 * rows : first + size, :], small.at[where], small_sems.at[place])
        target = pl.ds(where * rows, rows)
        for weight in range(3):
            for side in range(2):
                start(
                    ref.at[first + weight * rows : first + (weight + 1) * rows, side * half : (side + 1) * half],
                    held.at[side, target, weight * half : (weight + 1) * half],
                    sems.at[len(copies) - place - 1],
                )
    for copy in copies:
        copy.wait()
    save = pltpu.make_async_copy(held, out, out_sem)
    save.start()
    vec_ref[...] = jnp.concatenate([small[i, :, :rows] for i in range(devices)], axis=1).astype(jnp.float32)
    up_ref[...] = jnp.concatenate([small[i, vectors : vectors + 1, :wide] for i in range(devices)], axis=1).astype(jnp.float32)
    for weight, add, goal, source in ((1, None, k_ref, tokens), (1, None, ko_ref, far), (2, 1, v_ref, tokens), (2, 1, vo_ref, far), (0, 0, q_ref, tokens)):
        for side in range(2):
            cols = slice(side * half, (side + 1) * half)
            product = nn(source[...], held[side, :, weight * half : (weight + 1) * half])
            if add is not None:
                product = product + vec_ref[add : add + 1, cols]
            goal[:, cols] = product.astype(jnp.bfloat16)
    flipped = tokens[...].T
    for i in range(PARTS):
        turned[i] = flipped[i * rows : (i + 1) * rows, :]
    turn_parts(me[1], turned, ordered)
    save.wait()


def project(me, pieces, tokens, far, rows, wide, vectors):
    count, width = tokens.shape
    devices = width // rows
    lines = pieces[0].shape[-2] - 3 * rows
    whole = lambda shape: pl.BlockSpec(shape, lambda i, *_: (0,) * len(shape))
    result = jax.ShapeDtypeStruct(tokens.shape, jnp.bfloat16)
    any_space = pl.BlockSpec(memory_space=pl.ANY)
    return pl.pallas_call(
        functools.partial(project_body, (devices, rows, wide, vectors)),
        grid_spec=pltpu.PrefetchScalarGridSpec(
            num_scalar_prefetch=1,
            grid=(1,),
            in_specs=[any_space] * len(pieces) + [whole(tokens.shape)] * 2,
            out_specs=[whole(tokens.shape)] * 5
            + [whole((lines, width)), whole((1, wide * devices)), whole((2, PARTS // 2, rows, count)), any_space],
            scratch_shapes=[
                pltpu.VMEM((2, width, 3 * width // 2), jnp.bfloat16),
                pltpu.VMEM((devices, lines, width), jnp.bfloat16),
                pltpu.VMEM((PARTS, rows, count), jnp.bfloat16),
                pltpu.SemaphoreType.DMA((6 * devices,)),
                pltpu.SemaphoreType.DMA((devices,)),
                pltpu.SemaphoreType.DMA,
            ],
        ),
        out_shape=[result] * 5
        + [
            jax.ShapeDtypeStruct((lines, width), jnp.float32),
            jax.ShapeDtypeStruct((1, wide * devices), jnp.float32),
            jax.ShapeDtypeStruct((2, PARTS // 2, rows, count), jnp.bfloat16),
            jax.ShapeDtypeStruct((2, width, 3 * width // 2), jnp.bfloat16),
        ],
        cost_estimate=pl.CostEstimate(flops=1, transcendentals=0, bytes_accessed=1),
        compiler_params=pltpu.CompilerParams(vmem_limit_bytes=32 << 20),
        name="project",
    )(me, *pieces, tokens, far)


class Order:
    def __init__(self):
        self.last = ()

    def gate(self, value):
        return lax.optimization_barrier((value, *self.last))[0] if self.last else value

    def mark(self, *values):
        self.last = values
        return values[0] if len(values) == 1 else values


def all_rows(send, keep):
    return jnp.stack([keep, send], axis=1).reshape(-1, keep.shape[-1]).astype(jnp.float32)


def scatter_all(send, keep):
    return lax.psum_scatter(all_rows(send, keep), AXES, scatter_dimension=0, tiled=True)


def per_device(
    hidden_in, segment_ids, query_weight, query_bias, key_weight, value_weight, value_bias, out_weight, out_bias,
    first_gain, first_shift, up_weight, up_bias, down_weight, down_bias, second_gain, second_shift, cotangent,
):
    dps, seqs = lax.axis_size("dp"), lax.axis_size("seq")
    inner_width, width = up_weight.shape[1], query_weight.shape[1]
    block = hidden_in.shape[1]
    length = segment_ids.shape[1]
    share = width // (dps * seqs)
    qblock = chunk = 256

    vectors = [query_bias, value_bias, out_bias, first_gain, first_shift, down_bias, second_gain, second_shift]
    direct = dps == PARTS and seqs == 4
    scalars = jnp.zeros((6,), jnp.int32)
    if direct:
        dp, seq = lax.axis_index("dp"), lax.axis_index("seq")
        scalars = jnp.stack([dp, dp & 1, (dp >> 1) & 1, dp >> 2, seq & 1, seq >> 1]).astype(jnp.int32)
    shards = projection_shards([query_weight, key_weight, value_weight], vectors + [up_bias])
    ids = segment_ids.astype(jnp.bfloat16).reshape(segment_ids.shape[0], 2, length // 2)
    ids = jnp.pad(ids, ((0, 0), (0, 14), (0, width - length // 2)))
    order = Order()
    got, odd = to_sequences(jnp.concatenate([hidden_in, ids], axis=1), order)

    tokens = in_order(got, odd, block)
    tokens_other = swap_dp(tokens, 1)
    segment = got[0][block : block + 2, : length // 2].astype(jnp.int32)
    core = lax.axis_index("dp") & 1
    half = length // 2
    own = lax.dynamic_index_in_dim(segment, core, 0, keepdims=False)
    other = lax.dynamic_index_in_dim(segment, 1 - core, 0, keepdims=False)
    bounds = chunk_bounds(own, other, qblock, chunk)
    row, tiles = own[None, :], segment_tiles(own, other, chunk)

    out_up, down_part = lax.optimization_barrier(
        (jnp.concatenate([out_weight, up_weight], axis=1), down_weight, *shards[2:5])
    )[:2]
    out_up_shards = shards_of(out_up, False)
    query, keys, values, keys_other, values_other, vec, up_add, ordered, w_qkv = project(
        scalars, shards, tokens, tokens_other, width // PARTS, inner_width // PARTS, len(vectors)
    )
    got_up, _ = to_sequences(after(cotangent, query), order)
    attended, lse = attend_forward(query, keys, values, keys_other, values_other, row, tiles, bounds, qblock, chunk, 3)

    upstream = in_order(lax.optimization_barrier((*got_up, attended))[:2], odd, block)
    out_up_shards = last_shards(out_up_shards, attended, upstream)
    down_shards = shards_of(after(down_part, attended, *out_up_shards[2:5]), False)
    normal_one, scale_one, first_low, active, slope, wo, wu = widen(scalars, out_up_shards, attended, tokens, vec, up_add)
    layer_low, sum_two_grad, second_grad, sums_two, *halves, wd = narrow(
        scalars, last_shards(down_shards, active), active, normal_one, vec, upstream
    )
    swap = (lambda value: swap_dp(value, 1)) if direct else (lambda value: value)
    order = Order()
    order.mark(second_grad)
    down_send, down_keep = halves
    down_got = swap(down_send)
    out_pieces = from_sequences(layer_low, order)
    inner_grad, up_sum, *halves = inner_back(scalars, order.gate(second_grad), wd, slope, first_low)
    up_send, up_keep = halves
    up_got = swap(up_send)
    order.mark(inner_grad)
    if direct:
        (send, down_keep), (other, up_keep) = fold(
            order.gate(scalars), [(down_keep, down_got, (2, 1, 2)), (up_keep, up_got, (1, 2, 3))]
        )
        order.mark(send, other)
        down_got, up_got = swap_dp(send, 2), swap_dp(other, 4)
    sum_one_grad, attended_grad, sums_one, *halves = outer_back(
        order.gate(scalars), inner_grad, wu, sum_two_grad, normal_one, scale_one, vec, wo, attended
    )
    order.mark(attended_grad)
    layer_out = order.mark(both_sequences(order, out_pieces))
    devices = dps * seqs
    wide_sums = order.gate(up_sum).reshape(devices, 4, share).transpose(1, 0, 2).reshape(4, width)
    wide_sums = order.mark(jnp.pad(wide_sums, ((0, 4), (0, 0))))

    def attend(side):
        given = (query, keys, values, keys_other, values_other, attended, order.gate(attended_grad), lse, row, tiles, bounds)
        return order.mark(*attend_back(*given, qblock, chunk, 3, side))

    dq, dk, dv, far = attend(0)
    if direct:
        (send, down_keep), (other, up_keep) = fold(
            order.gate(scalars), [(down_keep, down_got, (1, 1, 3)), (up_keep, up_got, (1, 1, 2))]
        )
        order.mark(send, other)
        down_got, up_got = swap_dp(send, 4), swap_dp(other, 2)
    one_send, one_keep, gradient, sums_first = qkv_back(
        0, order.gate(scalars), dq, dk, dv, swap_dp(far, 1), ordered, w_qkv, sum_one_grad, *halves, sums_one, sums_two, wide_sums
    )
    order.mark(gradient)
    one_got = swap(one_send)
    dq, dk, dv, far = attend(1)
    if direct:
        ((send, one_keep),) = fold(order.gate(scalars), [(one_keep, one_got, (1, 2, 3))])
        one_got = swap_dp(order.mark(send), 4)
    two_send, two_keep, gradient, _ = qkv_back(
        1, order.gate(scalars), dq, dk, dv, swap_dp(far, 1), ordered, w_qkv, gradient, sums_first
    )
    order.mark(gradient)
    two_got = swap(two_send)
    if direct:
        send, ff_keep = merge(order.gate(scalars), [(down_keep, down_got), (up_keep, up_got)], share)
        ff_got = swap_seq(order.mark(send), 1)
    in_pieces = from_sequences(gradient, order)
    if not direct:
        down_grad, up_grad = scatter_all(down_send, down_keep), scatter_all(up_send, up_keep)
        one, two = scatter_all(one_send, one_keep), scatter_all(two_send, two_keep)
        cut = width // 2
        query_grad, key_grad, value_grad = [
            jnp.concatenate([side[:, i * cut : (i + 1) * cut] for side in (one, two)], axis=1) for i in range(3)
        ]
        out_grad = one[:, 3 * cut : 3 * cut + width]
        small, late = one[:, 3 * cut + width :].T, two[:, 3 * cut :].T
    else:
        (send, two_keep), (other, ff_keep) = fold(
            order.gate(scalars), [(two_keep, two_got, (2, 1, 2)), (ff_keep, ff_got, (1, 1, 5))]
        )
        order.mark(send, other)
        two_got, ff_got = swap_dp(send, 2), swap_seq(other, 2)
        (send, one_keep), (other, two_keep) = fold(
            order.gate(scalars), [(one_keep, one_got, (1, 1, 2)), (two_keep, two_got, (1, 1, 3))]
        )
        order.mark(send, other)
        one_got, two_got = swap_dp(send, 2), swap_dp(other, 4)
        down_grad, up_grad = order.mark(*last_ff(order.gate(scalars), ff_keep, ff_got, width))
        send, keep = merge(order.gate(scalars), [(one_keep, one_got), (two_keep, two_got)], share)
        got = swap_seq(order.mark(send), 1)
    input_grad = order.mark(both_sequences(order, in_pieces).astype(jnp.float32))
    if direct:
        ((send, keep),) = fold(order.gate(scalars), [(keep, got, (1, 1, 5))])
        got = swap_seq(order.mark(send), 2)
        query_grad, key_grad, value_grad, out_grad, small, late = last_qkv(order.gate(scalars), keep, got, width)
    ob, g1, s1 = [small[i, :share] for i in (0, 1, 2)]
    db, g2, s2 = [small[i, :share] for i in (8, 9, 10)]
    ub = small[16:20, :share].reshape(-1)
    qb, vb = [late[i, :share] for i in (0, 1)]
    return (
        layer_out, input_grad, query_grad, qb, key_grad, value_grad, vb, out_grad, ob, g1, s1, up_grad, ub, down_grad, db, g2, s2,
    )


def solution(mesh):
    wide, flat = P("dp", None), P("dp")
    in_specs = (
        P("dp", "seq", None), wide, wide, flat, wide, wide, flat, wide, flat, flat, flat, wide, flat, wide, flat,
        flat, flat, P("dp", "seq", None),
    )
    rows, cells = P(AXES, None), P(AXES)
    out_specs = (
        P("dp", "seq", None), P("dp", "seq", None), rows, cells, rows, rows, cells, rows, cells, cells, cells, rows,
        cells, rows, cells, cells, cells,
    )
    return jax.shard_map(per_device, mesh=mesh, in_specs=in_specs, out_specs=out_specs, check_vma=False)
```

```python
import functools
import math

import jax
import jax.numpy as jnp
from jax import lax
from jax.experimental import pallas as pl
from jax.experimental.pallas import tpu as pltpu
from jax.sharding import PartitionSpec as P

HEAD_DIM = 64
LANES = 128
NEGATIVE = -1e30


def nt(left, right):
    return lax.dot_general(left, right, (((1,), (1,)), ((), ())), preferred_element_type=jnp.float32)


def nn(left, right):
    return lax.dot_general(left, right, (((1,), (0,)), ((), ())), preferred_element_type=jnp.float32)


def head_parts(block):
    lane = lax.broadcasted_iota(jnp.int32, block.shape, 1)
    zero = jnp.zeros_like(block)
    return (jnp.where(lane < HEAD_DIM, block, zero), jnp.where(lane < HEAD_DIM, zero, block))


def same_document(column_tile, row):
    column = jnp.concatenate([column_tile] * (row.shape[1] // LANES), axis=1)
    return column == jnp.broadcast_to(row, column.shape)


def pair_lanes(pair):
    return slice(pair * LANES, (pair + 1) * LANES)


def segment_tables(segments, tiles, half, qblock, chunk):
    ids = segments[...]
    for j in range(tiles.shape[0]):
        for i in range(chunk // LANES):
            start = j * chunk + i * LANES
            tiles[j, i * LANES : (i + 1) * LANES, :] = jnp.broadcast_to(ids[:, start : start + LANES], (LANES, LANES)).T
    chunks = half // chunk
    low = [jnp.min(ids[:, j * chunk : (j + 1) * chunk]) for j in range(2 * chunks)]
    high = [jnp.max(ids[:, j * chunk : (j + 1) * chunk]) for j in range(2 * chunks)]
    found = []
    for b in range(half // qblock):
        mine = slice(b * qblock, (b + 1) * qblock)
        first, last = jnp.min(ids[:, mine]), jnp.max(ids[:, mine])
        bounds = []
        for side in range(2):
            before = sum((high[side * chunks + j] < first).astype(jnp.int32) for j in range(chunks))
            behind = sum((low[side * chunks + j] > last).astype(jnp.int32) for j in range(chunks))
            bounds += [before, chunks - behind]
        found.append((bounds[0], bounds[1] - bounds[0], bounds[2], bounds[1] - bounds[0] + bounds[3] - bounds[2]))
    return found


def chunk_of(bounds, step, chunks):
    first, own, other, _ = bounds
    return jnp.where(step < own, first + step, chunks + other + step - own)


def forward_body(qblock, chunk, lanes, q_all, k_all, v_all, ko_all, vo_all, segments, o_all, lse_all, kall, vt, sk_ref):
    half = k_all.shape[0]
    tables = segment_tables(segments, sk_ref, half, qblock, chunk)
    chunks, pairs = half // chunk, lanes // LANES

    @pl.loop(0, q_all.shape[1] // lanes)
    def _(group):
        cols = step_of(group, lanes)
        q_ref, k_ref, v_ref, ko_ref, vo_ref, o_ref = (r.at[:, cols] for r in (q_all, k_all, v_all, ko_all, vo_all, o_all))
        lse_ref = lse_all.at[pl.ds(group, 1)]
        for j in range(chunks):
            rows = slice(j * chunk, (j + 1) * chunk)
            kall[j] = k_ref[rows, :]
            kall[chunks + j] = ko_ref[rows, :]
            vt[j] = v_ref[rows, :].T
            vt[chunks + j] = vo_ref[rows, :].T
        for b in range(q_ref.shape[0] // qblock):
            span = slice(b * qblock, (b + 1) * qblock)
            parts = []
            for pair in range(pairs):
                parts += head_parts(q_ref[span, pair_lanes(pair)] * jnp.bfloat16(HEAD_DIM**-0.5))
            row = segments[:, span]

            def one(step, carry):
                j = chunk_of(tables[b], step, chunks)
                mask = same_document(sk_ref[j], row)
                scores = [jnp.where(mask, nt(kall[j, :, pair_lanes(h // 2)], part), NEGATIVE) for h, part in enumerate(parts)]
                out = []
                for h, score in enumerate(scores):
                    top, total, acc = carry[h]
                    new_top = jnp.maximum(top, jnp.max(score, axis=0, keepdims=True))
                    expo = jnp.exp(score - new_top)
                    scale = jnp.exp(top - new_top)
                    total = total * scale + jnp.sum(expo, axis=0, keepdims=True)
                    acc = acc * scale + nn(vt[j, h * HEAD_DIM : (h + 1) * HEAD_DIM, :], expo.astype(jnp.bfloat16))
                    out.append((new_top, total, acc))
                return tuple(out)

            init = (
                jnp.full((1, qblock), NEGATIVE, jnp.float32),
                jnp.zeros((1, qblock), jnp.float32),
                jnp.zeros((HEAD_DIM, qblock), jnp.float32),
            )
            carry = lax.fori_loop(0, tables[b][3], one, (init,) * len(parts))
            result = jnp.concatenate([acc / total for _, total, acc in carry], axis=0)
            o_ref[span, :] = result.T.astype(jnp.bfloat16)
            for h, (top, total, _) in enumerate(carry):
                lse_ref[0, h : h + 1, span] = top + jnp.log(total)


def backward_body(
    qblock, chunk, lanes, side, scalars, q_ref, k_ref, v_ref, ko_ref, vo_ref, o_ref, do_ref, lse_all, segments,
    dq_ref, dk_ref, dv_ref, far_ref, kall, vall, kt, dkall, dvall, sk_ref,
):
    half = k_ref.shape[0]
    tables = segment_tables(segments, sk_ref, half, qblock, chunk)
    lse_ref = lse_all.at[side : side + 1]
    chunks, pairs = half // chunk, lanes // LANES
    for j in range(chunks):
        rows = slice(j * chunk, (j + 1) * chunk)
        kall[j] = k_ref[rows, :]
        kall[chunks + j] = ko_ref[rows, :]
        vall[j] = v_ref[rows, :]
        vall[chunks + j] = vo_ref[rows, :]
        kt[j] = k_ref[rows, :].T
        kt[chunks + j] = ko_ref[rows, :].T
    dkall[...] = jnp.zeros_like(dkall)
    dvall[...] = jnp.zeros_like(dvall)
    for b in range(q_ref.shape[0] // qblock):
        span = slice(b * qblock, (b + 1) * qblock)
        parts, dparts, delta = [], [], []
        for pair in range(pairs):
            parts.append(head_parts(q_ref[span, pair_lanes(pair)] * jnp.bfloat16(HEAD_DIM**-0.5)))
            dparts.append(head_parts(do_ref[span, pair_lanes(pair)]))
            product = do_ref[span, pair_lanes(pair)].astype(jnp.float32) * o_ref[span, pair_lanes(pair)].astype(jnp.float32)
            product = product.T
            delta += [jnp.sum(product[h * HEAD_DIM : (h + 1) * HEAD_DIM], axis=0, keepdims=True) for h in range(2)]
        both = [jnp.concatenate(p, axis=0) for p in parts]
        dboth = [jnp.concatenate(p, axis=0) for p in dparts]
        row = segments[:, span]
        lse = [lse_ref[0, h : h + 1, span] for h in range(2 * pairs)]

        def one(step, carry):
            j = chunk_of(tables[b], step, chunks)
            mask = same_document(sk_ref[j], row)
            out = []
            for pair in range(pairs):
                key, val = kall[j, :, pair_lanes(pair)], vall[j, :, pair_lanes(pair)]
                probs, grads = [], []
                for side in range(2):
                    h = 2 * pair + side
                    score = jnp.where(mask, nt(key, parts[pair][side]), NEGATIVE)
                    prob = jnp.exp(score - lse[h])
                    grad = (prob * (nt(val, dparts[pair][side]) - delta[h])).astype(jnp.bfloat16)
                    probs.append(prob.astype(jnp.bfloat16))
                    grads.append(grad)
                    out.append(carry[h] + nn(kt[j, h * HEAD_DIM : (h + 1) * HEAD_DIM, :], grad))
                dvall[j, :, pair_lanes(pair)] += nn(jnp.concatenate(probs, axis=1), dboth[pair])
                dkall[j, :, pair_lanes(pair)] += nn(jnp.concatenate(grads, axis=1), both[pair])
            return tuple(out)

        zero = jnp.zeros((HEAD_DIM, qblock), jnp.float32)
        carry = lax.fori_loop(0, tables[b][3], one, (zero,) * (2 * pairs))
        dq_ref[span, :] = (jnp.concatenate(carry, axis=0).T * HEAD_DIM**-0.5).astype(jnp.bfloat16)
    for j in range(chunks):
        rows = slice(j * chunk, (j + 1) * chunk)
        dk_ref[rows, :] = dkall[j]
        dv_ref[rows, :] = dvall[j]
        far_ref[0, rows, :] = dkall[chunks + j].astype(jnp.bfloat16)
        far_ref[1, rows, :] = dvall[chunks + j].astype(jnp.bfloat16)


def attend_back(scalars, query, keys, values, keys_other, values_other, attended, grad, lse_rows, segments, qblock, chunk, pairs, side):
    tokens, width = query.shape
    half = keys.shape[0]
    lanes = pairs * LANES
    n = 2 * half // chunk
    f32, b16 = jnp.float32, jnp.bfloat16
    cols = slice(side * lanes, (side + 1) * lanes)
    far = [Far(x, cols) for x in (query, keys, values, keys_other, values_other, attended, grad)]
    return whole_call(
        functools.partial(backward_body, qblock, chunk, lanes, side), "attend_back", scalars, [], far + [lse_rows, segments],
        [array(b16, tokens, lanes), array(f32, half, lanes), array(f32, half, lanes), array(b16, 2, half, lanes)], [],
        [pltpu.VMEM((n, chunk, lanes), b16), pltpu.VMEM((n, chunk, lanes), b16), pltpu.VMEM((n, lanes, chunk), b16),
         pltpu.VMEM((n, chunk, lanes), f32), pltpu.VMEM((n, chunk, lanes), f32), pltpu.VMEM((n, chunk, LANES), f32)], 24,
    )


AXES = ("dp", "seq")
PARTS = 8
SHARDS = 8
epsilon = 1e-12


def tn(left, right):
    return lax.dot_general(left, right, (((0,), (0,)), ((), ())), preferred_element_type=jnp.float32)


def norm_parts(value):
    center = value - jnp.mean(value, axis=-1, keepdims=True)
    spread = jnp.mean(center * center, axis=-1, keepdims=True)
    scale = lax.rsqrt(spread + epsilon)
    return (center * scale, scale)


def norm_back(upstream, normal, scale, gain):
    scaled = upstream * gain
    return scale * (
        scaled
        - jnp.mean(scaled, axis=-1, keepdims=True)
        - normal * jnp.mean(scaled * normal, axis=-1, keepdims=True)
    )


def row_sum(matrix):
    return jnp.sum(matrix.astype(jnp.float32), axis=0, keepdims=True)


def parts_of(refs):
    return [(ref, 0, ref.shape[0]) for ref in refs]


def load_pieces(me, pieces, targets, sems):
    copies = [[] for _ in targets]
    for place, (ref, first, rows) in enumerate(pieces):
        where = pl.ds(pl.multiple_of((me ^ place) * rows, 32), rows)
        for i, (target, columns) in enumerate(targets):
            copy = pltpu.make_async_copy(ref.at[first : first + rows, columns], target.at[where, :], sems.at[i, place])
            copy.start()
            copies[i].append(copy)
    return copies


def wait_all(copies):
    for copy in copies:
        copy.wait()


def step_of(block, size):
    return pl.ds(pl.multiple_of(block * size, size), size)


BLOCK = 256
ROWS = 256


def widen_body(scalars, *refs):
    pieces = parts_of(refs[:SHARDS])
    (attended, tokens, vec, up_add, normal_ref, scale_ref, low_ref, active_ref, slope_ref, wo, wu, sems) = refs[SHARDS:]
    width, wide = wu.shape
    loads = load_pieces(scalars[0], pieces, [(wo, slice(0, width)), (wu, slice(width, width + wide))], sems)
    wait_all(loads[0])

    @pl.loop(0, tokens.shape[0] // ROWS)
    def _(i):
        rows = step_of(i, ROWS)
        branch = nn(attended[rows, :], wo[...]) + vec[2:3, :]
        normal, scale = norm_parts(tokens[rows, :].astype(jnp.float32) + branch)
        first = normal * vec[3:4, :] + vec[4:5, :]
        normal_ref[rows, :] = normal
        scale_ref[rows, :] = jnp.broadcast_to(scale, (ROWS, LANES))
        low_ref[rows, :] = first.astype(jnp.bfloat16)

    wait_all(loads[1])

    @pl.loop(0, wide // BLOCK)
    def _(j):
        cols = step_of(j, BLOCK)
        inner = nn(low_ref[...], wu[:, cols]) + up_add[:, cols]
        cumulative = 0.5 * (1.0 + lax.erf(inner * math.sqrt(0.5)))
        density = jnp.exp(-0.5 * inner * inner) * (1.0 / math.sqrt(2.0 * math.pi))
        active_ref[:, cols] = (inner * cumulative).astype(jnp.bfloat16)
        slope_ref[:, cols] = (cumulative + inner * density).astype(jnp.bfloat16)


def narrow_body(scalars, *refs):
    pieces = parts_of(refs[:SHARDS])
    (active, normal_one, vec, upstream, out_ref, grad_ref, low_ref, sums_ref, send_ref, keep_ref, wd, sums, sems) = refs[SHARDS:]
    wide, width = wd.shape
    (loads,) = load_pieces(scalars[0], pieces, [(wd, slice(0, width))], sems)
    wait_all(loads)
    sums[...] = jnp.zeros_like(sums)

    @pl.loop(0, normal_one.shape[0] // ROWS)
    def _(i):
        rows = step_of(i, ROWS)
        second = nn(active[rows, :], wd[...]) + vec[5:6, :]
        normal, scale = norm_parts(normal_one[rows, :] * vec[3:4, :] + vec[4:5, :] + second)
        out_ref[rows, :] = (normal * vec[6:7, :] + vec[7:8, :]).astype(jnp.bfloat16)
        up = upstream[rows, :].astype(jnp.float32)
        grad = norm_back(up, normal, scale, vec[6:7, :])
        low = grad.astype(jnp.bfloat16)
        grad_ref[rows, :] = grad
        low_ref[rows, :] = low
        sums[0:1, :] += row_sum(low)
        sums[1:2, :] += row_sum(up * normal)
        sums[2:3, :] += row_sum(up)

    sums_ref[...] = sums[...]
    size = wide // PARTS

    @pl.loop(0, PARTS // 2)
    def _(i):
        send_ref[i] = tn(active[:, step_of(2 * i + 1 - scalars[1], size)], low_ref[...]).astype(jnp.bfloat16)
        keep_ref[i] = tn(active[:, step_of(2 * i + scalars[1], size)], low_ref[...]).astype(jnp.bfloat16)


def turn_parts(core, turned, ordered):
    for i in range(PARTS // 2):
        ordered[0, i] = turned[2 * i + 1 - core]
        ordered[1, i] = turned[2 * i + core]


def inner_back_body(scalars, low, wd, slope, first_low, grad_ref, sums_ref, send_ref, keep_ref, turned, ordered):
    size = first_low.shape[1] // PARTS
    flipped = first_low[...].T
    for i in range(PARTS):
        turned[i] = flipped[i * size : (i + 1) * size, :]
    turn_parts(scalars[1], turned, ordered)
    rows = (PARTS // 2) * size

    @pl.loop(0, slope.shape[1] // BLOCK)
    def _(j):
        cols = step_of(j, BLOCK)
        grad = (nt(low[...], wd[cols, :]) * slope[:, cols].astype(jnp.float32)).astype(jnp.bfloat16)
        grad_ref[:, cols] = grad
        sums_ref[:, cols] = row_sum(grad)
        for side, ref in enumerate((send_ref, keep_ref)):
            left = ordered[side].reshape(rows, low.shape[0])
            ref[:, :, cols] = nn(left, grad).astype(jnp.bfloat16).reshape(PARTS // 2, size, BLOCK)


def outer_back_body(scalars, grad, wu, up_grad, normal_ref, scale_ref, vec, wo, attended, sum_ref, result_ref, sums_ref, send_ref, keep_ref, low, sums, turned):
    width = wo.shape[0]
    sums[...] = jnp.zeros_like(sums)

    @pl.loop(0, grad.shape[0] // ROWS)
    def _(i):
        rows = step_of(i, ROWS)
        first = up_grad[rows, :] + nt(grad[rows, :], wu[...])
        normal = normal_ref[rows, :]
        total = norm_back(first, normal, scale_ref[rows, 0:1], vec[3:4, :])
        branch = total.astype(jnp.bfloat16)
        sum_ref[rows, :] = total
        low[rows, :] = branch
        result_ref[rows, :] = nt(branch, wo[...]).astype(jnp.bfloat16)
        sums[0:1, :] += row_sum(branch)
        sums[1:2, :] += row_sum(first * normal)
        sums[2:3, :] += row_sum(first)

    sums_ref[...] = sums[...]
    size = width // PARTS
    product = tn(attended[...], low[...]).astype(jnp.bfloat16)
    for i in range(PARTS):
        turned[i] = product[i * size : (i + 1) * size, :]
    for i in range(PARTS // 2):
        send_ref[i] = turned[2 * i + 1 - scalars[1]]
        keep_ref[i] = turned[2 * i + scalars[1]]


class Far:
    def __init__(self, value, columns=None):
        self.value, self.columns = value, columns
        width = value.shape[-1] if columns is None else columns.stop - columns.start
        self.shape, self.dtype = value.shape[:-1] + (width,), value.dtype


def far_body(body, far, counts, scalars, *refs):
    hbm, inputs, outputs, held = counts
    given = list(refs[hbm : hbm + inputs])
    held_refs, sems = refs[len(refs) - held - 1 : -1], refs[-1]
    copies = []
    for i, (place, columns) in enumerate(far):
        source = given[place] if columns is None else given[place].at[:, columns]
        copies.append(pltpu.make_async_copy(source, held_refs[i], sems.at[i]))
        copies[-1].start()
        given[place] = held_refs[i]
    for copy in copies:
        copy.wait()
    body(scalars, *refs[:hbm], *given, *refs[hbm + inputs : len(refs) - held - 1])


def whole_call(body, name, scalars, hbm, inputs, outputs, hbm_outputs, scratch, room=8):
    shape_of = lambda x: jax.ShapeDtypeStruct(x.shape, x.dtype)
    near, stay = pl.BlockSpec(memory_space=pltpu.VMEM), pl.BlockSpec(memory_space=pltpu.HBM)
    far = [(i, x.columns) for i, x in enumerate(inputs) if isinstance(x, Far)]
    scratch = list(scratch)
    if far:
        held = [pltpu.VMEM(inputs[i].shape, inputs[i].dtype) for i, _ in far]
        counts = (len(hbm), len(inputs), len(outputs) + len(hbm_outputs), len(far))
        body = functools.partial(far_body, body, far, counts)
        scratch += held + [pltpu.SemaphoreType.DMA((len(far),))]
        room += sum(math.prod(inputs[i].shape) * inputs[i].dtype.itemsize for i, _ in far) // (1 << 20) + 1
    return pl.pallas_call(
        body,
        in_specs=[pl.BlockSpec(memory_space=pltpu.SMEM)]
        + [stay] * len(hbm)
        + [stay if isinstance(x, Far) else near for x in inputs],
        out_specs=[near] * len(outputs) + [stay] * len(hbm_outputs),
        scratch_shapes=scratch,
        out_shape=[shape_of(x) for x in list(outputs) + list(hbm_outputs)],
        cost_estimate=pl.CostEstimate(flops=1, transcendentals=0, bytes_accessed=1),
        compiler_params=pltpu.CompilerParams(vmem_limit_bytes=room << 20),
        name=name,
    )(scalars, *hbm, *[x.value if isinstance(x, Far) else x for x in inputs])


def array(dtype, *shape):
    return jax.ShapeDtypeStruct(shape, dtype)


def widen(scalars, pieces, attended, tokens, vec, up_add):
    count, width = tokens.shape
    wide = up_add.shape[1]
    f32, b16 = jnp.float32, jnp.bfloat16
    return whole_call(
        widen_body, "widen", scalars, pieces, [attended, tokens, vec, up_add],
        [array(f32, count, width), array(f32, count, LANES), array(b16, count, width),
         array(b16, count, wide), array(b16, count, wide), array(b16, width, width), array(b16, width, wide)],
        [], [pltpu.SemaphoreType.DMA((2, PARTS))],
    )


def narrow(scalars, pieces, active, normal, vec, upstream):
    count, wide = active.shape
    width = normal.shape[1]
    f32, b16 = jnp.float32, jnp.bfloat16
    half = array(b16, PARTS // 2, wide // PARTS, width)
    return whole_call(
        narrow_body, "narrow", scalars, pieces, [active, normal, vec, upstream],
        [array(b16, count, width), array(f32, count, width), array(b16, count, width), array(f32, 8, width), half, half, array(b16, wide, width)],
        [], [pltpu.VMEM((8, width), f32), pltpu.SemaphoreType.DMA((1, PARTS))],
    )


def inner_back(scalars, low, wd, slope, first_low):
    count, wide = slope.shape
    width = low.shape[1]
    size = width // PARTS
    f32, b16 = jnp.float32, jnp.bfloat16
    half = array(b16, PARTS // 2, size, wide)
    return whole_call(
        inner_back_body, "inner_back", scalars, [], [low, wd, slope, first_low],
        [array(b16, count, wide), array(f32, 1, wide), half, half], [],
        [pltpu.VMEM((PARTS, size, count), b16), pltpu.VMEM((2, PARTS // 2, size, count), b16)],
    )


def outer_back(scalars, grad, wu, up_grad, normal, scale, vec, wo, attended):
    count, width = normal.shape
    f32, b16 = jnp.float32, jnp.bfloat16
    half = array(b16, PARTS // 2, width // PARTS, width)
    return whole_call(
        outer_back_body, "outer_back", scalars, [], [grad, wu, up_grad, normal, scale, vec, wo, attended],
        [array(f32, count, width), array(b16, count, width), array(f32, 8, width), half, half], [],
        [pltpu.VMEM((count, width), b16), pltpu.VMEM((8, width), f32), pltpu.VMEM((PARTS, width // PARTS, width), b16)],
    )


def sums_to_slots(core, lines, parts, send, keep, first, wide=None):
    turned = lines[...].T
    rows = turned.shape[0] // PARTS
    for i in range(PARTS):
        parts[i] = turned[i * rows : (i + 1) * rows, :]
    if wide is not None:
        size = wide.shape[1] // (4 * PARTS)
        for i in range(4 * PARTS):
            place = (i % 4) * (rows // 4)
            parts[i // 4, place : place + 1, LANES - size :] = wide[:, i * size : (i + 1) * size]
    for i in range(PARTS // 2):
        send[i, :, first : first + LANES] = parts[2 * i + 1 - core].astype(jnp.bfloat16)
        keep[i, :, first : first + LANES] = parts[2 * i + core].astype(jnp.bfloat16)


def qkv_back_body(side, scalars, dq, dk, dv, far, ordered, weight, gradient, *refs):
    core = scalars[1]
    if side == 0:
        out_send, out_keep, sums_one, sums_two, wide_sums, send, keep, result, sums_ref, both, lines, parts = refs
    else:
        first_sums, send, keep, result, sums_ref, both, lines, parts = refs
    half = dq.shape[1]
    both[:, :half] = dq[...]
    both[:, half : 2 * half] = (dk[...] + far[0].astype(jnp.float32)).astype(jnp.bfloat16)
    both[:, 2 * half :] = (dv[...] + far[1].astype(jnp.float32)).astype(jnp.bfloat16)
    sums_ref[...] = jnp.zeros_like(sums_ref)
    sums_ref[0:1, :] = row_sum(dq[...])
    sums_ref[1:2, :] = row_sum(both[:, 2 * half :])
    rows = ordered.shape[1] * ordered.shape[2]
    for i, ref in enumerate((send, keep)):
        left = ordered[i].reshape(rows, ordered.shape[3])
        product = nn(left, both[...]).astype(jnp.bfloat16)
        ref[:, :, : 3 * half] = product.reshape(ordered.shape[1], ordered.shape[2], 3 * half)
    lines[...] = jnp.zeros_like(lines)
    if side == 0:
        width = out_send.shape[2]
        send[:, :, 3 * half : 3 * half + width] = out_send[...]
        keep[:, :, 3 * half : 3 * half + width] = out_keep[...]
        lines[0:8, :] = sums_one[...]
        lines[8:16, :] = sums_two[...]
        sums_to_slots(core, lines, parts, send, keep, 3 * half + width, wide_sums)
    else:
        lines[0:8, :half] = first_sums[...]
        lines[0:8, half:] = sums_ref[...]
        sums_to_slots(core, lines, parts, send, keep, 3 * half)
    result[...] = (gradient[...] + nt(both[...], weight[side])).astype(result.dtype)


def qkv_back(side, scalars, dq, dk, dv, far, ordered, weights, gradient, *more):
    count, half = dq.shape
    width = gradient.shape[1]
    f32, b16 = jnp.float32, jnp.bfloat16
    total = array(b16, PARTS // 2, width // PARTS, 3 * half + LANES + (width if side == 0 else 0))
    return whole_call(
        functools.partial(qkv_back_body, side), "qkv_back", scalars, [], [dq, dk, dv, far, Far(ordered), Far(weights), gradient, *more],
        [total, total, array(b16 if side else f32, count, width), array(f32, 8, half)], [],
        [pltpu.VMEM((count, 3 * half), b16), pltpu.VMEM((LANES, width), f32), pltpu.VMEM((PARTS, width // PARTS, LANES), f32)],
    )


STRIPE = 32


def fold_body(plans, scalars, *refs):
    for item, (outer, inner, bit) in enumerate(plans):
        keep, got = refs[2 * item : 2 * item + 2]
        send, left = refs[2 * (len(plans) + item) : 2 * (len(plans) + item) + 2]
        mine = scalars[bit]
        rows = keep.shape[1]
        stripe = STRIPE if rows % STRIPE == 0 else rows

        @pl.loop(0, rows // stripe)
        def _(k):
            span = step_of(k, stripe) if stripe != rows else slice(None)
            for i in range(outer):
                for j in range(inner):
                    for target, side in ((send, 1 - mine), (left, mine)):
                        place = (2 * i + side) * inner + j
                        value = keep[place, span, :].astype(jnp.float32) + got[place, span, :].astype(jnp.float32)
                        target[i * inner + j, span, :] = value.astype(target.dtype)


def fold(scalars, items):
    outs, plans = [], []
    for keep, got, (outer, inner, bit) in items:
        shape = (keep.shape[0] // 2,) + keep.shape[1:]
        outs += [array(jnp.bfloat16, *shape), array(keep.dtype, *shape)]
        plans.append((outer, inner, bit))
    got = whole_call(
        functools.partial(fold_body, plans), "fold", scalars, [], [x for keep, got, _ in items for x in (keep, got)], outs, [], []
    )
    return [(got[2 * i], got[2 * i + 1]) for i in range(len(items))]


def merge_body(shapes, scalars, *refs):
    send, left = refs[-2:]
    mine = scalars[4]
    low = send.shape[1]
    first = 0
    for item, (rows, wide) in enumerate(shapes):
        keep, got = refs[2 * item : 2 * item + 2]
        for part in range(rows // low):
            span = slice(part * low, (part + 1) * low)
            for high in range(2):
                for target, side in ((send, 1 - mine), (left, mine)):
                    value = keep[2 * high + side, span, :].astype(jnp.float32) + got[2 * high + side, span, :].astype(jnp.float32)
                    target[high, :, first : first + wide] = value.astype(target.dtype)
            first += wide


def merge(scalars, items, low):
    items = [(k.reshape(4, k.shape[-2] // 4, k.shape[-1]), g.reshape(4, g.shape[-2] // 4, g.shape[-1])) for k, g in items]
    shapes = [k.shape[1:] for k, _ in items]
    wide = sum(rows // low * n for rows, n in shapes)
    return whole_call(
        functools.partial(merge_body, shapes), "merge", scalars, [], [x for pair in items for x in pair],
        [array(jnp.bfloat16, 2, low, wide), array(jnp.float32, 2, low, wide)], [], [],
    )


def last_ff_body(scalars, keep, got, down_ref, up_ref):
    low = keep.shape[1]
    width = down_ref.shape[1]
    for part in range(down_ref.shape[0] // low):
        cols = slice(part * width, (part + 1) * width)
        down_ref[part * low : (part + 1) * low, :] = keep[0, :, cols] + got[0, :, cols].astype(jnp.float32)
    cols = slice(4 * width, 4 * width + up_ref.shape[1])
    up_ref[...] = keep[0, :, cols] + got[0, :, cols].astype(jnp.float32)


def last_ff(scalars, keep, got, width):
    low = keep.shape[1]
    return whole_call(
        last_ff_body, "last_ff", scalars, [], [keep, got], [array(jnp.float32, 4 * low, width), array(jnp.float32, low, 4 * width)], [], []
    )


def last_qkv_body(scalars, keep, got, query_ref, key_ref, value_ref, out_ref, small_ref, late_ref, wide_ref, turned):
    low = keep.shape[1]
    width = query_ref.shape[1]
    half = width // 2
    second = 3 * half + width + LANES

    def total(first, size):
        return keep[0, :, first : first + size] + got[0, :, first : first + size].astype(jnp.float32)

    for i, ref in enumerate((query_ref, key_ref, value_ref)):
        ref[:, :half] = total(i * half, half)
        ref[:, half:] = total(second + i * half, half)
    out_ref[...] = total(3 * half, width)
    wide_ref[...] = total(3 * half + width, LANES)[0:1, :]
    for ref, first in ((small_ref, 3 * half + width), (late_ref, second + 3 * half)):
        turned[...] = jnp.zeros_like(turned)
        turned[:low, :] = total(first, LANES)
        ref[...] = turned[...].T[: ref.shape[0], :]


def last_qkv(scalars, keep, got, width):
    low = keep.shape[1]
    f32 = jnp.float32
    return whole_call(
        last_qkv_body, "last_qkv", scalars, [], [keep, got],
        [array(f32, low, width)] * 4 + [array(f32, 24, LANES), array(f32, 8, LANES), array(f32, 1, LANES)], [], [pltpu.VMEM((LANES, LANES), f32)],
    )


def after(value, *others):
    return lax.optimization_barrier((value,) + others)[0]


def bit_count(size):
    return size.bit_length() - 1


def swap_dp(value, mask):
    return lax.ppermute(value, "dp", [(i, i ^ mask) for i in range(lax.axis_size("dp"))])


def swap_seq(value, mask):
    return lax.ppermute(value, "seq", [(i, i ^ mask) for i in range(lax.axis_size("seq"))])


def column_sum(matrix):
    return jnp.sum(matrix.astype(jnp.float32), axis=0)


def spread_pairs(first):
    dps, seqs = lax.axis_size("dp"), lax.axis_size("seq")
    pairs = []
    for dp in range(dps):
        for seq in range(seqs):
            piece = first ^ (seq & 1)
            to_dp = (dp & ~1) | (seq >> 1)
            to_seq = 2 * (dp & 1) + piece
            pairs.append((dp * seqs + seq, to_dp * seqs + to_seq))
    return pairs


def to_sequences(local, order):
    odd = (lax.axis_index("seq") & 1) == 1
    got = []
    pieces = [jnp.where(odd, local[1 - first], local[first]) for first in range(2)]
    order.mark(*pieces)
    for first, piece in enumerate(pieces):
        got.append(lax.ppermute(piece, AXES, spread_pairs(first)))
    return got, odd


def in_order(got, odd, rows):
    return jnp.where(odd, jnp.concatenate([g[:rows] for g in got[::-1]]), jnp.concatenate([g[:rows] for g in got]))


def from_sequences(tokens, order):
    odd = (lax.axis_index("seq") & 1) == 1
    half = tokens.shape[0] // 2
    got = []
    for first in range(2):
        near, far = tokens[first * half : (first + 1) * half], tokens[(1 - first) * half : (2 - first) * half]
        piece = order.mark(jnp.where(order.gate(odd), far, near))
        got.append(lax.ppermute(piece, AXES, [(b, a) for a, b in spread_pairs(first)]))
    return got


def both_sequences(order, got):
    odd = order.gate((lax.axis_index("seq") & 1) == 1)
    return jnp.where(odd, jnp.stack(got[::-1]), jnp.stack(got))


def weight_lines(weights, lines):
    width = weights[0].shape[-1]
    lines = [jnp.pad(v[..., None, :], [(0, 0)] * v.ndim + [(0, width - v.shape[-1])]) for v in lines]
    lines.append(jnp.zeros(lines[0].shape[:-2] + (16 - len(lines), width), jnp.bfloat16))
    return jnp.concatenate(weights + lines, axis=-2)


def near_shards(part):
    if lax.axis_size("dp") != PARTS:
        p = part if part.ndim == 3 else jnp.stack(jnp.split(lax.all_gather(part, "dp", axis=0, tiled=True), PARTS))
        return [p[i] for i in range(PARTS)]
    return [part, swap_dp(part, 2), swap_dp(part, 4), swap_dp(part, 6)]


def all_shards(near, *ready):
    if len(near) == PARTS:
        return near
    near = [near[0]] + list(lax.optimization_barrier((*near[1:], *ready))[:3])
    shards = []
    for part in near:
        shards += [part, swap_dp(part, 1)]
    return shards


def pack_body(scalars, query, key, value, *refs):
    vectors, (part, lines) = refs[:-2], refs[-2:]
    rows = query.shape[0]
    for i, ref in enumerate((query, key, value)):
        part[i * rows : (i + 1) * rows, :] = ref[...]
    lines[...] = jnp.zeros_like(lines)
    for i, ref in enumerate(vectors):
        lines[i : i + 1, : ref.shape[1]] = ref[...].astype(jnp.float32)
    part[3 * rows :, :] = lines[...].astype(jnp.bfloat16)


def projection_part(scalars, weights, vectors):
    if lax.axis_size("dp") == PARTS:
        rows, width = weights[0].shape
        return whole_call(
            pack_body, "pack", scalars, [], weights + [v[None, :] for v in vectors],
            [array(jnp.bfloat16, 3 * rows + 16, width)], [], [pltpu.VMEM((16, width), jnp.float32)],
        )[0]
    gather = lambda v: lax.all_gather(v, "dp", axis=0, tiled=True)
    split = lambda v: gather(v).reshape((PARTS, -1) + v.shape[1:])
    return weight_lines([split(w) for w in weights], [split(v) for v in vectors])


def spread_body(scalars, hidden, ids, *pieces):
    odd = scalars[7]
    block, half = hidden.shape[1], ids.shape[1] // 2
    for first, piece in enumerate(pieces):
        piece[:block, :] = hidden[first ^ odd]
        line = jnp.where(first ^ odd == 0, ids[0:1, :], ids[1:2, :]).astype(jnp.bfloat16)
        piece[block:, :] = jnp.zeros_like(piece[block:, :])
        piece[block : block + 1, :half] = line[:, :half]
        piece[block + 1 : block + 2, :half] = line[:, half:]


def spread_hidden(scalars, hidden, ids):
    piece = array(jnp.bfloat16, hidden.shape[1] + 16, hidden.shape[2])
    pieces = whole_call(spread_body, "spread", scalars, [], [hidden, ids], [piece, piece], [], [])
    return [lax.ppermute(piece, AXES, spread_pairs(first)) for first, piece in enumerate(pieces)]


def project_body(sizes, scalars, *refs):
    rows, wide, vectors, qblock, chunk, lanes = sizes
    pieces, hidden = parts_of(refs[:SHARDS]), refs[SHARDS : SHARDS + 4]
    (
        attended, lse, tokens, vec_ref, up_ref, segments, ordered, query_out, keys_out, values_out, keys_far_out, values_far_out, weights_out,
        query, keys, values, keys_far, values_far, far, held, small, turned, ids, sems, small_sems, hidden_sems, out_sems, kall, vt, tiles,
    ) = refs[SHARDS + 4 :]
    count, width = tokens.shape
    block = count // 2
    half = width // 2
    core, odd = scalars[6], scalars[7]
    copies, brought = [], []

    def start(copies, source, target, sem):
        copies.append(pltpu.make_async_copy(source, target, sem))
        copies[-1].start()

    for i, (ref, place) in enumerate(zip(hidden, (0, 1, 0, 1))):
        goal = tokens if i < 2 else far
        start(brought, ref.at[:block, :], goal.at[pl.ds(pl.multiple_of((place ^ odd) * block, block), block), :], hidden_sems.at[i])
    start(brought, hidden[0].at[block:, :], ids, hidden_sems.at[4])
    for place, (ref, _, size) in enumerate(pieces):
        where = scalars[0] ^ place
        start(copies, ref.at[3 * rows : size, :], small.at[where], small_sems.at[place])
        target = pl.ds(where * rows, rows)
        for weight in range(3):
            for side in range(2):
                start(
                    copies,
                    ref.at[weight * rows : (weight + 1) * rows, side * half : (side + 1) * half],
                    held.at[side, target, weight * half : (weight + 1) * half],
                    sems.at[len(copies) - place - 1],
                )
    wait_all(brought)
    line = ids[...].astype(jnp.float32)
    for i in range(2):
        segments[:, i * count : (i + 1) * count] = jnp.where(core == i, line[0:1, :count], line[1:2, :count])
    flipped = tokens[...].T
    for i in range(PARTS):
        turned[i] = flipped[i * rows : (i + 1) * rows, :]
    turn_parts(scalars[1], turned, ordered)
    wait_all(copies)
    saves = []
    start(saves, held, weights_out, out_sems.at[0])
    vec_ref[...] = jnp.concatenate([small[i, :, :rows] for i in range(PARTS)], axis=1).astype(jnp.float32)
    up_ref[...] = jnp.concatenate([small[i, vectors : vectors + 1, :wide] for i in range(PARTS)], axis=1).astype(jnp.float32)
    for i, (weight, add, goal, source, out) in enumerate((
        (1, None, keys, tokens, keys_out), (1, None, keys_far, far, keys_far_out), (2, 1, values, tokens, values_out),
        (2, 1, values_far, far, values_far_out), (0, 0, query, tokens, query_out),
    )):
        for side in range(2):
            cols = slice(side * half, (side + 1) * half)
            product = nn(source[...], held[side, :, weight * half : (weight + 1) * half])
            if add is not None:
                product = product + vec_ref[add : add + 1, cols]
            goal[:, cols] = product.astype(jnp.bfloat16)
        start(saves, goal, out, out_sems.at[i + 1])
    forward_body(qblock, chunk, lanes, query, keys, values, keys_far, values_far, segments, attended, lse, kall, vt, tiles)
    wait_all(saves)


def project(scalars, pieces, hidden, rows, wide, vectors, qblock, chunk, lanes):
    block, width = hidden[0].shape[0] - 16, hidden[0].shape[1]
    count = 2 * block
    lines = pieces[0].shape[-2] - 3 * rows
    n = 2 * count // chunk
    f32, b16 = jnp.float32, jnp.bfloat16
    whole = array(b16, count, width)
    vmem = lambda x: pltpu.VMEM(x.shape, x.dtype)
    return whole_call(
        functools.partial(project_body, (rows, wide, vectors, qblock, chunk, lanes)), "project", scalars, list(pieces) + list(hidden), [],
        [whole, array(f32, width // lanes, 8, count), whole, array(f32, lines, width), array(f32, 1, wide * PARTS), array(f32, 1, 2 * count),
         array(b16, 2, PARTS // 2, rows, count)],
        [whole] * 5 + [array(b16, 2, width, 3 * width // 2)],
        [vmem(whole)] * 6
        + [pltpu.VMEM((2, width, 3 * width // 2), b16), pltpu.VMEM((PARTS, lines, width), b16), pltpu.VMEM((PARTS, rows, count), b16),
           pltpu.VMEM((16, width), b16), pltpu.SemaphoreType.DMA((6 * PARTS,)), pltpu.SemaphoreType.DMA((PARTS,)),
           pltpu.SemaphoreType.DMA((5,)), pltpu.SemaphoreType.DMA((6,)), pltpu.VMEM((n, chunk, lanes), b16),
           pltpu.VMEM((n, lanes, chunk), b16), pltpu.VMEM((n, chunk, LANES), f32)],
        28,
    )


class Order:
    def __init__(self):
        self.last = ()

    def gate(self, value):
        return lax.optimization_barrier((value, *self.last))[0] if self.last else value

    def mark(self, *values):
        self.last = values
        return values[0] if len(values) == 1 else values


def all_rows(send, keep):
    return jnp.stack([keep, send], axis=1).reshape(-1, keep.shape[-1]).astype(jnp.float32)


def scatter_all(send, keep):
    return lax.psum_scatter(all_rows(send, keep), AXES, scatter_dimension=0, tiled=True)


def per_device(
    hidden_in, segment_ids, query_weight, query_bias, key_weight, value_weight, value_bias, out_weight, out_bias,
    first_gain, first_shift, up_weight, up_bias, down_weight, down_bias, second_gain, second_shift, cotangent,
):
    dps, seqs = lax.axis_size("dp"), lax.axis_size("seq")
    inner_width, width = up_weight.shape[1], query_weight.shape[1]
    devices = dps * seqs
    share = width // devices
    qblock = chunk = 256
    pairs = 3
    direct = dps == PARTS and seqs == 4
    dp, seq = lax.axis_index("dp"), lax.axis_index("seq")
    if direct:
        scalars = [dp, dp & 1, (dp >> 1) & 1, dp >> 2, seq & 1, seq >> 1, dp & 1, seq & 1]
    else:
        scalars = [0, 0, 0, 0, 0, 0, dp & 1, seq & 1]
    scalars = jnp.stack([jnp.asarray(v, jnp.int32) for v in scalars])

    vectors = [query_bias, value_bias, out_bias, first_gain, first_shift, down_bias, second_gain, second_shift]
    part = projection_part(scalars, [query_weight, key_weight, value_weight], vectors + [up_bias])
    near = near_shards(part)
    hidden = spread_hidden(after(scalars, part), hidden_in, segment_ids)
    out_up, down_part = lax.optimization_barrier((jnp.concatenate([out_weight, up_weight], axis=1), down_weight, *near[1:4]))[:2]
    shards = all_shards(near)
    hidden += [swap_dp(piece, 1) for piece in hidden]
    out_up_near = near_shards(out_up)
    attended, lse, tokens, vec, up_add, segments, ordered, query, keys, values, keys_other, values_other, w_qkv = project(
        scalars, shards, hidden, width // PARTS, inner_width // PARTS, len(vectors), qblock, chunk, pairs * LANES
    )
    order = Order()
    got_up, odd = to_sequences(after(cotangent, *near[1:4], *hidden[:2]), order)
    upstream = in_order(lax.optimization_barrier((*got_up, attended))[:2], odd, hidden_in.shape[1])
    out_up_shards = all_shards(out_up_near, attended, upstream)
    down_near = near_shards(after(down_part, attended, *out_up_near[1:4]))
    normal_one, scale_one, first_low, active, slope, wo, wu = widen(scalars, out_up_shards, attended, tokens, vec, up_add)
    layer_low, sum_two_grad, second_grad, sums_two, down_send, down_keep, wd = narrow(
        scalars, all_shards(down_near, active), active, normal_one, vec, upstream
    )
    swap = (lambda value: swap_dp(value, 1)) if direct else (lambda value: value)
    order = Order()
    order.mark(second_grad)
    down_got = swap(down_send)
    out_pieces = from_sequences(layer_low, order)
    inner_grad, up_sum, up_send, up_keep = inner_back(scalars, order.gate(second_grad), wd, slope, first_low)
    up_got = swap(up_send)
    order.mark(inner_grad)
    if direct:
        ((send, down_keep),) = fold(order.gate(scalars), [(down_keep, down_got, (2, 1, 2))])
        down_got = swap_dp(order.mark(send), 2)
        ((send, up_keep),) = fold(order.gate(scalars), [(up_keep, up_got, (1, 2, 3))])
        up_got = swap_dp(order.mark(send), 4)
    sum_one_grad, attended_grad, sums_one, out_send, out_keep = outer_back(
        order.gate(scalars), inner_grad, wu, sum_two_grad, normal_one, scale_one, vec, wo, attended
    )
    order.mark(attended_grad)
    layer_out = order.mark(both_sequences(order, out_pieces))

    def attend(side):
        given = (query, keys, values, keys_other, values_other, attended, attended_grad, lse, segments)
        return order.mark(*attend_back(order.gate(scalars), *given, qblock, chunk, pairs, side))

    dq, dk, dv, far = attend(0)
    if direct:
        (send, down_keep), (other, up_keep) = fold(
            order.gate(scalars), [(down_keep, down_got, (1, 1, 3)), (up_keep, up_got, (1, 1, 2))]
        )
        order.mark(send, other)
        down_got, up_got = swap_dp(send, 4), swap_dp(other, 2)
    one_send, one_keep, gradient, sums_first = qkv_back(
        0, order.gate(scalars), dq, dk, dv, swap_dp(order.gate(far), 1), ordered, w_qkv, sum_one_grad, out_send, out_keep,
        sums_one, sums_two, up_sum
    )
    order.mark(gradient)
    one_got = swap(one_send)
    dq, dk, dv, far = attend(1)
    if direct:
        send, ff_keep = merge(order.gate(scalars), [(down_keep, down_got), (up_keep, up_got)], share)
        ff_got = swap_seq(order.mark(send), 1)
        ((send, one_keep),) = fold(order.gate(scalars), [(one_keep, one_got, (1, 2, 3))])
        one_got = swap_dp(order.mark(send), 4)
    two_send, two_keep, gradient, _ = qkv_back(
        1, order.gate(scalars), dq, dk, dv, swap_dp(order.gate(far), 1), ordered, w_qkv, gradient, sums_first
    )
    order.mark(gradient)
    two_got = swap(two_send)
    in_pieces = from_sequences(gradient, order)
    if not direct:
        down_grad, up_grad = scatter_all(down_send, down_keep), scatter_all(up_send, up_keep)
        one, two = scatter_all(one_send, one_keep), scatter_all(two_send, two_keep)
        cut = width // 2
        query_grad, key_grad, value_grad = [
            jnp.concatenate([side[:, i * cut : (i + 1) * cut] for side in (one, two)], axis=1) for i in range(3)
        ]
        out_grad = one[:, 3 * cut : 3 * cut + width]
        small, late = one[:, 3 * cut + width :].T, two[:, 3 * cut :].T
        up_bias_grad = lax.psum_scatter(up_sum[0], AXES, scatter_dimension=0, tiled=True)
    else:
        ((send, two_keep),) = fold(order.gate(scalars), [(two_keep, two_got, (2, 1, 2))])
        two_got = swap_dp(order.mark(send), 2)
        ((send, one_keep),) = fold(order.gate(scalars), [(one_keep, one_got, (1, 1, 2))])
        one_got = swap_dp(order.mark(send), 2)
        ((send, ff_keep),) = fold(order.gate(scalars), [(ff_keep, ff_got, (1, 1, 5))])
        ff_got = swap_seq(order.mark(send), 2)
        ((send, two_keep),) = fold(order.gate(scalars), [(two_keep, two_got, (1, 1, 3))])
        two_got = swap_dp(order.mark(send), 4)
        send, keep = merge(order.gate(scalars), [(one_keep, one_got), (two_keep, two_got)], share)
        got = swap_seq(order.mark(send), 1)
        down_grad, up_grad = order.mark(*last_ff(order.gate(scalars), ff_keep, ff_got, width))
        ((send, keep),) = fold(order.gate(scalars), [(keep, got, (1, 1, 5))])
        got = swap_seq(order.mark(send), 2)
    input_grad = order.mark(both_sequences(order, in_pieces).astype(jnp.float32))
    if direct:
        query_grad, key_grad, value_grad, out_grad, small, late, line = last_qkv(order.gate(scalars), keep, got, width)
        up_bias_grad = line[0, LANES - inner_width // devices :]
    ob, g1, s1 = [small[i, :share] for i in (0, 1, 2)]
    db, g2, s2 = [small[i, :share] for i in (8, 9, 10)]
    qb, vb = [late[i, :share] for i in (0, 1)]
    return (
        layer_out, input_grad, query_grad, qb, key_grad, value_grad, vb, out_grad, ob, g1, s1, up_grad, up_bias_grad, down_grad, db, g2, s2,
    )


def solution(mesh):
    wide, flat = P("dp", None), P("dp")
    in_specs = (
        P("dp", "seq", None), wide, wide, flat, wide, wide, flat, wide, flat, flat, flat, wide, flat, wide, flat,
        flat, flat, P("dp", "seq", None),
    )
    rows, cells = P(AXES, None), P(AXES)
    out_specs = (
        P("dp", "seq", None), P("dp", "seq", None), rows, cells, rows, rows, cells, rows, cells, cells, cells, rows,
        cells, rows, cells, cells, cells,
    )
    return jax.shard_map(per_device, mesh=mesh, in_specs=in_specs, out_specs=out_specs, check_vma=False)
```

```python
import functools
import math

import jax
import jax.numpy as jnp
from jax import lax
from jax.experimental import pallas as pl
from jax.experimental.pallas import tpu as pltpu
from jax.sharding import PartitionSpec as P

HEAD_DIM = 64
LANES = 128
NEGATIVE = -1e30


def nt(left, right):
    return lax.dot_general(left, right, (((1,), (1,)), ((), ())), preferred_element_type=jnp.float32)


def nn(left, right):
    return lax.dot_general(left, right, (((1,), (0,)), ((), ())), preferred_element_type=jnp.float32)


def head_parts(block):
    lane = lax.broadcasted_iota(jnp.int32, block.shape, 1)
    zero = jnp.zeros_like(block)
    return (jnp.where(lane < HEAD_DIM, block, zero), jnp.where(lane < HEAD_DIM, zero, block))


def same_document(column_tile, row):
    column = jnp.concatenate([column_tile] * (row.shape[1] // LANES), axis=1)
    return column == jnp.broadcast_to(row, column.shape)


def pair_lanes(pair):
    return slice(pair * LANES, (pair + 1) * LANES)


def segment_tables(segments, tiles, half, qblock, chunk):
    ids = segments[...]
    for j in range(tiles.shape[0]):
        for i in range(chunk // LANES):
            start = j * chunk + i * LANES
            tiles[j, i * LANES : (i + 1) * LANES, :] = jnp.broadcast_to(ids[:, start : start + LANES], (LANES, LANES)).T
    chunks = half // chunk
    low = [jnp.min(ids[:, j * chunk : (j + 1) * chunk]) for j in range(2 * chunks)]
    high = [jnp.max(ids[:, j * chunk : (j + 1) * chunk]) for j in range(2 * chunks)]
    found = []
    for b in range(half // qblock):
        mine = slice(b * qblock, (b + 1) * qblock)
        first, last = jnp.min(ids[:, mine]), jnp.max(ids[:, mine])
        bounds = []
        for side in range(2):
            before = sum((high[side * chunks + j] < first).astype(jnp.int32) for j in range(chunks))
            behind = sum((low[side * chunks + j] > last).astype(jnp.int32) for j in range(chunks))
            bounds += [before, chunks - behind]
        found.append((bounds[0], bounds[1] - bounds[0], bounds[2], bounds[1] - bounds[0] + bounds[3] - bounds[2]))
    return found


def chunk_of(bounds, step, chunks):
    first, own, other, _ = bounds
    return jnp.where(step < own, first + step, chunks + other + step - own)


def forward_body(qblock, chunk, lanes, q_all, k_all, v_all, ko_all, vo_all, segments, o_all, lse_all, kall, vt, sk_ref):
    half = k_all.shape[0]
    tables = segment_tables(segments, sk_ref, half, qblock, chunk)
    chunks, pairs = half // chunk, lanes // LANES

    @pl.loop(0, q_all.shape[1] // lanes)
    def _(group):
        cols = step_of(group, lanes)
        q_ref, k_ref, v_ref, ko_ref, vo_ref, o_ref = (r.at[:, cols] for r in (q_all, k_all, v_all, ko_all, vo_all, o_all))
        lse_ref = lse_all.at[pl.ds(group, 1)]
        for j in range(chunks):
            rows = slice(j * chunk, (j + 1) * chunk)
            kall[j] = k_ref[rows, :]
            kall[chunks + j] = ko_ref[rows, :]
            vt[j] = v_ref[rows, :].T
            vt[chunks + j] = vo_ref[rows, :].T
        for b in range(q_ref.shape[0] // qblock):
            span = slice(b * qblock, (b + 1) * qblock)
            parts = []
            for pair in range(pairs):
                parts += head_parts(q_ref[span, pair_lanes(pair)] * jnp.bfloat16(HEAD_DIM**-0.5))
            row = segments[:, span]

            def one(step, carry):
                j = chunk_of(tables[b], step, chunks)
                mask = same_document(sk_ref[j], row)
                scores = [jnp.where(mask, nt(kall[j, :, pair_lanes(h // 2)], part), NEGATIVE) for h, part in enumerate(parts)]
                out = []
                for h, score in enumerate(scores):
                    top, total, acc = carry[h]
                    new_top = jnp.maximum(top, jnp.max(score, axis=0, keepdims=True))
                    expo = jnp.exp(score - new_top)
                    scale = jnp.exp(top - new_top)
                    total = total * scale + jnp.sum(expo, axis=0, keepdims=True)
                    acc = acc * scale + nn(vt[j, h * HEAD_DIM : (h + 1) * HEAD_DIM, :], expo.astype(jnp.bfloat16))
                    out.append((new_top, total, acc))
                return tuple(out)

            init = (
                jnp.full((1, qblock), NEGATIVE, jnp.float32),
                jnp.zeros((1, qblock), jnp.float32),
                jnp.zeros((HEAD_DIM, qblock), jnp.float32),
            )
            carry = lax.fori_loop(0, tables[b][3], one, (init,) * len(parts))
            result = jnp.concatenate([acc / total for _, total, acc in carry], axis=0)
            o_ref[span, :] = result.T.astype(jnp.bfloat16)
            for h, (top, total, _) in enumerate(carry):
                lse_ref[0, h : h + 1, span] = top + jnp.log(total)


def backward_body(
    qblock, chunk, lanes, side, scalars, q_ref, k_ref, v_ref, ko_ref, vo_ref, o_ref, do_ref, lse_all, segments,
    dq_ref, dk_ref, dv_ref, far_ref, kall, vall, kt, dkall, dvall, sk_ref,
):
    half = k_ref.shape[0]
    tables = segment_tables(segments, sk_ref, half, qblock, chunk)
    lse_ref = lse_all.at[side : side + 1]
    chunks, pairs = half // chunk, lanes // LANES
    for j in range(chunks):
        rows = slice(j * chunk, (j + 1) * chunk)
        kall[j] = k_ref[rows, :]
        kall[chunks + j] = ko_ref[rows, :]
        vall[j] = v_ref[rows, :]
        vall[chunks + j] = vo_ref[rows, :]
        kt[j] = k_ref[rows, :].T
        kt[chunks + j] = ko_ref[rows, :].T
    dkall[...] = jnp.zeros_like(dkall)
    dvall[...] = jnp.zeros_like(dvall)
    for b in range(q_ref.shape[0] // qblock):
        span = slice(b * qblock, (b + 1) * qblock)
        parts, dparts, delta = [], [], []
        for pair in range(pairs):
            parts.append(head_parts(q_ref[span, pair_lanes(pair)] * jnp.bfloat16(HEAD_DIM**-0.5)))
            dparts.append(head_parts(do_ref[span, pair_lanes(pair)]))
            product = do_ref[span, pair_lanes(pair)].astype(jnp.float32) * o_ref[span, pair_lanes(pair)].astype(jnp.float32)
            product = product.T
            delta += [jnp.sum(product[h * HEAD_DIM : (h + 1) * HEAD_DIM], axis=0, keepdims=True) for h in range(2)]
        both = [jnp.concatenate(p, axis=0) for p in parts]
        dboth = [jnp.concatenate(p, axis=0) for p in dparts]
        row = segments[:, span]
        lse = [lse_ref[0, h : h + 1, span] for h in range(2 * pairs)]

        def one(step, carry):
            j = chunk_of(tables[b], step, chunks)
            mask = same_document(sk_ref[j], row)
            out = []
            for pair in range(pairs):
                key, val = kall[j, :, pair_lanes(pair)], vall[j, :, pair_lanes(pair)]
                probs, grads = [], []
                for side in range(2):
                    h = 2 * pair + side
                    score = jnp.where(mask, nt(key, parts[pair][side]), NEGATIVE)
                    prob = jnp.exp(score - lse[h])
                    grad = (prob * (nt(val, dparts[pair][side]) - delta[h])).astype(jnp.bfloat16)
                    probs.append(prob.astype(jnp.bfloat16))
                    grads.append(grad)
                    out.append(carry[h] + nn(kt[j, h * HEAD_DIM : (h + 1) * HEAD_DIM, :], grad))
                dvall[j, :, pair_lanes(pair)] += nn(jnp.concatenate(probs, axis=1), dboth[pair])
                dkall[j, :, pair_lanes(pair)] += nn(jnp.concatenate(grads, axis=1), both[pair])
            return tuple(out)

        zero = jnp.zeros((HEAD_DIM, qblock), jnp.float32)
        carry = lax.fori_loop(0, tables[b][3], one, (zero,) * (2 * pairs))
        dq_ref[span, :] = (jnp.concatenate(carry, axis=0).T * HEAD_DIM**-0.5).astype(jnp.bfloat16)
    for j in range(chunks):
        rows = slice(j * chunk, (j + 1) * chunk)
        dk_ref[rows, :] = dkall[j]
        dv_ref[rows, :] = dvall[j]
        far_ref[0, rows, :] = dkall[chunks + j].astype(jnp.bfloat16)
        far_ref[1, rows, :] = dvall[chunks + j].astype(jnp.bfloat16)


def attend_back(scalars, query, keys, values, keys_other, values_other, attended, grad, lse_rows, segments, qblock, chunk, pairs, side):
    tokens, width = query.shape
    half = keys.shape[0]
    lanes = pairs * LANES
    n = 2 * half // chunk
    f32, b16 = jnp.float32, jnp.bfloat16
    cols = slice(side * lanes, (side + 1) * lanes)
    far = [Far(x, cols) for x in (query, keys, values, keys_other, values_other, attended, grad)]
    return whole_call(
        functools.partial(backward_body, qblock, chunk, lanes, side), "attend_back", scalars, [], far + [lse_rows, segments],
        [array(b16, tokens, lanes), array(f32, half, lanes), array(f32, half, lanes), array(b16, 2, half, lanes)], [],
        [pltpu.VMEM((n, chunk, lanes), b16), pltpu.VMEM((n, chunk, lanes), b16), pltpu.VMEM((n, lanes, chunk), b16),
         pltpu.VMEM((n, chunk, lanes), f32), pltpu.VMEM((n, chunk, lanes), f32), pltpu.VMEM((n, chunk, LANES), f32)], 24,
    )


AXES = ("dp", "seq")
PARTS = 8
epsilon = 1e-12


def tn(left, right):
    return lax.dot_general(left, right, (((0,), (0,)), ((), ())), preferred_element_type=jnp.float32)


def norm_parts(value):
    center = value - jnp.mean(value, axis=-1, keepdims=True)
    spread = jnp.mean(center * center, axis=-1, keepdims=True)
    scale = lax.rsqrt(spread + epsilon)
    return (center * scale, scale)


def norm_back(upstream, normal, scale, gain):
    scaled = upstream * gain
    return scale * (
        scaled
        - jnp.mean(scaled, axis=-1, keepdims=True)
        - normal * jnp.mean(scaled * normal, axis=-1, keepdims=True)
    )


def row_sum(matrix):
    return jnp.sum(matrix.astype(jnp.float32), axis=0, keepdims=True)


def parts_of(refs):
    if len(refs) == PARTS:
        return [(i, 0, ref) for i, ref in enumerate(refs)]
    pieces = [(i, 0, ref) for i, ref in enumerate(refs[:6])]
    for i in range(2):
        top, bottom = refs[6 + i], refs[8 + i]
        pieces += [(6 + i, 0, top), (6 + i, top.shape[0], bottom)]
    return pieces


def load_pieces(me, pieces, rows, targets, sems):
    copies = [[] for _ in targets]
    for place, (part, first, ref) in enumerate(pieces):
        size = ref.shape[0]
        where = pl.ds(pl.multiple_of((me ^ part) * rows + first, 32), size)
        for i, (target, columns) in enumerate(targets):
            copy = pltpu.make_async_copy(ref.at[:, columns], target.at[where, :], sems.at[i, place])
            copy.start()
            copies[i].append(copy)
    return copies


def wait_all(copies):
    for copy in copies:
        copy.wait()


def step_of(block, size):
    return pl.ds(pl.multiple_of(block * size, size), size)


BLOCK = 1024
GELU_BLOCK = 256
ROWS = 256


def widen_body(scalars, *refs):
    shards = len(refs) - 12
    pieces = parts_of(refs[:shards])
    (attended, tokens, vec, up_add, normal_ref, scale_ref, low_ref, active_ref, slope_ref, wo, wu, sems) = refs[shards:]
    width, wide = wu.shape
    loads = load_pieces(scalars[0], pieces, width // PARTS, [(wo, slice(0, width)), (wu, slice(width, width + wide))], sems)
    wait_all(loads[0])

    @pl.loop(0, tokens.shape[0] // ROWS)
    def _(i):
        rows = step_of(i, ROWS)
        branch = nn(attended[rows, :], wo[...]) + vec[2:3, :]
        normal, scale = norm_parts(tokens[rows, :].astype(jnp.float32) + branch)
        first = normal * vec[3:4, :] + vec[4:5, :]
        normal_ref[rows, :] = normal
        scale_ref[rows, :] = jnp.broadcast_to(scale, (ROWS, LANES))
        low_ref[rows, :] = first.astype(jnp.bfloat16)

    wait_all(loads[1])

    @pl.loop(0, wide // GELU_BLOCK)
    def _(j):
        cols = step_of(j, GELU_BLOCK)
        inner = nn(low_ref[...], wu[:, cols]) + up_add[:, cols]
        cumulative = 0.5 * (1.0 + lax.erf(inner * math.sqrt(0.5)))
        density = jnp.exp(-0.5 * inner * inner) * (1.0 / math.sqrt(2.0 * math.pi))
        active_ref[:, cols] = (inner * cumulative).astype(jnp.bfloat16)
        slope_ref[:, cols] = (cumulative + inner * density).astype(jnp.bfloat16)


def narrow_body(scalars, *refs):
    shards = len(refs) - 13
    pieces = parts_of(refs[:shards])
    (active, normal_one, vec, upstream, out_ref, grad_ref, low_ref, sums_ref, send_ref, keep_ref, wd, sums, sems) = refs[shards:]
    wide, width = wd.shape
    (loads,) = load_pieces(scalars[0], pieces, wide // PARTS, [(wd, slice(0, width))], sems)
    wait_all(loads)
    sums[...] = jnp.zeros_like(sums)

    @pl.loop(0, normal_one.shape[0] // ROWS)
    def _(i):
        rows = step_of(i, ROWS)
        second = nn(active[rows, :], wd[...]) + vec[5:6, :]
        normal, scale = norm_parts(normal_one[rows, :] * vec[3:4, :] + vec[4:5, :] + second)
        out_ref[rows, :] = (normal * vec[6:7, :] + vec[7:8, :]).astype(jnp.bfloat16)
        up = upstream[rows, :].astype(jnp.float32)
        grad = norm_back(up, normal, scale, vec[6:7, :])
        low = grad.astype(jnp.bfloat16)
        grad_ref[rows, :] = grad
        low_ref[rows, :] = low
        sums[0:1, :] += row_sum(low)
        sums[1:2, :] += row_sum(up * normal)
        sums[2:3, :] += row_sum(up)

    sums_ref[...] = sums[...]
    size = wide // PARTS

    @pl.loop(0, PARTS // 2)
    def _(i):
        send_ref[i] = tn(active[:, step_of(2 * i + 1 - scalars[1], size)], low_ref[...]).astype(jnp.bfloat16)
        keep_ref[i] = tn(active[:, step_of(2 * i + scalars[1], size)], low_ref[...]).astype(jnp.bfloat16)


def turn_parts(core, turned, ordered):
    for i in range(PARTS // 2):
        ordered[0, i] = turned[2 * i + 1 - core]
        ordered[1, i] = turned[2 * i + core]


def inner_back_body(scalars, low, wd, slope, first_low, grad_ref, sums_ref, send_ref, keep_ref, turned, ordered):
    size = first_low.shape[1] // PARTS
    flipped = first_low[...].T
    for i in range(PARTS):
        turned[i] = flipped[i * size : (i + 1) * size, :]
    turn_parts(scalars[1], turned, ordered)
    rows = (PARTS // 2) * size

    @pl.loop(0, slope.shape[1] // BLOCK)
    def _(j):
        cols = step_of(j, BLOCK)
        grad = (nt(low[...], wd[cols, :]) * slope[:, cols].astype(jnp.float32)).astype(jnp.bfloat16)
        grad_ref[:, cols] = grad
        sums_ref[:, cols] = row_sum(grad)
        for side, ref in enumerate((send_ref, keep_ref)):
            left = ordered[side].reshape(rows, low.shape[0])
            ref[:, :, cols] = nn(left, grad).astype(jnp.bfloat16).reshape(PARTS // 2, size, BLOCK)


def outer_back_body(scalars, grad, wu, up_grad, normal_ref, scale_ref, vec, wo, attended, sum_ref, result_ref, sums_ref, send_ref, keep_ref, low, sums, turned):
    width = wo.shape[0]
    sums[...] = jnp.zeros_like(sums)

    @pl.loop(0, grad.shape[0] // ROWS)
    def _(i):
        rows = step_of(i, ROWS)
        first = up_grad[rows, :] + nt(grad[rows, :], wu[...])
        normal = normal_ref[rows, :]
        total = norm_back(first, normal, scale_ref[rows, 0:1], vec[3:4, :])
        branch = total.astype(jnp.bfloat16)
        sum_ref[rows, :] = total
        low[rows, :] = branch
        result_ref[rows, :] = nt(branch, wo[...]).astype(jnp.bfloat16)
        sums[0:1, :] += row_sum(branch)
        sums[1:2, :] += row_sum(first * normal)
        sums[2:3, :] += row_sum(first)

    sums_ref[...] = sums[...]
    size = width // PARTS
    product = tn(attended[...], low[...]).astype(jnp.bfloat16)
    for i in range(PARTS):
        turned[i] = product[i * size : (i + 1) * size, :]
    for i in range(PARTS // 2):
        send_ref[i] = turned[2 * i + 1 - scalars[1]]
        keep_ref[i] = turned[2 * i + scalars[1]]


class Far:
    def __init__(self, value, columns=None):
        self.value, self.columns = value, columns
        width = value.shape[-1] if columns is None else columns.stop - columns.start
        self.shape, self.dtype = value.shape[:-1] + (width,), value.dtype


def far_body(body, far, counts, scalars, *refs):
    hbm, inputs, outputs, held = counts
    given = list(refs[hbm : hbm + inputs])
    held_refs, sems = refs[len(refs) - held - 1 : -1], refs[-1]
    copies = []
    for i, (place, columns) in enumerate(far):
        source = given[place] if columns is None else given[place].at[:, columns]
        copies.append(pltpu.make_async_copy(source, held_refs[i], sems.at[i]))
        copies[-1].start()
        given[place] = held_refs[i]
    for copy in copies:
        copy.wait()
    body(scalars, *refs[:hbm], *given, *refs[hbm + inputs : len(refs) - held - 1])


def in_hbm(value):
    return pltpu.with_memory_space_constraint(value, pltpu.HBM)


def whole_call(body, name, scalars, hbm, inputs, outputs, hbm_outputs, scratch, room=8):
    shape_of = lambda x: jax.ShapeDtypeStruct(x.shape, x.dtype)
    near, stay = pl.BlockSpec(memory_space=pltpu.VMEM), pl.BlockSpec(memory_space=pltpu.HBM)
    far = [(i, x.columns) for i, x in enumerate(inputs) if isinstance(x, Far)]
    scratch = list(scratch)
    if far:
        held = [pltpu.VMEM(inputs[i].shape, inputs[i].dtype) for i, _ in far]
        counts = (len(hbm), len(inputs), len(outputs) + len(hbm_outputs), len(far))
        body = functools.partial(far_body, body, far, counts)
        scratch += held + [pltpu.SemaphoreType.DMA((len(far),))]
        room += sum(math.prod(inputs[i].shape) * inputs[i].dtype.itemsize for i, _ in far) // (1 << 20) + 1
    return pl.pallas_call(
        body,
        in_specs=[pl.BlockSpec(memory_space=pltpu.SMEM)]
        + [stay] * len(hbm)
        + [stay if isinstance(x, Far) else near for x in inputs],
        out_specs=[near] * len(outputs) + [stay] * len(hbm_outputs),
        scratch_shapes=scratch,
        out_shape=[shape_of(x) for x in outputs] + [pltpu.HBM(x.shape, x.dtype) for x in hbm_outputs],
        cost_estimate=pl.CostEstimate(flops=1, transcendentals=0, bytes_accessed=1),
        compiler_params=pltpu.CompilerParams(vmem_limit_bytes=room << 20),
        name=name,
    )(scalars, *[in_hbm(x) for x in hbm], *[in_hbm(x.value) if isinstance(x, Far) else x for x in inputs])


def array(dtype, *shape):
    return jax.ShapeDtypeStruct(shape, dtype)


def widen(scalars, pieces, attended, tokens, vec, up_add):
    count, width = tokens.shape
    wide = up_add.shape[1]
    f32, b16 = jnp.float32, jnp.bfloat16
    return whole_call(
        widen_body, "widen", scalars, pieces, [attended, tokens, vec, up_add],
        [array(f32, count, width), array(f32, count, LANES), array(b16, count, width),
         array(b16, count, wide), array(b16, count, wide), array(b16, width, width), array(b16, width, wide)],
        [], [pltpu.SemaphoreType.DMA((2, len(pieces)))],
    )


def narrow(scalars, pieces, active, normal, vec, upstream):
    count, wide = active.shape
    width = normal.shape[1]
    f32, b16 = jnp.float32, jnp.bfloat16
    half = array(b16, PARTS // 2, wide // PARTS, width)
    return whole_call(
        narrow_body, "narrow", scalars, pieces, [active, normal, vec, upstream],
        [array(b16, count, width), array(f32, count, width), array(b16, count, width), array(f32, 8, width), half, half, array(b16, wide, width)],
        [], [pltpu.VMEM((8, width), f32), pltpu.SemaphoreType.DMA((1, len(pieces)))],
    )


def inner_back(scalars, low, wd, slope, first_low):
    count, wide = slope.shape
    width = low.shape[1]
    size = width // PARTS
    f32, b16 = jnp.float32, jnp.bfloat16
    half = array(b16, PARTS // 2, size, wide)
    return whole_call(
        inner_back_body, "inner_back", scalars, [], [low, wd, slope, first_low],
        [array(b16, count, wide), array(f32, 1, wide), half, half], [],
        [pltpu.VMEM((PARTS, size, count), b16), pltpu.VMEM((2, PARTS // 2, size, count), b16)],
    )


def outer_back(scalars, grad, wu, up_grad, normal, scale, vec, wo, attended):
    count, width = normal.shape
    f32, b16 = jnp.float32, jnp.bfloat16
    half = array(b16, PARTS // 2, width // PARTS, width)
    return whole_call(
        outer_back_body, "outer_back", scalars, [], [grad, wu, up_grad, normal, scale, vec, wo, attended],
        [array(f32, count, width), array(b16, count, width), array(f32, 8, width), half, half], [],
        [pltpu.VMEM((count, width), b16), pltpu.VMEM((8, width), f32), pltpu.VMEM((PARTS, width // PARTS, width), b16)],
    )


def sums_to_slots(core, lines, parts, send, keep, first, wide=None):
    turned = lines[...].T
    rows = turned.shape[0] // PARTS
    for i in range(PARTS):
        parts[i] = turned[i * rows : (i + 1) * rows, :]
    if wide is not None:
        size = wide.shape[1] // (4 * PARTS)
        for i in range(4 * PARTS):
            place = (i % 4) * (rows // 4)
            parts[i // 4, place : place + 1, LANES - size :] = wide[:, i * size : (i + 1) * size]
    for i in range(PARTS // 2):
        send[i, :, first : first + LANES] = parts[2 * i + 1 - core].astype(jnp.bfloat16)
        keep[i, :, first : first + LANES] = parts[2 * i + core].astype(jnp.bfloat16)


def qkv_back_body(side, scalars, dq, dk, dv, far, ordered, weight, gradient, *refs):
    core = scalars[1]
    if side == 0:
        out_send, out_keep, sums_one, sums_two, wide_sums, send, keep, result, sums_ref, both, lines, parts = refs
    else:
        first_sums, send, keep, result, sums_ref, both, lines, parts = refs
    half = dq.shape[1]
    both[:, :half] = dq[...]
    both[:, half : 2 * half] = (dk[...] + far[0].astype(jnp.float32)).astype(jnp.bfloat16)
    both[:, 2 * half :] = (dv[...] + far[1].astype(jnp.float32)).astype(jnp.bfloat16)
    sums_ref[...] = jnp.zeros_like(sums_ref)
    sums_ref[0:1, :] = row_sum(dq[...])
    sums_ref[1:2, :] = row_sum(both[:, 2 * half :])
    rows = ordered.shape[1] * ordered.shape[2]
    for i, ref in enumerate((send, keep)):
        left = ordered[i].reshape(rows, ordered.shape[3])
        product = nn(left, both[...]).astype(jnp.bfloat16)
        ref[:, :, : 3 * half] = product.reshape(ordered.shape[1], ordered.shape[2], 3 * half)
    lines[...] = jnp.zeros_like(lines)
    if side == 0:
        width = out_send.shape[2]
        send[:, :, 3 * half : 3 * half + width] = out_send[...]
        keep[:, :, 3 * half : 3 * half + width] = out_keep[...]
        lines[0:8, :] = sums_one[...]
        lines[8:16, :] = sums_two[...]
        sums_to_slots(core, lines, parts, send, keep, 3 * half + width, wide_sums)
    else:
        lines[0:8, :half] = first_sums[...]
        lines[0:8, half:] = sums_ref[...]
        sums_to_slots(core, lines, parts, send, keep, 3 * half)
    result[...] = (gradient[...] + nt(both[...], weight[side])).astype(result.dtype)


def qkv_back(side, scalars, dq, dk, dv, far, ordered, weights, gradient, *more):
    count, half = dq.shape
    width = gradient.shape[1]
    f32, b16 = jnp.float32, jnp.bfloat16
    total = array(b16, PARTS // 2, width // PARTS, 3 * half + LANES + (width if side == 0 else 0))
    return whole_call(
        functools.partial(qkv_back_body, side), "qkv_back", scalars, [], [dq, dk, dv, far, Far(ordered), Far(weights), gradient, *more],
        [total, total, array(b16 if side else f32, count, width), array(f32, 8, half)], [],
        [pltpu.VMEM((count, 3 * half), b16), pltpu.VMEM((LANES, width), f32), pltpu.VMEM((PARTS, width // PARTS, LANES), f32)],
    )


STRIPE = 32


def fold_body(plans, scalars, *refs):
    for item, (outer, inner, bit) in enumerate(plans):
        keep, got = refs[2 * item : 2 * item + 2]
        send, left = refs[2 * (len(plans) + item) : 2 * (len(plans) + item) + 2]
        mine = scalars[bit]
        rows = keep.shape[1]
        stripe = STRIPE if rows % STRIPE == 0 else rows

        @pl.loop(0, rows // stripe)
        def _(k):
            span = step_of(k, stripe) if stripe != rows else slice(None)
            for i in range(outer):
                for j in range(inner):
                    for target, side in ((send, 1 - mine), (left, mine)):
                        place = (2 * i + side) * inner + j
                        value = keep[place, span, :].astype(jnp.float32) + got[place, span, :].astype(jnp.float32)
                        target[i * inner + j, span, :] = value.astype(target.dtype)


def fold(scalars, items):
    outs, plans = [], []
    for keep, got, (outer, inner, bit) in items:
        shape = (keep.shape[0] // 2,) + keep.shape[1:]
        outs += [array(jnp.bfloat16, *shape), array(keep.dtype, *shape)]
        plans.append((outer, inner, bit))
    got = whole_call(
        functools.partial(fold_body, plans), "fold", scalars, [], [x for keep, got, _ in items for x in (keep, got)], outs, [], []
    )
    return [(got[2 * i], got[2 * i + 1]) for i in range(len(items))]


def merge_body(shapes, scalars, *refs):
    send, left = refs[-2:]
    mine = scalars[4]
    low = send.shape[1]
    first = 0
    for item, (rows, wide) in enumerate(shapes):
        keep, got = refs[2 * item : 2 * item + 2]
        for part in range(rows // low):
            span = slice(part * low, (part + 1) * low)
            for high in range(2):
                for target, side in ((send, 1 - mine), (left, mine)):
                    value = keep[2 * high + side, span, :].astype(jnp.float32) + got[2 * high + side, span, :].astype(jnp.float32)
                    target[high, :, first : first + wide] = value.astype(target.dtype)
            first += wide


def merge(scalars, items, low):
    items = [(k.reshape(4, k.shape[-2] // 4, k.shape[-1]), g.reshape(4, g.shape[-2] // 4, g.shape[-1])) for k, g in items]
    shapes = [k.shape[1:] for k, _ in items]
    wide = sum(rows // low * n for rows, n in shapes)
    return whole_call(
        functools.partial(merge_body, shapes), "merge", scalars, [], [x for pair in items for x in pair],
        [array(jnp.bfloat16, 2, low, wide), array(jnp.float32, 2, low, wide)], [], [],
    )


def last_ff_body(scalars, keep, got, down_ref, up_ref):
    low = keep.shape[1]
    width = down_ref.shape[1]
    for part in range(down_ref.shape[0] // low):
        cols = slice(part * width, (part + 1) * width)
        down_ref[part * low : (part + 1) * low, :] = keep[0, :, cols] + got[0, :, cols].astype(jnp.float32)
    cols = slice(4 * width, 4 * width + up_ref.shape[1])
    up_ref[...] = keep[0, :, cols] + got[0, :, cols].astype(jnp.float32)


def last_ff(scalars, keep, got, width):
    low = keep.shape[1]
    return whole_call(
        last_ff_body, "last_ff", scalars, [], [keep, got], [array(jnp.float32, 4 * low, width), array(jnp.float32, low, 4 * width)], [], []
    )


def last_qkv_body(scalars, keep, got, query_ref, key_ref, value_ref, out_ref, small_ref, late_ref, wide_ref, turned):
    low = keep.shape[1]
    width = query_ref.shape[1]
    half = width // 2
    second = 3 * half + width + LANES

    def total(first, size):
        return keep[0, :, first : first + size] + got[0, :, first : first + size].astype(jnp.float32)

    for i, ref in enumerate((query_ref, key_ref, value_ref)):
        ref[:, :half] = total(i * half, half)
        ref[:, half:] = total(second + i * half, half)
    out_ref[...] = total(3 * half, width)
    wide_ref[...] = total(3 * half + width, LANES)[0:1, :]
    for ref, first in ((small_ref, 3 * half + width), (late_ref, second + 3 * half)):
        turned[...] = jnp.zeros_like(turned)
        turned[:low, :] = total(first, LANES)
        ref[...] = turned[...].T[: ref.shape[0], :]


def last_qkv(scalars, keep, got, width):
    low = keep.shape[1]
    f32 = jnp.float32
    return whole_call(
        last_qkv_body, "last_qkv", scalars, [], [keep, got],
        [array(f32, low, width)] * 4 + [array(f32, 24, LANES), array(f32, 8, LANES), array(f32, 1, LANES)], [], [pltpu.VMEM((LANES, LANES), f32)],
    )


def after(value, *others):
    return lax.optimization_barrier((value,) + others)[0]


def bit_count(size):
    return size.bit_length() - 1


def swap_dp(value, mask):
    return lax.ppermute(value, "dp", [(i, i ^ mask) for i in range(lax.axis_size("dp"))])


def swap_seq(value, mask):
    return lax.ppermute(value, "seq", [(i, i ^ mask) for i in range(lax.axis_size("seq"))])


def column_sum(matrix):
    return jnp.sum(matrix.astype(jnp.float32), axis=0)


def spread_pairs(first):
    dps, seqs = lax.axis_size("dp"), lax.axis_size("seq")
    pairs = []
    for dp in range(dps):
        for seq in range(seqs):
            piece = first ^ (seq & 1)
            to_dp = (dp & ~1) | (seq >> 1)
            to_seq = 2 * (dp & 1) + piece
            pairs.append((dp * seqs + seq, to_dp * seqs + to_seq))
    return pairs


def to_sequences(local, order):
    odd = (lax.axis_index("seq") & 1) == 1
    got = []
    pieces = [jnp.where(odd, local[1 - first], local[first]) for first in range(2)]
    order.mark(*pieces)
    for first, piece in enumerate(pieces):
        got.append(lax.ppermute(piece, AXES, spread_pairs(first)))
    return got, odd


def in_order(got, odd, rows):
    return jnp.where(odd, jnp.concatenate([g[:rows] for g in got[::-1]]), jnp.concatenate([g[:rows] for g in got]))


def from_sequences(tokens, order):
    odd = (lax.axis_index("seq") & 1) == 1
    half = tokens.shape[0] // 2
    got = []
    for first in range(2):
        near, far = tokens[first * half : (first + 1) * half], tokens[(1 - first) * half : (2 - first) * half]
        piece = order.mark(jnp.where(order.gate(odd), far, near))
        got.append(lax.ppermute(piece, AXES, [(b, a) for a, b in spread_pairs(first)]))
    return got


def both_sequences(order, got):
    odd = order.gate((lax.axis_index("seq") & 1) == 1)
    return jnp.where(odd, jnp.stack(got[::-1]), jnp.stack(got))


def weight_lines(weights, lines):
    width = weights[0].shape[-1]
    lines = [jnp.pad(v[..., None, :], [(0, 0)] * v.ndim + [(0, width - v.shape[-1])]) for v in lines]
    lines.append(jnp.zeros(lines[0].shape[:-2] + (16 - len(lines), width), jnp.bfloat16))
    return jnp.concatenate(weights + lines, axis=-2)


def near_shards(part, across=True):
    if lax.axis_size("dp") != PARTS:
        p = part if part.ndim == 3 else jnp.stack(jnp.split(lax.all_gather(part, "dp", axis=0, tiled=True), PARTS))
        return [p[i] for i in range(PARTS)]
    return [part, swap_dp(part, 2), swap_dp(part, 4)] + ([swap_dp(part, 6)] if across else [])


def both_cores(parts):
    return [shard for part in parts for shard in (part, swap_dp(part, 1))]


def all_shards(near, *ready):
    if len(near) == PARTS:
        return near
    return both_cores([near[0]] + list(lax.optimization_barrier((*near[1:], *ready))[:3]))


def relayed_shards(near, cut, *ready):
    if len(near) == PARTS:
        return near
    own, along_x, along_y = near
    along_x, along_y = lax.optimization_barrier((along_x, along_y, *ready))[:2]
    sent = along_x[:cut], along_y[cut:]
    top, bottom = swap_dp(sent[0], 4), swap_dp(sent[1], 2)
    own, along_x, along_y = lax.optimization_barrier((own, along_x, along_y, *sent))[:3]
    return both_cores([own, along_x, along_y, top, bottom])


def pack_body(count, scalars, *refs):
    weights, vectors, hidden, ids = refs[: min(3, count)], refs[3:count], refs[count], refs[count + 1]
    pieces = refs[count + 2 : count + 4]
    if vectors:
        part, lines = refs[count + 4 :]
        rows = weights[0].shape[0]
        for i, ref in enumerate(weights):
            part[i * rows : (i + 1) * rows, :] = ref[...]
        lines[...] = jnp.zeros_like(lines)
        for i, ref in enumerate(vectors):
            lines[i : i + 1, : ref.shape[1]] = ref[...].astype(jnp.float32)
        part[3 * rows :, :] = lines[...].astype(jnp.bfloat16)
    odd = scalars[7]
    block, half = hidden.shape[1], ids.shape[1] // 2
    for first, piece in enumerate(pieces):
        piece[:block, :] = hidden[first ^ odd]
        line = jnp.where(first ^ odd == 0, ids[0:1, :], ids[1:2, :]).astype(jnp.bfloat16)
        piece[block:, :] = jnp.zeros_like(piece[block:, :])
        piece[block : block + 1, :half] = line[:, :half]
        piece[block + 1 : block + 2, :half] = line[:, half:]


def pack(scalars, weights, vectors, hidden, ids):
    piece = array(jnp.bfloat16, hidden.shape[1] + 16, hidden.shape[2])
    if lax.axis_size("dp") == PARTS:
        rows, width = weights[0].shape
        given = weights + [v[None, :] for v in vectors]
        return whole_call(
            functools.partial(pack_body, len(given)), "pack", scalars, [], [Far(x) for x in given + [hidden, ids]],
            [piece, piece, array(jnp.bfloat16, 3 * rows + 16, width)], [], [pltpu.VMEM((16, width), jnp.float32)],
        )
    gather = lambda v: lax.all_gather(v, "dp", axis=0, tiled=True)
    split = lambda v: gather(v).reshape((PARTS, -1) + v.shape[1:])
    pieces = whole_call(functools.partial(pack_body, 0), "pack", scalars, [], [Far(hidden), Far(ids)], [piece, piece], [], [])
    return *pieces, weight_lines([split(w) for w in weights], [split(v) for v in vectors])


def project_body(sizes, scalars, *refs):
    rows, wide, vectors, qblock, chunk, lanes, shards = sizes
    pieces, hidden = parts_of(refs[:shards]), refs[shards : shards + 4]
    (
        attended, lse, tokens, vec_ref, up_ref, segments, ordered, query_out, keys_out, values_out, keys_far_out, values_far_out, weights_out,
        query, keys, values, keys_far, values_far, far, held, small, turned, ids, sems, hidden_sems, out_sems, kall, vt, tiles,
    ) = refs[shards + 4 :]
    count, width = tokens.shape
    block = count // 2
    half = width // 2
    core, odd = scalars[6], scalars[7]
    copies, brought = [], []

    def start(copies, source, target, sem):
        copies.append(pltpu.make_async_copy(source, target, sem))
        copies[-1].start()

    for i, (ref, place) in enumerate(zip(hidden, (0, 1, 0, 1))):
        goal = tokens if i < 2 else far
        start(brought, ref.at[:block, :], goal.at[pl.ds(pl.multiple_of((place ^ odd) * block, block), block), :], hidden_sems.at[i])
    start(brought, hidden[0].at[block:, :], ids, hidden_sems.at[4])
    for part, first, ref in pieces:
        where = scalars[0] ^ part
        target = pl.ds(where * rows, rows)
        for weight in range(first // rows, (first + ref.shape[0]) // rows):
            for side in range(2):
                start(
                    copies,
                    ref.at[weight * rows - first : (weight + 1) * rows - first, side * half : (side + 1) * half],
                    held.at[side, target, weight * half : (weight + 1) * half],
                    sems.at[len(copies)],
                )
        if first + ref.shape[0] > 3 * rows:
            start(copies, ref.at[3 * rows - first :, :], small.at[where], sems.at[len(copies)])
    wait_all(brought)
    line = ids[...].astype(jnp.float32)
    for i in range(2):
        segments[:, i * count : (i + 1) * count] = jnp.where(core == i, line[0:1, :count], line[1:2, :count])
    flipped = tokens[...].T
    for i in range(PARTS):
        turned[i] = flipped[i * rows : (i + 1) * rows, :]
    turn_parts(scalars[1], turned, ordered)
    wait_all(copies)
    saves = []
    start(saves, held, weights_out, out_sems.at[0])
    vec_ref[...] = jnp.concatenate([small[i, :, :rows] for i in range(PARTS)], axis=1).astype(jnp.float32)
    up_ref[...] = jnp.concatenate([small[i, vectors : vectors + 1, :wide] for i in range(PARTS)], axis=1).astype(jnp.float32)
    for i, (weight, add, goal, source, out) in enumerate((
        (1, None, keys, tokens, keys_out), (1, None, keys_far, far, keys_far_out), (2, 1, values, tokens, values_out),
        (2, 1, values_far, far, values_far_out), (0, 0, query, tokens, query_out),
    )):
        for side in range(2):
            cols = slice(side * half, (side + 1) * half)
            product = nn(source[...], held[side, :, weight * half : (weight + 1) * half])
            if add is not None:
                product = product + vec_ref[add : add + 1, cols]
            goal[:, cols] = product.astype(jnp.bfloat16)
        start(saves, goal, out, out_sems.at[i + 1])
    forward_body(qblock, chunk, lanes, query, keys, values, keys_far, values_far, segments, attended, lse, kall, vt, tiles)
    wait_all(saves)


def project(scalars, pieces, hidden, rows, wide, vectors, qblock, chunk, lanes):
    block, width = hidden[0].shape[0] - 16, hidden[0].shape[1]
    count = 2 * block
    lines = 16
    n = 2 * count // chunk
    f32, b16 = jnp.float32, jnp.bfloat16
    whole = array(b16, count, width)
    vmem = lambda x: pltpu.VMEM(x.shape, x.dtype)
    return whole_call(
        functools.partial(project_body, (rows, wide, vectors, qblock, chunk, lanes, len(pieces))), "project", scalars, list(pieces) + list(hidden), [],
        [whole, array(f32, width // lanes, 8, count), whole, array(f32, lines, width), array(f32, 1, wide * PARTS), array(f32, 1, 2 * count),
         array(b16, 2, PARTS // 2, rows, count)],
        [whole] * 5 + [array(b16, 2, width, 3 * width // 2)],
        [vmem(whole)] * 6
        + [pltpu.VMEM((2, width, 3 * width // 2), b16), pltpu.VMEM((PARTS, lines, width), b16), pltpu.VMEM((PARTS, rows, count), b16),
           pltpu.VMEM((16, width), b16), pltpu.SemaphoreType.DMA((7 * PARTS,)),
           pltpu.SemaphoreType.DMA((5,)), pltpu.SemaphoreType.DMA((6,)), pltpu.VMEM((n, chunk, lanes), b16),
           pltpu.VMEM((n, lanes, chunk), b16), pltpu.VMEM((n, chunk, LANES), f32)],
        28,
    )


class Order:
    def __init__(self):
        self.last = ()

    def gate(self, value):
        return lax.optimization_barrier((value, *self.last))[0] if self.last else value

    def mark(self, *values):
        self.last = values
        return values[0] if len(values) == 1 else values


def all_rows(send, keep):
    return jnp.stack([keep, send], axis=1).reshape(-1, keep.shape[-1]).astype(jnp.float32)


def scatter_all(send, keep):
    return lax.psum_scatter(all_rows(send, keep), AXES, scatter_dimension=0, tiled=True)


def per_device(
    hidden_in, segment_ids, query_weight, query_bias, key_weight, value_weight, value_bias, out_weight, out_bias,
    first_gain, first_shift, up_weight, up_bias, down_weight, down_bias, second_gain, second_shift, cotangent,
):
    dps, seqs = lax.axis_size("dp"), lax.axis_size("seq")
    inner_width, width = up_weight.shape[1], query_weight.shape[1]
    devices = dps * seqs
    share = width // devices
    qblock = chunk = 256
    pairs = 3
    direct = dps == PARTS and seqs == 4
    dp, seq = lax.axis_index("dp"), lax.axis_index("seq")
    if direct:
        scalars = [dp, dp & 1, (dp >> 1) & 1, dp >> 2, seq & 1, seq >> 1, dp & 1, seq & 1]
    else:
        scalars = [0, 0, 0, 0, 0, 0, dp & 1, seq & 1]
    scalars = jnp.stack([jnp.asarray(v, jnp.int32) for v in scalars])

    vectors = [query_bias, value_bias, out_bias, first_gain, first_shift, down_bias, second_gain, second_shift]
    *hidden, part = pack(
        scalars, [query_weight, key_weight, value_weight], vectors + [up_bias], hidden_in, segment_ids
    )
    near = near_shards(part, False)
    hidden = [lax.ppermute(piece, AXES, spread_pairs(first)) for first, piece in enumerate(hidden)]
    shards = relayed_shards(near, 2 * width // PARTS)
    out_up, down_part = lax.optimization_barrier(
        (jnp.concatenate([out_weight, up_weight], axis=1), down_weight, *near[1:3])
    )[:2]
    if direct:
        hidden = list(lax.optimization_barrier((*hidden, near[1], near[2]))[:2])
    hidden += [swap_dp(piece, 1) for piece in hidden]
    out_up_near = near_shards(out_up)
    attended, lse, tokens, vec, up_add, segments, ordered, query, keys, values, keys_other, values_other, w_qkv = project(
        scalars, shards, hidden, width // PARTS, inner_width // PARTS, len(vectors), qblock, chunk, pairs * LANES
    )
    order = Order()
    down_near = near_shards(after(down_part, attended, *out_up_near[1:4]), False)
    got_up, odd = to_sequences(after(cotangent, attended), order)
    out_up_shards = all_shards(out_up_near, attended)
    normal_one, scale_one, first_low, active, slope, wo, wu = widen(scalars, out_up_shards, attended, tokens, vec, up_add)
    upstream = in_order(lax.optimization_barrier((*got_up, active))[:2], odd, hidden_in.shape[1])
    layer_low, sum_two_grad, second_grad, sums_two, down_send, down_keep, wd = narrow(
        scalars, relayed_shards(down_near, inner_width // PARTS // 2, active), active, normal_one, vec, upstream
    )
    swap = (lambda value: swap_dp(value, 1)) if direct else (lambda value: value)
    order = Order()
    order.mark(second_grad)
    down_got = swap(down_send)
    out_pieces = from_sequences(layer_low, order)
    inner_grad, up_sum, up_send, up_keep = inner_back(scalars, order.gate(second_grad), wd, slope, first_low)
    up_got = swap(up_send)
    order.mark(inner_grad)
    if direct:
        ((send, down_keep),) = fold(order.gate(scalars), [(down_keep, down_got, (2, 1, 2))])
        down_got = swap_dp(order.mark(send), 2)
        ((send, up_keep),) = fold(order.gate(scalars), [(up_keep, up_got, (1, 2, 3))])
        up_got = swap_dp(order.mark(send), 4)
    sum_one_grad, attended_grad, sums_one, out_send, out_keep = outer_back(
        order.gate(scalars), inner_grad, wu, sum_two_grad, normal_one, scale_one, vec, wo, attended
    )
    order.mark(attended_grad)

    def attend(side):
        given = (query, keys, values, keys_other, values_other, attended, attended_grad, lse, segments)
        return order.mark(*attend_back(order.gate(scalars), *given, qblock, chunk, pairs, side))

    dq, dk, dv, far = attend(0)
    if direct:
        (send, down_keep), (other, up_keep) = fold(
            order.gate(scalars), [(down_keep, down_got, (1, 1, 3)), (up_keep, up_got, (1, 1, 2))]
        )
        order.mark(send, other)
        down_got, up_got = swap_dp(send, 4), swap_dp(other, 2)
    layer_out = order.mark(both_sequences(order, out_pieces))
    one_send, one_keep, gradient, sums_first = qkv_back(
        0, order.gate(scalars), dq, dk, dv, swap_dp(order.gate(far), 1), ordered, w_qkv, sum_one_grad, out_send, out_keep,
        sums_one, sums_two, up_sum
    )
    order.mark(gradient)
    one_got = swap(one_send)
    dq, dk, dv, far = attend(1)
    if direct:
        send, ff_keep = merge(order.gate(scalars), [(down_keep, down_got), (up_keep, up_got)], share)
        ff_got = swap_seq(order.mark(send), 1)
        ((send, one_keep),) = fold(order.gate(scalars), [(one_keep, one_got, (1, 2, 3))])
        one_got = swap_dp(order.mark(send), 4)
    two_send, two_keep, gradient, _ = qkv_back(
        1, order.gate(scalars), dq, dk, dv, swap_dp(order.gate(far), 1), ordered, w_qkv, gradient, sums_first
    )
    order.mark(gradient)
    two_got = swap(two_send)
    in_pieces = from_sequences(gradient, order)
    if not direct:
        down_grad, up_grad = scatter_all(down_send, down_keep), scatter_all(up_send, up_keep)
        one, two = scatter_all(one_send, one_keep), scatter_all(two_send, two_keep)
        cut = width // 2
        query_grad, key_grad, value_grad = [
            jnp.concatenate([side[:, i * cut : (i + 1) * cut] for side in (one, two)], axis=1) for i in range(3)
        ]
        out_grad = one[:, 3 * cut : 3 * cut + width]
        small, late = one[:, 3 * cut + width :].T, two[:, 3 * cut :].T
        up_bias_grad = lax.psum_scatter(up_sum[0], AXES, scatter_dimension=0, tiled=True)
    else:
        ((send, two_keep),) = fold(order.gate(scalars), [(two_keep, two_got, (2, 1, 2))])
        two_got = swap_dp(order.mark(send), 2)
        ((send, one_keep),) = fold(order.gate(scalars), [(one_keep, one_got, (1, 1, 2))])
        one_got = swap_dp(order.mark(send), 2)
        ((send, ff_keep),) = fold(order.gate(scalars), [(ff_keep, ff_got, (1, 1, 5))])
        ff_got = swap_seq(order.mark(send), 2)
        ((send, two_keep),) = fold(order.gate(scalars), [(two_keep, two_got, (1, 1, 3))])
        two_got = swap_dp(order.mark(send), 4)
    input_grad = order.mark(both_sequences(order, in_pieces).astype(jnp.float32))
    if direct:
        send, keep = merge(order.gate(scalars), [(one_keep, one_got), (two_keep, two_got)], share)
        got = swap_seq(order.mark(send), 1)
        ((send, keep),) = fold(order.gate(scalars), [(keep, got, (1, 1, 5))])
        got = swap_seq(order.mark(send), 2)
        down_grad, up_grad = order.mark(*last_ff(order.gate(scalars), ff_keep, ff_got, width))
    if direct:
        query_grad, key_grad, value_grad, out_grad, small, late, line = last_qkv(order.gate(scalars), keep, got, width)
        up_bias_grad = line[0, LANES - inner_width // devices :]
    ob, g1, s1 = [small[i, :share] for i in (0, 1, 2)]
    db, g2, s2 = [small[i, :share] for i in (8, 9, 10)]
    qb, vb = [late[i, :share] for i in (0, 1)]
    return (
        layer_out, input_grad, query_grad, qb, key_grad, value_grad, vb, out_grad, ob, g1, s1, up_grad, up_bias_grad, down_grad, db, g2, s2,
    )


def solution(mesh):
    wide, flat = P("dp", None), P("dp")
    in_specs = (
        P("dp", "seq", None), wide, wide, flat, wide, wide, flat, wide, flat, flat, flat, wide, flat, wide, flat,
        flat, flat, P("dp", "seq", None),
    )
    rows, cells = P(AXES, None), P(AXES)
    out_specs = (
        P("dp", "seq", None), P("dp", "seq", None), rows, cells, rows, rows, cells, rows, cells, cells, cells, rows,
        cells, rows, cells, cells, cells,
    )
    return jax.shard_map(per_device, mesh=mesh, in_specs=in_specs, out_specs=out_specs, check_vma=False)
```

```python
import functools
import math

import jax
import jax.numpy as jnp
from jax import lax
from jax.experimental import pallas as pl
from jax.experimental.pallas import tpu as pltpu
from jax.sharding import PartitionSpec as P

HEAD_DIM = 64
LANES = 128
NEGATIVE = -1e30


def nt(left, right):
    return lax.dot_general(left, right, (((1,), (1,)), ((), ())), preferred_element_type=jnp.float32)


def nn(left, right):
    return lax.dot_general(left, right, (((1,), (0,)), ((), ())), preferred_element_type=jnp.float32)


def head_parts(block):
    lane = lax.broadcasted_iota(jnp.int32, block.shape, 1)
    zero = jnp.zeros_like(block)
    return (jnp.where(lane < HEAD_DIM, block, zero), jnp.where(lane < HEAD_DIM, zero, block))


def same_document(column_tile, row):
    column = jnp.concatenate([column_tile] * (row.shape[1] // LANES), axis=1)
    return column == jnp.broadcast_to(row, column.shape)


def pair_lanes(pair):
    return slice(pair * LANES, (pair + 1) * LANES)


def segment_tables(segments, tiles, half, qblock, chunk):
    ids = segments[...]
    for j in range(tiles.shape[0]):
        for i in range(chunk // LANES):
            start = j * chunk + i * LANES
            tiles[j, i * LANES : (i + 1) * LANES, :] = jnp.broadcast_to(ids[:, start : start + LANES], (LANES, LANES)).T
    chunks = half // chunk
    low = [jnp.min(ids[:, j * chunk : (j + 1) * chunk]) for j in range(2 * chunks)]
    high = [jnp.max(ids[:, j * chunk : (j + 1) * chunk]) for j in range(2 * chunks)]
    found = []
    for b in range(half // qblock):
        mine = slice(b * qblock, (b + 1) * qblock)
        first, last = jnp.min(ids[:, mine]), jnp.max(ids[:, mine])
        bounds = []
        for side in range(2):
            before = sum((high[side * chunks + j] < first).astype(jnp.int32) for j in range(chunks))
            behind = sum((low[side * chunks + j] > last).astype(jnp.int32) for j in range(chunks))
            bounds += [before, chunks - behind]
        found.append((bounds[0], bounds[1] - bounds[0], bounds[2], bounds[1] - bounds[0] + bounds[3] - bounds[2]))
    return found


def chunk_of(bounds, step, chunks):
    first, own, other, _ = bounds
    return jnp.where(step < own, first + step, chunks + other + step - own)


def forward_body(qblock, chunk, lanes, q_all, k_all, v_all, ko_all, vo_all, segments, o_all, lse_all, kall, vt, sk_ref):
    half = k_all.shape[0]
    tables = segment_tables(segments, sk_ref, half, qblock, chunk)
    chunks, pairs = half // chunk, lanes // LANES

    @pl.loop(0, q_all.shape[1] // lanes)
    def _(group):
        cols = step_of(group, lanes)
        q_ref, k_ref, v_ref, ko_ref, vo_ref, o_ref = (r.at[:, cols] for r in (q_all, k_all, v_all, ko_all, vo_all, o_all))
        lse_ref = lse_all.at[pl.ds(group, 1)]
        for j in range(chunks):
            rows = slice(j * chunk, (j + 1) * chunk)
            kall[j] = k_ref[rows, :]
            kall[chunks + j] = ko_ref[rows, :]
            vt[j] = v_ref[rows, :].T
            vt[chunks + j] = vo_ref[rows, :].T
        for b in range(q_ref.shape[0] // qblock):
            span = slice(b * qblock, (b + 1) * qblock)
            parts = []
            for pair in range(pairs):
                parts += head_parts(q_ref[span, pair_lanes(pair)] * jnp.bfloat16(HEAD_DIM**-0.5))
            row = segments[:, span]

            def one(step, carry):
                j = chunk_of(tables[b], step, chunks)
                mask = same_document(sk_ref[j], row)
                scores = [jnp.where(mask, nt(kall[j, :, pair_lanes(h // 2)], part), NEGATIVE) for h, part in enumerate(parts)]
                out = []
                for h, score in enumerate(scores):
                    top, total, acc = carry[h]
                    new_top = jnp.maximum(top, jnp.max(score, axis=0, keepdims=True))
                    expo = jnp.exp(score - new_top)
                    scale = jnp.exp(top - new_top)
                    total = total * scale + jnp.sum(expo, axis=0, keepdims=True)
                    acc = acc * scale + nn(vt[j, h * HEAD_DIM : (h + 1) * HEAD_DIM, :], expo.astype(jnp.bfloat16))
                    out.append((new_top, total, acc))
                return tuple(out)

            init = (
                jnp.full((1, qblock), NEGATIVE, jnp.float32),
                jnp.zeros((1, qblock), jnp.float32),
                jnp.zeros((HEAD_DIM, qblock), jnp.float32),
            )
            carry = lax.fori_loop(0, tables[b][3], one, (init,) * len(parts))
            result = jnp.concatenate([acc / total for _, total, acc in carry], axis=0)
            o_ref[span, :] = result.T.astype(jnp.bfloat16)
            for h, (top, total, _) in enumerate(carry):
                lse_ref[0, h : h + 1, span] = top + jnp.log(total)


def backward_body(
    qblock, chunk, lanes, side, copies, scalars, q_ref, k_ref, v_ref, ko_ref, vo_ref, o_ref, do_ref, lse_all, segments,
    dq_ref, dk_ref, dv_ref, far_keys, far_values, kall, vall, kt, dkall, dvall, sk_ref,
):
    half = k_ref.shape[0]
    tables = segment_tables(segments, sk_ref, half, qblock, chunk)
    lse_ref = lse_all.at[side : side + 1]
    chunks, pairs = half // chunk, lanes // LANES
    dkall[...] = jnp.zeros_like(dkall)
    dvall[...] = jnp.zeros_like(dvall)
    for first, keys, values in ((0, k_ref, v_ref), (chunks, ko_ref, vo_ref)):
        wait_all(copies[1:3] if first == 0 else copies[3:5])
        for j in range(chunks):
            rows = slice(j * chunk, (j + 1) * chunk)
            kall[first + j] = keys[rows, :]
            vall[first + j] = values[rows, :]
            kt[first + j] = keys[rows, :].T
    wait_all(copies[:1] + copies[5:])
    for b in range(q_ref.shape[0] // qblock):
        span = slice(b * qblock, (b + 1) * qblock)
        parts, dparts, delta = [], [], []
        for pair in range(pairs):
            parts.append(head_parts(q_ref[span, pair_lanes(pair)] * jnp.bfloat16(HEAD_DIM**-0.5)))
            dparts.append(head_parts(do_ref[span, pair_lanes(pair)]))
            product = do_ref[span, pair_lanes(pair)].astype(jnp.float32) * o_ref[span, pair_lanes(pair)].astype(jnp.float32)
            product = product.T
            delta += [jnp.sum(product[h * HEAD_DIM : (h + 1) * HEAD_DIM], axis=0, keepdims=True) for h in range(2)]
        both = [jnp.concatenate(p, axis=0) for p in parts]
        dboth = [jnp.concatenate(p, axis=0) for p in dparts]
        row = segments[:, span]
        lse = [lse_ref[0, h : h + 1, span] for h in range(2 * pairs)]

        def one(step, carry):
            j = chunk_of(tables[b], step, chunks)
            mask = same_document(sk_ref[j], row)
            out = []
            both_mask = jnp.concatenate([mask, mask], axis=1)
            scores = [nt(kall[j, :, pair_lanes(pair)], both[pair]) for pair in range(pairs)]
            products = [nt(vall[j, :, pair_lanes(pair)], dboth[pair]) for pair in range(pairs)]
            adds = []
            for pair in range(pairs):
                score = jnp.where(both_mask, scores[pair], NEGATIVE)
                prob = jnp.exp(score - jnp.concatenate(lse[2 * pair : 2 * pair + 2], axis=1))
                grad = (prob * (products[pair] - jnp.concatenate(delta[2 * pair : 2 * pair + 2], axis=1))).astype(jnp.bfloat16)
                for side in range(2):
                    h = 2 * pair + side
                    out.append(carry[h] + nn(kt[j, h * HEAD_DIM : (h + 1) * HEAD_DIM, :], grad[:, side * qblock : (side + 1) * qblock]))
                adds.append((nn(prob.astype(jnp.bfloat16), dboth[pair]), nn(grad, both[pair])))
            for pair in range(pairs):
                dvall[j, :, pair_lanes(pair)] += adds[pair][0]
                dkall[j, :, pair_lanes(pair)] += adds[pair][1]
            return tuple(out)

        zero = jnp.zeros((HEAD_DIM, qblock), jnp.float32)
        carry = lax.fori_loop(0, tables[b][3], one, (zero,) * (2 * pairs))
        dq_ref[span, :] = (jnp.concatenate(carry, axis=0).T * HEAD_DIM**-0.5).astype(jnp.bfloat16)
    for j in range(chunks):
        rows = slice(j * chunk, (j + 1) * chunk)
        dk_ref[rows, :] = dkall[j]
        dv_ref[rows, :] = dvall[j]
        far_keys[rows, :] = dkall[chunks + j].astype(jnp.bfloat16)
        far_values[rows, :] = dvall[chunks + j].astype(jnp.bfloat16)


def attend_back(scalars, query, keys, values, keys_other, values_other, attended, grad, lse_rows, segments, qblock, chunk, pairs, side):
    tokens, width = query.shape
    half = keys.shape[0]
    lanes = pairs * LANES
    n = 2 * half // chunk
    f32, b16 = jnp.float32, jnp.bfloat16
    cols = slice(side * lanes, (side + 1) * lanes)
    far = [Far(x, cols) for x in (query, keys, values, keys_other, values_other, attended, grad)]
    return whole_call(
        functools.partial(backward_body, qblock, chunk, lanes, side), "attend_back", scalars, [], far + [lse_rows, segments],
        [array(b16, tokens, lanes), array(f32, half, lanes), array(f32, half, lanes), array(b16, half, lanes), array(b16, half, lanes)], [],
        [pltpu.VMEM((n, chunk, lanes), b16), pltpu.VMEM((n, chunk, lanes), b16), pltpu.VMEM((n, lanes, chunk), b16),
         pltpu.VMEM((n, chunk, lanes), f32), pltpu.VMEM((n, chunk, lanes), f32), pltpu.VMEM((n, chunk, LANES), f32)], 24, True,
    )


AXES = ("dp", "seq")
PARTS = 8
epsilon = 1e-12


def tn(left, right):
    return lax.dot_general(left, right, (((0,), (0,)), ((), ())), preferred_element_type=jnp.float32)


def norm_parts(value):
    center = value - jnp.mean(value, axis=-1, keepdims=True)
    spread = jnp.mean(center * center, axis=-1, keepdims=True)
    scale = lax.rsqrt(spread + epsilon)
    return (center * scale, scale)


def norm_back(upstream, normal, scale, gain):
    scaled = upstream * gain
    return scale * (
        scaled
        - jnp.mean(scaled, axis=-1, keepdims=True)
        - normal * jnp.mean(scaled * normal, axis=-1, keepdims=True)
    )


def row_sum(matrix):
    return jnp.sum(matrix.astype(jnp.float32), axis=0, keepdims=True)


def parts_of(refs):
    if len(refs) == PARTS:
        return [(i, 0, ref) for i, ref in enumerate(refs)]
    pieces = [(i, 0, ref) for i, ref in enumerate(refs[:6])]
    for i in range(2):
        top, bottom = refs[6 + i], refs[8 + i]
        pieces += [(6 + i, 0, top), (6 + i, top.shape[0], bottom)]
    return pieces


def load_pieces(me, pieces, rows, targets, sems):
    copies = [[] for _ in targets]
    for place, (part, first, ref) in enumerate(pieces):
        size = ref.shape[0]
        where = pl.ds(pl.multiple_of((me ^ part) * rows + first, 32), size)
        for i, (target, columns) in enumerate(targets):
            copy = pltpu.make_async_copy(ref.at[:, columns], target.at[where, :], sems.at[i, place])
            copy.start()
            copies[i].append(copy)
    return copies


def wait_all(copies):
    for copy in copies:
        copy.wait()


def step_of(block, size):
    return pl.ds(pl.multiple_of(block * size, size), size)


BLOCK = 1024
GELU_BLOCK = 256
ROWS = 256


def widen_body(scalars, *refs):
    shards = len(refs) - 12
    pieces = parts_of(refs[:shards])
    (attended, tokens, vec, up_add, normal_ref, scale_ref, low_ref, active_ref, slope_ref, wo, wu, sems) = refs[shards:]
    width, wide = wu.shape
    loads = load_pieces(scalars[0], pieces, width // PARTS, [(wo, slice(0, width)), (wu, slice(width, width + wide))], sems)
    wait_all(loads[0])

    @pl.loop(0, tokens.shape[0] // ROWS)
    def _(i):
        rows = step_of(i, ROWS)
        branch = nn(attended[rows, :], wo[...]) + vec[2:3, :]
        normal, scale = norm_parts(tokens[rows, :].astype(jnp.float32) + branch)
        first = normal * vec[3:4, :] + vec[4:5, :]
        normal_ref[rows, :] = normal
        scale_ref[rows, :] = jnp.broadcast_to(scale, (ROWS, LANES))
        low_ref[rows, :] = first.astype(jnp.bfloat16)

    wait_all(loads[1])

    @pl.loop(0, wide // GELU_BLOCK)
    def _(j):
        cols = step_of(j, GELU_BLOCK)
        inner = nn(low_ref[...], wu[:, cols]) + up_add[:, cols]
        cumulative = 0.5 * (1.0 + lax.erf(inner * math.sqrt(0.5)))
        density = jnp.exp(-0.5 * inner * inner) * (1.0 / math.sqrt(2.0 * math.pi))
        active_ref[:, cols] = (inner * cumulative).astype(jnp.bfloat16)
        slope_ref[:, cols] = (cumulative + inner * density).astype(jnp.bfloat16)


def narrow_body(scalars, *refs):
    shards = len(refs) - 13
    pieces = parts_of(refs[:shards])
    (active, normal_one, vec, upstream, out_ref, grad_ref, low_ref, sums_ref, send_ref, keep_ref, wd, sums, sems) = refs[shards:]
    wide, width = wd.shape
    (loads,) = load_pieces(scalars[0], pieces, wide // PARTS, [(wd, slice(0, width))], sems)
    wait_all(loads)
    sums[...] = jnp.zeros_like(sums)

    @pl.loop(0, normal_one.shape[0] // ROWS)
    def _(i):
        rows = step_of(i, ROWS)
        second = nn(active[rows, :], wd[...]) + vec[5:6, :]
        normal, scale = norm_parts(normal_one[rows, :] * vec[3:4, :] + vec[4:5, :] + second)
        out_ref[rows, :] = (normal * vec[6:7, :] + vec[7:8, :]).astype(jnp.bfloat16)
        up = upstream[rows, :].astype(jnp.float32)
        grad = norm_back(up, normal, scale, vec[6:7, :])
        low = grad.astype(jnp.bfloat16)
        grad_ref[rows, :] = grad
        low_ref[rows, :] = low
        sums[0:1, :] += row_sum(low)
        sums[1:2, :] += row_sum(up * normal)
        sums[2:3, :] += row_sum(up)

    sums_ref[...] = sums[...]
    size = wide // PARTS

    @pl.loop(0, PARTS // 2)
    def _(i):
        send_ref[i] = tn(active[:, step_of(2 * i + 1 - scalars[1], size)], low_ref[...]).astype(jnp.bfloat16)
        keep_ref[i] = tn(active[:, step_of(2 * i + scalars[1], size)], low_ref[...]).astype(jnp.bfloat16)


def turn_parts(core, turned, ordered):
    for i in range(PARTS // 2):
        ordered[0, i] = turned[2 * i + 1 - core]
        ordered[1, i] = turned[2 * i + core]


def inner_back_body(scalars, low, wd, slope, first_low, grad_ref, sums_ref, send_ref, keep_ref, turned, ordered):
    size = first_low.shape[1] // PARTS
    flipped = first_low[...].T
    for i in range(PARTS):
        turned[i] = flipped[i * size : (i + 1) * size, :]
    turn_parts(scalars[1], turned, ordered)
    rows = (PARTS // 2) * size

    @pl.loop(0, slope.shape[1] // BLOCK)
    def _(j):
        cols = step_of(j, BLOCK)
        grad = (nt(low[...], wd[cols, :]) * slope[:, cols].astype(jnp.float32)).astype(jnp.bfloat16)
        grad_ref[:, cols] = grad
        sums_ref[:, cols] = row_sum(grad)
        for side, ref in enumerate((send_ref, keep_ref)):
            left = ordered[side].reshape(rows, low.shape[0])
            ref[:, :, cols] = nn(left, grad).astype(jnp.bfloat16).reshape(PARTS // 2, size, BLOCK)


def outer_back_body(scalars, grad, wu, up_grad, normal_ref, scale_ref, vec, wo, attended, sum_ref, result_ref, sums_ref, send_ref, keep_ref, low, sums, turned):
    width = wo.shape[0]
    sums[...] = jnp.zeros_like(sums)

    @pl.loop(0, grad.shape[0] // ROWS)
    def _(i):
        rows = step_of(i, ROWS)
        first = up_grad[rows, :] + nt(grad[rows, :], wu[...])
        normal = normal_ref[rows, :]
        total = norm_back(first, normal, scale_ref[rows, 0:1], vec[3:4, :])
        branch = total.astype(jnp.bfloat16)
        sum_ref[rows, :] = total
        low[rows, :] = branch
        result_ref[rows, :] = nt(branch, wo[...]).astype(jnp.bfloat16)
        sums[0:1, :] += row_sum(branch)
        sums[1:2, :] += row_sum(first * normal)
        sums[2:3, :] += row_sum(first)

    sums_ref[...] = sums[...]
    size = width // PARTS
    product = tn(attended[...], low[...]).astype(jnp.bfloat16)
    for i in range(PARTS):
        turned[i] = product[i * size : (i + 1) * size, :]
    for i in range(PARTS // 2):
        send_ref[i] = turned[2 * i + 1 - scalars[1]]
        keep_ref[i] = turned[2 * i + scalars[1]]


class Far:
    def __init__(self, value, columns=None, index=None):
        self.value, self.columns, self.index = value, columns, index
        shape = value.shape if index is None else value.shape[1:]
        width = shape[-1] if columns is None else columns.stop - columns.start
        self.shape, self.dtype = shape[:-1] + (width,), value.dtype


def far_body(body, far, counts, scalars, *refs):
    hbm, inputs, outputs, held, lazy = counts
    given = list(refs[hbm : hbm + inputs])
    held_refs, sems = refs[len(refs) - held - 1 : -1], refs[-1]
    copies = []
    for i, (place, columns, index) in enumerate(far):
        source = given[place]
        if index is not None:
            source = source.at[index]
        if columns is not None:
            source = source.at[:, columns]
        copies.append(pltpu.make_async_copy(source, held_refs[i], sems.at[i]))
        copies[-1].start()
        given[place] = held_refs[i]
    rest = (*refs[:hbm], *given, *refs[hbm + inputs : len(refs) - held - 1])
    if lazy:
        body(copies, scalars, *rest)
    else:
        wait_all(copies)
        body(scalars, *rest)


def in_hbm(value):
    return pltpu.with_memory_space_constraint(value, pltpu.HBM)


def whole_call(body, name, scalars, hbm, inputs, outputs, hbm_outputs, scratch, room=8, lazy=False):
    shape_of = lambda x: jax.ShapeDtypeStruct(x.shape, x.dtype)
    near, stay = pl.BlockSpec(memory_space=pltpu.VMEM), pl.BlockSpec(memory_space=pltpu.HBM)
    far = [(i, x.columns, x.index) for i, x in enumerate(inputs) if isinstance(x, Far)]
    scratch = list(scratch)
    if far:
        held = [pltpu.VMEM(inputs[i].shape, inputs[i].dtype) for i, *_ in far]
        counts = (len(hbm), len(inputs), len(outputs) + len(hbm_outputs), len(far), lazy)
        body = functools.partial(far_body, body, far, counts)
        scratch += held + [pltpu.SemaphoreType.DMA((len(far),))]
        room += sum(math.prod(inputs[i].shape) * inputs[i].dtype.itemsize for i, *_ in far) // (1 << 20) + 1
    return pl.pallas_call(
        body,
        in_specs=[pl.BlockSpec(memory_space=pltpu.SMEM)]
        + [stay] * len(hbm)
        + [stay if isinstance(x, Far) else near for x in inputs],
        out_specs=[near] * len(outputs) + [stay] * len(hbm_outputs),
        scratch_shapes=scratch,
        out_shape=[shape_of(x) for x in outputs] + [pltpu.HBM(x.shape, x.dtype) for x in hbm_outputs],
        cost_estimate=pl.CostEstimate(flops=1, transcendentals=0, bytes_accessed=1),
        compiler_params=pltpu.CompilerParams(vmem_limit_bytes=room << 20),
        name=name,
    )(scalars, *[in_hbm(x) for x in hbm], *[in_hbm(x.value) if isinstance(x, Far) else x for x in inputs])


def array(dtype, *shape):
    return jax.ShapeDtypeStruct(shape, dtype)


def widen(scalars, pieces, attended, tokens, vec, up_add):
    count, width = tokens.shape
    wide = up_add.shape[1]
    f32, b16 = jnp.float32, jnp.bfloat16
    return whole_call(
        widen_body, "widen", scalars, pieces, [attended, tokens, vec, up_add],
        [array(f32, count, width), array(f32, count, LANES), array(b16, count, width),
         array(b16, count, wide), array(b16, count, wide), array(b16, width, width), array(b16, width, wide)],
        [], [pltpu.SemaphoreType.DMA((2, len(pieces)))],
    )


def narrow(scalars, pieces, active, normal, vec, upstream):
    count, wide = active.shape
    width = normal.shape[1]
    f32, b16 = jnp.float32, jnp.bfloat16
    half = array(b16, PARTS // 2, wide // PARTS, width)
    return whole_call(
        narrow_body, "narrow", scalars, pieces, [active, normal, vec, upstream],
        [array(b16, count, width), array(f32, count, width), array(b16, count, width), array(f32, 8, width), half, half, array(b16, wide, width)],
        [], [pltpu.VMEM((8, width), f32), pltpu.SemaphoreType.DMA((1, len(pieces)))],
    )


def inner_back(scalars, low, wd, slope, first_low):
    count, wide = slope.shape
    width = low.shape[1]
    size = width // PARTS
    f32, b16 = jnp.float32, jnp.bfloat16
    half = array(b16, PARTS // 2, size, wide)
    return whole_call(
        inner_back_body, "inner_back", scalars, [], [low, wd, slope, first_low],
        [array(b16, count, wide), array(f32, 1, wide), half, half], [],
        [pltpu.VMEM((PARTS, size, count), b16), pltpu.VMEM((2, PARTS // 2, size, count), b16)],
    )


def outer_back(scalars, grad, wu, up_grad, normal, scale, vec, wo, attended):
    count, width = normal.shape
    f32, b16 = jnp.float32, jnp.bfloat16
    half = array(b16, PARTS // 2, width // PARTS, width)
    return whole_call(
        outer_back_body, "outer_back", scalars, [], [grad, wu, up_grad, normal, scale, vec, wo, attended],
        [array(f32, count, width), array(b16, count, width), array(f32, 8, width), half, half], [],
        [pltpu.VMEM((count, width), b16), pltpu.VMEM((8, width), f32), pltpu.VMEM((PARTS, width // PARTS, width), b16)],
    )


def sums_to_slots(core, lines, parts, send, keep, first, wide=None):
    turned = lines[...].T
    rows = turned.shape[0] // PARTS
    for i in range(PARTS):
        parts[i] = turned[i * rows : (i + 1) * rows, :]
    if wide is not None:
        size = wide.shape[1] // (4 * PARTS)
        for i in range(4 * PARTS):
            place = (i % 4) * (rows // 4)
            parts[i // 4, place : place + 1, LANES - size :] = wide[:, i * size : (i + 1) * size]
    for i in range(PARTS // 2):
        send[i, :, first : first + LANES] = parts[2 * i + 1 - core].astype(jnp.bfloat16)
        keep[i, :, first : first + LANES] = parts[2 * i + core].astype(jnp.bfloat16)


def qkv_back_body(side, copies, scalars, dq, dk, dv, far_keys, far_values, ordered, weight, gradient, *refs):
    core = scalars[1]
    if side == 0:
        sums_one, sums_two, wide_sums, send_low, send_high, keep, result, sums_ref, both, lines, parts, send = refs
    else:
        first_sums, send_low, send_high, keep, result, sums_ref, both, lines, parts, send = refs
    half = dq.shape[1]
    both[:, :half] = dq[...]
    both[:, half : 2 * half] = (dk[...] + far_keys[...].astype(jnp.float32)).astype(jnp.bfloat16)
    both[:, 2 * half :] = (dv[...] + far_values[...].astype(jnp.float32)).astype(jnp.bfloat16)
    sums_ref[...] = jnp.zeros_like(sums_ref)
    sums_ref[0:1, :] = row_sum(dq[...])
    sums_ref[1:2, :] = row_sum(both[:, 2 * half :])
    rows = ordered.shape[1] * ordered.shape[2]
    copies[0].wait()
    for i, ref in enumerate((send, keep)):
        left = ordered[i].reshape(rows, ordered.shape[3])
        product = nn(left, both[...]).astype(jnp.bfloat16)
        ref[:, :, : 3 * half] = product.reshape(ordered.shape[1], ordered.shape[2], 3 * half)
    lines[...] = jnp.zeros_like(lines)
    if side == 0:
        lines[0:8, :] = sums_one[...]
        lines[8:16, :] = sums_two[...]
        sums_to_slots(core, lines, parts, send, keep, 3 * half, wide_sums)
    else:
        lines[0:8, :half] = first_sums[...]
        lines[0:8, half:] = sums_ref[...]
        sums_to_slots(core, lines, parts, send, keep, 3 * half)
    send_low[...] = send[:2]
    send_high[...] = send[2:]
    copies[1].wait()
    result[...] = (gradient[...] + nt(both[...], weight[...])).astype(result.dtype)


def qkv_back(side, scalars, dq, dk, dv, far_keys, far_values, ordered, weights, gradient, *more):
    count, half = dq.shape
    width = gradient.shape[1]
    f32, b16 = jnp.float32, jnp.bfloat16
    total = array(b16, PARTS // 2, width // PARTS, 3 * half + LANES)
    part = array(b16, PARTS // 4, width // PARTS, 3 * half + LANES)
    return whole_call(
        functools.partial(qkv_back_body, side), "qkv_back", scalars, [], [dq, dk, dv, far_keys, far_values, Far(ordered), Far(weights, None, side), gradient, *more],
        [part, part, total, array(b16 if side else f32, count, width), array(f32, 8, half)], [],
        [pltpu.VMEM((count, 3 * half), b16), pltpu.VMEM((LANES, width), f32), pltpu.VMEM((PARTS, width // PARTS, LANES), f32),
         pltpu.VMEM(total.shape, b16)],
        8, True,
    )


STRIPE = 32


def fold_body(plans, scalars, *refs):
    places = [0]
    for *_, count in plans:
        places.append(places[-1] + 1 + count)
    for item, (outer, inner, bit, count) in enumerate(plans):
        keep, *gots = refs[places[item] : places[item + 1]]
        send, left = refs[places[-1] + 2 * item : places[-1] + 2 * item + 2]
        mine = scalars[bit]
        rows = keep.shape[1]
        stripe = STRIPE if rows % STRIPE == 0 else rows

        @pl.loop(0, rows // stripe)
        def _(k):
            span = step_of(k, stripe) if stripe != rows else slice(None)
            for i in range(outer):
                for j in range(inner):
                    for target, side in ((send, 1 - mine), (left, mine)):
                        place = (2 * i + side) * inner + j
                        got = gots[0][place, span, :] if count == 1 else gots[i][side * inner + j, span, :]
                        value = keep[place, span, :].astype(jnp.float32) + got.astype(jnp.float32)
                        target[i * inner + j, span, :] = value.astype(target.dtype)


def fold(scalars, items):
    outs, plans, given = [], [], []
    for keep, got, (outer, inner, bit) in items:
        gots = got if isinstance(got, tuple) else (got,)
        shape = (keep.shape[0] // 2,) + keep.shape[1:]
        outs += [array(jnp.bfloat16, *shape), array(keep.dtype, *shape)]
        plans.append((outer, inner, bit, len(gots)))
        given += [keep, *gots]
    got = whole_call(functools.partial(fold_body, plans), "fold", scalars, [], given, outs, [], [])
    return [(got[2 * i], got[2 * i + 1]) for i in range(len(items))]


def merge_body(shapes, scalars, *refs):
    send, left = refs[-2:]
    mine = scalars[4]
    low = send.shape[1]
    first = 0
    for item, (rows, wide) in enumerate(shapes):
        keep, got = refs[2 * item : 2 * item + 2]
        for part in range(rows // low):
            span = slice(part * low, (part + 1) * low)
            for high in range(2):
                for target, side in ((send, 1 - mine), (left, mine)):
                    value = keep[2 * high + side, span, :].astype(jnp.float32) + got[2 * high + side, span, :].astype(jnp.float32)
                    target[high, :, first : first + wide] = value.astype(target.dtype)
            first += wide


def merge(scalars, items, low):
    items = [(k.reshape(4, k.shape[-2] // 4, k.shape[-1]), g.reshape(4, g.shape[-2] // 4, g.shape[-1])) for k, g in items]
    shapes = [k.shape[1:] for k, _ in items]
    wide = sum(rows // low * n for rows, n in shapes)
    return whole_call(
        functools.partial(merge_body, shapes), "merge", scalars, [], [x for pair in items for x in pair],
        [array(jnp.bfloat16, 2, low, wide), array(jnp.float32, 2, low, wide)], [], [],
    )


def last_ff_body(scalars, keep, got, down_ref, up_ref):
    low = keep.shape[1]
    width = down_ref.shape[1]
    for part in range(down_ref.shape[0] // low):
        cols = slice(part * width, (part + 1) * width)
        down_ref[part * low : (part + 1) * low, :] = keep[0, :, cols] + got[0, :, cols].astype(jnp.float32)
    cols = slice(4 * width, 4 * width + up_ref.shape[1])
    up_ref[...] = keep[0, :, cols] + got[0, :, cols].astype(jnp.float32)


def last_ff(scalars, keep, got, width):
    low = keep.shape[1]
    return whole_call(
        last_ff_body, "last_ff", scalars, [], [keep, got], [array(jnp.float32, 4 * low, width), array(jnp.float32, low, 4 * width)], [], []
    )


def last_qkv_body(scalars, keep, got, query_ref, key_ref, value_ref, out_ref, small_ref, late_ref, wide_ref, turned):
    low = keep.shape[1]
    width = query_ref.shape[1]
    half = width // 2
    second = 3 * half + LANES
    third = 2 * second

    def total(first, size):
        return keep[0, :, first : first + size] + got[0, :, first : first + size].astype(jnp.float32)

    for i, ref in enumerate((query_ref, key_ref, value_ref)):
        ref[:, :half] = total(i * half, half)
        ref[:, half:] = total(second + i * half, half)
    out_ref[...] = total(third, width)
    wide_ref[...] = total(3 * half, LANES)[0:1, :]
    for ref, first in ((small_ref, 3 * half), (late_ref, second + 3 * half)):
        turned[...] = jnp.zeros_like(turned)
        turned[:low, :] = total(first, LANES)
        ref[...] = turned[...].T[: ref.shape[0], :]


def last_qkv(scalars, keep, got, width):
    low = keep.shape[1]
    f32 = jnp.float32
    return whole_call(
        last_qkv_body, "last_qkv", scalars, [], [keep, got],
        [array(f32, low, width)] * 4 + [array(f32, 24, LANES), array(f32, 8, LANES), array(f32, 1, LANES)], [], [pltpu.VMEM((LANES, LANES), f32)],
    )


def after(value, *others):
    return lax.optimization_barrier((value,) + others)[0]


def bit_count(size):
    return size.bit_length() - 1


def swap_dp(value, mask):
    return lax.ppermute(value, "dp", [(i, i ^ mask) for i in range(lax.axis_size("dp"))])


def swap_seq(value, mask):
    return lax.ppermute(value, "seq", [(i, i ^ mask) for i in range(lax.axis_size("seq"))])


def column_sum(matrix):
    return jnp.sum(matrix.astype(jnp.float32), axis=0)


def spread_pairs(first):
    dps, seqs = lax.axis_size("dp"), lax.axis_size("seq")
    pairs = []
    for dp in range(dps):
        for seq in range(seqs):
            piece = first ^ (seq & 1)
            to_dp = (dp & ~1) | (seq >> 1)
            to_seq = 2 * (dp & 1) + piece
            pairs.append((dp * seqs + seq, to_dp * seqs + to_seq))
    return pairs


def to_sequences(local, order):
    odd = (lax.axis_index("seq") & 1) == 1
    got = []
    pieces = [jnp.where(odd, local[1 - first], local[first]) for first in range(2)]
    order.mark(*pieces)
    for first, piece in enumerate(pieces):
        got.append(lax.ppermute(piece, AXES, spread_pairs(first)))
    return got, odd


def in_order(got, odd, rows):
    return jnp.where(odd, jnp.concatenate([g[:rows] for g in got[::-1]]), jnp.concatenate([g[:rows] for g in got]))


def from_sequences(tokens, order):
    odd = (lax.axis_index("seq") & 1) == 1
    half = tokens.shape[0] // 2
    got = []
    for first in range(2):
        near, far = tokens[first * half : (first + 1) * half], tokens[(1 - first) * half : (2 - first) * half]
        piece = order.mark(jnp.where(order.gate(odd), far, near))
        got.append(lax.ppermute(piece, AXES, [(b, a) for a, b in spread_pairs(first)]))
    return got


def both_sequences(order, got):
    odd = order.gate((lax.axis_index("seq") & 1) == 1)
    return jnp.where(odd, jnp.stack(got[::-1]), jnp.stack(got))


def weight_lines(weights, lines):
    width = weights[0].shape[-1]
    lines = [jnp.pad(v[..., None, :], [(0, 0)] * v.ndim + [(0, width - v.shape[-1])]) for v in lines]
    lines.append(jnp.zeros(lines[0].shape[:-2] + (16 - len(lines), width), jnp.bfloat16))
    return jnp.concatenate(weights + lines, axis=-2)


def near_shards(part, across=True):
    if lax.axis_size("dp") != PARTS:
        p = part if part.ndim == 3 else jnp.stack(jnp.split(lax.all_gather(part, "dp", axis=0, tiled=True), PARTS))
        return [p[i] for i in range(PARTS)]
    return [part, swap_dp(part, 2), swap_dp(part, 4)] + ([swap_dp(part, 6)] if across else [])


def both_cores(parts):
    return [shard for part in parts for shard in (part, swap_dp(part, 1))]


def all_shards(near, *ready):
    if len(near) == PARTS:
        return near
    return both_cores([near[0]] + list(lax.optimization_barrier((*near[1:], *ready))[:3]))


def relayed_shards(near, cut, *ready):
    if len(near) == PARTS:
        return near
    own, along_x, along_y = near
    along_x, along_y = lax.optimization_barrier((along_x, along_y, *ready))[:2]
    sent = along_x[:cut], along_y[cut:]
    top, bottom = swap_dp(sent[0], 4), swap_dp(sent[1], 2)
    own, along_x, along_y = lax.optimization_barrier((own, along_x, along_y, *sent))[:3]
    return both_cores([own, along_x, along_y, top, bottom])


def pack_body(count, scalars, *refs):
    weights, vectors, hidden, ids = refs[: min(3, count)], refs[3:count], refs[count], refs[count + 1]
    pieces = refs[count + 2 : count + 4]
    if vectors:
        part, lines = refs[count + 4 :]
        rows = weights[0].shape[0]
        for i, ref in enumerate(weights):
            part[i * rows : (i + 1) * rows, :] = ref[...]
        lines[...] = jnp.zeros_like(lines)
        for i, ref in enumerate(vectors):
            lines[i : i + 1, : ref.shape[1]] = ref[...].astype(jnp.float32)
        part[3 * rows :, :] = lines[...].astype(jnp.bfloat16)
    odd = scalars[7]
    block, half = hidden.shape[1], ids.shape[1] // 2
    for first, piece in enumerate(pieces):
        piece[:block, :] = hidden[first ^ odd]
        line = jnp.where(first ^ odd == 0, ids[0:1, :], ids[1:2, :]).astype(jnp.bfloat16)
        piece[block:, :] = jnp.zeros_like(piece[block:, :])
        piece[block : block + 1, :half] = line[:, :half]
        piece[block + 1 : block + 2, :half] = line[:, half:]


def pack(scalars, weights, vectors, hidden, ids):
    piece = array(jnp.bfloat16, hidden.shape[1] + 16, hidden.shape[2])
    if lax.axis_size("dp") == PARTS:
        rows, width = weights[0].shape
        given = weights + [v[None, :] for v in vectors]
        return whole_call(
            functools.partial(pack_body, len(given)), "pack", scalars, [], [Far(x) for x in given + [hidden, ids]],
            [piece, piece, array(jnp.bfloat16, 3 * rows + 16, width)], [], [pltpu.VMEM((16, width), jnp.float32)],
        )
    gather = lambda v: lax.all_gather(v, "dp", axis=0, tiled=True)
    split = lambda v: gather(v).reshape((PARTS, -1) + v.shape[1:])
    pieces = whole_call(functools.partial(pack_body, 0), "pack", scalars, [], [Far(hidden), Far(ids)], [piece, piece], [], [])
    return *pieces, weight_lines([split(w) for w in weights], [split(v) for v in vectors])


def project_body(sizes, scalars, *refs):
    rows, wide, vectors, qblock, chunk, lanes, shards = sizes
    pieces, hidden = parts_of(refs[:shards]), refs[shards : shards + 4]
    (
        attended, lse, tokens, vec_ref, up_ref, segments, ordered, query_out, keys_out, values_out, keys_far_out, values_far_out, weights_out,
        query, keys, values, keys_far, values_far, far, held, small, turned, ids, sems, hidden_sems, out_sems, kall, vt, tiles,
    ) = refs[shards + 4 :]
    count, width = tokens.shape
    block = count // 2
    half = width // 2
    core, odd = scalars[6], scalars[7]
    copies, brought = [], []

    def start(copies, source, target, sem):
        copies.append(pltpu.make_async_copy(source, target, sem))
        copies[-1].start()

    for i, (ref, place) in enumerate(zip(hidden, (0, 1, 0, 1))):
        goal = tokens if i < 2 else far
        start(brought, ref.at[:block, :], goal.at[pl.ds(pl.multiple_of((place ^ odd) * block, block), block), :], hidden_sems.at[i])
    start(brought, hidden[0].at[block:, :], ids, hidden_sems.at[4])
    for part, first, ref in pieces:
        where = scalars[0] ^ part
        target = pl.ds(where * rows, rows)
        for weight in range(first // rows, (first + ref.shape[0]) // rows):
            for side in range(2):
                start(
                    copies,
                    ref.at[weight * rows - first : (weight + 1) * rows - first, side * half : (side + 1) * half],
                    held.at[side, target, weight * half : (weight + 1) * half],
                    sems.at[len(copies)],
                )
        if first + ref.shape[0] > 3 * rows:
            start(copies, ref.at[3 * rows - first :, :], small.at[where], sems.at[len(copies)])
    wait_all(brought)
    line = ids[...].astype(jnp.float32)
    for i in range(2):
        segments[:, i * count : (i + 1) * count] = jnp.where(core == i, line[0:1, :count], line[1:2, :count])
    flipped = tokens[...].T
    for i in range(PARTS):
        turned[i] = flipped[i * rows : (i + 1) * rows, :]
    turn_parts(scalars[1], turned, ordered)
    wait_all(copies)
    saves = []
    start(saves, held, weights_out, out_sems.at[0])
    vec_ref[...] = jnp.concatenate([small[i, :, :rows] for i in range(PARTS)], axis=1).astype(jnp.float32)
    up_ref[...] = jnp.concatenate([small[i, vectors : vectors + 1, :wide] for i in range(PARTS)], axis=1).astype(jnp.float32)
    for i, (weight, add, goal, source, out) in enumerate((
        (1, None, keys, tokens, keys_out), (1, None, keys_far, far, keys_far_out), (2, 1, values, tokens, values_out),
        (2, 1, values_far, far, values_far_out), (0, 0, query, tokens, query_out),
    )):
        for side in range(2):
            cols = slice(side * half, (side + 1) * half)
            product = nn(source[...], held[side, :, weight * half : (weight + 1) * half])
            if add is not None:
                product = product + vec_ref[add : add + 1, cols]
            goal[:, cols] = product.astype(jnp.bfloat16)
        start(saves, goal, out, out_sems.at[i + 1])
    forward_body(qblock, chunk, lanes, query, keys, values, keys_far, values_far, segments, attended, lse, kall, vt, tiles)
    wait_all(saves)


def project(scalars, pieces, hidden, rows, wide, vectors, qblock, chunk, lanes):
    block, width = hidden[0].shape[0] - 16, hidden[0].shape[1]
    count = 2 * block
    lines = 16
    n = 2 * count // chunk
    f32, b16 = jnp.float32, jnp.bfloat16
    whole = array(b16, count, width)
    vmem = lambda x: pltpu.VMEM(x.shape, x.dtype)
    return whole_call(
        functools.partial(project_body, (rows, wide, vectors, qblock, chunk, lanes, len(pieces))), "project", scalars, list(pieces) + list(hidden), [],
        [whole, array(f32, width // lanes, 8, count), whole, array(f32, lines, width), array(f32, 1, wide * PARTS), array(f32, 1, 2 * count),
         array(b16, 2, PARTS // 2, rows, count)],
        [whole] * 5 + [array(b16, 2, width, 3 * width // 2)],
        [vmem(whole)] * 6
        + [pltpu.VMEM((2, width, 3 * width // 2), b16), pltpu.VMEM((PARTS, lines, width), b16), pltpu.VMEM((PARTS, rows, count), b16),
           pltpu.VMEM((16, width), b16), pltpu.SemaphoreType.DMA((7 * PARTS,)),
           pltpu.SemaphoreType.DMA((5,)), pltpu.SemaphoreType.DMA((6,)), pltpu.VMEM((n, chunk, lanes), b16),
           pltpu.VMEM((n, lanes, chunk), b16), pltpu.VMEM((n, chunk, LANES), f32)],
        28,
    )


class Order:
    def __init__(self):
        self.last = ()

    def gate(self, value):
        return lax.optimization_barrier((value, *self.last))[0] if self.last else value

    def mark(self, *values):
        self.last = values
        return values[0] if len(values) == 1 else values


def all_rows(send, keep):
    return jnp.stack([keep, send], axis=1).reshape(-1, keep.shape[-1]).astype(jnp.float32)


def scatter_all(send, keep):
    return lax.psum_scatter(all_rows(send, keep), AXES, scatter_dimension=0, tiled=True)


def per_device(
    hidden_in, segment_ids, query_weight, query_bias, key_weight, value_weight, value_bias, out_weight, out_bias,
    first_gain, first_shift, up_weight, up_bias, down_weight, down_bias, second_gain, second_shift, cotangent,
):
    dps, seqs = lax.axis_size("dp"), lax.axis_size("seq")
    inner_width, width = up_weight.shape[1], query_weight.shape[1]
    devices = dps * seqs
    share = width // devices
    qblock = chunk = 256
    pairs = 3
    direct = dps == PARTS and seqs == 4
    dp, seq = lax.axis_index("dp"), lax.axis_index("seq")
    if direct:
        scalars = [dp, dp & 1, (dp >> 1) & 1, dp >> 2, seq & 1, seq >> 1, dp & 1, seq & 1]
    else:
        scalars = [0, 0, 0, 0, 0, 0, dp & 1, seq & 1]
    scalars = jnp.stack([jnp.asarray(v, jnp.int32) for v in scalars])

    vectors = [query_bias, value_bias, out_bias, first_gain, first_shift, down_bias, second_gain, second_shift]
    *hidden, part = pack(
        scalars, [query_weight, key_weight, value_weight], vectors + [up_bias], hidden_in, segment_ids
    )
    near = near_shards(part)
    hidden = [lax.ppermute(piece, AXES, spread_pairs(first)) for first, piece in enumerate(hidden)]
    out_up, down_part = lax.optimization_barrier(
        (jnp.concatenate([out_weight, up_weight], axis=1), down_weight, *near[1:4])
    )[:2]
    hidden += [swap_dp(piece, 1) for piece in hidden]
    if direct:
        near = list(lax.optimization_barrier((*near, *hidden))[:4])
    shards = both_cores(near) if direct else near
    out_up_near = near_shards(out_up)
    attended, lse, tokens, vec, up_add, segments, ordered, query, keys, values, keys_other, values_other, w_qkv = project(
        scalars, shards, hidden, width // PARTS, inner_width // PARTS, len(vectors), qblock, chunk, pairs * LANES
    )
    order = Order()
    down_near = near_shards(after(down_part, attended, *out_up_near[1:4]), False)
    got_up, odd = to_sequences(after(cotangent, attended), order)
    out_up_shards = all_shards(out_up_near, attended)
    normal_one, scale_one, first_low, active, slope, wo, wu = widen(scalars, out_up_shards, attended, tokens, vec, up_add)
    upstream = in_order(lax.optimization_barrier((*got_up, active))[:2], odd, hidden_in.shape[1])
    layer_low, sum_two_grad, second_grad, sums_two, down_send, down_keep, wd = narrow(
        scalars, relayed_shards(down_near, inner_width // PARTS // 2, active), active, normal_one, vec, upstream
    )
    swap = (lambda value: swap_dp(value, 1)) if direct else (lambda value: value)
    order = Order()
    order.mark(second_grad)
    down_got = swap(down_send)
    out_pieces = from_sequences(layer_low, order)
    inner_grad, up_sum, up_send, up_keep = inner_back(scalars, order.gate(second_grad), wd, slope, first_low)
    up_got = swap(up_send)
    order.mark(inner_grad)
    if direct:
        ((send, down_keep),) = fold(order.gate(scalars), [(down_keep, down_got, (2, 1, 2))])
        down_got = swap_dp(order.mark(send), 2)
        ((send, up_keep),) = fold(order.gate(scalars), [(up_keep, up_got, (1, 2, 3))])
        up_got = swap_dp(order.mark(send), 4)
    sum_one_grad, attended_grad, sums_one, out_send, out_keep = outer_back(
        order.gate(scalars), inner_grad, wu, sum_two_grad, normal_one, scale_one, vec, wo, attended
    )
    order.mark(attended_grad)
    out_got = swap(out_send)

    def attend(side):
        given = (query, keys, values, keys_other, values_other, attended, attended_grad, lse, segments)
        return order.mark(*attend_back(order.gate(scalars), *given, qblock, chunk, pairs, side))

    dq, dk, dv, *far = attend(0)
    if direct:
        (send, down_keep), (other, up_keep), (third, out_keep) = fold(
            order.gate(scalars),
            [(down_keep, down_got, (1, 1, 3)), (up_keep, up_got, (1, 1, 2)), (out_keep, out_got, (1, 2, 3))],
        )
        order.mark(send, other, third)
        down_got, up_got, out_got = swap_dp(send, 4), swap_dp(other, 2), swap_dp(third, 4)
    layer_out = order.mark(both_sequences(order, out_pieces))
    one_low, one_high, one_keep, gradient, sums_first = qkv_back(
        0, order.gate(scalars), dq, dk, dv, *[swap_dp(x, 1) for x in order.gate(far)], ordered, w_qkv, sum_one_grad,
        sums_one, sums_two, up_sum
    )
    order.mark(gradient)
    one_got = (swap(one_low), swap(one_high))
    dq, dk, dv, *far = attend(1)
    if direct:
        send, ff_keep = merge(order.gate(scalars), [(down_keep, down_got), (up_keep, up_got)], share)
        ff_got = swap_seq(order.mark(send), 1)
        (send, one_keep), (other, out_keep) = fold(
            order.gate(scalars), [(one_keep, one_got, (2, 1, 2)), (out_keep, out_got, (1, 1, 2))]
        )
        order.mark(send, other)
        one_got, out_got = swap_dp(send, 2), swap_dp(other, 2)
    two_low, two_high, two_keep, gradient, _ = qkv_back(
        1, order.gate(scalars), dq, dk, dv, *[swap_dp(x, 1) for x in order.gate(far)], ordered, w_qkv, gradient, sums_first
    )
    order.mark(gradient)
    two_got = (swap(two_low), swap(two_high))
    in_pieces = from_sequences(gradient, order)
    if not direct:
        down_grad, up_grad = scatter_all(down_send, down_keep), scatter_all(up_send, up_keep)
        one, two = scatter_all(jnp.concatenate([one_low, one_high]), one_keep), scatter_all(jnp.concatenate([two_low, two_high]), two_keep)
        cut = width // 2
        query_grad, key_grad, value_grad = [
            jnp.concatenate([side[:, i * cut : (i + 1) * cut] for side in (one, two)], axis=1) for i in range(3)
        ]
        out_grad = scatter_all(out_send, out_keep)
        small, late = one[:, 3 * cut :].T, two[:, 3 * cut :].T
        up_bias_grad = lax.psum_scatter(up_sum[0], AXES, scatter_dimension=0, tiled=True)
    else:
        ((send, one_keep),) = fold(order.gate(scalars), [(one_keep, one_got, (1, 1, 3))])
        one_got = swap_dp(order.mark(send), 4)
        ((send, ff_keep),) = fold(order.gate(scalars), [(ff_keep, ff_got, (1, 1, 5))])
        ff_got = swap_seq(order.mark(send), 2)
        ((send, two_keep),) = fold(order.gate(scalars), [(two_keep, two_got, (2, 1, 2))])
        two_got = swap_dp(order.mark(send), 2)
        ((send, two_keep),) = fold(order.gate(scalars), [(two_keep, two_got, (1, 1, 3))])
        two_got = swap_dp(order.mark(send), 4)
    input_grad = order.mark(both_sequences(order, in_pieces).astype(jnp.float32))
    if direct:
        send, keep = merge(order.gate(scalars), [(one_keep, one_got), (two_keep, two_got), (out_keep, out_got)], share)
        got = swap_seq(order.mark(send), 1)
        ((send, keep),) = fold(order.gate(scalars), [(keep, got, (1, 1, 5))])
        got = swap_seq(order.mark(send), 2)
        down_grad, up_grad = order.mark(*last_ff(order.gate(scalars), ff_keep, ff_got, width))
    if direct:
        query_grad, key_grad, value_grad, out_grad, small, late, line = last_qkv(order.gate(scalars), keep, got, width)
        up_bias_grad = line[0, LANES - inner_width // devices :]
    ob, g1, s1 = [small[i, :share] for i in (0, 1, 2)]
    db, g2, s2 = [small[i, :share] for i in (8, 9, 10)]
    qb, vb = [late[i, :share] for i in (0, 1)]
    return (
        layer_out, input_grad, query_grad, qb, key_grad, value_grad, vb, out_grad, ob, g1, s1, up_grad, up_bias_grad, down_grad, db, g2, s2,
    )


def solution(mesh):
    wide, flat = P("dp", None), P("dp")
    in_specs = (
        P("dp", "seq", None), wide, wide, flat, wide, wide, flat, wide, flat, flat, flat, wide, flat, wide, flat,
        flat, flat, P("dp", "seq", None),
    )
    rows, cells = P(AXES, None), P(AXES)
    out_specs = (
        P("dp", "seq", None), P("dp", "seq", None), rows, cells, rows, rows, cells, rows, cells, cells, cells, rows,
        cells, rows, cells, cells, cells,
    )
    return jax.shard_map(per_device, mesh=mesh, in_specs=in_specs, out_specs=out_specs, check_vma=False)
```

```python
import functools
import math

import jax
import jax.numpy as jnp
from jax import lax
from jax.experimental import pallas as pl
from jax.experimental.pallas import tpu as pltpu
from jax.sharding import PartitionSpec as P

HEAD_DIM = 64
LANES = 128
NEGATIVE = -1e30


def nt(left, right):
    return lax.dot_general(left, right, (((1,), (1,)), ((), ())), preferred_element_type=jnp.float32)


def nn(left, right):
    return lax.dot_general(left, right, (((1,), (0,)), ((), ())), preferred_element_type=jnp.float32)


def head_parts(block):
    lane = lax.broadcasted_iota(jnp.int32, block.shape, 1)
    zero = jnp.zeros_like(block)
    return (jnp.where(lane < HEAD_DIM, block, zero), jnp.where(lane < HEAD_DIM, zero, block))


def same_document(column_tile, row):
    column = jnp.concatenate([column_tile] * (row.shape[1] // LANES), axis=1)
    return column == jnp.broadcast_to(row, column.shape)


def pair_lanes(pair):
    return slice(pair * LANES, (pair + 1) * LANES)


def segment_tables(segments, tiles, half, qblock, chunk):
    ids = segments[...]
    for j in range(tiles.shape[0]):
        for i in range(chunk // LANES):
            start = j * chunk + i * LANES
            tiles[j, i * LANES : (i + 1) * LANES, :] = jnp.broadcast_to(ids[:, start : start + LANES], (LANES, LANES)).T
    chunks = half // chunk
    low = [jnp.min(ids[:, j * chunk : (j + 1) * chunk]) for j in range(2 * chunks)]
    high = [jnp.max(ids[:, j * chunk : (j + 1) * chunk]) for j in range(2 * chunks)]
    found = []
    for b in range(half // qblock):
        mine = slice(b * qblock, (b + 1) * qblock)
        first, last = jnp.min(ids[:, mine]), jnp.max(ids[:, mine])
        bounds = []
        for side in range(2):
            before = sum((high[side * chunks + j] < first).astype(jnp.int32) for j in range(chunks))
            behind = sum((low[side * chunks + j] > last).astype(jnp.int32) for j in range(chunks))
            bounds += [before, chunks - behind]
        found.append((bounds[0], bounds[1] - bounds[0], bounds[2], bounds[1] - bounds[0] + bounds[3] - bounds[2]))
    return found


def chunk_of(bounds, step, chunks):
    first, own, other, _ = bounds
    return jnp.where(step < own, first + step, chunks + other + step - own)


def forward_body(qblock, chunk, lanes, q_all, k_all, v_all, ko_all, vo_all, segments, o_all, lse_all, kall, vt, sk_ref):
    half = k_all.shape[0]
    tables = segment_tables(segments, sk_ref, half, qblock, chunk)
    chunks, pairs = half // chunk, lanes // LANES

    @pl.loop(0, q_all.shape[1] // lanes)
    def _(group):
        cols = step_of(group, lanes)
        q_ref, k_ref, v_ref, ko_ref, vo_ref, o_ref = (r.at[:, cols] for r in (q_all, k_all, v_all, ko_all, vo_all, o_all))
        lse_ref = lse_all.at[pl.ds(group, 1)]
        for j in range(chunks):
            rows = slice(j * chunk, (j + 1) * chunk)
            kall[j] = k_ref[rows, :]
            kall[chunks + j] = ko_ref[rows, :]
            vt[j] = v_ref[rows, :].T
            vt[chunks + j] = vo_ref[rows, :].T
        for b in range(q_ref.shape[0] // qblock):
            span = slice(b * qblock, (b + 1) * qblock)
            parts = []
            for pair in range(pairs):
                parts += head_parts(q_ref[span, pair_lanes(pair)] * jnp.bfloat16(HEAD_DIM**-0.5))
            row = segments[:, span]

            def one(step, carry):
                j = chunk_of(tables[b], step, chunks)
                mask = same_document(sk_ref[j], row)
                scores = [jnp.where(mask, nt(kall[j, :, pair_lanes(h // 2)], part), NEGATIVE) for h, part in enumerate(parts)]
                out = []
                for h, score in enumerate(scores):
                    top, total, acc = carry[h]
                    new_top = jnp.maximum(top, jnp.max(score, axis=0, keepdims=True))
                    expo = jnp.exp(score - new_top)
                    scale = jnp.exp(top - new_top)
                    total = total * scale + jnp.sum(expo, axis=0, keepdims=True)
                    acc = acc * scale + nn(vt[j, h * HEAD_DIM : (h + 1) * HEAD_DIM, :], expo.astype(jnp.bfloat16))
                    out.append((new_top, total, acc))
                return tuple(out)

            init = (
                jnp.full((1, qblock), NEGATIVE, jnp.float32),
                jnp.zeros((1, qblock), jnp.float32),
                jnp.zeros((HEAD_DIM, qblock), jnp.float32),
            )
            carry = lax.fori_loop(0, tables[b][3], one, (init,) * len(parts))
            result = jnp.concatenate([acc / total for _, total, acc in carry], axis=0)
            o_ref[span, :] = result.T.astype(jnp.bfloat16)
            for h, (top, total, _) in enumerate(carry):
                lse_ref[0, h : h + 1, span] = top + jnp.log(total)


def backward_body(
    qblock, chunk, lanes, side, copies, scalars, q_ref, k_ref, v_ref, ko_ref, vo_ref, o_ref, do_ref, lse_all, segments,
    dq_ref, dk_ref, dv_ref, far_keys, far_values, kall, vall, kt, dkall, dvall, sk_ref,
):
    half = k_ref.shape[0]
    tables = segment_tables(segments, sk_ref, half, qblock, chunk)
    lse_ref = lse_all.at[side : side + 1]
    chunks, pairs = half // chunk, lanes // LANES
    dkall[...] = jnp.zeros_like(dkall)
    dvall[...] = jnp.zeros_like(dvall)
    for first, keys, values in ((0, k_ref, v_ref), (chunks, ko_ref, vo_ref)):
        wait_all(copies[1:3] if first == 0 else copies[3:5])
        for j in range(chunks):
            rows = slice(j * chunk, (j + 1) * chunk)
            kall[first + j] = keys[rows, :]
            vall[first + j] = values[rows, :]
            kt[first + j] = keys[rows, :].T
    wait_all(copies[:1] + copies[5:])
    for b in range(q_ref.shape[0] // qblock):
        span = slice(b * qblock, (b + 1) * qblock)
        parts, dparts, delta = [], [], []
        for pair in range(pairs):
            parts.append(head_parts(q_ref[span, pair_lanes(pair)] * jnp.bfloat16(HEAD_DIM**-0.5)))
            dparts.append(head_parts(do_ref[span, pair_lanes(pair)]))
            product = do_ref[span, pair_lanes(pair)].astype(jnp.float32) * o_ref[span, pair_lanes(pair)].astype(jnp.float32)
            product = product.T
            delta += [jnp.sum(product[h * HEAD_DIM : (h + 1) * HEAD_DIM], axis=0, keepdims=True) for h in range(2)]
        both = [jnp.concatenate(p, axis=0) for p in parts]
        dboth = [jnp.concatenate(p, axis=0) for p in dparts]
        row = segments[:, span]
        lse = [lse_ref[0, h : h + 1, span] for h in range(2 * pairs)]

        def one(step, carry):
            j = chunk_of(tables[b], step, chunks)
            mask = same_document(sk_ref[j], row)
            out = []
            both_mask = jnp.concatenate([mask, mask], axis=1)
            scores = [nt(kall[j, :, pair_lanes(pair)], both[pair]) for pair in range(pairs)]
            products = [nt(vall[j, :, pair_lanes(pair)], dboth[pair]) for pair in range(pairs)]
            adds = []
            for pair in range(pairs):
                score = jnp.where(both_mask, scores[pair], NEGATIVE)
                prob = jnp.exp(score - jnp.concatenate(lse[2 * pair : 2 * pair + 2], axis=1))
                grad = (prob * (products[pair] - jnp.concatenate(delta[2 * pair : 2 * pair + 2], axis=1))).astype(jnp.bfloat16)
                for side in range(2):
                    h = 2 * pair + side
                    out.append(carry[h] + nn(kt[j, h * HEAD_DIM : (h + 1) * HEAD_DIM, :], grad[:, side * qblock : (side + 1) * qblock]))
                adds.append((nn(prob.astype(jnp.bfloat16), dboth[pair]), nn(grad, both[pair])))
            for pair in range(pairs):
                dvall[j, :, pair_lanes(pair)] += adds[pair][0]
                dkall[j, :, pair_lanes(pair)] += adds[pair][1]
            return tuple(out)

        zero = jnp.zeros((HEAD_DIM, qblock), jnp.float32)
        carry = lax.fori_loop(0, tables[b][3], one, (zero,) * (2 * pairs))
        dq_ref[span, :] = (jnp.concatenate(carry, axis=0).T * HEAD_DIM**-0.5).astype(jnp.bfloat16)
    for j in range(chunks):
        rows = slice(j * chunk, (j + 1) * chunk)
        dk_ref[rows, :] = dkall[j]
        dv_ref[rows, :] = dvall[j]
        far_keys[rows, :] = dkall[chunks + j].astype(jnp.bfloat16)
        far_values[rows, :] = dvall[chunks + j].astype(jnp.bfloat16)


def attend_back(scalars, query, keys, values, keys_other, values_other, attended, grad, lse_rows, segments, qblock, chunk, pairs, side):
    tokens, width = query.shape
    half = keys.shape[0]
    lanes = pairs * LANES
    n = 2 * half // chunk
    f32, b16 = jnp.float32, jnp.bfloat16
    cols = slice(side * lanes, (side + 1) * lanes)
    far = [Far(x, cols) for x in (query, keys, values, keys_other, values_other, attended, grad)]
    return whole_call(
        functools.partial(backward_body, qblock, chunk, lanes, side), "attend_back", scalars, [], far + [lse_rows, segments],
        [array(b16, tokens, lanes), array(f32, half, lanes), array(f32, half, lanes), array(b16, half, lanes), array(b16, half, lanes)], [],
        [pltpu.VMEM((n, chunk, lanes), b16), pltpu.VMEM((n, chunk, lanes), b16), pltpu.VMEM((n, lanes, chunk), b16),
         pltpu.VMEM((n, chunk, lanes), f32), pltpu.VMEM((n, chunk, lanes), f32), pltpu.VMEM((n, chunk, LANES), f32)], 24, True,
    )


AXES = ("dp", "seq")
PARTS = 8
epsilon = 1e-12


def tn(left, right):
    return lax.dot_general(left, right, (((0,), (0,)), ((), ())), preferred_element_type=jnp.float32)


def norm_parts(value):
    center = value - jnp.mean(value, axis=-1, keepdims=True)
    spread = jnp.mean(center * center, axis=-1, keepdims=True)
    scale = lax.rsqrt(spread + epsilon)
    return (center * scale, scale)


def norm_back(upstream, normal, scale, gain):
    scaled = upstream * gain
    return scale * (
        scaled
        - jnp.mean(scaled, axis=-1, keepdims=True)
        - normal * jnp.mean(scaled * normal, axis=-1, keepdims=True)
    )


def row_sum(matrix):
    return jnp.sum(matrix.astype(jnp.float32), axis=0, keepdims=True)


def parts_of(refs):
    if len(refs) == PARTS:
        return [(i, 0, ref) for i, ref in enumerate(refs)]
    pieces = [(i, 0, ref) for i, ref in enumerate(refs[:6])]
    for i in range(2):
        top, bottom = refs[6 + i], refs[8 + i]
        pieces += [(6 + i, 0, top), (6 + i, top.shape[0], bottom)]
    return pieces


def load_pieces(me, pieces, rows, targets, sems):
    copies = [[] for _ in targets]
    for place, (part, first, ref) in enumerate(pieces):
        size = ref.shape[0]
        where = pl.ds(pl.multiple_of((me ^ part) * rows + first, 32), size)
        for i, (target, columns) in enumerate(targets):
            copy = pltpu.make_async_copy(ref.at[:, columns], target.at[where, :], sems.at[i, place])
            copy.start()
            copies[i].append(copy)
    return copies


def wait_all(copies):
    for copy in copies:
        copy.wait()


def step_of(block, size):
    return pl.ds(pl.multiple_of(block * size, size), size)


BLOCK = 1024
GELU_BLOCK = 256
ROWS = 256


def widen_body(scalars, *refs):
    shards = len(refs) - 12
    pieces = parts_of(refs[:shards])
    (attended, tokens, vec, up_add, normal_ref, scale_ref, low_ref, active_ref, slope_ref, wo, wu, sems) = refs[shards:]
    width, wide = wu.shape
    loads = load_pieces(scalars[0], pieces, width // PARTS, [(wo, slice(0, width)), (wu, slice(width, width + wide))], sems)
    wait_all(loads[0])

    @pl.loop(0, tokens.shape[0] // ROWS)
    def _(i):
        rows = step_of(i, ROWS)
        branch = nn(attended[rows, :], wo[...]) + vec[2:3, :]
        normal, scale = norm_parts(tokens[rows, :].astype(jnp.float32) + branch)
        first = normal * vec[3:4, :] + vec[4:5, :]
        normal_ref[rows, :] = normal
        scale_ref[rows, :] = jnp.broadcast_to(scale, (ROWS, LANES))
        low_ref[rows, :] = first.astype(jnp.bfloat16)

    wait_all(loads[1])

    @pl.loop(0, wide // GELU_BLOCK)
    def _(j):
        cols = step_of(j, GELU_BLOCK)
        inner = nn(low_ref[...], wu[:, cols]) + up_add[:, cols]
        cumulative = 0.5 * (1.0 + lax.erf(inner * math.sqrt(0.5)))
        density = jnp.exp(-0.5 * inner * inner) * (1.0 / math.sqrt(2.0 * math.pi))
        active_ref[:, cols] = (inner * cumulative).astype(jnp.bfloat16)
        slope_ref[:, cols] = (cumulative + inner * density).astype(jnp.bfloat16)


def narrow_body(scalars, *refs):
    shards = len(refs) - 13
    pieces = parts_of(refs[:shards])
    (active, normal_one, vec, upstream, out_ref, grad_ref, low_ref, sums_ref, send_ref, keep_ref, wd, sums, sems) = refs[shards:]
    wide, width = wd.shape
    (loads,) = load_pieces(scalars[0], pieces, wide // PARTS, [(wd, slice(0, width))], sems)
    wait_all(loads)
    sums[...] = jnp.zeros_like(sums)

    @pl.loop(0, normal_one.shape[0] // ROWS)
    def _(i):
        rows = step_of(i, ROWS)
        second = nn(active[rows, :], wd[...]) + vec[5:6, :]
        normal, scale = norm_parts(normal_one[rows, :] * vec[3:4, :] + vec[4:5, :] + second)
        out_ref[rows, :] = (normal * vec[6:7, :] + vec[7:8, :]).astype(jnp.bfloat16)
        up = upstream[rows, :].astype(jnp.float32)
        grad = norm_back(up, normal, scale, vec[6:7, :])
        low = grad.astype(jnp.bfloat16)
        grad_ref[rows, :] = grad
        low_ref[rows, :] = low
        sums[0:1, :] += row_sum(low)
        sums[1:2, :] += row_sum(up * normal)
        sums[2:3, :] += row_sum(up)

    sums_ref[...] = sums[...]
    size = wide // PARTS

    @pl.loop(0, PARTS // 2)
    def _(i):
        send_ref[i] = tn(active[:, step_of(2 * i + 1 - scalars[1], size)], low_ref[...]).astype(jnp.bfloat16)
        keep_ref[i] = tn(active[:, step_of(2 * i + scalars[1], size)], low_ref[...]).astype(jnp.bfloat16)


def turn_parts(core, turned, ordered):
    for i in range(PARTS // 2):
        ordered[0, i] = turned[2 * i + 1 - core]
        ordered[1, i] = turned[2 * i + core]


def inner_back_body(scalars, low, wd, slope, first_low, grad_ref, sums_ref, send_ref, keep_ref, turned, ordered):
    size = first_low.shape[1] // PARTS
    flipped = first_low[...].T
    for i in range(PARTS):
        turned[i] = flipped[i * size : (i + 1) * size, :]
    turn_parts(scalars[1], turned, ordered)
    rows = (PARTS // 2) * size

    @pl.loop(0, slope.shape[1] // BLOCK)
    def _(j):
        cols = step_of(j, BLOCK)
        grad = (nt(low[...], wd[cols, :]) * slope[:, cols].astype(jnp.float32)).astype(jnp.bfloat16)
        grad_ref[:, cols] = grad
        sums_ref[:, cols] = row_sum(grad)
        for side, ref in enumerate((send_ref, keep_ref)):
            left = ordered[side].reshape(rows, low.shape[0])
            ref[:, :, cols] = nn(left, grad).astype(jnp.bfloat16).reshape(PARTS // 2, size, BLOCK)


def outer_back_body(scalars, grad, wu, up_grad, normal_ref, scale_ref, vec, wo, attended, sum_ref, result_ref, sums_ref, send_ref, keep_ref, low, sums, turned):
    width = wo.shape[0]
    sums[...] = jnp.zeros_like(sums)

    @pl.loop(0, grad.shape[0] // ROWS)
    def _(i):
        rows = step_of(i, ROWS)
        first = up_grad[rows, :] + nt(grad[rows, :], wu[...])
        normal = normal_ref[rows, :]
        total = norm_back(first, normal, scale_ref[rows, 0:1], vec[3:4, :])
        branch = total.astype(jnp.bfloat16)
        sum_ref[rows, :] = total
        low[rows, :] = branch
        result_ref[rows, :] = nt(branch, wo[...]).astype(jnp.bfloat16)
        sums[0:1, :] += row_sum(branch)
        sums[1:2, :] += row_sum(first * normal)
        sums[2:3, :] += row_sum(first)

    sums_ref[...] = sums[...]
    size = width // PARTS
    product = tn(attended[...], low[...]).astype(jnp.bfloat16)
    for i in range(PARTS):
        turned[i] = product[i * size : (i + 1) * size, :]
    for i in range(PARTS // 2):
        send_ref[i] = turned[2 * i + 1 - scalars[1]]
        keep_ref[i] = turned[2 * i + scalars[1]]


class Far:
    def __init__(self, value, columns=None, index=None):
        self.value, self.columns, self.index = value, columns, index
        shape = value.shape if index is None else value.shape[1:]
        width = shape[-1] if columns is None else columns.stop - columns.start
        self.shape, self.dtype = shape[:-1] + (width,), value.dtype


def far_body(body, far, counts, scalars, *refs):
    hbm, inputs, outputs, held, lazy = counts
    given = list(refs[hbm : hbm + inputs])
    held_refs, sems = refs[len(refs) - held - 1 : -1], refs[-1]
    copies = []
    for i, (place, columns, index) in enumerate(far):
        source = given[place]
        if index is not None:
            source = source.at[index]
        if columns is not None:
            source = source.at[:, columns]
        copies.append(pltpu.make_async_copy(source, held_refs[i], sems.at[i]))
        copies[-1].start()
        given[place] = held_refs[i]
    rest = (*refs[:hbm], *given, *refs[hbm + inputs : len(refs) - held - 1])
    if lazy:
        body(copies, scalars, *rest)
    else:
        wait_all(copies)
        body(scalars, *rest)


def in_hbm(value):
    return pltpu.with_memory_space_constraint(value, pltpu.HBM)


def whole_call(body, name, scalars, hbm, inputs, outputs, hbm_outputs, scratch, room=8, lazy=False):
    shape_of = lambda x: jax.ShapeDtypeStruct(x.shape, x.dtype)
    near, stay = pl.BlockSpec(memory_space=pltpu.VMEM), pl.BlockSpec(memory_space=pltpu.HBM)
    far = [(i, x.columns, x.index) for i, x in enumerate(inputs) if isinstance(x, Far)]
    scratch = list(scratch)
    if far:
        held = [pltpu.VMEM(inputs[i].shape, inputs[i].dtype) for i, *_ in far]
        counts = (len(hbm), len(inputs), len(outputs) + len(hbm_outputs), len(far), lazy)
        body = functools.partial(far_body, body, far, counts)
        scratch += held + [pltpu.SemaphoreType.DMA((len(far),))]
        room += sum(math.prod(inputs[i].shape) * inputs[i].dtype.itemsize for i, *_ in far) // (1 << 20) + 1
    return pl.pallas_call(
        body,
        in_specs=[pl.BlockSpec(memory_space=pltpu.SMEM)]
        + [stay] * len(hbm)
        + [stay if isinstance(x, Far) else near for x in inputs],
        out_specs=[near] * len(outputs) + [stay] * len(hbm_outputs),
        scratch_shapes=scratch,
        out_shape=[shape_of(x) for x in outputs] + [pltpu.HBM(x.shape, x.dtype) for x in hbm_outputs],
        cost_estimate=pl.CostEstimate(flops=1, transcendentals=0, bytes_accessed=1),
        compiler_params=pltpu.CompilerParams(vmem_limit_bytes=room << 20),
        name=name,
    )(scalars, *[in_hbm(x) for x in hbm], *[in_hbm(x.value) if isinstance(x, Far) else x for x in inputs])


def array(dtype, *shape):
    return jax.ShapeDtypeStruct(shape, dtype)


def widen(scalars, pieces, attended, tokens, vec, up_add):
    count, width = tokens.shape
    wide = up_add.shape[1]
    f32, b16 = jnp.float32, jnp.bfloat16
    return whole_call(
        widen_body, "widen", scalars, pieces, [attended, tokens, vec, up_add],
        [array(f32, count, width), array(f32, count, LANES), array(b16, count, width),
         array(b16, count, wide), array(b16, count, wide), array(b16, width, width), array(b16, width, wide)],
        [], [pltpu.SemaphoreType.DMA((2, len(pieces)))],
    )


def narrow(scalars, pieces, active, normal, vec, upstream):
    count, wide = active.shape
    width = normal.shape[1]
    f32, b16 = jnp.float32, jnp.bfloat16
    half = array(b16, PARTS // 2, wide // PARTS, width)
    return whole_call(
        narrow_body, "narrow", scalars, pieces, [active, normal, vec, upstream],
        [array(b16, count, width), array(f32, count, width), array(b16, count, width), array(f32, 8, width), half, half, array(b16, wide, width)],
        [], [pltpu.VMEM((8, width), f32), pltpu.SemaphoreType.DMA((1, len(pieces)))],
    )


def inner_back(scalars, low, wd, slope, first_low):
    count, wide = slope.shape
    width = low.shape[1]
    size = width // PARTS
    f32, b16 = jnp.float32, jnp.bfloat16
    half = array(b16, PARTS // 2, size, wide)
    return whole_call(
        inner_back_body, "inner_back", scalars, [], [low, wd, slope, first_low],
        [array(b16, count, wide), array(f32, 1, wide), half, half], [],
        [pltpu.VMEM((PARTS, size, count), b16), pltpu.VMEM((2, PARTS // 2, size, count), b16)],
    )


def outer_back(scalars, grad, wu, up_grad, normal, scale, vec, wo, attended):
    count, width = normal.shape
    f32, b16 = jnp.float32, jnp.bfloat16
    half = array(b16, PARTS // 2, width // PARTS, width)
    return whole_call(
        outer_back_body, "outer_back", scalars, [], [grad, wu, up_grad, normal, scale, vec, wo, attended],
        [array(f32, count, width), array(b16, count, width), array(f32, 8, width), half, half], [],
        [pltpu.VMEM((count, width), b16), pltpu.VMEM((8, width), f32), pltpu.VMEM((PARTS, width // PARTS, width), b16)],
    )


def sums_to_slots(core, lines, parts, send, keep, first, wide=None):
    turned = lines[...].T
    rows = turned.shape[0] // PARTS
    for i in range(PARTS):
        parts[i] = turned[i * rows : (i + 1) * rows, :]
    if wide is not None:
        size = wide.shape[1] // (4 * PARTS)
        for i in range(4 * PARTS):
            place = (i % 4) * (rows // 4)
            parts[i // 4, place : place + 1, LANES - size :] = wide[:, i * size : (i + 1) * size]
    for i in range(PARTS // 2):
        send[i, :, first : first + LANES] = parts[2 * i + 1 - core].astype(jnp.bfloat16)
        keep[i, :, first : first + LANES] = parts[2 * i + core].astype(jnp.bfloat16)


def qkv_back_body(side, copies, scalars, dq, dk, dv, far_keys, far_values, ordered, weight, gradient, *refs):
    core = scalars[1]
    if side == 0:
        sums_one, sums_two, wide_sums, send_low, send_high, keep, result, sums_ref, both, lines, parts, send = refs
    else:
        first_sums, send_low, send_high, keep, result, sums_ref, both, lines, parts, send = refs
    half = dq.shape[1]
    both[:, :half] = dq[...]
    both[:, half : 2 * half] = (dk[...] + far_keys[...].astype(jnp.float32)).astype(jnp.bfloat16)
    both[:, 2 * half :] = (dv[...] + far_values[...].astype(jnp.float32)).astype(jnp.bfloat16)
    sums_ref[...] = jnp.zeros_like(sums_ref)
    sums_ref[0:1, :] = row_sum(dq[...])
    sums_ref[1:2, :] = row_sum(both[:, 2 * half :])
    rows = ordered.shape[1] * ordered.shape[2]
    copies[0].wait()
    for i, ref in enumerate((send, keep)):
        left = ordered[i].reshape(rows, ordered.shape[3])
        product = nn(left, both[...]).astype(jnp.bfloat16)
        ref[:, :, : 3 * half] = product.reshape(ordered.shape[1], ordered.shape[2], 3 * half)
    lines[...] = jnp.zeros_like(lines)
    if side == 0:
        lines[0:8, :] = sums_one[...]
        lines[8:16, :] = sums_two[...]
        sums_to_slots(core, lines, parts, send, keep, 3 * half, wide_sums)
    else:
        lines[0:8, :half] = first_sums[...]
        lines[0:8, half:] = sums_ref[...]
        sums_to_slots(core, lines, parts, send, keep, 3 * half)
    send_low[...] = send[:2]
    send_high[...] = send[2:]
    copies[1].wait()
    result[...] = (gradient[...] + nt(both[...], weight[...])).astype(result.dtype)


def qkv_back(side, scalars, dq, dk, dv, far_keys, far_values, ordered, weights, gradient, *more):
    count, half = dq.shape
    width = gradient.shape[1]
    f32, b16 = jnp.float32, jnp.bfloat16
    total = array(b16, PARTS // 2, width // PARTS, 3 * half + LANES)
    part = array(b16, PARTS // 4, width // PARTS, 3 * half + LANES)
    return whole_call(
        functools.partial(qkv_back_body, side), "qkv_back", scalars, [], [dq, dk, dv, far_keys, far_values, Far(ordered), Far(weights, None, side), gradient, *more],
        [part, part, total, array(b16 if side else f32, count, width), array(f32, 8, half)], [],
        [pltpu.VMEM((count, 3 * half), b16), pltpu.VMEM((LANES, width), f32), pltpu.VMEM((PARTS, width // PARTS, LANES), f32),
         pltpu.VMEM(total.shape, b16)],
        8, True,
    )


STRIPE = 32


def fold_body(plans, scalars, *refs):
    places, outs = [0], [0]
    for *_, count, sends in plans:
        places.append(places[-1] + 1 + count)
        outs.append(outs[-1] + 1 + sends)
    for item, (outer, inner, bit, count, sends) in enumerate(plans):
        keep, *gots = refs[places[item] : places[item + 1]]
        *sent, left = refs[places[-1] + outs[item] : places[-1] + outs[item + 1]]
        mine = scalars[bit]
        rows = keep.shape[1]
        stripe = STRIPE if rows % STRIPE == 0 else rows

        @pl.loop(0, rows // stripe)
        def _(k):
            span = step_of(k, stripe) if stripe != rows else slice(None)
            for i in range(outer):
                for j in range(inner):
                    for away, side in ((True, 1 - mine), (False, mine)):
                        place = (2 * i + side) * inner + j
                        if count == 1:
                            got = gots[0][place, span, :]
                        elif outer == 1:
                            got = jnp.where(side == 0, gots[0][j, span, :], gots[1][j, span, :])
                        else:
                            got = gots[i][side * inner + j, span, :]
                        value = keep[place, span, :].astype(jnp.float32) + got.astype(jnp.float32)
                        if away and sends == 2:
                            sent[i][j, span, :] = value.astype(sent[i].dtype)
                        else:
                            target = sent[0] if away else left
                            target[i * inner + j, span, :] = value.astype(target.dtype)


def fold(scalars, items):
    outs, plans, given = [], [], []
    for keep, got, (outer, inner, bit, *more) in items:
        gots = got if isinstance(got, tuple) else (got,)
        sends = 2 if more else 1
        shape = (keep.shape[0] // 2,) + keep.shape[1:]
        outs += [array(jnp.bfloat16, shape[0] // sends, *shape[1:])] * sends + [array(keep.dtype, *shape)]
        plans.append((outer, inner, bit, len(gots), sends))
        given += [keep, *gots]
    got = list(whole_call(functools.partial(fold_body, plans), "fold", scalars, [], given, outs, [], []))
    result = []
    for *_, sends in plans:
        sent = tuple(got.pop(0) for _ in range(sends))
        result.append((sent if sends == 2 else sent[0], got.pop(0)))
    return result


def merge_body(shapes, scalars, *refs):
    send, left = refs[-2:]
    mine = scalars[4]
    low = send.shape[1]
    first = 0
    for item, (rows, wide) in enumerate(shapes):
        keep, got = refs[2 * item : 2 * item + 2]
        for part in range(rows // low):
            span = slice(part * low, (part + 1) * low)
            for high in range(2):
                for target, side in ((send, 1 - mine), (left, mine)):
                    value = keep[2 * high + side, span, :].astype(jnp.float32) + got[2 * high + side, span, :].astype(jnp.float32)
                    target[high, :, first : first + wide] = value.astype(target.dtype)
            first += wide


def merge(scalars, items, low):
    items = [(k.reshape(4, k.shape[-2] // 4, k.shape[-1]), g.reshape(4, g.shape[-2] // 4, g.shape[-1])) for k, g in items]
    shapes = [k.shape[1:] for k, _ in items]
    wide = sum(rows // low * n for rows, n in shapes)
    return whole_call(
        functools.partial(merge_body, shapes), "merge", scalars, [], [x for pair in items for x in pair],
        [array(jnp.bfloat16, 2, low, wide), array(jnp.float32, 2, low, wide)], [], [],
    )


def last_ff_body(scalars, keep, got, down_ref, up_ref):
    low = keep.shape[1]
    width = down_ref.shape[1]
    for part in range(down_ref.shape[0] // low):
        cols = slice(part * width, (part + 1) * width)
        down_ref[part * low : (part + 1) * low, :] = keep[0, :, cols] + got[0, :, cols].astype(jnp.float32)
    cols = slice(4 * width, 4 * width + up_ref.shape[1])
    up_ref[...] = keep[0, :, cols] + got[0, :, cols].astype(jnp.float32)


def last_ff(scalars, keep, got, width):
    low = keep.shape[1]
    return whole_call(
        last_ff_body, "last_ff", scalars, [], [keep, got], [array(jnp.float32, 4 * low, width), array(jnp.float32, low, 4 * width)], [], []
    )


def last_qkv_body(scalars, keep, got, more_keep, more_got, query_ref, key_ref, value_ref, out_ref, small_ref, late_ref, wide_ref, turned):
    low = keep.shape[1]
    width = query_ref.shape[1]
    half = width // 2

    def total(pair, first, size):
        return pair[0][0, :, first : first + size] + pair[1][0, :, first : first + size].astype(jnp.float32)

    one, two = (keep, got), (more_keep, more_got)
    for i, ref in enumerate((query_ref, key_ref, value_ref)):
        ref[:, :half] = total(one, i * half, half)
        ref[:, half:] = total(two, i * half, half)
    out_ref[...] = total(one, 3 * half + LANES, width)
    wide_ref[...] = total(one, 3 * half, LANES)[0:1, :]
    for ref, pair in ((small_ref, one), (late_ref, two)):
        turned[...] = jnp.zeros_like(turned)
        turned[:low, :] = total(pair, 3 * half, LANES)
        ref[...] = turned[...].T[: ref.shape[0], :]


def last_qkv(scalars, keep, got, more_keep, more_got, width):
    low = keep.shape[1]
    f32 = jnp.float32
    return whole_call(
        last_qkv_body, "last_qkv", scalars, [], [keep, got, more_keep, more_got],
        [array(f32, low, width)] * 4 + [array(f32, 24, LANES), array(f32, 8, LANES), array(f32, 1, LANES)], [], [pltpu.VMEM((LANES, LANES), f32)],
    )


def after(value, *others):
    return lax.optimization_barrier((value,) + others)[0]


def bit_count(size):
    return size.bit_length() - 1


def swap_dp(value, mask):
    return lax.ppermute(value, "dp", [(i, i ^ mask) for i in range(lax.axis_size("dp"))])


def swap_seq(value, mask):
    return lax.ppermute(value, "seq", [(i, i ^ mask) for i in range(lax.axis_size("seq"))])


def column_sum(matrix):
    return jnp.sum(matrix.astype(jnp.float32), axis=0)


def spread_pairs(first):
    dps, seqs = lax.axis_size("dp"), lax.axis_size("seq")
    pairs = []
    for dp in range(dps):
        for seq in range(seqs):
            piece = first ^ (seq & 1)
            to_dp = (dp & ~1) | (seq >> 1)
            to_seq = 2 * (dp & 1) + piece
            pairs.append((dp * seqs + seq, to_dp * seqs + to_seq))
    return pairs


def to_sequences(local, order):
    odd = (lax.axis_index("seq") & 1) == 1
    got = []
    pieces = [jnp.where(odd, local[1 - first], local[first]) for first in range(2)]
    order.mark(*pieces)
    for first, piece in enumerate(pieces):
        got.append(lax.ppermute(piece, AXES, spread_pairs(first)))
    return got, odd


def in_order(got, odd, rows):
    return jnp.where(odd, jnp.concatenate([g[:rows] for g in got[::-1]]), jnp.concatenate([g[:rows] for g in got]))


def from_sequences(tokens, order):
    odd = (lax.axis_index("seq") & 1) == 1
    half = tokens.shape[0] // 2
    got = []
    for first in range(2):
        near, far = tokens[first * half : (first + 1) * half], tokens[(1 - first) * half : (2 - first) * half]
        piece = order.mark(jnp.where(order.gate(odd), far, near))
        got.append(lax.ppermute(piece, AXES, [(b, a) for a, b in spread_pairs(first)]))
    return got


def both_sequences(order, got):
    odd = order.gate((lax.axis_index("seq") & 1) == 1)
    return jnp.where(odd, jnp.stack(got[::-1]), jnp.stack(got))


def weight_lines(weights, lines):
    width = weights[0].shape[-1]
    lines = [jnp.pad(v[..., None, :], [(0, 0)] * v.ndim + [(0, width - v.shape[-1])]) for v in lines]
    lines.append(jnp.zeros(lines[0].shape[:-2] + (16 - len(lines), width), jnp.bfloat16))
    return jnp.concatenate(weights + lines, axis=-2)


def near_shards(part, across=True):
    if lax.axis_size("dp") != PARTS:
        p = part if part.ndim == 3 else jnp.stack(jnp.split(lax.all_gather(part, "dp", axis=0, tiled=True), PARTS))
        return [p[i] for i in range(PARTS)]
    return [part, swap_dp(part, 2), swap_dp(part, 4)] + ([swap_dp(part, 6)] if across else [])


def both_cores(parts):
    return [shard for part in parts for shard in (part, swap_dp(part, 1))]


def all_shards(near, *ready):
    if len(near) == PARTS:
        return near
    return both_cores([near[0]] + list(lax.optimization_barrier((*near[1:], *ready))[:3]))


def relayed_shards(near, cut, *ready):
    if len(near) == PARTS:
        return near
    own, along_x, along_y = near
    along_x, along_y = lax.optimization_barrier((along_x, along_y, *ready))[:2]
    sent = along_x[:cut], along_y[cut:]
    top, bottom = swap_dp(sent[0], 4), swap_dp(sent[1], 2)
    own, along_x, along_y = lax.optimization_barrier((own, along_x, along_y, *sent))[:3]
    return both_cores([own, along_x, along_y, top, bottom])


def pack_body(count, scalars, *refs):
    weights, vectors, hidden, ids = refs[: min(3, count)], refs[3:count], refs[count], refs[count + 1]
    pieces = refs[count + 2 : count + 4]
    if vectors:
        part, lines = refs[count + 4 :]
        rows = weights[0].shape[0]
        for i, ref in enumerate(weights):
            part[i * rows : (i + 1) * rows, :] = ref[...]
        lines[...] = jnp.zeros_like(lines)
        for i, ref in enumerate(vectors):
            lines[i : i + 1, : ref.shape[1]] = ref[...].astype(jnp.float32)
        part[3 * rows :, :] = lines[...].astype(jnp.bfloat16)
    odd = scalars[7]
    block, half = hidden.shape[1], ids.shape[1] // 2
    for first, piece in enumerate(pieces):
        piece[:block, :] = hidden[first ^ odd]
        line = jnp.where(first ^ odd == 0, ids[0:1, :], ids[1:2, :]).astype(jnp.bfloat16)
        piece[block:, :] = jnp.zeros_like(piece[block:, :])
        piece[block : block + 1, :half] = line[:, :half]
        piece[block + 1 : block + 2, :half] = line[:, half:]


def pack(scalars, weights, vectors, hidden, ids):
    piece = array(jnp.bfloat16, hidden.shape[1] + 16, hidden.shape[2])
    if lax.axis_size("dp") == PARTS:
        rows, width = weights[0].shape
        given = weights + [v[None, :] for v in vectors]
        return whole_call(
            functools.partial(pack_body, len(given)), "pack", scalars, [], [Far(x) for x in given + [hidden, ids]],
            [piece, piece, array(jnp.bfloat16, 3 * rows + 16, width)], [], [pltpu.VMEM((16, width), jnp.float32)],
        )
    gather = lambda v: lax.all_gather(v, "dp", axis=0, tiled=True)
    split = lambda v: gather(v).reshape((PARTS, -1) + v.shape[1:])
    pieces = whole_call(functools.partial(pack_body, 0), "pack", scalars, [], [Far(hidden), Far(ids)], [piece, piece], [], [])
    return *pieces, weight_lines([split(w) for w in weights], [split(v) for v in vectors])


def project_body(sizes, scalars, *refs):
    rows, wide, vectors, qblock, chunk, lanes, shards = sizes
    pieces, hidden = parts_of(refs[:shards]), refs[shards : shards + 4]
    (
        attended, lse, tokens, vec_ref, up_ref, segments, ordered, query_out, keys_out, values_out, keys_far_out, values_far_out, weights_out,
        query, keys, values, keys_far, values_far, far, held, small, turned, ids, sems, hidden_sems, out_sems, kall, vt, tiles,
    ) = refs[shards + 4 :]
    count, width = tokens.shape
    block = count // 2
    half = width // 2
    core, odd = scalars[6], scalars[7]
    copies, brought = [], []

    def start(copies, source, target, sem):
        copies.append(pltpu.make_async_copy(source, target, sem))
        copies[-1].start()

    for i, (ref, place) in enumerate(zip(hidden, (0, 1, 0, 1))):
        goal = tokens if i < 2 else far
        start(brought, ref.at[:block, :], goal.at[pl.ds(pl.multiple_of((place ^ odd) * block, block), block), :], hidden_sems.at[i])
    start(brought, hidden[0].at[block:, :], ids, hidden_sems.at[4])
    for part, first, ref in pieces:
        where = scalars[0] ^ part
        target = pl.ds(where * rows, rows)
        for weight in range(first // rows, (first + ref.shape[0]) // rows):
            for side in range(2):
                start(
                    copies,
                    ref.at[weight * rows - first : (weight + 1) * rows - first, side * half : (side + 1) * half],
                    held.at[side, target, weight * half : (weight + 1) * half],
                    sems.at[len(copies)],
                )
        if first + ref.shape[0] > 3 * rows:
            start(copies, ref.at[3 * rows - first :, :], small.at[where], sems.at[len(copies)])
    wait_all(brought)
    line = ids[...].astype(jnp.float32)
    for i in range(2):
        segments[:, i * count : (i + 1) * count] = jnp.where(core == i, line[0:1, :count], line[1:2, :count])
    flipped = tokens[...].T
    for i in range(PARTS):
        turned[i] = flipped[i * rows : (i + 1) * rows, :]
    turn_parts(scalars[1], turned, ordered)
    wait_all(copies)
    saves = []
    start(saves, held, weights_out, out_sems.at[0])
    vec_ref[...] = jnp.concatenate([small[i, :, :rows] for i in range(PARTS)], axis=1).astype(jnp.float32)
    up_ref[...] = jnp.concatenate([small[i, vectors : vectors + 1, :wide] for i in range(PARTS)], axis=1).astype(jnp.float32)
    for i, (weight, add, goal, source, out) in enumerate((
        (1, None, keys, tokens, keys_out), (1, None, keys_far, far, keys_far_out), (2, 1, values, tokens, values_out),
        (2, 1, values_far, far, values_far_out), (0, 0, query, tokens, query_out),
    )):
        for side in range(2):
            cols = slice(side * half, (side + 1) * half)
            product = nn(source[...], held[side, :, weight * half : (weight + 1) * half])
            if add is not None:
                product = product + vec_ref[add : add + 1, cols]
            goal[:, cols] = product.astype(jnp.bfloat16)
        start(saves, goal, out, out_sems.at[i + 1])
    forward_body(qblock, chunk, lanes, query, keys, values, keys_far, values_far, segments, attended, lse, kall, vt, tiles)
    wait_all(saves)


def project(scalars, pieces, hidden, rows, wide, vectors, qblock, chunk, lanes):
    block, width = hidden[0].shape[0] - 16, hidden[0].shape[1]
    count = 2 * block
    lines = 16
    n = 2 * count // chunk
    f32, b16 = jnp.float32, jnp.bfloat16
    whole = array(b16, count, width)
    vmem = lambda x: pltpu.VMEM(x.shape, x.dtype)
    return whole_call(
        functools.partial(project_body, (rows, wide, vectors, qblock, chunk, lanes, len(pieces))), "project", scalars, list(pieces) + list(hidden), [],
        [whole, array(f32, width // lanes, 8, count), whole, array(f32, lines, width), array(f32, 1, wide * PARTS), array(f32, 1, 2 * count),
         array(b16, 2, PARTS // 2, rows, count)],
        [whole] * 5 + [array(b16, 2, width, 3 * width // 2)],
        [vmem(whole)] * 6
        + [pltpu.VMEM((2, width, 3 * width // 2), b16), pltpu.VMEM((PARTS, lines, width), b16), pltpu.VMEM((PARTS, rows, count), b16),
           pltpu.VMEM((16, width), b16), pltpu.SemaphoreType.DMA((7 * PARTS,)),
           pltpu.SemaphoreType.DMA((5,)), pltpu.SemaphoreType.DMA((6,)), pltpu.VMEM((n, chunk, lanes), b16),
           pltpu.VMEM((n, lanes, chunk), b16), pltpu.VMEM((n, chunk, LANES), f32)],
        28,
    )


class Order:
    def __init__(self):
        self.last = ()

    def gate(self, value):
        return lax.optimization_barrier((value, *self.last))[0] if self.last else value

    def mark(self, *values):
        self.last = values
        return values[0] if len(values) == 1 else values


def all_rows(send, keep):
    return jnp.stack([keep, send], axis=1).reshape(-1, keep.shape[-1]).astype(jnp.float32)


def scatter_all(send, keep):
    return lax.psum_scatter(all_rows(send, keep), AXES, scatter_dimension=0, tiled=True)


def per_device(
    hidden_in, segment_ids, query_weight, query_bias, key_weight, value_weight, value_bias, out_weight, out_bias,
    first_gain, first_shift, up_weight, up_bias, down_weight, down_bias, second_gain, second_shift, cotangent,
):
    dps, seqs = lax.axis_size("dp"), lax.axis_size("seq")
    inner_width, width = up_weight.shape[1], query_weight.shape[1]
    devices = dps * seqs
    share = width // devices
    qblock = chunk = 256
    pairs = 3
    direct = dps == PARTS and seqs == 4
    dp, seq = lax.axis_index("dp"), lax.axis_index("seq")
    if direct:
        scalars = [dp, dp & 1, (dp >> 1) & 1, dp >> 2, seq & 1, seq >> 1, dp & 1, seq & 1]
    else:
        scalars = [0, 0, 0, 0, 0, 0, dp & 1, seq & 1]
    scalars = jnp.stack([jnp.asarray(v, jnp.int32) for v in scalars])

    vectors = [query_bias, value_bias, out_bias, first_gain, first_shift, down_bias, second_gain, second_shift]
    *hidden, part = pack(
        scalars, [query_weight, key_weight, value_weight], vectors + [up_bias], hidden_in, segment_ids
    )
    near = near_shards(part)
    hidden = [lax.ppermute(piece, AXES, spread_pairs(first)) for first, piece in enumerate(hidden)]
    out_up, down_part = lax.optimization_barrier(
        (jnp.concatenate([out_weight, up_weight], axis=1), down_weight, *near[1:4])
    )[:2]
    hidden += [swap_dp(piece, 1) for piece in hidden]
    if direct:
        near = list(lax.optimization_barrier((*near, *hidden))[:4])
    shards = both_cores(near) if direct else near
    out_up_near = near_shards(out_up)
    attended, lse, tokens, vec, up_add, segments, ordered, query, keys, values, keys_other, values_other, w_qkv = project(
        scalars, shards, hidden, width // PARTS, inner_width // PARTS, len(vectors), qblock, chunk, pairs * LANES
    )
    order = Order()
    down_near = near_shards(after(down_part, attended, *out_up_near[1:4]), False)
    got_up, odd = to_sequences(after(cotangent, attended), order)
    out_up_shards = all_shards(out_up_near, attended)
    normal_one, scale_one, first_low, active, slope, wo, wu = widen(scalars, out_up_shards, attended, tokens, vec, up_add)
    upstream = in_order(lax.optimization_barrier((*got_up, active))[:2], odd, hidden_in.shape[1])
    layer_low, sum_two_grad, second_grad, sums_two, down_send, down_keep, wd = narrow(
        scalars, relayed_shards(down_near, inner_width // PARTS // 2, active), active, normal_one, vec, upstream
    )
    swap = (lambda value: swap_dp(value, 1)) if direct else (lambda value: value)
    order = Order()
    order.mark(second_grad)
    down_got = swap(down_send)
    out_pieces = from_sequences(layer_low, order)
    inner_grad, up_sum, up_send, up_keep = inner_back(scalars, order.gate(second_grad), wd, slope, first_low)
    up_got = swap(up_send)
    order.mark(inner_grad)
    if direct:
        ((send, down_keep),) = fold(order.gate(scalars), [(down_keep, down_got, (2, 1, 2))])
        down_got = swap_dp(order.mark(send), 2)
        ((send, up_keep),) = fold(order.gate(scalars), [(up_keep, up_got, (1, 2, 3))])
        up_got = swap_dp(order.mark(send), 4)
    sum_one_grad, attended_grad, sums_one, out_send, out_keep = outer_back(
        order.gate(scalars), inner_grad, wu, sum_two_grad, normal_one, scale_one, vec, wo, attended
    )
    order.mark(attended_grad)
    out_got = swap(out_send)

    def attend(side):
        given = (query, keys, values, keys_other, values_other, attended, attended_grad, lse, segments)
        return order.mark(*attend_back(order.gate(scalars), *given, qblock, chunk, pairs, side))

    dq, dk, dv, *far = attend(0)
    if direct:
        (send, down_keep), (other, up_keep), (third, out_keep) = fold(
            order.gate(scalars),
            [(down_keep, down_got, (1, 1, 3)), (up_keep, up_got, (1, 1, 2)), (out_keep, out_got, (1, 2, 3))],
        )
        order.mark(send, other, third)
        down_got, up_got, out_got = swap_dp(send, 4), swap_dp(other, 2), swap_dp(third, 4)
    layer_out = order.mark(both_sequences(order, out_pieces))
    one_low, one_high, one_keep, gradient, sums_first = qkv_back(
        0, order.gate(scalars), dq, dk, dv, *[swap_dp(x, 1) for x in order.gate(far)], ordered, w_qkv, sum_one_grad,
        sums_one, sums_two, up_sum
    )
    order.mark(gradient)
    one_got = (swap(one_low), swap(one_high))
    dq, dk, dv, *far = attend(1)
    if direct:
        send, ff_keep = merge(order.gate(scalars), [(down_keep, down_got), (up_keep, up_got)], share)
        ff_got = swap_seq(order.mark(send), 1)
        (send, one_keep), (other, out_keep) = fold(
            order.gate(scalars), [(one_keep, one_got, (2, 1, 2)), (out_keep, out_got, (1, 1, 2))]
        )
        order.mark(send, other)
        one_got, out_got = swap_dp(send, 2), swap_dp(other, 2)
    two_low, two_high, two_keep, gradient, _ = qkv_back(
        1, order.gate(scalars), dq, dk, dv, *[swap_dp(x, 1) for x in order.gate(far)], ordered, w_qkv, gradient, sums_first
    )
    order.mark(gradient)
    two_got = (swap(two_low), swap(two_high))
    in_pieces = from_sequences(gradient, order)
    if not direct:
        down_grad, up_grad = scatter_all(down_send, down_keep), scatter_all(up_send, up_keep)
        one, two = scatter_all(jnp.concatenate([one_low, one_high]), one_keep), scatter_all(jnp.concatenate([two_low, two_high]), two_keep)
        cut = width // 2
        query_grad, key_grad, value_grad = [
            jnp.concatenate([side[:, i * cut : (i + 1) * cut] for side in (one, two)], axis=1) for i in range(3)
        ]
        out_grad = scatter_all(out_send, out_keep)
        small, late = one[:, 3 * cut :].T, two[:, 3 * cut :].T
        up_bias_grad = lax.psum_scatter(up_sum[0], AXES, scatter_dimension=0, tiled=True)
    else:
        ((send, one_keep),) = fold(order.gate(scalars), [(one_keep, one_got, (1, 1, 3))])
        one_got = swap_dp(order.mark(send), 4)
        ((send, ff_keep),) = fold(order.gate(scalars), [(ff_keep, ff_got, (1, 1, 5))])
        ff_got = swap_seq(order.mark(send), 2)
        ((sent, two_keep),) = fold(order.gate(scalars), [(two_keep, two_got, (2, 1, 2, True))])
        two_got = tuple(swap_dp(x, 2) for x in order.mark(*sent))
        send, keep = merge(order.gate(scalars), [(one_keep, one_got), (out_keep, out_got)], share)
        got = swap_seq(order.mark(send), 1)
        ((send, two_keep),) = fold(order.gate(scalars), [(two_keep, two_got, (1, 1, 3))])
        two_got = swap_dp(order.mark(send), 4)
    input_grad = order.mark(both_sequences(order, in_pieces).astype(jnp.float32))
    if direct:
        ((send, keep),) = fold(order.gate(scalars), [(keep, got, (1, 1, 5))])
        got = swap_seq(order.mark(send), 2)
        send, two_keep = merge(order.gate(scalars), [(two_keep, two_got)], share)
        two_got = swap_seq(order.mark(send), 1)
        ((send, two_keep),) = fold(order.gate(scalars), [(two_keep, two_got, (1, 1, 5))])
        two_got = swap_seq(order.mark(send), 2)
        down_grad, up_grad = order.mark(*last_ff(order.gate(scalars), ff_keep, ff_got, width))
        query_grad, key_grad, value_grad, out_grad, small, late, line = last_qkv(
            order.gate(scalars), keep, got, two_keep, two_got, width
        )
        up_bias_grad = line[0, LANES - inner_width // devices :]
    ob, g1, s1 = [small[i, :share] for i in (0, 1, 2)]
    db, g2, s2 = [small[i, :share] for i in (8, 9, 10)]
    qb, vb = [late[i, :share] for i in (0, 1)]
    return (
        layer_out, input_grad, query_grad, qb, key_grad, value_grad, vb, out_grad, ob, g1, s1, up_grad, up_bias_grad, down_grad, db, g2, s2,
    )


def solution(mesh):
    wide, flat = P("dp", None), P("dp")
    in_specs = (
        P("dp", "seq", None), wide, wide, flat, wide, wide, flat, wide, flat, flat, flat, wide, flat, wide, flat,
        flat, flat, P("dp", "seq", None),
    )
    rows, cells = P(AXES, None), P(AXES)
    out_specs = (
        P("dp", "seq", None), P("dp", "seq", None), rows, cells, rows, rows, cells, rows, cells, cells, cells, rows,
        cells, rows, cells, cells, cells,
    )
    return jax.shard_map(per_device, mesh=mesh, in_specs=in_specs, out_specs=out_specs, check_vma=False)
```

```python
import functools
import math

import jax
import jax.numpy as jnp
from jax import lax
from jax.experimental import pallas as pl
from jax.experimental.pallas import tpu as pltpu
from jax.sharding import PartitionSpec as P

HEAD_DIM = 64
LANES = 128
NEGATIVE = -1e30


def nt(left, right):
    return lax.dot_general(left, right, (((1,), (1,)), ((), ())), preferred_element_type=jnp.float32)


def nn(left, right):
    return lax.dot_general(left, right, (((1,), (0,)), ((), ())), preferred_element_type=jnp.float32)


def head_parts(block):
    lane = lax.broadcasted_iota(jnp.int32, block.shape, 1)
    zero = jnp.zeros_like(block)
    return (jnp.where(lane < HEAD_DIM, block, zero), jnp.where(lane < HEAD_DIM, zero, block))


def same_document(column_tile, row):
    column = jnp.concatenate([column_tile] * (row.shape[1] // LANES), axis=1)
    return column == jnp.broadcast_to(row, column.shape)


def pair_lanes(pair):
    return slice(pair * LANES, (pair + 1) * LANES)


def segment_tables(segments, tiles, half, qblock, chunk):
    ids = segments[...]
    for j in range(tiles.shape[0]):
        for i in range(chunk // LANES):
            start = j * chunk + i * LANES
            tiles[j, i * LANES : (i + 1) * LANES, :] = jnp.broadcast_to(ids[:, start : start + LANES], (LANES, LANES)).T
    chunks = half // chunk
    low = [jnp.min(ids[:, j * chunk : (j + 1) * chunk]) for j in range(2 * chunks)]
    high = [jnp.max(ids[:, j * chunk : (j + 1) * chunk]) for j in range(2 * chunks)]
    found = []
    for b in range(half // qblock):
        mine = slice(b * qblock, (b + 1) * qblock)
        first, last = jnp.min(ids[:, mine]), jnp.max(ids[:, mine])
        bounds = []
        for side in range(2):
            before = sum((high[side * chunks + j] < first).astype(jnp.int32) for j in range(chunks))
            behind = sum((low[side * chunks + j] > last).astype(jnp.int32) for j in range(chunks))
            bounds += [before, chunks - behind]
        found.append((bounds[0], bounds[1] - bounds[0], bounds[2], bounds[1] - bounds[0] + bounds[3] - bounds[2]))
    return found


def chunk_of(bounds, step, chunks):
    first, own, other, _ = bounds
    return jnp.where(step < own, first + step, chunks + other + step - own)


def forward_body(qblock, chunk, lanes, q_all, k_all, v_all, ko_all, vo_all, segments, o_all, lse_all, kall, vt, sk_ref):
    half = k_all.shape[0]
    tables = segment_tables(segments, sk_ref, half, qblock, chunk)
    chunks, pairs = half // chunk, lanes // LANES

    @pl.loop(0, q_all.shape[1] // lanes)
    def _(group):
        cols = step_of(group, lanes)
        q_ref, k_ref, v_ref, ko_ref, vo_ref, o_ref = (r.at[:, cols] for r in (q_all, k_all, v_all, ko_all, vo_all, o_all))
        lse_ref = lse_all.at[pl.ds(group, 1)]
        for j in range(chunks):
            rows = slice(j * chunk, (j + 1) * chunk)
            kall[j] = k_ref[rows, :]
            kall[chunks + j] = ko_ref[rows, :]
            vt[j] = v_ref[rows, :].T
            vt[chunks + j] = vo_ref[rows, :].T
        for b in range(q_ref.shape[0] // qblock):
            span = slice(b * qblock, (b + 1) * qblock)
            parts = []
            for pair in range(pairs):
                parts += head_parts(q_ref[span, pair_lanes(pair)] * jnp.bfloat16(HEAD_DIM**-0.5))
            row = segments[:, span]

            def one(step, carry):
                j = chunk_of(tables[b], step, chunks)
                mask = same_document(sk_ref[j], row)
                scores = [jnp.where(mask, nt(kall[j, :, pair_lanes(h // 2)], part), NEGATIVE) for h, part in enumerate(parts)]
                out = []
                for h, score in enumerate(scores):
                    top, total, acc = carry[h]
                    new_top = jnp.maximum(top, jnp.max(score, axis=0, keepdims=True))
                    expo = jnp.exp(score - new_top)
                    scale = jnp.exp(top - new_top)
                    total = total * scale + jnp.sum(expo, axis=0, keepdims=True)
                    acc = acc * scale + nn(vt[j, h * HEAD_DIM : (h + 1) * HEAD_DIM, :], expo.astype(jnp.bfloat16))
                    out.append((new_top, total, acc))
                return tuple(out)

            init = (
                jnp.full((1, qblock), NEGATIVE, jnp.float32),
                jnp.zeros((1, qblock), jnp.float32),
                jnp.zeros((HEAD_DIM, qblock), jnp.float32),
            )
            carry = lax.fori_loop(0, tables[b][3], one, (init,) * len(parts))
            result = jnp.concatenate([acc / total for _, total, acc in carry], axis=0)
            o_ref[span, :] = result.T.astype(jnp.bfloat16)
            for h, (top, total, _) in enumerate(carry):
                lse_ref[0, h : h + 1, span] = top + jnp.log(total)


def backward_body(
    qblock, chunk, lanes, side, copies, scalars, q_ref, k_ref, v_ref, ko_ref, vo_ref, o_ref, do_ref, lse_all, segments,
    dq_ref, dk_ref, dv_ref, far_keys, far_values, kall, vall, kt, dkall, dvall, sk_ref,
):
    half = k_ref.shape[0]
    tables = segment_tables(segments, sk_ref, half, qblock, chunk)
    lse_ref = lse_all.at[side : side + 1]
    chunks, pairs = half // chunk, lanes // LANES
    dkall[...] = jnp.zeros_like(dkall)
    dvall[...] = jnp.zeros_like(dvall)
    for first, keys, values in ((0, k_ref, v_ref), (chunks, ko_ref, vo_ref)):
        wait_all(copies[1:3] if first == 0 else copies[3:5])
        for j in range(chunks):
            rows = slice(j * chunk, (j + 1) * chunk)
            kall[first + j] = keys[rows, :]
            vall[first + j] = values[rows, :]
            kt[first + j] = keys[rows, :].T
    wait_all(copies[:1] + copies[5:])
    for b in range(q_ref.shape[0] // qblock):
        span = slice(b * qblock, (b + 1) * qblock)
        parts, dparts, delta = [], [], []
        for pair in range(pairs):
            parts.append(head_parts(q_ref[span, pair_lanes(pair)] * jnp.bfloat16(HEAD_DIM**-0.5)))
            dparts.append(head_parts(do_ref[span, pair_lanes(pair)]))
            product = do_ref[span, pair_lanes(pair)].astype(jnp.float32) * o_ref[span, pair_lanes(pair)].astype(jnp.float32)
            product = product.T
            delta += [jnp.sum(product[h * HEAD_DIM : (h + 1) * HEAD_DIM], axis=0, keepdims=True) for h in range(2)]
        both = [jnp.concatenate(p, axis=0) for p in parts]
        dboth = [jnp.concatenate(p, axis=0) for p in dparts]
        row = segments[:, span]
        lse = [lse_ref[0, h : h + 1, span] for h in range(2 * pairs)]

        def one(step, carry):
            j = chunk_of(tables[b], step, chunks)
            mask = same_document(sk_ref[j], row)
            out = []
            both_mask = jnp.concatenate([mask, mask], axis=1)
            scores = [nt(kall[j, :, pair_lanes(pair)], both[pair]) for pair in range(pairs)]
            products = [nt(vall[j, :, pair_lanes(pair)], dboth[pair]) for pair in range(pairs)]
            adds = []
            for pair in range(pairs):
                score = jnp.where(both_mask, scores[pair], NEGATIVE)
                prob = jnp.exp(score - jnp.concatenate(lse[2 * pair : 2 * pair + 2], axis=1))
                grad = (prob * (products[pair] - jnp.concatenate(delta[2 * pair : 2 * pair + 2], axis=1))).astype(jnp.bfloat16)
                for side in range(2):
                    h = 2 * pair + side
                    out.append(carry[h] + nn(kt[j, h * HEAD_DIM : (h + 1) * HEAD_DIM, :], grad[:, side * qblock : (side + 1) * qblock]))
                adds.append((nn(prob.astype(jnp.bfloat16), dboth[pair]), nn(grad, both[pair])))
            for pair in range(pairs):
                dvall[j, :, pair_lanes(pair)] += adds[pair][0]
                dkall[j, :, pair_lanes(pair)] += adds[pair][1]
            return tuple(out)

        zero = jnp.zeros((HEAD_DIM, qblock), jnp.float32)
        carry = lax.fori_loop(0, tables[b][3], one, (zero,) * (2 * pairs))
        dq_ref[span, :] = (jnp.concatenate(carry, axis=0).T * HEAD_DIM**-0.5).astype(jnp.bfloat16)
    for j in range(chunks):
        rows = slice(j * chunk, (j + 1) * chunk)
        dk_ref[rows, :] = dkall[j]
        dv_ref[rows, :] = dvall[j]
        far_keys[rows, :] = dkall[chunks + j].astype(jnp.bfloat16)
        far_values[rows, :] = dvall[chunks + j].astype(jnp.bfloat16)


def attend_back(scalars, query, keys, values, keys_other, values_other, attended, grad, lse_rows, segments, qblock, chunk, pairs, side):
    tokens, width = query.shape
    half = keys.shape[0]
    lanes = pairs * LANES
    n = 2 * half // chunk
    f32, b16 = jnp.float32, jnp.bfloat16
    cols = slice(side * lanes, (side + 1) * lanes)
    far = [Far(x, cols) for x in (query, keys, values, keys_other, values_other, attended, grad)]
    return whole_call(
        functools.partial(backward_body, qblock, chunk, lanes, side), "attend_back", scalars, [], far + [lse_rows, segments],
        [array(b16, tokens, lanes), array(f32, half, lanes), array(f32, half, lanes), array(b16, half, lanes), array(b16, half, lanes)], [],
        [pltpu.VMEM((n, chunk, lanes), b16), pltpu.VMEM((n, chunk, lanes), b16), pltpu.VMEM((n, lanes, chunk), b16),
         pltpu.VMEM((n, chunk, lanes), f32), pltpu.VMEM((n, chunk, lanes), f32), pltpu.VMEM((n, chunk, LANES), f32)], 24, True,
    )


AXES = ("dp", "seq")
PARTS = 8
epsilon = 1e-12


def tn(left, right):
    return lax.dot_general(left, right, (((0,), (0,)), ((), ())), preferred_element_type=jnp.float32)


def norm_parts(value):
    center = value - jnp.mean(value, axis=-1, keepdims=True)
    spread = jnp.mean(center * center, axis=-1, keepdims=True)
    scale = lax.rsqrt(spread + epsilon)
    return (center * scale, scale)


def norm_back(upstream, normal, scale, gain):
    scaled = upstream * gain
    return scale * (
        scaled
        - jnp.mean(scaled, axis=-1, keepdims=True)
        - normal * jnp.mean(scaled * normal, axis=-1, keepdims=True)
    )


def row_sum(matrix):
    return jnp.sum(matrix.astype(jnp.float32), axis=0, keepdims=True)


def parts_of(refs):
    if len(refs) == PARTS:
        return [(i, 0, ref) for i, ref in enumerate(refs)]
    if len(refs) == 6:
        own, own_far, near_x, near_y, near_d, far = refs
        rows = own.shape[0]
        other = [far.at[i * rows : (i + 1) * rows, :] for i in range(3)]
        return [(i, 0, ref) for i, ref in enumerate((own, own_far, near_x, other[0], near_y, other[1], near_d, other[2]))]
    pieces = [(i, 0, ref) for i, ref in enumerate(refs[:6])]
    for i in range(2):
        top, bottom = refs[6 + i], refs[8 + i]
        pieces += [(6 + i, 0, top), (6 + i, top.shape[0], bottom)]
    return pieces


def load_pieces(me, pieces, rows, targets, sems):
    copies = [[] for _ in targets]
    for place, (part, first, ref) in enumerate(pieces):
        size = ref.shape[0]
        where = pl.ds(pl.multiple_of((me ^ part) * rows + first, 32), size)
        for i, (target, columns) in enumerate(targets):
            copy = pltpu.make_async_copy(ref.at[:, columns], target.at[where, :], sems.at[i, place])
            copy.start()
            copies[i].append(copy)
    return copies


def wait_all(copies):
    for copy in copies:
        copy.wait()


def step_of(block, size):
    return pl.ds(pl.multiple_of(block * size, size), size)


BLOCK = 1024
GELU_BLOCK = 256
ROWS = 256


def widen_body(scalars, *refs):
    shards = len(refs) - 12
    pieces = parts_of(refs[:shards])
    (attended, tokens, vec, up_add, normal_ref, scale_ref, low_ref, active_ref, slope_ref, wo, wu, sems) = refs[shards:]
    width, wide = wu.shape
    loads = load_pieces(scalars[0], pieces, width // PARTS, [(wo, slice(0, width)), (wu, slice(width, width + wide))], sems)
    wait_all(loads[0])

    @pl.loop(0, tokens.shape[0] // ROWS)
    def _(i):
        rows = step_of(i, ROWS)
        branch = nn(attended[rows, :], wo[...]) + vec[2:3, :]
        normal, scale = norm_parts(tokens[rows, :].astype(jnp.float32) + branch)
        first = normal * vec[3:4, :] + vec[4:5, :]
        normal_ref[rows, :] = normal
        scale_ref[rows, :] = jnp.broadcast_to(scale, (ROWS, LANES))
        low_ref[rows, :] = first.astype(jnp.bfloat16)

    wait_all(loads[1])

    @pl.loop(0, wide // GELU_BLOCK)
    def _(j):
        cols = step_of(j, GELU_BLOCK)
        inner = nn(low_ref[...], wu[:, cols]) + up_add[:, cols]
        cumulative = 0.5 * (1.0 + lax.erf(inner * math.sqrt(0.5)))
        density = jnp.exp(-0.5 * inner * inner) * (1.0 / math.sqrt(2.0 * math.pi))
        active_ref[:, cols] = (inner * cumulative).astype(jnp.bfloat16)
        slope_ref[:, cols] = (cumulative + inner * density).astype(jnp.bfloat16)


def narrow_body(scalars, *refs):
    shards = len(refs) - 13
    pieces = parts_of(refs[:shards])
    (active, normal_one, vec, upstream, out_ref, grad_ref, low_ref, sums_ref, send_ref, keep_ref, wd, sums, sems) = refs[shards:]
    wide, width = wd.shape
    (loads,) = load_pieces(scalars[0], pieces, wide // PARTS, [(wd, slice(0, width))], sems)
    wait_all(loads)
    sums[...] = jnp.zeros_like(sums)

    @pl.loop(0, normal_one.shape[0] // ROWS)
    def _(i):
        rows = step_of(i, ROWS)
        second = nn(active[rows, :], wd[...]) + vec[5:6, :]
        normal, scale = norm_parts(normal_one[rows, :] * vec[3:4, :] + vec[4:5, :] + second)
        out_ref[rows, :] = (normal * vec[6:7, :] + vec[7:8, :]).astype(jnp.bfloat16)
        up = upstream[rows, :].astype(jnp.float32)
        grad = norm_back(up, normal, scale, vec[6:7, :])
        low = grad.astype(jnp.bfloat16)
        grad_ref[rows, :] = grad
        low_ref[rows, :] = low
        sums[0:1, :] += row_sum(low)
        sums[1:2, :] += row_sum(up * normal)
        sums[2:3, :] += row_sum(up)

    sums_ref[...] = sums[...]
    size = wide // PARTS

    @pl.loop(0, PARTS // 2)
    def _(i):
        send_ref[i] = tn(active[:, step_of(2 * i + 1 - scalars[1], size)], low_ref[...]).astype(jnp.bfloat16)
        keep_ref[i] = tn(active[:, step_of(2 * i + scalars[1], size)], low_ref[...]).astype(jnp.bfloat16)


def turn_parts(core, turned, ordered):
    for i in range(PARTS // 2):
        ordered[0, i] = turned[2 * i + 1 - core]
        ordered[1, i] = turned[2 * i + core]


def inner_back_body(scalars, low, wd, slope, first_low, grad_ref, sums_ref, send_ref, keep_ref, turned, ordered):
    size = first_low.shape[1] // PARTS
    flipped = first_low[...].T
    for i in range(PARTS):
        turned[i] = flipped[i * size : (i + 1) * size, :]
    turn_parts(scalars[1], turned, ordered)
    rows = (PARTS // 2) * size

    @pl.loop(0, slope.shape[1] // BLOCK)
    def _(j):
        cols = step_of(j, BLOCK)
        grad = (nt(low[...], wd[cols, :]) * slope[:, cols].astype(jnp.float32)).astype(jnp.bfloat16)
        grad_ref[:, cols] = grad
        sums_ref[:, cols] = row_sum(grad)
        for side, ref in enumerate((send_ref, keep_ref)):
            left = ordered[side].reshape(rows, low.shape[0])
            ref[:, :, cols] = nn(left, grad).astype(jnp.bfloat16).reshape(PARTS // 2, size, BLOCK)


def outer_back_body(scalars, grad, wu, up_grad, normal_ref, scale_ref, vec, wo, attended, sum_ref, result_ref, sums_ref, send_ref, keep_ref, low, sums, turned):
    width = wo.shape[0]
    sums[...] = jnp.zeros_like(sums)

    @pl.loop(0, grad.shape[0] // ROWS)
    def _(i):
        rows = step_of(i, ROWS)
        first = up_grad[rows, :] + nt(grad[rows, :], wu[...])
        normal = normal_ref[rows, :]
        total = norm_back(first, normal, scale_ref[rows, 0:1], vec[3:4, :])
        branch = total.astype(jnp.bfloat16)
        sum_ref[rows, :] = total
        low[rows, :] = branch
        result_ref[rows, :] = nt(branch, wo[...]).astype(jnp.bfloat16)
        sums[0:1, :] += row_sum(branch)
        sums[1:2, :] += row_sum(first * normal)
        sums[2:3, :] += row_sum(first)

    sums_ref[...] = sums[...]
    size = width // PARTS
    product = tn(attended[...], low[...]).astype(jnp.bfloat16)
    for i in range(PARTS):
        turned[i] = product[i * size : (i + 1) * size, :]
    for i in range(PARTS // 2):
        send_ref[i] = turned[2 * i + 1 - scalars[1]]
        keep_ref[i] = turned[2 * i + scalars[1]]


class Far:
    def __init__(self, value, columns=None, index=None):
        self.value, self.columns, self.index = value, columns, index
        shape = value.shape if index is None else value.shape[1:]
        width = shape[-1] if columns is None else columns.stop - columns.start
        self.shape, self.dtype = shape[:-1] + (width,), value.dtype


def far_body(body, far, counts, scalars, *refs):
    hbm, inputs, outputs, held, lazy = counts
    given = list(refs[hbm : hbm + inputs])
    held_refs, sems = refs[len(refs) - held - 1 : -1], refs[-1]
    copies = []
    for i, (place, columns, index) in enumerate(far):
        source = given[place]
        if index is not None:
            source = source.at[index]
        if columns is not None:
            source = source.at[:, columns]
        copies.append(pltpu.make_async_copy(source, held_refs[i], sems.at[i]))
        copies[-1].start()
        given[place] = held_refs[i]
    rest = (*refs[:hbm], *given, *refs[hbm + inputs : len(refs) - held - 1])
    if lazy:
        body(copies, scalars, *rest)
    else:
        wait_all(copies)
        body(scalars, *rest)


def in_hbm(value):
    return pltpu.with_memory_space_constraint(value, pltpu.HBM)


def whole_call(body, name, scalars, hbm, inputs, outputs, hbm_outputs, scratch, room=8, lazy=False):
    shape_of = lambda x: jax.ShapeDtypeStruct(x.shape, x.dtype)
    near, stay = pl.BlockSpec(memory_space=pltpu.VMEM), pl.BlockSpec(memory_space=pltpu.HBM)
    far = [(i, x.columns, x.index) for i, x in enumerate(inputs) if isinstance(x, Far)]
    scratch = list(scratch)
    if far:
        held = [pltpu.VMEM(inputs[i].shape, inputs[i].dtype) for i, *_ in far]
        counts = (len(hbm), len(inputs), len(outputs) + len(hbm_outputs), len(far), lazy)
        body = functools.partial(far_body, body, far, counts)
        scratch += held + [pltpu.SemaphoreType.DMA((len(far),))]
        room += sum(math.prod(inputs[i].shape) * inputs[i].dtype.itemsize for i, *_ in far) // (1 << 20) + 1
    return pl.pallas_call(
        body,
        in_specs=[pl.BlockSpec(memory_space=pltpu.SMEM)]
        + [stay] * len(hbm)
        + [stay if isinstance(x, Far) else near for x in inputs],
        out_specs=[near] * len(outputs) + [stay] * len(hbm_outputs),
        scratch_shapes=scratch,
        out_shape=[shape_of(x) for x in outputs] + [pltpu.HBM(x.shape, x.dtype) for x in hbm_outputs],
        cost_estimate=pl.CostEstimate(flops=1, transcendentals=0, bytes_accessed=1),
        compiler_params=pltpu.CompilerParams(vmem_limit_bytes=room << 20),
        name=name,
    )(scalars, *[in_hbm(x) for x in hbm], *[in_hbm(x.value) if isinstance(x, Far) else x for x in inputs])


def array(dtype, *shape):
    return jax.ShapeDtypeStruct(shape, dtype)


def widen(scalars, pieces, attended, tokens, vec, up_add):
    count, width = tokens.shape
    wide = up_add.shape[1]
    f32, b16 = jnp.float32, jnp.bfloat16
    return whole_call(
        widen_body, "widen", scalars, pieces, [attended, tokens, vec, up_add],
        [array(f32, count, width), array(f32, count, LANES), array(b16, count, width),
         array(b16, count, wide), array(b16, count, wide), array(b16, width, width), array(b16, width, wide)],
        [], [pltpu.SemaphoreType.DMA((2, len(pieces)))],
    )


def narrow(scalars, pieces, active, normal, vec, upstream):
    count, wide = active.shape
    width = normal.shape[1]
    f32, b16 = jnp.float32, jnp.bfloat16
    half = array(b16, PARTS // 2, wide // PARTS, width)
    return whole_call(
        narrow_body, "narrow", scalars, pieces, [active, normal, vec, upstream],
        [array(b16, count, width), array(f32, count, width), array(b16, count, width), array(f32, 8, width), half, half, array(b16, wide, width)],
        [], [pltpu.VMEM((8, width), f32), pltpu.SemaphoreType.DMA((1, len(pieces)))],
    )


def inner_back(scalars, low, wd, slope, first_low):
    count, wide = slope.shape
    width = low.shape[1]
    size = width // PARTS
    f32, b16 = jnp.float32, jnp.bfloat16
    half = array(b16, PARTS // 2, size, wide)
    return whole_call(
        inner_back_body, "inner_back", scalars, [], [low, wd, slope, first_low],
        [array(b16, count, wide), array(f32, 1, wide), half, half], [],
        [pltpu.VMEM((PARTS, size, count), b16), pltpu.VMEM((2, PARTS // 2, size, count), b16)],
    )


def outer_back(scalars, grad, wu, up_grad, normal, scale, vec, wo, attended):
    count, width = normal.shape
    f32, b16 = jnp.float32, jnp.bfloat16
    half = array(b16, PARTS // 2, width // PARTS, width)
    return whole_call(
        outer_back_body, "outer_back", scalars, [], [grad, wu, up_grad, normal, scale, vec, wo, attended],
        [array(f32, count, width), array(b16, count, width), array(f32, 8, width), half, half], [],
        [pltpu.VMEM((count, width), b16), pltpu.VMEM((8, width), f32), pltpu.VMEM((PARTS, width // PARTS, width), b16)],
    )


def sums_to_slots(core, lines, parts, send, keep, first, wide=None):
    turned = lines[...].T
    rows = turned.shape[0] // PARTS
    for i in range(PARTS):
        parts[i] = turned[i * rows : (i + 1) * rows, :]
    if wide is not None:
        size = wide.shape[1] // (4 * PARTS)
        for i in range(4 * PARTS):
            place = (i % 4) * (rows // 4)
            parts[i // 4, place : place + 1, LANES - size :] = wide[:, i * size : (i + 1) * size]
    for i in range(PARTS // 2):
        send[i, :, first : first + LANES] = parts[2 * i + 1 - core].astype(jnp.bfloat16)
        keep[i, :, first : first + LANES] = parts[2 * i + core].astype(jnp.bfloat16)


def qkv_back_body(side, copies, scalars, dq, dk, dv, far_keys, far_values, ordered, weight, gradient, *refs):
    core = scalars[1]
    if side == 0:
        sums_one, sums_two, wide_sums, send_low, send_high, keep, result, sums_ref, both, lines, parts, send = refs
    else:
        first_sums, send_low, send_high, keep, result, sums_ref, both, lines, parts, send = refs
    half = dq.shape[1]
    both[:, :half] = dq[...]
    both[:, half : 2 * half] = (dk[...] + far_keys[...].astype(jnp.float32)).astype(jnp.bfloat16)
    both[:, 2 * half :] = (dv[...] + far_values[...].astype(jnp.float32)).astype(jnp.bfloat16)
    sums_ref[...] = jnp.zeros_like(sums_ref)
    sums_ref[0:1, :] = row_sum(dq[...])
    sums_ref[1:2, :] = row_sum(both[:, 2 * half :])
    rows = ordered.shape[1] * ordered.shape[2]
    copies[0].wait()
    for i, ref in enumerate((send, keep)):
        left = ordered[i].reshape(rows, ordered.shape[3])
        product = nn(left, both[...]).astype(jnp.bfloat16)
        ref[:, :, : 3 * half] = product.reshape(ordered.shape[1], ordered.shape[2], 3 * half)
    lines[...] = jnp.zeros_like(lines)
    if side == 0:
        lines[0:8, :] = sums_one[...]
        lines[8:16, :] = sums_two[...]
        sums_to_slots(core, lines, parts, send, keep, 3 * half, wide_sums)
    else:
        lines[0:8, :half] = first_sums[...]
        lines[0:8, half:] = sums_ref[...]
        sums_to_slots(core, lines, parts, send, keep, 3 * half)
    send_low[...] = send[:2]
    send_high[...] = send[2:]
    copies[1].wait()
    result[...] = (gradient[...] + nt(both[...], weight[...])).astype(result.dtype)


def qkv_back(side, scalars, dq, dk, dv, far_keys, far_values, ordered, weights, gradient, *more):
    count, half = dq.shape
    width = gradient.shape[1]
    f32, b16 = jnp.float32, jnp.bfloat16
    total = array(b16, PARTS // 2, width // PARTS, 3 * half + LANES)
    part = array(b16, PARTS // 4, width // PARTS, 3 * half + LANES)
    return whole_call(
        functools.partial(qkv_back_body, side), "qkv_back", scalars, [], [dq, dk, dv, far_keys, far_values, Far(ordered), Far(weights, None, side), gradient, *more],
        [part, part, total, array(b16 if side else f32, count, width), array(f32, 8, half)], [],
        [pltpu.VMEM((count, 3 * half), b16), pltpu.VMEM((LANES, width), f32), pltpu.VMEM((PARTS, width // PARTS, LANES), f32),
         pltpu.VMEM(total.shape, b16)],
        8, True,
    )


STRIPE = 32


def fold_body(plans, scalars, *refs):
    places, outs = [0], [0]
    for *_, count, sends in plans:
        places.append(places[-1] + 1 + count)
        outs.append(outs[-1] + 1 + sends)
    for item, (outer, inner, bit, count, sends) in enumerate(plans):
        keep, *gots = refs[places[item] : places[item + 1]]
        *sent, left = refs[places[-1] + outs[item] : places[-1] + outs[item + 1]]
        mine = scalars[bit]
        rows = keep.shape[1]
        stripe = STRIPE if rows % STRIPE == 0 else rows

        @pl.loop(0, rows // stripe)
        def _(k):
            span = step_of(k, stripe) if stripe != rows else slice(None)
            for i in range(outer):
                for j in range(inner):
                    for away, side in ((True, 1 - mine), (False, mine)):
                        place = (2 * i + side) * inner + j
                        if count == 1:
                            got = gots[0][place, span, :]
                        elif outer == 1:
                            got = jnp.where(side == 0, gots[0][j, span, :], gots[1][j, span, :])
                        else:
                            got = gots[i][side * inner + j, span, :]
                        value = keep[place, span, :].astype(jnp.float32) + got.astype(jnp.float32)
                        if away and sends == 2:
                            sent[i][j, span, :] = value.astype(sent[i].dtype)
                        else:
                            target = sent[0] if away else left
                            target[i * inner + j, span, :] = value.astype(target.dtype)


def fold(scalars, items):
    outs, plans, given = [], [], []
    for keep, got, (outer, inner, bit, *more) in items:
        gots = got if isinstance(got, tuple) else (got,)
        sends = 2 if more else 1
        shape = (keep.shape[0] // 2,) + keep.shape[1:]
        outs += [array(jnp.bfloat16, shape[0] // sends, *shape[1:])] * sends + [array(keep.dtype, *shape)]
        plans.append((outer, inner, bit, len(gots), sends))
        given += [keep, *gots]
    got = list(whole_call(functools.partial(fold_body, plans), "fold", scalars, [], given, outs, [], []))
    result = []
    for *_, sends in plans:
        sent = tuple(got.pop(0) for _ in range(sends))
        result.append((sent if sends == 2 else sent[0], got.pop(0)))
    return result


def merge_body(shapes, scalars, *refs):
    send, left = refs[-2:]
    mine = scalars[4]
    low = send.shape[1]
    first = 0
    for item, (rows, wide) in enumerate(shapes):
        keep, got = refs[2 * item : 2 * item + 2]
        for part in range(rows // low):
            span = slice(part * low, (part + 1) * low)
            for high in range(2):
                for target, side in ((send, 1 - mine), (left, mine)):
                    value = keep[2 * high + side, span, :].astype(jnp.float32) + got[2 * high + side, span, :].astype(jnp.float32)
                    target[high, :, first : first + wide] = value.astype(target.dtype)
            first += wide


def merge(scalars, items, low):
    items = [(k.reshape(4, k.shape[-2] // 4, k.shape[-1]), g.reshape(4, g.shape[-2] // 4, g.shape[-1])) for k, g in items]
    shapes = [k.shape[1:] for k, _ in items]
    wide = sum(rows // low * n for rows, n in shapes)
    return whole_call(
        functools.partial(merge_body, shapes), "merge", scalars, [], [x for pair in items for x in pair],
        [array(jnp.bfloat16, 2, low, wide), array(jnp.float32, 2, low, wide)], [], [],
    )


def last_ff_body(scalars, keep, got, down_ref, up_ref):
    low = keep.shape[1]
    width = down_ref.shape[1]
    for part in range(down_ref.shape[0] // low):
        cols = slice(part * width, (part + 1) * width)
        down_ref[part * low : (part + 1) * low, :] = keep[0, :, cols] + got[0, :, cols].astype(jnp.float32)
    cols = slice(4 * width, 4 * width + up_ref.shape[1])
    up_ref[...] = keep[0, :, cols] + got[0, :, cols].astype(jnp.float32)


def last_ff(scalars, keep, got, width):
    low = keep.shape[1]
    return whole_call(
        last_ff_body, "last_ff", scalars, [], [keep, got], [array(jnp.float32, 4 * low, width), array(jnp.float32, low, 4 * width)], [], []
    )


def last_qkv_body(scalars, keep, got, more_keep, more_got, query_ref, key_ref, value_ref, out_ref, small_ref, late_ref, wide_ref, turned):
    low = keep.shape[1]
    width = query_ref.shape[1]
    half = width // 2

    def total(pair, first, size):
        return pair[0][0, :, first : first + size] + pair[1][0, :, first : first + size].astype(jnp.float32)

    one, two = (keep, got), (more_keep, more_got)
    for i, ref in enumerate((query_ref, key_ref, value_ref)):
        ref[:, :half] = total(one, i * half, half)
        ref[:, half:] = total(two, i * half, half)
    out_ref[...] = total(one, 3 * half + LANES, width)
    wide_ref[...] = total(one, 3 * half, LANES)[0:1, :]
    for ref, pair in ((small_ref, one), (late_ref, two)):
        turned[...] = jnp.zeros_like(turned)
        turned[:low, :] = total(pair, 3 * half, LANES)
        ref[...] = turned[...].T[: ref.shape[0], :]


def last_qkv(scalars, keep, got, more_keep, more_got, width):
    low = keep.shape[1]
    f32 = jnp.float32
    return whole_call(
        last_qkv_body, "last_qkv", scalars, [], [keep, got, more_keep, more_got],
        [array(f32, low, width)] * 4 + [array(f32, 24, LANES), array(f32, 8, LANES), array(f32, 1, LANES)], [], [pltpu.VMEM((LANES, LANES), f32)],
    )


def after(value, *others):
    return lax.optimization_barrier((value,) + others)[0]


def bit_count(size):
    return size.bit_length() - 1


def swap_dp(value, mask):
    return lax.ppermute(value, "dp", [(i, i ^ mask) for i in range(lax.axis_size("dp"))])


def swap_seq(value, mask):
    return lax.ppermute(value, "seq", [(i, i ^ mask) for i in range(lax.axis_size("seq"))])


def column_sum(matrix):
    return jnp.sum(matrix.astype(jnp.float32), axis=0)


def spread_pairs(first):
    dps, seqs = lax.axis_size("dp"), lax.axis_size("seq")
    pairs = []
    for dp in range(dps):
        for seq in range(seqs):
            piece = first ^ (seq & 1)
            to_dp = (dp & ~1) | (seq >> 1)
            to_seq = 2 * (dp & 1) + piece
            pairs.append((dp * seqs + seq, to_dp * seqs + to_seq))
    return pairs


def to_sequences(local, order):
    odd = (lax.axis_index("seq") & 1) == 1
    got = []
    pieces = [jnp.where(odd, local[1 - first], local[first]) for first in range(2)]
    order.mark(*pieces)
    for first, piece in enumerate(pieces):
        got.append(lax.ppermute(piece, AXES, spread_pairs(first)))
    return got, odd


def in_order(got, odd, rows):
    return jnp.where(odd, jnp.concatenate([g[:rows] for g in got[::-1]]), jnp.concatenate([g[:rows] for g in got]))


def from_sequences(tokens, order):
    odd = (lax.axis_index("seq") & 1) == 1
    half = tokens.shape[0] // 2
    got = []
    for first in range(2):
        near, far = tokens[first * half : (first + 1) * half], tokens[(1 - first) * half : (2 - first) * half]
        piece = order.mark(jnp.where(order.gate(odd), far, near))
        got.append(lax.ppermute(piece, AXES, [(b, a) for a, b in spread_pairs(first)]))
    return got


def both_sequences(order, got):
    odd = order.gate((lax.axis_index("seq") & 1) == 1)
    return jnp.where(odd, jnp.stack(got[::-1]), jnp.stack(got))


def weight_lines(weights, lines):
    width = weights[0].shape[-1]
    lines = [jnp.pad(v[..., None, :], [(0, 0)] * v.ndim + [(0, width - v.shape[-1])]) for v in lines]
    lines.append(jnp.zeros(lines[0].shape[:-2] + (16 - len(lines), width), jnp.bfloat16))
    return jnp.concatenate(weights + lines, axis=-2)


def near_shards(part, across=True):
    if lax.axis_size("dp") != PARTS:
        p = part if part.ndim == 3 else jnp.stack(jnp.split(lax.all_gather(part, "dp", axis=0, tiled=True), PARTS))
        return [p[i] for i in range(PARTS)]
    return [part, swap_dp(part, 2), swap_dp(part, 4)] + ([swap_dp(part, 6)] if across else [])


def both_cores(parts):
    return [shard for part in parts for shard in (part, swap_dp(part, 1))]


def all_shards(near, *ready):
    if len(near) == PARTS:
        return near
    return both_cores([near[0]] + list(lax.optimization_barrier((*near[1:], *ready))[:3]))


def relayed_shards(near, cut, *ready):
    if len(near) == PARTS:
        return near
    own, along_x, along_y = near
    along_x, along_y = lax.optimization_barrier((along_x, along_y, *ready))[:2]
    sent = along_x[:cut], along_y[cut:]
    top, bottom = swap_dp(sent[0], 4), swap_dp(sent[1], 2)
    own, along_x, along_y = lax.optimization_barrier((own, along_x, along_y, *sent))[:3]
    return both_cores([own, along_x, along_y, top, bottom])


def pack_body(count, scalars, *refs):
    weights, vectors, hidden, ids = refs[: min(3, count)], refs[3:count], refs[count], refs[count + 1]
    pieces = refs[count + 2 : count + 4]
    if vectors:
        part, lines = refs[count + 4 :]
        rows = weights[0].shape[0]
        for i, ref in enumerate(weights):
            part[i * rows : (i + 1) * rows, :] = ref[...]
        lines[...] = jnp.zeros_like(lines)
        for i, ref in enumerate(vectors):
            lines[i : i + 1, : ref.shape[1]] = ref[...].astype(jnp.float32)
        part[3 * rows :, :] = lines[...].astype(jnp.bfloat16)
    odd = scalars[7]
    block, half = hidden.shape[1], ids.shape[1] // 2
    for first, piece in enumerate(pieces):
        piece[:block, :] = hidden[first ^ odd]
        line = jnp.where(first ^ odd == 0, ids[0:1, :], ids[1:2, :]).astype(jnp.bfloat16)
        piece[block:, :] = jnp.zeros_like(piece[block:, :])
        piece[block : block + 1, :half] = line[:, :half]
        piece[block + 1 : block + 2, :half] = line[:, half:]


def pack(scalars, weights, vectors, hidden, ids):
    piece = array(jnp.bfloat16, hidden.shape[1] + 16, hidden.shape[2])
    if lax.axis_size("dp") == PARTS:
        rows, width = weights[0].shape
        given = weights + [v[None, :] for v in vectors]
        return whole_call(
            functools.partial(pack_body, len(given)), "pack", scalars, [], [Far(x) for x in given + [hidden, ids]],
            [piece, piece, array(jnp.bfloat16, 3 * rows + 16, width)], [], [pltpu.VMEM((16, width), jnp.float32)],
        )
    gather = lambda v: lax.all_gather(v, "dp", axis=0, tiled=True)
    split = lambda v: gather(v).reshape((PARTS, -1) + v.shape[1:])
    pieces = whole_call(functools.partial(pack_body, 0), "pack", scalars, [], [Far(hidden), Far(ids)], [piece, piece], [], [])
    return *pieces, weight_lines([split(w) for w in weights], [split(v) for v in vectors])


def project_body(sizes, scalars, *refs):
    rows, wide, vectors, qblock, chunk, lanes, shards = sizes
    pieces, hidden = parts_of(refs[:shards]), list(refs[shards : shards + 3])
    size = hidden[0].shape[0]
    hidden = hidden[:2] + [hidden[2].at[:size, :], hidden[2].at[size:, :]]
    (
        attended, lse, tokens, vec_ref, up_ref, segments, ordered, query_out, keys_out, values_out, keys_far_out, values_far_out, weights_out,
        query, keys, values, keys_far, values_far, far, held, small, turned, ids, sems, hidden_sems, out_sems, kall, vt, tiles,
    ) = refs[shards + 3 :]
    count, width = tokens.shape
    block = count // 2
    half = width // 2
    core, odd = scalars[6], scalars[7]
    copies, brought = [], []

    def start(copies, source, target, sem):
        copies.append(pltpu.make_async_copy(source, target, sem))
        copies[-1].start()

    for i, (ref, place) in enumerate(zip(hidden, (0, 1, 0, 1))):
        goal = tokens if i < 2 else far
        start(brought, ref.at[:block, :], goal.at[pl.ds(pl.multiple_of((place ^ odd) * block, block), block), :], hidden_sems.at[i])
    start(brought, hidden[0].at[block:, :], ids, hidden_sems.at[4])
    for part, first, ref in pieces:
        where = scalars[0] ^ part
        target = pl.ds(where * rows, rows)
        for weight in range(first // rows, (first + ref.shape[0]) // rows):
            for side in range(2):
                start(
                    copies,
                    ref.at[weight * rows - first : (weight + 1) * rows - first, side * half : (side + 1) * half],
                    held.at[side, target, weight * half : (weight + 1) * half],
                    sems.at[len(copies)],
                )
        if first + ref.shape[0] > 3 * rows:
            start(copies, ref.at[3 * rows - first :, :], small.at[where], sems.at[len(copies)])
    wait_all(brought)
    line = ids[...].astype(jnp.float32)
    for i in range(2):
        segments[:, i * count : (i + 1) * count] = jnp.where(core == i, line[0:1, :count], line[1:2, :count])
    flipped = tokens[...].T
    for i in range(PARTS):
        turned[i] = flipped[i * rows : (i + 1) * rows, :]
    turn_parts(scalars[1], turned, ordered)
    wait_all(copies)
    saves = []
    start(saves, held, weights_out, out_sems.at[0])
    vec_ref[...] = jnp.concatenate([small[i, :, :rows] for i in range(PARTS)], axis=1).astype(jnp.float32)
    up_ref[...] = jnp.concatenate([small[i, vectors : vectors + 1, :wide] for i in range(PARTS)], axis=1).astype(jnp.float32)
    for i, (weight, add, goal, source, out) in enumerate((
        (1, None, keys, tokens, keys_out), (1, None, keys_far, far, keys_far_out), (2, 1, values, tokens, values_out),
        (2, 1, values_far, far, values_far_out), (0, 0, query, tokens, query_out),
    )):
        for side in range(2):
            cols = slice(side * half, (side + 1) * half)
            product = nn(source[...], held[side, :, weight * half : (weight + 1) * half])
            if add is not None:
                product = product + vec_ref[add : add + 1, cols]
            goal[:, cols] = product.astype(jnp.bfloat16)
        start(saves, goal, out, out_sems.at[i + 1])
    forward_body(qblock, chunk, lanes, query, keys, values, keys_far, values_far, segments, attended, lse, kall, vt, tiles)
    wait_all(saves)


def project(scalars, pieces, hidden, rows, wide, vectors, qblock, chunk, lanes):
    block, width = hidden[0].shape[0] - 16, hidden[0].shape[1]
    count = 2 * block
    lines = 16
    n = 2 * count // chunk
    f32, b16 = jnp.float32, jnp.bfloat16
    whole = array(b16, count, width)
    vmem = lambda x: pltpu.VMEM(x.shape, x.dtype)
    return whole_call(
        functools.partial(project_body, (rows, wide, vectors, qblock, chunk, lanes, len(pieces))), "project", scalars, list(pieces) + list(hidden), [],
        [whole, array(f32, width // lanes, 8, count), whole, array(f32, lines, width), array(f32, 1, wide * PARTS), array(f32, 1, 2 * count),
         array(b16, 2, PARTS // 2, rows, count)],
        [whole] * 5 + [array(b16, 2, width, 3 * width // 2)],
        [vmem(whole)] * 6
        + [pltpu.VMEM((2, width, 3 * width // 2), b16), pltpu.VMEM((PARTS, lines, width), b16), pltpu.VMEM((PARTS, rows, count), b16),
           pltpu.VMEM((16, width), b16), pltpu.SemaphoreType.DMA((7 * PARTS,)),
           pltpu.SemaphoreType.DMA((5,)), pltpu.SemaphoreType.DMA((6,)), pltpu.VMEM((n, chunk, lanes), b16),
           pltpu.VMEM((n, lanes, chunk), b16), pltpu.VMEM((n, chunk, LANES), f32)],
        28,
    )


class Order:
    def __init__(self):
        self.last = ()

    def gate(self, value):
        return lax.optimization_barrier((value, *self.last))[0] if self.last else value

    def mark(self, *values):
        self.last = values
        return values[0] if len(values) == 1 else values


def all_rows(send, keep):
    return jnp.stack([keep, send], axis=1).reshape(-1, keep.shape[-1]).astype(jnp.float32)


def scatter_all(send, keep):
    return lax.psum_scatter(all_rows(send, keep), AXES, scatter_dimension=0, tiled=True)


def per_device(
    hidden_in, segment_ids, query_weight, query_bias, key_weight, value_weight, value_bias, out_weight, out_bias,
    first_gain, first_shift, up_weight, up_bias, down_weight, down_bias, second_gain, second_shift, cotangent,
):
    dps, seqs = lax.axis_size("dp"), lax.axis_size("seq")
    inner_width, width = up_weight.shape[1], query_weight.shape[1]
    devices = dps * seqs
    share = width // devices
    qblock = chunk = 256
    pairs = 3
    direct = dps == PARTS and seqs == 4
    dp, seq = lax.axis_index("dp"), lax.axis_index("seq")
    if direct:
        scalars = [dp, dp & 1, (dp >> 1) & 1, dp >> 2, seq & 1, seq >> 1, dp & 1, seq & 1]
    else:
        scalars = [0, 0, 0, 0, 0, 0, dp & 1, seq & 1]
    scalars = jnp.stack([jnp.asarray(v, jnp.int32) for v in scalars])

    vectors = [query_bias, value_bias, out_bias, first_gain, first_shift, down_bias, second_gain, second_shift]
    *hidden, part = pack(
        scalars, [query_weight, key_weight, value_weight], vectors + [up_bias], hidden_in, segment_ids
    )
    near = near_shards(part)
    hidden = [lax.ppermute(piece, AXES, spread_pairs(first)) for first, piece in enumerate(hidden)]
    out_up, down_part = lax.optimization_barrier(
        (jnp.concatenate([out_weight, up_weight], axis=1), down_weight, *near[1:4])
    )[:2]
    hidden.append(swap_dp(jnp.concatenate(hidden), 1))
    if direct:
        own_far, *arrived = lax.optimization_barrier((swap_dp(part, 1), *near[1:4]))
        shards = [part, own_far, *arrived, swap_dp(jnp.concatenate(arrived), 1)]
    else:
        shards = near
    out_up_near = near_shards(out_up)
    attended, lse, tokens, vec, up_add, segments, ordered, query, keys, values, keys_other, values_other, w_qkv = project(
        scalars, shards, hidden, width // PARTS, inner_width // PARTS, len(vectors), qblock, chunk, pairs * LANES
    )
    order = Order()
    down_near = near_shards(after(down_part, attended, *out_up_near[1:4]), False)
    got_up, odd = to_sequences(after(cotangent, attended), order)
    out_up_shards = all_shards(out_up_near, attended)
    normal_one, scale_one, first_low, active, slope, wo, wu = widen(scalars, out_up_shards, attended, tokens, vec, up_add)
    upstream = in_order(lax.optimization_barrier((*got_up, active))[:2], odd, hidden_in.shape[1])
    layer_low, sum_two_grad, second_grad, sums_two, down_send, down_keep, wd = narrow(
        scalars, relayed_shards(down_near, inner_width // PARTS // 2, active), active, normal_one, vec, upstream
    )
    swap = (lambda value: swap_dp(value, 1)) if direct else (lambda value: value)
    order = Order()
    order.mark(second_grad)
    down_got = swap(down_send)
    out_pieces = from_sequences(layer_low, order)
    inner_grad, up_sum, up_send, up_keep = inner_back(scalars, order.gate(second_grad), wd, slope, first_low)
    up_got = swap(up_send)
    order.mark(inner_grad)
    if direct:
        ((send, down_keep),) = fold(order.gate(scalars), [(down_keep, down_got, (2, 1, 2))])
        down_got = swap_dp(order.mark(send), 2)
    sum_one_grad, attended_grad, sums_one, out_send, out_keep = outer_back(
        order.gate(scalars), inner_grad, wu, sum_two_grad, normal_one, scale_one, vec, wo, attended
    )
    order.mark(attended_grad)
    if direct:
        ((send, up_keep),) = fold(order.gate(scalars), [(up_keep, up_got, (1, 2, 3))])
        up_got = swap_dp(order.mark(send), 4)
    out_got = swap(out_send)

    def attend(side):
        given = (query, keys, values, keys_other, values_other, attended, attended_grad, lse, segments)
        return order.mark(*attend_back(order.gate(scalars), *given, qblock, chunk, pairs, side))

    dq, dk, dv, *far = attend(0)
    if direct:
        (send, down_keep), (third, out_keep) = fold(
            order.gate(scalars), [(down_keep, down_got, (1, 1, 3)), (out_keep, out_got, (1, 2, 3))]
        )
        order.mark(send, third)
        down_got, out_got = swap_dp(send, 4), swap_dp(third, 4)
    layer_out = order.mark(both_sequences(order, out_pieces))
    one_low, one_high, one_keep, gradient, sums_first = qkv_back(
        0, order.gate(scalars), dq, dk, dv, *[swap_dp(x, 1) for x in order.gate(far)], ordered, w_qkv, sum_one_grad,
        sums_one, sums_two, up_sum
    )
    order.mark(gradient)
    one_got = (swap(one_low), swap(one_high))
    if direct:
        ((send, up_keep),) = fold(order.gate(scalars), [(up_keep, up_got, (1, 1, 2))])
        up_got = swap_dp(order.mark(send), 2)
    dq, dk, dv, *far = attend(1)
    if direct:
        send, ff_keep = merge(order.gate(scalars), [(down_keep, down_got), (up_keep, up_got)], share)
        ff_got = swap_seq(order.mark(send), 1)
        (send, one_keep), (other, out_keep) = fold(
            order.gate(scalars), [(one_keep, one_got, (2, 1, 2)), (out_keep, out_got, (1, 1, 2))]
        )
        order.mark(send, other)
        one_got, out_got = swap_dp(send, 2), swap_dp(other, 2)
    two_low, two_high, two_keep, gradient, _ = qkv_back(
        1, order.gate(scalars), dq, dk, dv, *[swap_dp(x, 1) for x in order.gate(far)], ordered, w_qkv, gradient, sums_first
    )
    order.mark(gradient)
    two_got = (swap(two_low), swap(two_high))
    in_pieces = from_sequences(gradient, order)
    if not direct:
        down_grad, up_grad = scatter_all(down_send, down_keep), scatter_all(up_send, up_keep)
        one, two = scatter_all(jnp.concatenate([one_low, one_high]), one_keep), scatter_all(jnp.concatenate([two_low, two_high]), two_keep)
        cut = width // 2
        query_grad, key_grad, value_grad = [
            jnp.concatenate([side[:, i * cut : (i + 1) * cut] for side in (one, two)], axis=1) for i in range(3)
        ]
        out_grad = scatter_all(out_send, out_keep)
        small, late = one[:, 3 * cut :].T, two[:, 3 * cut :].T
        up_bias_grad = lax.psum_scatter(up_sum[0], AXES, scatter_dimension=0, tiled=True)
    else:
        ((send, one_keep),) = fold(order.gate(scalars), [(one_keep, one_got, (1, 1, 3))])
        one_got = swap_dp(order.mark(send), 4)
        ((send, ff_keep),) = fold(order.gate(scalars), [(ff_keep, ff_got, (1, 1, 5))])
        ff_got = swap_seq(order.mark(send), 2)
        ((sent, two_keep),) = fold(order.gate(scalars), [(two_keep, two_got, (2, 1, 2, True))])
        two_got = tuple(swap_dp(x, 2) for x in order.mark(*sent))
        send, keep = merge(order.gate(scalars), [(one_keep, one_got), (out_keep, out_got)], share)
        got = swap_seq(order.mark(send), 1)
        ((send, two_keep),) = fold(order.gate(scalars), [(two_keep, two_got, (1, 1, 3))])
        two_got = swap_dp(order.mark(send), 4)
    input_grad = order.mark(both_sequences(order, in_pieces).astype(jnp.float32))
    if direct:
        ((send, keep),) = fold(order.gate(scalars), [(keep, got, (1, 1, 5))])
        got = swap_seq(order.mark(send), 2)
        send, two_keep = merge(order.gate(scalars), [(two_keep, two_got)], share)
        two_got = swap_seq(order.mark(send), 1)
        ((send, two_keep),) = fold(order.gate(scalars), [(two_keep, two_got, (1, 1, 5))])
        two_got = swap_seq(order.mark(send), 2)
        down_grad, up_grad = order.mark(*last_ff(order.gate(scalars), ff_keep, ff_got, width))
        query_grad, key_grad, value_grad, out_grad, small, late, line = last_qkv(
            order.gate(scalars), keep, got, two_keep, two_got, width
        )
        up_bias_grad = line[0, LANES - inner_width // devices :]
    ob, g1, s1 = [small[i, :share] for i in (0, 1, 2)]
    db, g2, s2 = [small[i, :share] for i in (8, 9, 10)]
    qb, vb = [late[i, :share] for i in (0, 1)]
    return (
        layer_out, input_grad, query_grad, qb, key_grad, value_grad, vb, out_grad, ob, g1, s1, up_grad, up_bias_grad, down_grad, db, g2, s2,
    )


def solution(mesh):
    wide, flat = P("dp", None), P("dp")
    in_specs = (
        P("dp", "seq", None), wide, wide, flat, wide, wide, flat, wide, flat, flat, flat, wide, flat, wide, flat,
        flat, flat, P("dp", "seq", None),
    )
    rows, cells = P(AXES, None), P(AXES)
    out_specs = (
        P("dp", "seq", None), P("dp", "seq", None), rows, cells, rows, rows, cells, rows, cells, cells, cells, rows,
        cells, rows, cells, cells, cells,
    )
    return jax.shard_map(per_device, mesh=mesh, in_specs=in_specs, out_specs=out_specs, check_vma=False)
```

```python
import functools
import math

import jax
import jax.numpy as jnp
from jax import lax
from jax.experimental import pallas as pl
from jax.experimental.pallas import tpu as pltpu
from jax.sharding import PartitionSpec as P

HEAD_DIM = 64
LANES = 128
NEGATIVE = -1e30


def nt(left, right):
    return lax.dot_general(left, right, (((1,), (1,)), ((), ())), preferred_element_type=jnp.float32)


def nn(left, right):
    return lax.dot_general(left, right, (((1,), (0,)), ((), ())), preferred_element_type=jnp.float32)


def head_parts(block):
    lane = lax.broadcasted_iota(jnp.int32, block.shape, 1)
    zero = jnp.zeros_like(block)
    return (jnp.where(lane < HEAD_DIM, block, zero), jnp.where(lane < HEAD_DIM, zero, block))


def same_document(column_tile, row):
    column = jnp.concatenate([column_tile] * (row.shape[1] // LANES), axis=1)
    return column == jnp.broadcast_to(row, column.shape)


def pair_lanes(pair):
    return slice(pair * LANES, (pair + 1) * LANES)


def segment_tables(segments, tiles, half, qblock, chunk):
    ids = segments[...]
    for j in range(tiles.shape[0]):
        for i in range(chunk // LANES):
            start = j * chunk + i * LANES
            tiles[j, i * LANES : (i + 1) * LANES, :] = jnp.broadcast_to(ids[:, start : start + LANES], (LANES, LANES)).T
    chunks = half // chunk
    low = [jnp.min(ids[:, j * chunk : (j + 1) * chunk]) for j in range(2 * chunks)]
    high = [jnp.max(ids[:, j * chunk : (j + 1) * chunk]) for j in range(2 * chunks)]
    found = []
    for b in range(half // qblock):
        mine = slice(b * qblock, (b + 1) * qblock)
        first, last = jnp.min(ids[:, mine]), jnp.max(ids[:, mine])
        bounds = []
        for side in range(2):
            before = sum((high[side * chunks + j] < first).astype(jnp.int32) for j in range(chunks))
            behind = sum((low[side * chunks + j] > last).astype(jnp.int32) for j in range(chunks))
            bounds += [before, chunks - behind]
        found.append((bounds[0], bounds[1] - bounds[0], bounds[2], bounds[1] - bounds[0] + bounds[3] - bounds[2]))
    return found


def chunk_of(bounds, step, chunks):
    first, own, other, _ = bounds
    return jnp.where(step < own, first + step, chunks + other + step - own)


def forward_body(qblock, chunk, lanes, q_all, k_all, v_all, ko_all, vo_all, segments, o_all, lse_all, kall, vt, sk_ref):
    half = k_all.shape[0]
    tables = segment_tables(segments, sk_ref, half, qblock, chunk)
    chunks, pairs = half // chunk, lanes // LANES

    @pl.loop(0, q_all.shape[1] // lanes)
    def _(group):
        cols = step_of(group, lanes)
        q_ref, k_ref, v_ref, ko_ref, vo_ref, o_ref = (r.at[:, cols] for r in (q_all, k_all, v_all, ko_all, vo_all, o_all))
        lse_ref = lse_all.at[pl.ds(group, 1)]
        for j in range(chunks):
            rows = slice(j * chunk, (j + 1) * chunk)
            kall[j] = k_ref[rows, :]
            kall[chunks + j] = ko_ref[rows, :]
            vt[j] = v_ref[rows, :].T
            vt[chunks + j] = vo_ref[rows, :].T
        for b in range(q_ref.shape[0] // qblock):
            span = slice(b * qblock, (b + 1) * qblock)
            parts = []
            for pair in range(pairs):
                parts += head_parts(q_ref[span, pair_lanes(pair)] * jnp.bfloat16(HEAD_DIM**-0.5))
            row = segments[:, span]

            def one(step, carry):
                j = chunk_of(tables[b], step, chunks)
                mask = same_document(sk_ref[j], row)
                scores = [jnp.where(mask, nt(kall[j, :, pair_lanes(h // 2)], part), NEGATIVE) for h, part in enumerate(parts)]
                out = []
                for h, score in enumerate(scores):
                    top, total, acc = carry[h]
                    new_top = jnp.maximum(top, jnp.max(score, axis=0, keepdims=True))
                    expo = jnp.exp(score - new_top)
                    scale = jnp.exp(top - new_top)
                    total = total * scale + jnp.sum(expo, axis=0, keepdims=True)
                    acc = acc * scale + nn(vt[j, h * HEAD_DIM : (h + 1) * HEAD_DIM, :], expo.astype(jnp.bfloat16))
                    out.append((new_top, total, acc))
                return tuple(out)

            init = (
                jnp.full((1, qblock), NEGATIVE, jnp.float32),
                jnp.zeros((1, qblock), jnp.float32),
                jnp.zeros((HEAD_DIM, qblock), jnp.float32),
            )
            carry = lax.fori_loop(0, tables[b][3], one, (init,) * len(parts))
            result = jnp.concatenate([acc / total for _, total, acc in carry], axis=0)
            o_ref[span, :] = result.T.astype(jnp.bfloat16)
            for h, (top, total, _) in enumerate(carry):
                lse_ref[0, h : h + 1, span] = top + jnp.log(total)


def backward_body(
    qblock, chunk, lanes, side, copies, scalars, q_ref, k_ref, v_ref, ko_ref, vo_ref, o_ref, do_ref, lse_all, segments,
    dq_ref, dk_ref, dv_ref, far_keys, far_values, kall, vall, kt, dkall, dvall, sk_ref,
):
    half = k_ref.shape[0]
    tables = segment_tables(segments, sk_ref, half, qblock, chunk)
    lse_ref = lse_all.at[side : side + 1]
    chunks, pairs = half // chunk, lanes // LANES
    dkall[...] = jnp.zeros_like(dkall)
    dvall[...] = jnp.zeros_like(dvall)
    for first, keys, values in ((0, k_ref, v_ref), (chunks, ko_ref, vo_ref)):
        wait_all(copies[1:3] if first == 0 else copies[3:5])
        for j in range(chunks):
            rows = slice(j * chunk, (j + 1) * chunk)
            kall[first + j] = keys[rows, :]
            vall[first + j] = values[rows, :]
            kt[first + j] = keys[rows, :].T
    wait_all(copies[:1] + copies[5:])
    for b in range(q_ref.shape[0] // qblock):
        span = slice(b * qblock, (b + 1) * qblock)
        parts, dparts, delta = [], [], []
        for pair in range(pairs):
            parts.append(head_parts(q_ref[span, pair_lanes(pair)] * jnp.bfloat16(HEAD_DIM**-0.5)))
            dparts.append(head_parts(do_ref[span, pair_lanes(pair)]))
            product = do_ref[span, pair_lanes(pair)].astype(jnp.float32) * o_ref[span, pair_lanes(pair)].astype(jnp.float32)
            product = product.T
            delta += [jnp.sum(product[h * HEAD_DIM : (h + 1) * HEAD_DIM], axis=0, keepdims=True) for h in range(2)]
        both = [jnp.concatenate(p, axis=0) for p in parts]
        dboth = [jnp.concatenate(p, axis=0) for p in dparts]
        row = segments[:, span]
        lse = [lse_ref[0, h : h + 1, span] for h in range(2 * pairs)]

        def one(step, carry):
            j = chunk_of(tables[b], step, chunks)
            mask = same_document(sk_ref[j], row)
            out = []
            both_mask = jnp.concatenate([mask, mask], axis=1)
            scores = [nt(kall[j, :, pair_lanes(pair)], both[pair]) for pair in range(pairs)]
            products = [nt(vall[j, :, pair_lanes(pair)], dboth[pair]) for pair in range(pairs)]
            adds = []
            for pair in range(pairs):
                score = jnp.where(both_mask, scores[pair], NEGATIVE)
                prob = jnp.exp(score - jnp.concatenate(lse[2 * pair : 2 * pair + 2], axis=1))
                grad = (prob * (products[pair] - jnp.concatenate(delta[2 * pair : 2 * pair + 2], axis=1))).astype(jnp.bfloat16)
                for side in range(2):
                    h = 2 * pair + side
                    out.append(carry[h] + nn(kt[j, h * HEAD_DIM : (h + 1) * HEAD_DIM, :], grad[:, side * qblock : (side + 1) * qblock]))
                adds.append((nn(prob.astype(jnp.bfloat16), dboth[pair]), nn(grad, both[pair])))
            for pair in range(pairs):
                dvall[j, :, pair_lanes(pair)] += adds[pair][0]
                dkall[j, :, pair_lanes(pair)] += adds[pair][1]
            return tuple(out)

        zero = jnp.zeros((HEAD_DIM, qblock), jnp.float32)
        carry = lax.fori_loop(0, tables[b][3], one, (zero,) * (2 * pairs))
        dq_ref[span, :] = (jnp.concatenate(carry, axis=0).T * HEAD_DIM**-0.5).astype(jnp.bfloat16)
    for j in range(chunks):
        rows = slice(j * chunk, (j + 1) * chunk)
        dk_ref[rows, :] = dkall[j]
        dv_ref[rows, :] = dvall[j]
        far_keys[rows, :] = dkall[chunks + j].astype(jnp.bfloat16)
        far_values[rows, :] = dvall[chunks + j].astype(jnp.bfloat16)


def attend_back(scalars, query, keys, values, keys_other, values_other, attended, grad, lse_rows, segments, qblock, chunk, pairs, side):
    tokens, width = query.shape
    half = keys.shape[0]
    lanes = pairs * LANES
    n = 2 * half // chunk
    f32, b16 = jnp.float32, jnp.bfloat16
    cols = slice(side * lanes, (side + 1) * lanes)
    far = [Far(x, cols) for x in (query, keys, values, keys_other, values_other, attended, grad)]
    return whole_call(
        functools.partial(backward_body, qblock, chunk, lanes, side), "attend_back", scalars, [], far + [lse_rows, segments],
        [array(b16, tokens, lanes), array(f32, half, lanes), array(f32, half, lanes), array(b16, half, lanes), array(b16, half, lanes)], [],
        [pltpu.VMEM((n, chunk, lanes), b16), pltpu.VMEM((n, chunk, lanes), b16), pltpu.VMEM((n, lanes, chunk), b16),
         pltpu.VMEM((n, chunk, lanes), f32), pltpu.VMEM((n, chunk, lanes), f32), pltpu.VMEM((n, chunk, LANES), f32)], 24, True,
    )


AXES = ("dp", "seq")
PARTS = 8
epsilon = 1e-12


def tn(left, right):
    return lax.dot_general(left, right, (((0,), (0,)), ((), ())), preferred_element_type=jnp.float32)


def norm_parts(value):
    center = value - jnp.mean(value, axis=-1, keepdims=True)
    spread = jnp.mean(center * center, axis=-1, keepdims=True)
    scale = lax.rsqrt(spread + epsilon)
    return (center * scale, scale)


def norm_back(upstream, normal, scale, gain):
    scaled = upstream * gain
    return scale * (
        scaled
        - jnp.mean(scaled, axis=-1, keepdims=True)
        - normal * jnp.mean(scaled * normal, axis=-1, keepdims=True)
    )


def row_sum(matrix):
    return jnp.sum(matrix.astype(jnp.float32), axis=0, keepdims=True)


def parts_of(refs):
    if len(refs) == PARTS:
        return [(i, 0, ref) for i, ref in enumerate(refs)]
    if len(refs) == 6:
        own, own_far, near_x, near_y, near_d, far = refs
        rows = own.shape[0]
        other = [far.at[i * rows : (i + 1) * rows, :] for i in range(3)]
        return [(i, 0, ref) for i, ref in enumerate((own, own_far, near_x, other[0], near_y, other[1], near_d, other[2]))]
    pieces = [(i, 0, ref) for i, ref in enumerate(refs[:6])]
    for i in range(2):
        top, bottom = refs[6 + i], refs[8 + i]
        pieces += [(6 + i, 0, top), (6 + i, top.shape[0], bottom)]
    return pieces


def load_pieces(me, pieces, rows, targets, sems):
    copies = [[] for _ in targets]
    for place, (part, first, ref) in enumerate(pieces):
        size = ref.shape[0]
        where = pl.ds(pl.multiple_of((me ^ part) * rows + first, 32), size)
        for i, (target, columns) in enumerate(targets):
            copy = pltpu.make_async_copy(ref.at[:, columns], target.at[where, :], sems.at[i, place])
            copy.start()
            copies[i].append(copy)
    return copies


def wait_all(copies):
    for copy in copies:
        copy.wait()


def step_of(block, size):
    return pl.ds(pl.multiple_of(block * size, size), size)


BLOCK = 1024
GELU_BLOCK = 256
ROWS = 256


def widen_body(scalars, *refs):
    shards = len(refs) - 12
    pieces = parts_of(refs[:shards])
    (attended, tokens, vec, up_add, normal_ref, scale_ref, low_ref, active_ref, slope_ref, wo, wu, sems) = refs[shards:]
    width, wide = wu.shape
    loads = load_pieces(scalars[0], pieces, width // PARTS, [(wo, slice(0, width)), (wu, slice(width, width + wide))], sems)
    wait_all(loads[0])

    @pl.loop(0, tokens.shape[0] // ROWS)
    def _(i):
        rows = step_of(i, ROWS)
        branch = nn(attended[rows, :], wo[...]) + vec[2:3, :]
        normal, scale = norm_parts(tokens[rows, :].astype(jnp.float32) + branch)
        first = normal * vec[3:4, :] + vec[4:5, :]
        normal_ref[rows, :] = normal
        scale_ref[rows, :] = jnp.broadcast_to(scale, (ROWS, LANES))
        low_ref[rows, :] = first.astype(jnp.bfloat16)

    wait_all(loads[1])

    @pl.loop(0, wide // GELU_BLOCK)
    def _(j):
        cols = step_of(j, GELU_BLOCK)
        inner = nn(low_ref[...], wu[:, cols]) + up_add[:, cols]
        cumulative = 0.5 * (1.0 + lax.erf(inner * math.sqrt(0.5)))
        density = jnp.exp(-0.5 * inner * inner) * (1.0 / math.sqrt(2.0 * math.pi))
        active_ref[:, cols] = (inner * cumulative).astype(jnp.bfloat16)
        slope_ref[:, cols] = (cumulative + inner * density).astype(jnp.bfloat16)


def narrow_body(scalars, *refs):
    shards = len(refs) - 13
    pieces = parts_of(refs[:shards])
    (active, normal_one, vec, upstream, out_ref, grad_ref, low_ref, sums_ref, send_ref, keep_ref, wd, sums, sems) = refs[shards:]
    wide, width = wd.shape
    (loads,) = load_pieces(scalars[0], pieces, wide // PARTS, [(wd, slice(0, width))], sems)
    wait_all(loads)
    sums[...] = jnp.zeros_like(sums)

    @pl.loop(0, normal_one.shape[0] // ROWS)
    def _(i):
        rows = step_of(i, ROWS)
        second = nn(active[rows, :], wd[...]) + vec[5:6, :]
        normal, scale = norm_parts(normal_one[rows, :] * vec[3:4, :] + vec[4:5, :] + second)
        out_ref[rows, :] = (normal * vec[6:7, :] + vec[7:8, :]).astype(jnp.bfloat16)
        up = upstream[rows, :].astype(jnp.float32)
        grad = norm_back(up, normal, scale, vec[6:7, :])
        low = grad.astype(jnp.bfloat16)
        grad_ref[rows, :] = grad
        low_ref[rows, :] = low
        sums[0:1, :] += row_sum(low)
        sums[1:2, :] += row_sum(up * normal)
        sums[2:3, :] += row_sum(up)

    sums_ref[...] = sums[...]
    size = wide // PARTS

    @pl.loop(0, PARTS // 2)
    def _(i):
        send_ref[i] = tn(active[:, step_of(2 * i + 1 - scalars[1], size)], low_ref[...]).astype(jnp.bfloat16)
        keep_ref[i] = tn(active[:, step_of(2 * i + scalars[1], size)], low_ref[...]).astype(jnp.bfloat16)


def turn_parts(core, turned, ordered):
    for i in range(PARTS // 2):
        ordered[0, i] = turned[2 * i + 1 - core]
        ordered[1, i] = turned[2 * i + core]


def inner_back_body(scalars, low, wd, slope, first_low, grad_ref, sums_ref, send_ref, keep_ref, turned, ordered):
    size = first_low.shape[1] // PARTS
    flipped = first_low[...].T
    for i in range(PARTS):
        turned[i] = flipped[i * size : (i + 1) * size, :]
    turn_parts(scalars[1], turned, ordered)
    rows = (PARTS // 2) * size

    @pl.loop(0, slope.shape[1] // BLOCK)
    def _(j):
        cols = step_of(j, BLOCK)
        grad = (nt(low[...], wd[cols, :]) * slope[:, cols].astype(jnp.float32)).astype(jnp.bfloat16)
        grad_ref[:, cols] = grad
        sums_ref[:, cols] = row_sum(grad)
        for side, ref in enumerate((send_ref, keep_ref)):
            left = ordered[side].reshape(rows, low.shape[0])
            ref[:, :, cols] = nn(left, grad).astype(jnp.bfloat16).reshape(PARTS // 2, size, BLOCK)


def outer_back_body(scalars, grad, wu, up_grad, normal_ref, scale_ref, vec, wo, attended, sum_ref, result_ref, sums_ref, send_ref, keep_ref, low, sums, turned):
    width = wo.shape[0]
    sums[...] = jnp.zeros_like(sums)

    @pl.loop(0, grad.shape[0] // ROWS)
    def _(i):
        rows = step_of(i, ROWS)
        first = up_grad[rows, :] + nt(grad[rows, :], wu[...])
        normal = normal_ref[rows, :]
        total = norm_back(first, normal, scale_ref[rows, 0:1], vec[3:4, :])
        branch = total.astype(jnp.bfloat16)
        sum_ref[rows, :] = total
        low[rows, :] = branch
        result_ref[rows, :] = nt(branch, wo[...]).astype(jnp.bfloat16)
        sums[0:1, :] += row_sum(branch)
        sums[1:2, :] += row_sum(first * normal)
        sums[2:3, :] += row_sum(first)

    sums_ref[...] = sums[...]
    size = width // PARTS
    product = tn(attended[...], low[...]).astype(jnp.bfloat16)
    for i in range(PARTS):
        turned[i] = product[i * size : (i + 1) * size, :]
    for i in range(PARTS // 2):
        send_ref[i] = turned[2 * i + 1 - scalars[1]]
        keep_ref[i] = turned[2 * i + scalars[1]]


class Far:
    def __init__(self, value, columns=None, index=None):
        self.value, self.columns, self.index = value, columns, index
        shape = value.shape if index is None else value.shape[1:]
        width = shape[-1] if columns is None else columns.stop - columns.start
        self.shape, self.dtype = shape[:-1] + (width,), value.dtype


def far_body(body, far, counts, scalars, *refs):
    hbm, inputs, outputs, held, lazy = counts
    given = list(refs[hbm : hbm + inputs])
    held_refs, sems = refs[len(refs) - held - 1 : -1], refs[-1]
    copies = []
    for i, (place, columns, index) in enumerate(far):
        source = given[place]
        if index is not None:
            source = source.at[index]
        if columns is not None:
            source = source.at[:, columns]
        copies.append(pltpu.make_async_copy(source, held_refs[i], sems.at[i]))
        copies[-1].start()
        given[place] = held_refs[i]
    rest = (*refs[:hbm], *given, *refs[hbm + inputs : len(refs) - held - 1])
    if lazy:
        body(copies, scalars, *rest)
    else:
        wait_all(copies)
        body(scalars, *rest)


def in_hbm(value):
    return pltpu.with_memory_space_constraint(value, pltpu.HBM)


def whole_call(body, name, scalars, hbm, inputs, outputs, hbm_outputs, scratch, room=8, lazy=False):
    shape_of = lambda x: jax.ShapeDtypeStruct(x.shape, x.dtype)
    near, stay = pl.BlockSpec(memory_space=pltpu.VMEM), pl.BlockSpec(memory_space=pltpu.HBM)
    far = [(i, x.columns, x.index) for i, x in enumerate(inputs) if isinstance(x, Far)]
    scratch = list(scratch)
    if far:
        held = [pltpu.VMEM(inputs[i].shape, inputs[i].dtype) for i, *_ in far]
        counts = (len(hbm), len(inputs), len(outputs) + len(hbm_outputs), len(far), lazy)
        body = functools.partial(far_body, body, far, counts)
        scratch += held + [pltpu.SemaphoreType.DMA((len(far),))]
        room += sum(math.prod(inputs[i].shape) * inputs[i].dtype.itemsize for i, *_ in far) // (1 << 20) + 1
    return pl.pallas_call(
        body,
        in_specs=[pl.BlockSpec(memory_space=pltpu.SMEM)]
        + [stay] * len(hbm)
        + [stay if isinstance(x, Far) else near for x in inputs],
        out_specs=[near] * len(outputs) + [stay] * len(hbm_outputs),
        scratch_shapes=scratch,
        out_shape=[shape_of(x) for x in outputs] + [pltpu.HBM(x.shape, x.dtype) for x in hbm_outputs],
        cost_estimate=pl.CostEstimate(flops=1, transcendentals=0, bytes_accessed=1),
        compiler_params=pltpu.CompilerParams(vmem_limit_bytes=room << 20),
        name=name,
    )(scalars, *[in_hbm(x) for x in hbm], *[in_hbm(x.value) if isinstance(x, Far) else x for x in inputs])


def array(dtype, *shape):
    return jax.ShapeDtypeStruct(shape, dtype)


def widen(scalars, pieces, attended, tokens, vec, up_add):
    count, width = tokens.shape
    wide = up_add.shape[1]
    f32, b16 = jnp.float32, jnp.bfloat16
    return whole_call(
        widen_body, "widen", scalars, pieces, [attended, tokens, vec, up_add],
        [array(f32, count, width), array(f32, count, LANES), array(b16, count, width),
         array(b16, count, wide), array(b16, count, wide), array(b16, width, width), array(b16, width, wide)],
        [], [pltpu.SemaphoreType.DMA((2, len(pieces)))],
    )


def narrow(scalars, pieces, active, normal, vec, upstream):
    count, wide = active.shape
    width = normal.shape[1]
    f32, b16 = jnp.float32, jnp.bfloat16
    half = array(b16, PARTS // 2, wide // PARTS, width)
    return whole_call(
        narrow_body, "narrow", scalars, pieces, [active, normal, vec, upstream],
        [array(b16, count, width), array(f32, count, width), array(b16, count, width), array(f32, 8, width), half, half, array(b16, wide, width)],
        [], [pltpu.VMEM((8, width), f32), pltpu.SemaphoreType.DMA((1, len(pieces)))],
    )


def inner_back(scalars, low, wd, slope, first_low):
    count, wide = slope.shape
    width = low.shape[1]
    size = width // PARTS
    f32, b16 = jnp.float32, jnp.bfloat16
    half = array(b16, PARTS // 2, size, wide)
    return whole_call(
        inner_back_body, "inner_back", scalars, [], [low, wd, slope, first_low],
        [array(b16, count, wide), array(f32, 1, wide), half, half], [],
        [pltpu.VMEM((PARTS, size, count), b16), pltpu.VMEM((2, PARTS // 2, size, count), b16)],
    )


def outer_back(scalars, grad, wu, up_grad, normal, scale, vec, wo, attended):
    count, width = normal.shape
    f32, b16 = jnp.float32, jnp.bfloat16
    half = array(b16, PARTS // 2, width // PARTS, width)
    return whole_call(
        outer_back_body, "outer_back", scalars, [], [grad, wu, up_grad, normal, scale, vec, wo, attended],
        [array(f32, count, width), array(b16, count, width), array(f32, 8, width), half, half], [],
        [pltpu.VMEM((count, width), b16), pltpu.VMEM((8, width), f32), pltpu.VMEM((PARTS, width // PARTS, width), b16)],
    )


def sums_to_slots(core, lines, parts, send, keep, first, wide=None):
    turned = lines[...].T
    rows = turned.shape[0] // PARTS
    for i in range(PARTS):
        parts[i] = turned[i * rows : (i + 1) * rows, :]
    if wide is not None:
        size = wide.shape[1] // (4 * PARTS)
        for i in range(4 * PARTS):
            place = (i % 4) * (rows // 4)
            parts[i // 4, place : place + 1, LANES - size :] = wide[:, i * size : (i + 1) * size]
    for i in range(PARTS // 2):
        send[i, :, first : first + LANES] = parts[2 * i + 1 - core].astype(jnp.bfloat16)
        keep[i, :, first : first + LANES] = parts[2 * i + core].astype(jnp.bfloat16)


def qkv_back_body(side, copies, scalars, dq, dk, dv, far_keys, far_values, ordered, weight, gradient, *refs):
    core = scalars[1]
    if side == 0:
        sums_one, sums_two, wide_sums, send_low, send_high, keep, result, sums_ref, both, lines, parts, send = refs
    else:
        first_sums, send_low, send_high, keep, result, sums_ref, both, lines, parts, send = refs
    half = dq.shape[1]
    both[:, :half] = dq[...]
    both[:, half : 2 * half] = (dk[...] + far_keys[...].astype(jnp.float32)).astype(jnp.bfloat16)
    both[:, 2 * half :] = (dv[...] + far_values[...].astype(jnp.float32)).astype(jnp.bfloat16)
    sums_ref[...] = jnp.zeros_like(sums_ref)
    sums_ref[0:1, :] = row_sum(dq[...])
    sums_ref[1:2, :] = row_sum(both[:, 2 * half :])
    rows = ordered.shape[1] * ordered.shape[2]
    copies[0].wait()
    for i, ref in enumerate((send, keep)):
        left = ordered[i].reshape(rows, ordered.shape[3])
        product = nn(left, both[...]).astype(jnp.bfloat16)
        ref[:, :, : 3 * half] = product.reshape(ordered.shape[1], ordered.shape[2], 3 * half)
    lines[...] = jnp.zeros_like(lines)
    if side == 0:
        lines[0:8, :] = sums_one[...]
        lines[8:16, :] = sums_two[...]
        sums_to_slots(core, lines, parts, send, keep, 3 * half, wide_sums)
    else:
        lines[0:8, :half] = first_sums[...]
        lines[0:8, half:] = sums_ref[...]
        sums_to_slots(core, lines, parts, send, keep, 3 * half)
    send_low[...] = send[:2]
    send_high[...] = send[2:]
    copies[1].wait()
    result[...] = (gradient[...] + nt(both[...], weight[...])).astype(result.dtype)


def qkv_back(side, scalars, dq, dk, dv, far_keys, far_values, ordered, weights, gradient, *more):
    count, half = dq.shape
    width = gradient.shape[1]
    f32, b16 = jnp.float32, jnp.bfloat16
    total = array(b16, PARTS // 2, width // PARTS, 3 * half + LANES)
    part = array(b16, PARTS // 4, width // PARTS, 3 * half + LANES)
    return whole_call(
        functools.partial(qkv_back_body, side), "qkv_back", scalars, [], [dq, dk, dv, far_keys, far_values, Far(ordered), Far(weights, None, side), gradient, *more],
        [part, part, total, array(b16 if side else f32, count, width), array(f32, 8, half)], [],
        [pltpu.VMEM((count, 3 * half), b16), pltpu.VMEM((LANES, width), f32), pltpu.VMEM((PARTS, width // PARTS, LANES), f32),
         pltpu.VMEM(total.shape, b16)],
        8, True,
    )


STRIPE = 32


def fold_body(plans, scalars, *refs):
    places, outs = [0], [0]
    for *_, count, sends in plans:
        places.append(places[-1] + 1 + count)
        outs.append(outs[-1] + 1 + sends)
    for item, (outer, inner, bit, count, sends) in enumerate(plans):
        keep, *gots = refs[places[item] : places[item + 1]]
        *sent, left = refs[places[-1] + outs[item] : places[-1] + outs[item + 1]]
        mine = scalars[bit]
        rows = keep.shape[1]
        stripe = STRIPE if rows % STRIPE == 0 else rows

        @pl.loop(0, rows // stripe)
        def _(k):
            span = step_of(k, stripe) if stripe != rows else slice(None)
            for i in range(outer):
                for j in range(inner):
                    for away, side in ((True, 1 - mine), (False, mine)):
                        place = (2 * i + side) * inner + j
                        if count == 1:
                            got = gots[0][place, span, :]
                        elif outer == 1:
                            got = jnp.where(side == 0, gots[0][j, span, :], gots[1][j, span, :])
                        else:
                            got = gots[i][side * inner + j, span, :]
                        value = keep[place, span, :].astype(jnp.float32) + got.astype(jnp.float32)
                        if away and sends == 2:
                            sent[i][j, span, :] = value.astype(sent[i].dtype)
                        else:
                            target = sent[0] if away else left
                            target[i * inner + j, span, :] = value.astype(target.dtype)


def fold(scalars, items):
    outs, plans, given = [], [], []
    for keep, got, (outer, inner, bit, *more) in items:
        gots = got if isinstance(got, tuple) else (got,)
        sends = 2 if more else 1
        shape = (keep.shape[0] // 2,) + keep.shape[1:]
        outs += [array(jnp.bfloat16, shape[0] // sends, *shape[1:])] * sends + [array(keep.dtype, *shape)]
        plans.append((outer, inner, bit, len(gots), sends))
        given += [keep, *gots]
    got = list(whole_call(functools.partial(fold_body, plans), "fold", scalars, [], given, outs, [], []))
    result = []
    for *_, sends in plans:
        sent = tuple(got.pop(0) for _ in range(sends))
        result.append((sent if sends == 2 else sent[0], got.pop(0)))
    return result


def merge_body(shapes, scalars, *refs):
    send, left = refs[-2:]
    mine = scalars[4]
    low = send.shape[1]
    first = 0
    for item, (rows, wide) in enumerate(shapes):
        keep, got = refs[2 * item : 2 * item + 2]
        for part in range(rows // low):
            span = slice(part * low, (part + 1) * low)
            for high in range(2):
                for target, side in ((send, 1 - mine), (left, mine)):
                    value = keep[2 * high + side, span, :].astype(jnp.float32) + got[2 * high + side, span, :].astype(jnp.float32)
                    target[high, :, first : first + wide] = value.astype(target.dtype)
            first += wide


def merge(scalars, items, low):
    items = [(k.reshape(4, k.shape[-2] // 4, k.shape[-1]), g.reshape(4, g.shape[-2] // 4, g.shape[-1])) for k, g in items]
    shapes = [k.shape[1:] for k, _ in items]
    wide = sum(rows // low * n for rows, n in shapes)
    return whole_call(
        functools.partial(merge_body, shapes), "merge", scalars, [], [x for pair in items for x in pair],
        [array(jnp.bfloat16, 2, low, wide), array(jnp.float32, 2, low, wide)], [], [],
    )


def last_ff_body(scalars, keep, got, down_ref, up_ref):
    low = keep.shape[1]
    width = down_ref.shape[1]
    for part in range(down_ref.shape[0] // low):
        cols = slice(part * width, (part + 1) * width)
        down_ref[part * low : (part + 1) * low, :] = keep[0, :, cols] + got[0, :, cols].astype(jnp.float32)
    cols = slice(4 * width, 4 * width + up_ref.shape[1])
    up_ref[...] = keep[0, :, cols] + got[0, :, cols].astype(jnp.float32)


def last_ff(scalars, keep, got, width):
    low = keep.shape[1]
    return whole_call(
        last_ff_body, "last_ff", scalars, [], [keep, got], [array(jnp.float32, 4 * low, width), array(jnp.float32, low, 4 * width)], [], []
    )


def last_qkv_body(scalars, keep, got, more_keep, more_got, query_ref, key_ref, value_ref, out_ref, small_ref, late_ref, wide_ref, turned):
    low = keep.shape[1]
    width = query_ref.shape[1]
    half = width // 2

    def total(pair, first, size):
        return pair[0][0, :, first : first + size] + pair[1][0, :, first : first + size].astype(jnp.float32)

    one, two = (keep, got), (more_keep, more_got)
    for i, ref in enumerate((query_ref, key_ref, value_ref)):
        ref[:, :half] = total(one, i * half, half)
        ref[:, half:] = total(two, i * half, half)
    out_ref[...] = total(one, 3 * half + LANES, width)
    wide_ref[...] = total(one, 3 * half, LANES)[0:1, :]
    for ref, pair in ((small_ref, one), (late_ref, two)):
        turned[...] = jnp.zeros_like(turned)
        turned[:low, :] = total(pair, 3 * half, LANES)
        ref[...] = turned[...].T[: ref.shape[0], :]


def last_qkv(scalars, keep, got, more_keep, more_got, width):
    low = keep.shape[1]
    f32 = jnp.float32
    return whole_call(
        last_qkv_body, "last_qkv", scalars, [], [keep, got, more_keep, more_got],
        [array(f32, low, width)] * 4 + [array(f32, 24, LANES), array(f32, 8, LANES), array(f32, 1, LANES)], [], [pltpu.VMEM((LANES, LANES), f32)],
    )


def after(value, *others):
    return lax.optimization_barrier((value,) + others)[0]


def bit_count(size):
    return size.bit_length() - 1


def swap_dp(value, mask):
    return lax.ppermute(value, "dp", [(i, i ^ mask) for i in range(lax.axis_size("dp"))])


def swap_seq(value, mask):
    return lax.ppermute(value, "seq", [(i, i ^ mask) for i in range(lax.axis_size("seq"))])


def column_sum(matrix):
    return jnp.sum(matrix.astype(jnp.float32), axis=0)


def spread_pairs(first):
    dps, seqs = lax.axis_size("dp"), lax.axis_size("seq")
    pairs = []
    for dp in range(dps):
        for seq in range(seqs):
            piece = first ^ (seq & 1)
            to_dp = (dp & ~1) | (seq >> 1)
            to_seq = 2 * (dp & 1) + piece
            pairs.append((dp * seqs + seq, to_dp * seqs + to_seq))
    return pairs


def to_sequences(local, order):
    odd = (lax.axis_index("seq") & 1) == 1
    got = []
    pieces = [jnp.where(odd, local[1 - first], local[first]) for first in range(2)]
    order.mark(*pieces)
    for first, piece in enumerate(pieces):
        got.append(lax.ppermute(piece, AXES, spread_pairs(first)))
    return got, odd


def in_order(got, odd, rows):
    return jnp.where(odd, jnp.concatenate([g[:rows] for g in got[::-1]]), jnp.concatenate([g[:rows] for g in got]))


def from_sequences(tokens, order):
    odd = (lax.axis_index("seq") & 1) == 1
    half = tokens.shape[0] // 2
    got = []
    for first in range(2):
        near, far = tokens[first * half : (first + 1) * half], tokens[(1 - first) * half : (2 - first) * half]
        piece = order.mark(jnp.where(order.gate(odd), far, near))
        got.append(lax.ppermute(piece, AXES, [(b, a) for a, b in spread_pairs(first)]))
    return got


def both_sequences(order, got):
    odd = order.gate((lax.axis_index("seq") & 1) == 1)
    return jnp.where(odd, jnp.stack(got[::-1]), jnp.stack(got))


def weight_lines(weights, lines):
    width = weights[0].shape[-1]
    lines = [jnp.pad(v[..., None, :], [(0, 0)] * v.ndim + [(0, width - v.shape[-1])]) for v in lines]
    lines.append(jnp.zeros(lines[0].shape[:-2] + (16 - len(lines), width), jnp.bfloat16))
    return jnp.concatenate(weights + lines, axis=-2)


def near_shards(part, across=True):
    if lax.axis_size("dp") != PARTS:
        p = part if part.ndim == 3 else jnp.stack(jnp.split(lax.all_gather(part, "dp", axis=0, tiled=True), PARTS))
        return [p[i] for i in range(PARTS)]
    return [part, swap_dp(part, 2), swap_dp(part, 4)] + ([swap_dp(part, 6)] if across else [])


def both_cores(parts):
    return [shard for part in parts for shard in (part, swap_dp(part, 1))]


def all_shards(near, *ready):
    if len(near) == PARTS:
        return near
    return both_cores([near[0]] + list(lax.optimization_barrier((*near[1:], *ready))[:3]))


def relayed_shards(near, cut, *ready):
    if len(near) == PARTS:
        return near
    own, along_x, along_y = near
    along_x, along_y = lax.optimization_barrier((along_x, along_y, *ready))[:2]
    sent = along_x[:cut], along_y[cut:]
    top, bottom = swap_dp(sent[0], 4), swap_dp(sent[1], 2)
    own, along_x, along_y = lax.optimization_barrier((own, along_x, along_y, *sent))[:3]
    return both_cores([own, along_x, along_y, top, bottom])


def pack_body(count, scalars, *refs):
    weights, vectors, hidden, ids = refs[: min(3, count)], refs[3:count], refs[count], refs[count + 1]
    pieces = refs[count + 2 : count + 4]
    if vectors:
        part, lines = refs[count + 4 :]
        rows = weights[0].shape[0]
        for i, ref in enumerate(weights):
            part[i * rows : (i + 1) * rows, :] = ref[...]
        lines[...] = jnp.zeros_like(lines)
        for i, ref in enumerate(vectors):
            lines[i, : ref.shape[-1]] = (ref[...] if len(ref.shape) == 1 else ref[0]).astype(jnp.float32)
        part[3 * rows :, :] = lines[...].astype(jnp.bfloat16)
    odd = scalars[7]
    block, half = hidden.shape[1], ids.shape[1] // 2
    for first, piece in enumerate(pieces):
        piece[:block, :] = hidden[first ^ odd]
        line = jnp.where(first ^ odd == 0, ids[0:1, :], ids[1:2, :]).astype(jnp.bfloat16)
        piece[block:, :] = jnp.zeros_like(piece[block:, :])
        piece[block : block + 1, :half] = line[:, :half]
        piece[block + 1 : block + 2, :half] = line[:, half:]


def pack(scalars, weights, vectors, hidden, ids):
    piece = array(jnp.bfloat16, hidden.shape[1] + 16, hidden.shape[2])
    if lax.axis_size("dp") == PARTS:
        rows, width = weights[0].shape
        given = weights + [v[None, :] for v in vectors[:-1]] + vectors[-1:]
        return whole_call(
            functools.partial(pack_body, len(given)), "pack", scalars, [], [Far(x) for x in given + [hidden, ids]],
            [piece, piece, array(jnp.bfloat16, 3 * rows + 16, width)], [], [pltpu.VMEM((16, width), jnp.float32)],
        )
    gather = lambda v: lax.all_gather(v, "dp", axis=0, tiled=True)
    split = lambda v: gather(v).reshape((PARTS, -1) + v.shape[1:])
    pieces = whole_call(functools.partial(pack_body, 0), "pack", scalars, [], [Far(hidden), Far(ids)], [piece, piece], [], [])
    return *pieces, weight_lines([split(w) for w in weights], [split(v) for v in vectors])


def project_body(sizes, scalars, *refs):
    rows, wide, vectors, qblock, chunk, lanes, shards = sizes
    pieces, hidden = parts_of(refs[:shards]), list(refs[shards : shards + 3])
    size = hidden[0].shape[0]
    hidden = hidden[:2] + [hidden[2].at[:size, :], hidden[2].at[size:, :]]
    (
        attended, lse, tokens, vec_ref, up_ref, segments, ordered, query_out, keys_out, values_out, keys_far_out, values_far_out, weights_out,
        query, keys, values, keys_far, values_far, far, held, small, turned, ids, sems, hidden_sems, out_sems, kall, vt, tiles,
    ) = refs[shards + 3 :]
    count, width = tokens.shape
    block = count // 2
    half = width // 2
    core, odd = scalars[6], scalars[7]
    copies, brought = [], []

    def start(copies, source, target, sem):
        copies.append(pltpu.make_async_copy(source, target, sem))
        copies[-1].start()

    for i, (ref, place) in enumerate(zip(hidden, (0, 1, 0, 1))):
        goal = tokens if i < 2 else far
        start(brought, ref.at[:block, :], goal.at[pl.ds(pl.multiple_of((place ^ odd) * block, block), block), :], hidden_sems.at[i])
    start(brought, hidden[0].at[block:, :], ids, hidden_sems.at[4])
    for part, first, ref in pieces:
        where = scalars[0] ^ part
        target = pl.ds(where * rows, rows)
        for weight in range(first // rows, (first + ref.shape[0]) // rows):
            for side in range(2):
                start(
                    copies,
                    ref.at[weight * rows - first : (weight + 1) * rows - first, side * half : (side + 1) * half],
                    held.at[side, target, weight * half : (weight + 1) * half],
                    sems.at[len(copies)],
                )
        if first + ref.shape[0] > 3 * rows:
            start(copies, ref.at[3 * rows - first :, :], small.at[where], sems.at[len(copies)])
    wait_all(brought)
    line = ids[...].astype(jnp.float32)
    for i in range(2):
        segments[:, i * count : (i + 1) * count] = jnp.where(core == i, line[0:1, :count], line[1:2, :count])
    flipped = tokens[...].T
    for i in range(PARTS):
        turned[i] = flipped[i * rows : (i + 1) * rows, :]
    turn_parts(scalars[1], turned, ordered)
    wait_all(copies)
    saves = []
    start(saves, held, weights_out, out_sems.at[0])
    vec_ref[...] = jnp.concatenate([small[i, :, :rows] for i in range(PARTS)], axis=1).astype(jnp.float32)
    up_ref[...] = jnp.concatenate([small[i, vectors : vectors + 1, :wide] for i in range(PARTS)], axis=1).astype(jnp.float32)
    for i, (weight, add, goal, source, out) in enumerate((
        (1, None, keys, tokens, keys_out), (1, None, keys_far, far, keys_far_out), (2, 1, values, tokens, values_out),
        (2, 1, values_far, far, values_far_out), (0, 0, query, tokens, query_out),
    )):
        for side in range(2):
            cols = slice(side * half, (side + 1) * half)
            product = nn(source[...], held[side, :, weight * half : (weight + 1) * half])
            if add is not None:
                product = product + vec_ref[add : add + 1, cols]
            goal[:, cols] = product.astype(jnp.bfloat16)
        start(saves, goal, out, out_sems.at[i + 1])
    forward_body(qblock, chunk, lanes, query, keys, values, keys_far, values_far, segments, attended, lse, kall, vt, tiles)
    wait_all(saves)


def project(scalars, pieces, hidden, rows, wide, vectors, qblock, chunk, lanes):
    block, width = hidden[0].shape[0] - 16, hidden[0].shape[1]
    count = 2 * block
    lines = 16
    n = 2 * count // chunk
    f32, b16 = jnp.float32, jnp.bfloat16
    whole = array(b16, count, width)
    vmem = lambda x: pltpu.VMEM(x.shape, x.dtype)
    return whole_call(
        functools.partial(project_body, (rows, wide, vectors, qblock, chunk, lanes, len(pieces))), "project", scalars, list(pieces) + list(hidden), [],
        [whole, array(f32, width // lanes, 8, count), whole, array(f32, lines, width), array(f32, 1, wide * PARTS), array(f32, 1, 2 * count),
         array(b16, 2, PARTS // 2, rows, count)],
        [whole] * 5 + [array(b16, 2, width, 3 * width // 2)],
        [vmem(whole)] * 6
        + [pltpu.VMEM((2, width, 3 * width // 2), b16), pltpu.VMEM((PARTS, lines, width), b16), pltpu.VMEM((PARTS, rows, count), b16),
           pltpu.VMEM((16, width), b16), pltpu.SemaphoreType.DMA((7 * PARTS,)),
           pltpu.SemaphoreType.DMA((5,)), pltpu.SemaphoreType.DMA((6,)), pltpu.VMEM((n, chunk, lanes), b16),
           pltpu.VMEM((n, lanes, chunk), b16), pltpu.VMEM((n, chunk, LANES), f32)],
        28,
    )


class Order:
    def __init__(self):
        self.last = ()

    def gate(self, value):
        return lax.optimization_barrier((value, *self.last))[0] if self.last else value

    def mark(self, *values):
        self.last = values
        return values[0] if len(values) == 1 else values


def all_rows(send, keep):
    return jnp.stack([keep, send], axis=1).reshape(-1, keep.shape[-1]).astype(jnp.float32)


def scatter_all(send, keep):
    return lax.psum_scatter(all_rows(send, keep), AXES, scatter_dimension=0, tiled=True)


def per_device(
    hidden_in, segment_ids, query_weight, query_bias, key_weight, value_weight, value_bias, out_weight, out_bias,
    first_gain, first_shift, up_weight, up_bias, down_weight, down_bias, second_gain, second_shift, cotangent,
):
    dps, seqs = lax.axis_size("dp"), lax.axis_size("seq")
    inner_width, width = up_weight.shape[1], query_weight.shape[1]
    devices = dps * seqs
    share = width // devices
    qblock = chunk = 256
    pairs = 3
    direct = dps == PARTS and seqs == 4
    dp, seq = lax.axis_index("dp"), lax.axis_index("seq")
    if direct:
        scalars = [dp, dp & 1, (dp >> 1) & 1, dp >> 2, seq & 1, seq >> 1, dp & 1, seq & 1]
    else:
        scalars = [0, 0, 0, 0, 0, 0, dp & 1, seq & 1]
    scalars = jnp.stack([jnp.asarray(v, jnp.int32) for v in scalars])

    vectors = [query_bias, value_bias, out_bias, first_gain, first_shift, down_bias, second_gain, second_shift]
    *hidden, part = pack(
        scalars, [query_weight, key_weight, value_weight], vectors + [up_bias], hidden_in, segment_ids
    )
    near = near_shards(part)
    hidden = [lax.ppermute(piece, AXES, spread_pairs(first)) for first, piece in enumerate(hidden)]
    out_up, down_part = lax.optimization_barrier(
        (jnp.concatenate([out_weight, up_weight], axis=1), down_weight, *near[1:4])
    )[:2]
    hidden.append(swap_dp(jnp.concatenate(hidden), 1))
    if direct:
        own_far, *arrived = lax.optimization_barrier((swap_dp(part, 1), *near[1:4]))
        shards = [part, own_far, *arrived, swap_dp(jnp.concatenate(arrived), 1)]
    else:
        shards = near
    out_up_near = near_shards(out_up)
    attended, lse, tokens, vec, up_add, segments, ordered, query, keys, values, keys_other, values_other, w_qkv = project(
        scalars, shards, hidden, width // PARTS, inner_width // PARTS, len(vectors), qblock, chunk, pairs * LANES
    )
    order = Order()
    down_near = near_shards(after(down_part, attended, *out_up_near[1:4]), False)
    got_up, odd = to_sequences(after(cotangent, attended), order)
    out_up_shards = all_shards(out_up_near, attended)
    normal_one, scale_one, first_low, active, slope, wo, wu = widen(scalars, out_up_shards, attended, tokens, vec, up_add)
    upstream = in_order(lax.optimization_barrier((*got_up, active))[:2], odd, hidden_in.shape[1])
    layer_low, sum_two_grad, second_grad, sums_two, down_send, down_keep, wd = narrow(
        scalars, relayed_shards(down_near, inner_width // PARTS // 2, active), active, normal_one, vec, upstream
    )
    swap = (lambda value: swap_dp(value, 1)) if direct else (lambda value: value)
    order = Order()
    order.mark(second_grad)
    down_got = swap(down_send)
    out_pieces = from_sequences(layer_low, order)
    inner_grad, up_sum, up_send, up_keep = inner_back(scalars, order.gate(second_grad), wd, slope, first_low)
    up_got = swap(up_send)
    order.mark(inner_grad)
    if direct:
        ((send, down_keep),) = fold(order.gate(scalars), [(down_keep, down_got, (2, 1, 2))])
        down_got = swap_dp(order.mark(send), 2)
    sum_one_grad, attended_grad, sums_one, out_send, out_keep = outer_back(
        order.gate(scalars), inner_grad, wu, sum_two_grad, normal_one, scale_one, vec, wo, attended
    )
    order.mark(attended_grad)
    if direct:
        ((send, up_keep),) = fold(order.gate(scalars), [(up_keep, up_got, (1, 2, 3))])
        up_got = swap_dp(order.mark(send), 4)
    out_got = swap(out_send)

    def attend(side):
        given = (query, keys, values, keys_other, values_other, attended, attended_grad, lse, segments)
        return order.mark(*attend_back(order.gate(scalars), *given, qblock, chunk, pairs, side))

    dq, dk, dv, *far = attend(0)
    if direct:
        (send, down_keep), (third, out_keep) = fold(
            order.gate(scalars), [(down_keep, down_got, (1, 1, 3)), (out_keep, out_got, (1, 2, 3))]
        )
        order.mark(send, third)
        down_got, out_got = swap_dp(send, 4), swap_dp(third, 4)
    layer_out = order.mark(both_sequences(order, out_pieces))
    one_low, one_high, one_keep, gradient, sums_first = qkv_back(
        0, order.gate(scalars), dq, dk, dv, *[swap_dp(x, 1) for x in order.gate(far)], ordered, w_qkv, sum_one_grad,
        sums_one, sums_two, up_sum
    )
    order.mark(gradient)
    one_got = (swap(one_low), swap(one_high))
    if direct:
        ((send, up_keep),) = fold(order.gate(scalars), [(up_keep, up_got, (1, 1, 2))])
        up_got = swap_dp(order.mark(send), 2)
    dq, dk, dv, *far = attend(1)
    if direct:
        send, ff_keep = merge(order.gate(scalars), [(down_keep, down_got), (up_keep, up_got)], share)
        ff_got = swap_seq(order.mark(send), 1)
        (send, one_keep), (other, out_keep) = fold(
            order.gate(scalars), [(one_keep, one_got, (2, 1, 2)), (out_keep, out_got, (1, 1, 2))]
        )
        order.mark(send, other)
        one_got, out_got = swap_dp(send, 2), swap_dp(other, 2)
    two_low, two_high, two_keep, gradient, _ = qkv_back(
        1, order.gate(scalars), dq, dk, dv, *[swap_dp(x, 1) for x in order.gate(far)], ordered, w_qkv, gradient, sums_first
    )
    order.mark(gradient)
    two_got = (swap(two_low), swap(two_high))
    in_pieces = from_sequences(gradient, order)
    if not direct:
        down_grad, up_grad = scatter_all(down_send, down_keep), scatter_all(up_send, up_keep)
        one, two = scatter_all(jnp.concatenate([one_low, one_high]), one_keep), scatter_all(jnp.concatenate([two_low, two_high]), two_keep)
        cut = width // 2
        query_grad, key_grad, value_grad = [
            jnp.concatenate([side[:, i * cut : (i + 1) * cut] for side in (one, two)], axis=1) for i in range(3)
        ]
        out_grad = scatter_all(out_send, out_keep)
        small, late = one[:, 3 * cut :].T, two[:, 3 * cut :].T
        up_bias_grad = lax.psum_scatter(up_sum[0], AXES, scatter_dimension=0, tiled=True)
    else:
        ((send, one_keep),) = fold(order.gate(scalars), [(one_keep, one_got, (1, 1, 3))])
        one_got = swap_dp(order.mark(send), 4)
        ((send, ff_keep),) = fold(order.gate(scalars), [(ff_keep, ff_got, (1, 1, 5))])
        ff_got = swap_seq(order.mark(send), 2)
        ((sent, two_keep),) = fold(order.gate(scalars), [(two_keep, two_got, (2, 1, 2, True))])
        two_got = tuple(swap_dp(x, 2) for x in order.mark(*sent))
        send, keep = merge(order.gate(scalars), [(one_keep, one_got), (out_keep, out_got)], share)
        got = swap_seq(order.mark(send), 1)
        ((send, two_keep),) = fold(order.gate(scalars), [(two_keep, two_got, (1, 1, 3))])
        two_got = swap_dp(order.mark(send), 4)
    input_grad = order.mark(both_sequences(order, in_pieces).astype(jnp.float32))
    if direct:
        ((send, keep),) = fold(order.gate(scalars), [(keep, got, (1, 1, 5))])
        got = swap_seq(order.mark(send), 2)
        send, two_keep = merge(order.gate(scalars), [(two_keep, two_got)], share)
        two_got = swap_seq(order.mark(send), 1)
        ((send, two_keep),) = fold(order.gate(scalars), [(two_keep, two_got, (1, 1, 5))])
        two_got = swap_seq(order.mark(send), 2)
        down_grad, up_grad = order.mark(*last_ff(order.gate(scalars), ff_keep, ff_got, width))
        query_grad, key_grad, value_grad, out_grad, small, late, line = last_qkv(
            order.gate(scalars), keep, got, two_keep, two_got, width
        )
        up_bias_grad = line[0, LANES - inner_width // devices :]
    ob, g1, s1 = [small[i, :share] for i in (0, 1, 2)]
    db, g2, s2 = [small[i, :share] for i in (8, 9, 10)]
    qb, vb = [late[i, :share] for i in (0, 1)]
    return (
        layer_out, input_grad, query_grad, qb, key_grad, value_grad, vb, out_grad, ob, g1, s1, up_grad, up_bias_grad, down_grad, db, g2, s2,
    )


def solution(mesh):
    wide, flat = P("dp", None), P("dp")
    in_specs = (
        P("dp", "seq", None), wide, wide, flat, wide, wide, flat, wide, flat, flat, flat, wide, flat, wide, flat,
        flat, flat, P("dp", "seq", None),
    )
    rows, cells = P(AXES, None), P(AXES)
    out_specs = (
        P("dp", "seq", None), P("dp", "seq", None), rows, cells, rows, rows, cells, rows, cells, cells, cells, rows,
        cells, rows, cells, cells, cells,
    )
    return jax.shard_map(per_device, mesh=mesh, in_specs=in_specs, out_specs=out_specs, check_vma=False)
```

```python
import functools
import math

import jax
import jax.numpy as jnp
from jax import lax
from jax.experimental import pallas as pl
from jax.experimental.pallas import tpu as pltpu
from jax.sharding import PartitionSpec as P

HEAD_DIM = 64
LANES = 128
NEGATIVE = -1e30


def nt(left, right):
    return lax.dot_general(left, right, (((1,), (1,)), ((), ())), preferred_element_type=jnp.float32)


def nn(left, right):
    return lax.dot_general(left, right, (((1,), (0,)), ((), ())), preferred_element_type=jnp.float32)


def head_parts(block):
    lane = lax.broadcasted_iota(jnp.int32, block.shape, 1)
    zero = jnp.zeros_like(block)
    return (jnp.where(lane < HEAD_DIM, block, zero), jnp.where(lane < HEAD_DIM, zero, block))


def same_document(column_tile, row):
    column = jnp.concatenate([column_tile] * (row.shape[1] // LANES), axis=1)
    return column == jnp.broadcast_to(row, column.shape)


def pair_lanes(pair):
    return slice(pair * LANES, (pair + 1) * LANES)


def segment_tables(segments, tiles, half, qblock, chunk):
    ids = segments[...]
    for j in range(tiles.shape[0]):
        for i in range(chunk // LANES):
            start = j * chunk + i * LANES
            tiles[j, i * LANES : (i + 1) * LANES, :] = jnp.broadcast_to(ids[:, start : start + LANES], (LANES, LANES)).T
    chunks = half // chunk
    low = [jnp.min(ids[:, j * chunk : (j + 1) * chunk]) for j in range(2 * chunks)]
    high = [jnp.max(ids[:, j * chunk : (j + 1) * chunk]) for j in range(2 * chunks)]
    found = []
    for b in range(half // qblock):
        mine = slice(b * qblock, (b + 1) * qblock)
        first, last = jnp.min(ids[:, mine]), jnp.max(ids[:, mine])
        bounds = []
        for side in range(2):
            before = sum((high[side * chunks + j] < first).astype(jnp.int32) for j in range(chunks))
            behind = sum((low[side * chunks + j] > last).astype(jnp.int32) for j in range(chunks))
            bounds += [before, chunks - behind]
        found.append((bounds[0], bounds[1] - bounds[0], bounds[2], bounds[1] - bounds[0] + bounds[3] - bounds[2]))
    return found


def chunk_of(bounds, step, chunks):
    first, own, other, _ = bounds
    return jnp.where(step < own, first + step, chunks + other + step - own)


def forward_body(qblock, chunk, lanes, q_all, k_all, v_all, ko_all, vo_all, segments, o_all, lse_all, kall, vt, sk_ref):
    half = k_all.shape[0]
    tables = segment_tables(segments, sk_ref, half, qblock, chunk)
    chunks, pairs = half // chunk, lanes // LANES

    @pl.loop(0, q_all.shape[1] // lanes)
    def _(group):
        cols = step_of(group, lanes)
        q_ref, k_ref, v_ref, ko_ref, vo_ref, o_ref = (r.at[:, cols] for r in (q_all, k_all, v_all, ko_all, vo_all, o_all))
        lse_ref = lse_all.at[pl.ds(group, 1)]
        for j in range(chunks):
            rows = slice(j * chunk, (j + 1) * chunk)
            kall[j] = k_ref[rows, :]
            kall[chunks + j] = ko_ref[rows, :]
            vt[j] = v_ref[rows, :].T
            vt[chunks + j] = vo_ref[rows, :].T
        for b in range(q_ref.shape[0] // qblock):
            span = slice(b * qblock, (b + 1) * qblock)
            parts = []
            for pair in range(pairs):
                parts += head_parts(q_ref[span, pair_lanes(pair)] * jnp.bfloat16(HEAD_DIM**-0.5))
            row = segments[:, span]

            def one(step, carry):
                j = chunk_of(tables[b], step, chunks)
                mask = same_document(sk_ref[j], row)
                scores = [jnp.where(mask, nt(kall[j, :, pair_lanes(h // 2)], part), NEGATIVE) for h, part in enumerate(parts)]
                out = []
                for h, score in enumerate(scores):
                    top, total, acc = carry[h]
                    new_top = jnp.maximum(top, jnp.max(score, axis=0, keepdims=True))
                    expo = jnp.exp(score - new_top)
                    scale = jnp.exp(top - new_top)
                    total = total * scale + jnp.sum(expo, axis=0, keepdims=True)
                    acc = acc * scale + nn(vt[j, h * HEAD_DIM : (h + 1) * HEAD_DIM, :], expo.astype(jnp.bfloat16))
                    out.append((new_top, total, acc))
                return tuple(out)

            init = (
                jnp.full((1, qblock), NEGATIVE, jnp.float32),
                jnp.zeros((1, qblock), jnp.float32),
                jnp.zeros((HEAD_DIM, qblock), jnp.float32),
            )
            carry = lax.fori_loop(0, tables[b][3], one, (init,) * len(parts))
            result = jnp.concatenate([acc / total for _, total, acc in carry], axis=0)
            o_ref[span, :] = result.T.astype(jnp.bfloat16)
            for h, (top, total, _) in enumerate(carry):
                lse_ref[0, h : h + 1, span] = top + jnp.log(total)


def backward_body(
    qblock, chunk, lanes, side, copies, scalars, q_ref, k_ref, v_ref, ko_ref, vo_ref, o_ref, do_ref, lse_all, segments,
    dq_ref, dk_ref, dv_ref, far_keys, far_values, kall, vall, kt, dkall, dvall, sk_ref,
):
    half = k_ref.shape[0]
    tables = segment_tables(segments, sk_ref, half, qblock, chunk)
    lse_ref = lse_all.at[side : side + 1]
    chunks, pairs = half // chunk, lanes // LANES
    dkall[...] = jnp.zeros_like(dkall)
    dvall[...] = jnp.zeros_like(dvall)
    for first, keys, values in ((0, k_ref, v_ref), (chunks, ko_ref, vo_ref)):
        wait_all(copies[1:3] if first == 0 else copies[3:5])
        for j in range(chunks):
            rows = slice(j * chunk, (j + 1) * chunk)
            kall[first + j] = keys[rows, :]
            vall[first + j] = values[rows, :]
            kt[first + j] = keys[rows, :].T
    wait_all(copies[:1] + copies[5:])
    for b in range(q_ref.shape[0] // qblock):
        span = slice(b * qblock, (b + 1) * qblock)
        parts, dparts, delta = [], [], []
        for pair in range(pairs):
            parts.append(head_parts(q_ref[span, pair_lanes(pair)] * jnp.bfloat16(HEAD_DIM**-0.5)))
            dparts.append(head_parts(do_ref[span, pair_lanes(pair)]))
            product = do_ref[span, pair_lanes(pair)].astype(jnp.float32) * o_ref[span, pair_lanes(pair)].astype(jnp.float32)
            product = product.T
            delta += [jnp.sum(product[h * HEAD_DIM : (h + 1) * HEAD_DIM], axis=0, keepdims=True) for h in range(2)]
        both = [jnp.concatenate(p, axis=0) for p in parts]
        dboth = [jnp.concatenate(p, axis=0) for p in dparts]
        row = segments[:, span]
        lse = [lse_ref[0, h : h + 1, span] for h in range(2 * pairs)]

        def one(step, carry):
            j = chunk_of(tables[b], step, chunks)
            mask = same_document(sk_ref[j], row)
            out = []
            both_mask = jnp.concatenate([mask, mask], axis=1)
            scores = [nt(kall[j, :, pair_lanes(pair)], both[pair]) for pair in range(pairs)]
            products = [nt(vall[j, :, pair_lanes(pair)], dboth[pair]) for pair in range(pairs)]
            adds = []
            for pair in range(pairs):
                score = jnp.where(both_mask, scores[pair], NEGATIVE)
                prob = jnp.exp(score - jnp.concatenate(lse[2 * pair : 2 * pair + 2], axis=1))
                grad = (prob * (products[pair] - jnp.concatenate(delta[2 * pair : 2 * pair + 2], axis=1))).astype(jnp.bfloat16)
                for side in range(2):
                    h = 2 * pair + side
                    out.append(carry[h] + nn(kt[j, h * HEAD_DIM : (h + 1) * HEAD_DIM, :], grad[:, side * qblock : (side + 1) * qblock]))
                adds.append((nn(prob.astype(jnp.bfloat16), dboth[pair]), nn(grad, both[pair])))
            for pair in range(pairs):
                dvall[j, :, pair_lanes(pair)] += adds[pair][0]
                dkall[j, :, pair_lanes(pair)] += adds[pair][1]
            return tuple(out)

        zero = jnp.zeros((HEAD_DIM, qblock), jnp.float32)
        carry = lax.fori_loop(0, tables[b][3], one, (zero,) * (2 * pairs))
        dq_ref[span, :] = (jnp.concatenate(carry, axis=0).T * HEAD_DIM**-0.5).astype(jnp.bfloat16)
    for j in range(chunks):
        rows = slice(j * chunk, (j + 1) * chunk)
        dk_ref[rows, :] = dkall[j]
        dv_ref[rows, :] = dvall[j]
        far_keys[rows, :] = dkall[chunks + j].astype(jnp.bfloat16)
        far_values[rows, :] = dvall[chunks + j].astype(jnp.bfloat16)


def attend_back(scalars, query, keys, values, keys_other, values_other, attended, grad, lse_rows, segments, qblock, chunk, pairs, side):
    tokens, width = query.shape
    half = keys.shape[0]
    lanes = pairs * LANES
    n = 2 * half // chunk
    f32, b16 = jnp.float32, jnp.bfloat16
    cols = slice(side * lanes, (side + 1) * lanes)
    far = [Far(x, cols) for x in (query, keys, values, keys_other, values_other, attended, grad)]
    return whole_call(
        functools.partial(backward_body, qblock, chunk, lanes, side), "attend_back", scalars, [], far + [lse_rows, segments],
        [array(b16, tokens, lanes), array(f32, half, lanes), array(f32, half, lanes), array(b16, half, lanes), array(b16, half, lanes)], [],
        [pltpu.VMEM((n, chunk, lanes), b16), pltpu.VMEM((n, chunk, lanes), b16), pltpu.VMEM((n, lanes, chunk), b16),
         pltpu.VMEM((n, chunk, lanes), f32), pltpu.VMEM((n, chunk, lanes), f32), pltpu.VMEM((n, chunk, LANES), f32)], 24, True,
    )


AXES = ("dp", "seq")
PARTS = 8
epsilon = 1e-12


def tn(left, right):
    return lax.dot_general(left, right, (((0,), (0,)), ((), ())), preferred_element_type=jnp.float32)


def norm_parts(value):
    center = value - jnp.mean(value, axis=-1, keepdims=True)
    spread = jnp.mean(center * center, axis=-1, keepdims=True)
    scale = lax.rsqrt(spread + epsilon)
    return (center * scale, scale)


def norm_back(upstream, normal, scale, gain):
    scaled = upstream * gain
    return scale * (
        scaled
        - jnp.mean(scaled, axis=-1, keepdims=True)
        - normal * jnp.mean(scaled * normal, axis=-1, keepdims=True)
    )


def row_sum(matrix):
    return jnp.sum(matrix.astype(jnp.float32), axis=0, keepdims=True)


def parts_of(refs):
    if len(refs) == PARTS:
        return [(i, 0, ref) for i, ref in enumerate(refs)]
    if len(refs) == 6:
        own, own_far, near_x, near_y, near_d, far = refs
        rows = own.shape[0]
        other = [far.at[i * rows : (i + 1) * rows, :] for i in range(3)]
        return [(i, 0, ref) for i, ref in enumerate((own, own_far, near_x, other[0], near_y, other[1], near_d, other[2]))]
    pieces = [(i, 0, ref) for i, ref in enumerate(refs[:6])]
    for i in range(2):
        top, bottom = refs[6 + i], refs[8 + i]
        pieces += [(6 + i, 0, top), (6 + i, top.shape[0], bottom)]
    return pieces


def load_pieces(me, pieces, rows, targets, sems):
    copies = [[] for _ in targets]
    for place, (part, first, ref) in enumerate(pieces):
        size = ref.shape[0]
        where = pl.ds(pl.multiple_of((me ^ part) * rows + first, 32), size)
        for i, (target, columns) in enumerate(targets):
            copy = pltpu.make_async_copy(ref.at[:, columns], target.at[where, :], sems.at[i, place])
            copy.start()
            copies[i].append(copy)
    return copies


def wait_all(copies):
    for copy in copies:
        copy.wait()


def step_of(block, size):
    return pl.ds(pl.multiple_of(block * size, size), size)


BLOCK = 1024
GELU_BLOCK = 512
ROWS = 256


def widen_body(scalars, *refs):
    shards = len(refs) - 12
    pieces = parts_of(refs[:shards])
    (attended, tokens, vec, up_add, normal_ref, scale_ref, low_ref, active_ref, slope_ref, wo, wu, sems) = refs[shards:]
    width, wide = wu.shape
    loads = load_pieces(scalars[0], pieces, width // PARTS, [(wo, slice(0, width)), (wu, slice(width, width + wide))], sems)
    wait_all(loads[0])

    @pl.loop(0, tokens.shape[0] // ROWS)
    def _(i):
        rows = step_of(i, ROWS)
        branch = nn(attended[rows, :], wo[...]) + vec[2:3, :]
        normal, scale = norm_parts(tokens[rows, :].astype(jnp.float32) + branch)
        first = normal * vec[3:4, :] + vec[4:5, :]
        normal_ref[rows, :] = normal
        scale_ref[rows, :] = jnp.broadcast_to(scale, (ROWS, LANES))
        low_ref[rows, :] = first.astype(jnp.bfloat16)

    wait_all(loads[1])

    @pl.loop(0, wide // GELU_BLOCK)
    def _(j):
        cols = step_of(j, GELU_BLOCK)
        inner = nn(low_ref[...], wu[:, cols]) + up_add[:, cols]
        cumulative = 0.5 * (1.0 + lax.erf(inner * math.sqrt(0.5)))
        density = jnp.exp(-0.5 * inner * inner) * (1.0 / math.sqrt(2.0 * math.pi))
        active_ref[:, cols] = (inner * cumulative).astype(jnp.bfloat16)
        slope_ref[:, cols] = (cumulative + inner * density).astype(jnp.bfloat16)


def narrow_body(scalars, *refs):
    shards = len(refs) - 13
    pieces = parts_of(refs[:shards])
    (active, normal_one, vec, upstream, out_ref, grad_ref, low_ref, sums_ref, send_ref, keep_ref, wd, sums, sems) = refs[shards:]
    wide, width = wd.shape
    (loads,) = load_pieces(scalars[0], pieces, wide // PARTS, [(wd, slice(0, width))], sems)
    wait_all(loads)
    sums[...] = jnp.zeros_like(sums)

    @pl.loop(0, normal_one.shape[0] // ROWS)
    def _(i):
        rows = step_of(i, ROWS)
        second = nn(active[rows, :], wd[...]) + vec[5:6, :]
        normal, scale = norm_parts(normal_one[rows, :] * vec[3:4, :] + vec[4:5, :] + second)
        out_ref[rows, :] = (normal * vec[6:7, :] + vec[7:8, :]).astype(jnp.bfloat16)
        up = upstream[rows, :].astype(jnp.float32)
        grad = norm_back(up, normal, scale, vec[6:7, :])
        low = grad.astype(jnp.bfloat16)
        grad_ref[rows, :] = grad
        low_ref[rows, :] = low
        sums[0:1, :] += row_sum(low)
        sums[1:2, :] += row_sum(up * normal)
        sums[2:3, :] += row_sum(up)

    sums_ref[...] = sums[...]
    size = wide // PARTS

    @pl.loop(0, PARTS // 2)
    def _(i):
        send_ref[i] = tn(active[:, step_of(2 * i + 1 - scalars[1], size)], low_ref[...]).astype(jnp.bfloat16)
        keep_ref[i] = tn(active[:, step_of(2 * i + scalars[1], size)], low_ref[...]).astype(jnp.bfloat16)


def turn_parts(core, turned, ordered):
    for i in range(PARTS // 2):
        ordered[0, i] = turned[2 * i + 1 - core]
        ordered[1, i] = turned[2 * i + core]


def inner_back_body(scalars, low, wd, slope, first_low, grad_ref, sums_ref, send_ref, keep_ref, turned, ordered):
    size = first_low.shape[1] // PARTS
    flipped = first_low[...].T
    for i in range(PARTS):
        turned[i] = flipped[i * size : (i + 1) * size, :]
    turn_parts(scalars[1], turned, ordered)
    rows = (PARTS // 2) * size

    @pl.loop(0, slope.shape[1] // BLOCK)
    def _(j):
        cols = step_of(j, BLOCK)
        grad = (nt(low[...], wd[cols, :]) * slope[:, cols].astype(jnp.float32)).astype(jnp.bfloat16)
        grad_ref[:, cols] = grad
        sums_ref[:, cols] = row_sum(grad)
        for side, ref in enumerate((send_ref, keep_ref)):
            left = ordered[side].reshape(rows, low.shape[0])
            ref[:, :, cols] = nn(left, grad).astype(jnp.bfloat16).reshape(PARTS // 2, size, BLOCK)


def outer_back_body(scalars, grad, wu, up_grad, normal_ref, scale_ref, vec, wo, attended, sum_ref, result_ref, sums_ref, send_ref, keep_ref, low, sums, turned):
    width = wo.shape[0]
    sums[...] = jnp.zeros_like(sums)

    @pl.loop(0, grad.shape[0] // ROWS)
    def _(i):
        rows = step_of(i, ROWS)
        first = up_grad[rows, :] + nt(grad[rows, :], wu[...])
        normal = normal_ref[rows, :]
        total = norm_back(first, normal, scale_ref[rows, 0:1], vec[3:4, :])
        branch = total.astype(jnp.bfloat16)
        sum_ref[rows, :] = total
        low[rows, :] = branch
        result_ref[rows, :] = nt(branch, wo[...]).astype(jnp.bfloat16)
        sums[0:1, :] += row_sum(branch)
        sums[1:2, :] += row_sum(first * normal)
        sums[2:3, :] += row_sum(first)

    sums_ref[...] = sums[...]
    size = width // PARTS
    product = tn(attended[...], low[...]).astype(jnp.bfloat16)
    for i in range(PARTS):
        turned[i] = product[i * size : (i + 1) * size, :]
    for i in range(PARTS // 2):
        send_ref[i] = turned[2 * i + 1 - scalars[1]]
        keep_ref[i] = turned[2 * i + scalars[1]]


class Far:
    def __init__(self, value, columns=None, index=None):
        self.value, self.columns, self.index = value, columns, index
        shape = value.shape if index is None else value.shape[1:]
        width = shape[-1] if columns is None else columns.stop - columns.start
        self.shape, self.dtype = shape[:-1] + (width,), value.dtype


def far_body(body, far, counts, scalars, *refs):
    hbm, inputs, outputs, held, lazy = counts
    given = list(refs[hbm : hbm + inputs])
    held_refs, sems = refs[len(refs) - held - 1 : -1], refs[-1]
    copies = []
    for i, (place, columns, index) in enumerate(far):
        source = given[place]
        if index is not None:
            source = source.at[index]
        if columns is not None:
            source = source.at[:, columns]
        copies.append(pltpu.make_async_copy(source, held_refs[i], sems.at[i]))
        copies[-1].start()
        given[place] = held_refs[i]
    rest = (*refs[:hbm], *given, *refs[hbm + inputs : len(refs) - held - 1])
    if lazy:
        body(copies, scalars, *rest)
    else:
        wait_all(copies)
        body(scalars, *rest)


def in_hbm(value):
    return pltpu.with_memory_space_constraint(value, pltpu.HBM)


def whole_call(body, name, scalars, hbm, inputs, outputs, hbm_outputs, scratch, room=8, lazy=False):
    shape_of = lambda x: jax.ShapeDtypeStruct(x.shape, x.dtype)
    near, stay = pl.BlockSpec(memory_space=pltpu.VMEM), pl.BlockSpec(memory_space=pltpu.HBM)
    far = [(i, x.columns, x.index) for i, x in enumerate(inputs) if isinstance(x, Far)]
    scratch = list(scratch)
    if far:
        held = [pltpu.VMEM(inputs[i].shape, inputs[i].dtype) for i, *_ in far]
        counts = (len(hbm), len(inputs), len(outputs) + len(hbm_outputs), len(far), lazy)
        body = functools.partial(far_body, body, far, counts)
        scratch += held + [pltpu.SemaphoreType.DMA((len(far),))]
        room += sum(math.prod(inputs[i].shape) * inputs[i].dtype.itemsize for i, *_ in far) // (1 << 20) + 1
    return pl.pallas_call(
        body,
        in_specs=[pl.BlockSpec(memory_space=pltpu.SMEM)]
        + [stay] * len(hbm)
        + [stay if isinstance(x, Far) else near for x in inputs],
        out_specs=[near] * len(outputs) + [stay] * len(hbm_outputs),
        scratch_shapes=scratch,
        out_shape=[shape_of(x) for x in outputs] + [pltpu.HBM(x.shape, x.dtype) for x in hbm_outputs],
        cost_estimate=pl.CostEstimate(flops=1, transcendentals=0, bytes_accessed=1),
        compiler_params=pltpu.CompilerParams(vmem_limit_bytes=room << 20),
        name=name,
    )(scalars, *[in_hbm(x) for x in hbm], *[in_hbm(x.value) if isinstance(x, Far) else x for x in inputs])


def array(dtype, *shape):
    return jax.ShapeDtypeStruct(shape, dtype)


def widen(scalars, pieces, attended, tokens, vec, up_add):
    count, width = tokens.shape
    wide = up_add.shape[1]
    f32, b16 = jnp.float32, jnp.bfloat16
    return whole_call(
        widen_body, "widen", scalars, pieces, [attended, tokens, vec, up_add],
        [array(f32, count, width), array(f32, count, LANES), array(b16, count, width),
         array(b16, count, wide), array(b16, count, wide), array(b16, width, width), array(b16, width, wide)],
        [], [pltpu.SemaphoreType.DMA((2, len(pieces)))],
    )


def narrow(scalars, pieces, active, normal, vec, upstream):
    count, wide = active.shape
    width = normal.shape[1]
    f32, b16 = jnp.float32, jnp.bfloat16
    half = array(b16, PARTS // 2, wide // PARTS, width)
    return whole_call(
        narrow_body, "narrow", scalars, pieces, [active, normal, vec, upstream],
        [array(b16, count, width), array(f32, count, width), array(b16, count, width), array(f32, 8, width), half, half, array(b16, wide, width)],
        [], [pltpu.VMEM((8, width), f32), pltpu.SemaphoreType.DMA((1, len(pieces)))],
    )


def inner_back(scalars, low, wd, slope, first_low):
    count, wide = slope.shape
    width = low.shape[1]
    size = width // PARTS
    f32, b16 = jnp.float32, jnp.bfloat16
    half = array(b16, PARTS // 2, size, wide)
    return whole_call(
        inner_back_body, "inner_back", scalars, [], [low, wd, slope, first_low],
        [array(b16, count, wide), array(f32, 1, wide), half, half], [],
        [pltpu.VMEM((PARTS, size, count), b16), pltpu.VMEM((2, PARTS // 2, size, count), b16)],
    )


def outer_back(scalars, grad, wu, up_grad, normal, scale, vec, wo, attended):
    count, width = normal.shape
    f32, b16 = jnp.float32, jnp.bfloat16
    half = array(b16, PARTS // 2, width // PARTS, width)
    return whole_call(
        outer_back_body, "outer_back", scalars, [], [grad, wu, up_grad, normal, scale, vec, wo, attended],
        [array(f32, count, width), array(b16, count, width), array(f32, 8, width), half, half], [],
        [pltpu.VMEM((count, width), b16), pltpu.VMEM((8, width), f32), pltpu.VMEM((PARTS, width // PARTS, width), b16)],
    )


def sums_to_slots(core, lines, parts, send, keep, first, wide=None):
    turned = lines[...].T
    rows = turned.shape[0] // PARTS
    for i in range(PARTS):
        parts[i] = turned[i * rows : (i + 1) * rows, :]
    if wide is not None:
        size = wide.shape[1] // (4 * PARTS)
        for i in range(4 * PARTS):
            place = (i % 4) * (rows // 4)
            parts[i // 4, place : place + 1, LANES - size :] = wide[:, i * size : (i + 1) * size]
    for i in range(PARTS // 2):
        send[i, :, first : first + LANES] = parts[2 * i + 1 - core].astype(jnp.bfloat16)
        keep[i, :, first : first + LANES] = parts[2 * i + core].astype(jnp.bfloat16)


def qkv_back_body(side, copies, scalars, dq, dk, dv, far_keys, far_values, ordered, weight, gradient, *refs):
    core = scalars[1]
    if side == 0:
        sums_one, sums_two, wide_sums, send_low, send_high, keep, result, sums_ref, both, lines, parts, send = refs
    else:
        first_sums, send_low, send_high, keep, result, sums_ref, both, lines, parts, send = refs
    half = dq.shape[1]
    both[:, :half] = dq[...]
    both[:, half : 2 * half] = (dk[...] + far_keys[...].astype(jnp.float32)).astype(jnp.bfloat16)
    both[:, 2 * half :] = (dv[...] + far_values[...].astype(jnp.float32)).astype(jnp.bfloat16)
    sums_ref[...] = jnp.zeros_like(sums_ref)
    sums_ref[0:1, :] = row_sum(dq[...])
    sums_ref[1:2, :] = row_sum(both[:, 2 * half :])
    rows = ordered.shape[1] * ordered.shape[2]
    copies[0].wait()
    for i, ref in enumerate((send, keep)):
        left = ordered[i].reshape(rows, ordered.shape[3])
        product = nn(left, both[...]).astype(jnp.bfloat16)
        ref[:, :, : 3 * half] = product.reshape(ordered.shape[1], ordered.shape[2], 3 * half)
    lines[...] = jnp.zeros_like(lines)
    if side == 0:
        lines[0:8, :] = sums_one[...]
        lines[8:16, :] = sums_two[...]
        sums_to_slots(core, lines, parts, send, keep, 3 * half, wide_sums)
    else:
        lines[0:8, :half] = first_sums[...]
        lines[0:8, half:] = sums_ref[...]
        sums_to_slots(core, lines, parts, send, keep, 3 * half)
    send_low[...] = send[:2]
    send_high[...] = send[2:]
    copies[1].wait()
    result[...] = (gradient[...] + nt(both[...], weight[...])).astype(result.dtype)


def qkv_back(side, scalars, dq, dk, dv, far_keys, far_values, ordered, weights, gradient, *more):
    count, half = dq.shape
    width = gradient.shape[1]
    f32, b16 = jnp.float32, jnp.bfloat16
    total = array(b16, PARTS // 2, width // PARTS, 3 * half + LANES)
    part = array(b16, PARTS // 4, width // PARTS, 3 * half + LANES)
    return whole_call(
        functools.partial(qkv_back_body, side), "qkv_back", scalars, [], [dq, dk, dv, far_keys, far_values, Far(ordered), Far(weights, None, side), gradient, *more],
        [part, part, total, array(b16 if side else f32, count, width), array(f32, 8, half)], [],
        [pltpu.VMEM((count, 3 * half), b16), pltpu.VMEM((LANES, width), f32), pltpu.VMEM((PARTS, width // PARTS, LANES), f32),
         pltpu.VMEM(total.shape, b16)],
        8, True,
    )


STRIPE = 32


def fold_body(plans, scalars, *refs):
    places, outs = [0], [0]
    for *_, count, sends in plans:
        places.append(places[-1] + 1 + count)
        outs.append(outs[-1] + 1 + sends)
    for item, (outer, inner, bit, count, sends) in enumerate(plans):
        keep, *gots = refs[places[item] : places[item + 1]]
        *sent, left = refs[places[-1] + outs[item] : places[-1] + outs[item + 1]]
        mine = scalars[bit]
        rows = keep.shape[1]
        stripe = STRIPE if rows % STRIPE == 0 else rows

        @pl.loop(0, rows // stripe)
        def _(k):
            span = step_of(k, stripe) if stripe != rows else slice(None)
            for i in range(outer):
                for j in range(inner):
                    for away, side in ((True, 1 - mine), (False, mine)):
                        place = (2 * i + side) * inner + j
                        if count == 1:
                            got = gots[0][place, span, :]
                        elif outer == 1:
                            got = jnp.where(side == 0, gots[0][j, span, :], gots[1][j, span, :])
                        else:
                            got = gots[i][side * inner + j, span, :]
                        value = keep[place, span, :].astype(jnp.float32) + got.astype(jnp.float32)
                        if away and sends == 2:
                            sent[i][j, span, :] = value.astype(sent[i].dtype)
                        else:
                            target = sent[0] if away else left
                            target[i * inner + j, span, :] = value.astype(target.dtype)


def fold(scalars, items):
    outs, plans, given = [], [], []
    for keep, got, (outer, inner, bit, *more) in items:
        gots = got if isinstance(got, tuple) else (got,)
        sends = 2 if more else 1
        shape = (keep.shape[0] // 2,) + keep.shape[1:]
        outs += [array(jnp.bfloat16, shape[0] // sends, *shape[1:])] * sends + [array(keep.dtype, *shape)]
        plans.append((outer, inner, bit, len(gots), sends))
        given += [keep, *gots]
    got = list(whole_call(functools.partial(fold_body, plans), "fold", scalars, [], given, outs, [], []))
    result = []
    for *_, sends in plans:
        sent = tuple(got.pop(0) for _ in range(sends))
        result.append((sent if sends == 2 else sent[0], got.pop(0)))
    return result


def merge_body(shapes, scalars, *refs):
    send, left = refs[-2:]
    mine = scalars[4]
    low = send.shape[1]
    first = 0
    for item, (rows, wide) in enumerate(shapes):
        keep, got = refs[2 * item : 2 * item + 2]
        for part in range(rows // low):
            span = slice(part * low, (part + 1) * low)
            for high in range(2):
                for target, side in ((send, 1 - mine), (left, mine)):
                    value = keep[2 * high + side, span, :].astype(jnp.float32) + got[2 * high + side, span, :].astype(jnp.float32)
                    target[high, :, first : first + wide] = value.astype(target.dtype)
            first += wide


def merge(scalars, items, low):
    items = [(k.reshape(4, k.shape[-2] // 4, k.shape[-1]), g.reshape(4, g.shape[-2] // 4, g.shape[-1])) for k, g in items]
    shapes = [k.shape[1:] for k, _ in items]
    wide = sum(rows // low * n for rows, n in shapes)
    return whole_call(
        functools.partial(merge_body, shapes), "merge", scalars, [], [x for pair in items for x in pair],
        [array(jnp.bfloat16, 2, low, wide), array(jnp.float32, 2, low, wide)], [], [],
    )


def last_ff_body(scalars, keep, got, down_ref, up_ref):
    low = keep.shape[1]
    width = down_ref.shape[1]
    for part in range(down_ref.shape[0] // low):
        cols = slice(part * width, (part + 1) * width)
        down_ref[part * low : (part + 1) * low, :] = keep[0, :, cols] + got[0, :, cols].astype(jnp.float32)
    cols = slice(4 * width, 4 * width + up_ref.shape[1])
    up_ref[...] = keep[0, :, cols] + got[0, :, cols].astype(jnp.float32)


def last_ff(scalars, keep, got, width):
    low = keep.shape[1]
    return whole_call(
        last_ff_body, "last_ff", scalars, [], [keep, got], [array(jnp.float32, 4 * low, width), array(jnp.float32, low, 4 * width)], [], []
    )


def last_qkv_body(scalars, keep, got, more_keep, more_got, query_ref, key_ref, value_ref, out_ref, small_ref, late_ref, wide_ref, turned):
    low = keep.shape[1]
    width = query_ref.shape[1]
    half = width // 2

    def total(pair, first, size):
        return pair[0][0, :, first : first + size] + pair[1][0, :, first : first + size].astype(jnp.float32)

    one, two = (keep, got), (more_keep, more_got)
    for i, ref in enumerate((query_ref, key_ref, value_ref)):
        ref[:, :half] = total(one, i * half, half)
        ref[:, half:] = total(two, i * half, half)
    out_ref[...] = total(one, 3 * half + LANES, width)
    wide_ref[...] = total(one, 3 * half, LANES)[0:1, :]
    for ref, pair in ((small_ref, one), (late_ref, two)):
        turned[...] = jnp.zeros_like(turned)
        turned[:low, :] = total(pair, 3 * half, LANES)
        ref[...] = turned[...].T[: ref.shape[0], :]


def last_qkv(scalars, keep, got, more_keep, more_got, width):
    low = keep.shape[1]
    f32 = jnp.float32
    return whole_call(
        last_qkv_body, "last_qkv", scalars, [], [keep, got, more_keep, more_got],
        [array(f32, low, width)] * 4 + [array(f32, 24, LANES), array(f32, 8, LANES), array(f32, 1, LANES)], [], [pltpu.VMEM((LANES, LANES), f32)],
    )


def after(value, *others):
    return lax.optimization_barrier((value,) + others)[0]


def bit_count(size):
    return size.bit_length() - 1


def swap_dp(value, mask):
    return lax.ppermute(value, "dp", [(i, i ^ mask) for i in range(lax.axis_size("dp"))])


def swap_seq(value, mask):
    return lax.ppermute(value, "seq", [(i, i ^ mask) for i in range(lax.axis_size("seq"))])


def column_sum(matrix):
    return jnp.sum(matrix.astype(jnp.float32), axis=0)


def spread_pairs(first):
    dps, seqs = lax.axis_size("dp"), lax.axis_size("seq")
    pairs = []
    for dp in range(dps):
        for seq in range(seqs):
            piece = first ^ (seq & 1)
            to_dp = (dp & ~1) | (seq >> 1)
            to_seq = 2 * (dp & 1) + piece
            pairs.append((dp * seqs + seq, to_dp * seqs + to_seq))
    return pairs


def to_sequences(local, order):
    odd = (lax.axis_index("seq") & 1) == 1
    got = []
    pieces = [jnp.where(odd, local[1 - first], local[first]) for first in range(2)]
    order.mark(*pieces)
    for first, piece in enumerate(pieces):
        got.append(lax.ppermute(piece, AXES, spread_pairs(first)))
    return got, odd


def in_order(got, odd, rows):
    return jnp.where(odd, jnp.concatenate([g[:rows] for g in got[::-1]]), jnp.concatenate([g[:rows] for g in got]))


def from_sequences(tokens, order):
    odd = (lax.axis_index("seq") & 1) == 1
    half = tokens.shape[0] // 2
    got = []
    for first in range(2):
        near, far = tokens[first * half : (first + 1) * half], tokens[(1 - first) * half : (2 - first) * half]
        piece = order.mark(jnp.where(order.gate(odd), far, near))
        got.append(lax.ppermute(piece, AXES, [(b, a) for a, b in spread_pairs(first)]))
    return got


def both_sequences(order, got):
    odd = order.gate((lax.axis_index("seq") & 1) == 1)
    return jnp.where(odd, jnp.stack(got[::-1]), jnp.stack(got))


def weight_lines(weights, lines):
    width = weights[0].shape[-1]
    lines = [jnp.pad(v[..., None, :], [(0, 0)] * v.ndim + [(0, width - v.shape[-1])]) for v in lines]
    lines.append(jnp.zeros(lines[0].shape[:-2] + (16 - len(lines), width), jnp.bfloat16))
    return jnp.concatenate(weights + lines, axis=-2)


def near_shards(part, across=True):
    if lax.axis_size("dp") != PARTS:
        p = part if part.ndim == 3 else jnp.stack(jnp.split(lax.all_gather(part, "dp", axis=0, tiled=True), PARTS))
        return [p[i] for i in range(PARTS)]
    return [part, swap_dp(part, 2), swap_dp(part, 4)] + ([swap_dp(part, 6)] if across else [])


def both_cores(parts):
    return [shard for part in parts for shard in (part, swap_dp(part, 1))]


def all_shards(near, *ready):
    if len(near) == PARTS:
        return near
    return both_cores([near[0]] + list(lax.optimization_barrier((*near[1:], *ready))[:3]))


def relayed_shards(near, cut, *ready):
    if len(near) == PARTS:
        return near
    own, along_x, along_y = near
    along_x, along_y = lax.optimization_barrier((along_x, along_y, *ready))[:2]
    sent = along_x[:cut], along_y[cut:]
    top, bottom = swap_dp(sent[0], 4), swap_dp(sent[1], 2)
    own, along_x, along_y = lax.optimization_barrier((own, along_x, along_y, *sent))[:3]
    return both_cores([own, along_x, along_y, top, bottom])


def pack_body(count, scalars, *refs):
    weights, vectors, hidden, ids = refs[: min(3, count)], refs[3:count], refs[count], refs[count + 1]
    pieces = refs[count + 2 : count + 4]
    if vectors:
        part, lines = refs[count + 4 :]
        rows = weights[0].shape[0]
        for i, ref in enumerate(weights):
            part[i * rows : (i + 1) * rows, :] = ref[...]
        lines[...] = jnp.zeros_like(lines)
        for i, ref in enumerate(vectors):
            lines[i, : ref.shape[-1]] = (ref[...] if len(ref.shape) == 1 else ref[0]).astype(jnp.float32)
        part[3 * rows :, :] = lines[...].astype(jnp.bfloat16)
    odd = scalars[7]
    block, half = hidden.shape[1], ids.shape[1] // 2
    for first, piece in enumerate(pieces):
        piece[:block, :] = hidden[first ^ odd]
        line = jnp.where(first ^ odd == 0, ids[0:1, :], ids[1:2, :]).astype(jnp.bfloat16)
        piece[block:, :] = jnp.zeros_like(piece[block:, :])
        piece[block : block + 1, :half] = line[:, :half]
        piece[block + 1 : block + 2, :half] = line[:, half:]


def pack(scalars, weights, vectors, hidden, ids):
    piece = array(jnp.bfloat16, hidden.shape[1] + 16, hidden.shape[2])
    if lax.axis_size("dp") == PARTS:
        rows, width = weights[0].shape
        given = weights + [v[None, :] for v in vectors[:-1]] + vectors[-1:]
        return whole_call(
            functools.partial(pack_body, len(given)), "pack", scalars, [], [Far(x) for x in given + [hidden, ids]],
            [piece, piece, array(jnp.bfloat16, 3 * rows + 16, width)], [], [pltpu.VMEM((16, width), jnp.float32)],
        )
    gather = lambda v: lax.all_gather(v, "dp", axis=0, tiled=True)
    split = lambda v: gather(v).reshape((PARTS, -1) + v.shape[1:])
    pieces = whole_call(functools.partial(pack_body, 0), "pack", scalars, [], [Far(hidden), Far(ids)], [piece, piece], [], [])
    return *pieces, weight_lines([split(w) for w in weights], [split(v) for v in vectors])


def project_body(sizes, scalars, *refs):
    rows, wide, vectors, qblock, chunk, lanes, shards = sizes
    pieces, hidden = parts_of(refs[:shards]), list(refs[shards : shards + 3])
    size = hidden[0].shape[0]
    hidden = hidden[:2] + [hidden[2].at[:size, :], hidden[2].at[size:, :]]
    (
        attended, lse, tokens, vec_ref, up_ref, segments, ordered, query_out, keys_out, values_out, keys_far_out, values_far_out, weights_out,
        query, keys, values, keys_far, values_far, far, held, small, turned, ids, sems, hidden_sems, out_sems, kall, vt, tiles,
    ) = refs[shards + 3 :]
    count, width = tokens.shape
    block = count // 2
    half = width // 2
    core, odd = scalars[6], scalars[7]
    copies, brought = [], []

    def start(copies, source, target, sem):
        copies.append(pltpu.make_async_copy(source, target, sem))
        copies[-1].start()

    for i, (ref, place) in enumerate(zip(hidden, (0, 1, 0, 1))):
        goal = tokens if i < 2 else far
        start(brought, ref.at[:block, :], goal.at[pl.ds(pl.multiple_of((place ^ odd) * block, block), block), :], hidden_sems.at[i])
    start(brought, hidden[0].at[block:, :], ids, hidden_sems.at[4])
    for part, first, ref in pieces:
        where = scalars[0] ^ part
        target = pl.ds(where * rows, rows)
        for weight in range(first // rows, (first + ref.shape[0]) // rows):
            for side in range(2):
                start(
                    copies,
                    ref.at[weight * rows - first : (weight + 1) * rows - first, side * half : (side + 1) * half],
                    held.at[side, target, weight * half : (weight + 1) * half],
                    sems.at[len(copies)],
                )
        if first + ref.shape[0] > 3 * rows:
            start(copies, ref.at[3 * rows - first :, :], small.at[where], sems.at[len(copies)])
    wait_all(brought)
    line = ids[...].astype(jnp.float32)
    for i in range(2):
        segments[:, i * count : (i + 1) * count] = jnp.where(core == i, line[0:1, :count], line[1:2, :count])
    flipped = tokens[...].T
    for i in range(PARTS):
        turned[i] = flipped[i * rows : (i + 1) * rows, :]
    turn_parts(scalars[1], turned, ordered)
    wait_all(copies)
    saves = []
    start(saves, held, weights_out, out_sems.at[0])
    vec_ref[...] = jnp.concatenate([small[i, :, :rows] for i in range(PARTS)], axis=1).astype(jnp.float32)
    up_ref[...] = jnp.concatenate([small[i, vectors : vectors + 1, :wide] for i in range(PARTS)], axis=1).astype(jnp.float32)
    for i, (weight, add, goal, source, out) in enumerate((
        (1, None, keys, tokens, keys_out), (1, None, keys_far, far, keys_far_out), (2, 1, values, tokens, values_out),
        (2, 1, values_far, far, values_far_out), (0, 0, query, tokens, query_out),
    )):
        for side in range(2):
            cols = slice(side * half, (side + 1) * half)
            product = nn(source[...], held[side, :, weight * half : (weight + 1) * half])
            if add is not None:
                product = product + vec_ref[add : add + 1, cols]
            goal[:, cols] = product.astype(jnp.bfloat16)
        start(saves, goal, out, out_sems.at[i + 1])
    forward_body(qblock, chunk, lanes, query, keys, values, keys_far, values_far, segments, attended, lse, kall, vt, tiles)
    wait_all(saves)


def project(scalars, pieces, hidden, rows, wide, vectors, qblock, chunk, lanes):
    block, width = hidden[0].shape[0] - 16, hidden[0].shape[1]
    count = 2 * block
    lines = 16
    n = 2 * count // chunk
    f32, b16 = jnp.float32, jnp.bfloat16
    whole = array(b16, count, width)
    vmem = lambda x: pltpu.VMEM(x.shape, x.dtype)
    return whole_call(
        functools.partial(project_body, (rows, wide, vectors, qblock, chunk, lanes, len(pieces))), "project", scalars, list(pieces) + list(hidden), [],
        [whole, array(f32, width // lanes, 8, count), whole, array(f32, lines, width), array(f32, 1, wide * PARTS), array(f32, 1, 2 * count),
         array(b16, 2, PARTS // 2, rows, count)],
        [whole] * 5 + [array(b16, 2, width, 3 * width // 2)],
        [vmem(whole)] * 6
        + [pltpu.VMEM((2, width, 3 * width // 2), b16), pltpu.VMEM((PARTS, lines, width), b16), pltpu.VMEM((PARTS, rows, count), b16),
           pltpu.VMEM((16, width), b16), pltpu.SemaphoreType.DMA((7 * PARTS,)),
           pltpu.SemaphoreType.DMA((5,)), pltpu.SemaphoreType.DMA((6,)), pltpu.VMEM((n, chunk, lanes), b16),
           pltpu.VMEM((n, lanes, chunk), b16), pltpu.VMEM((n, chunk, LANES), f32)],
        28,
    )


class Order:
    def __init__(self):
        self.last = ()

    def gate(self, value):
        return lax.optimization_barrier((value, *self.last))[0] if self.last else value

    def mark(self, *values):
        self.last = values
        return values[0] if len(values) == 1 else values


def all_rows(send, keep):
    return jnp.stack([keep, send], axis=1).reshape(-1, keep.shape[-1]).astype(jnp.float32)


def scatter_all(send, keep):
    return lax.psum_scatter(all_rows(send, keep), AXES, scatter_dimension=0, tiled=True)


def per_device(
    hidden_in, segment_ids, query_weight, query_bias, key_weight, value_weight, value_bias, out_weight, out_bias,
    first_gain, first_shift, up_weight, up_bias, down_weight, down_bias, second_gain, second_shift, cotangent,
):
    dps, seqs = lax.axis_size("dp"), lax.axis_size("seq")
    inner_width, width = up_weight.shape[1], query_weight.shape[1]
    devices = dps * seqs
    share = width // devices
    qblock = chunk = 256
    pairs = 3
    direct = dps == PARTS and seqs == 4
    dp, seq = lax.axis_index("dp"), lax.axis_index("seq")
    if direct:
        scalars = [dp, dp & 1, (dp >> 1) & 1, dp >> 2, seq & 1, seq >> 1, dp & 1, seq & 1]
    else:
        scalars = [0, 0, 0, 0, 0, 0, dp & 1, seq & 1]
    scalars = jnp.stack([jnp.asarray(v, jnp.int32) for v in scalars])

    vectors = [query_bias, value_bias, out_bias, first_gain, first_shift, down_bias, second_gain, second_shift]
    *hidden, part = pack(
        scalars, [query_weight, key_weight, value_weight], vectors + [up_bias], hidden_in, segment_ids
    )
    near = near_shards(part)
    hidden = [lax.ppermute(piece, AXES, spread_pairs(first)) for first, piece in enumerate(hidden)]
    out_up, down_part = lax.optimization_barrier(
        (jnp.concatenate([out_weight, up_weight], axis=1), down_weight, *near[1:4])
    )[:2]
    hidden.append(swap_dp(jnp.concatenate(hidden), 1))
    if direct:
        own_far, *arrived = lax.optimization_barrier((swap_dp(part, 1), *near[1:4]))
        shards = [part, own_far, *arrived, swap_dp(jnp.concatenate(arrived), 1)]
    else:
        shards = near
    out_up_near = near_shards(out_up)
    attended, lse, tokens, vec, up_add, segments, ordered, query, keys, values, keys_other, values_other, w_qkv = project(
        scalars, shards, hidden, width // PARTS, inner_width // PARTS, len(vectors), qblock, chunk, pairs * LANES
    )
    order = Order()
    down_near = near_shards(after(down_part, attended, *out_up_near[1:4]), False)
    got_up, odd = to_sequences(after(cotangent, attended), order)
    out_up_shards = all_shards(out_up_near, attended)
    normal_one, scale_one, first_low, active, slope, wo, wu = widen(scalars, out_up_shards, attended, tokens, vec, up_add)
    upstream = in_order(lax.optimization_barrier((*got_up, active))[:2], odd, hidden_in.shape[1])
    layer_low, sum_two_grad, second_grad, sums_two, down_send, down_keep, wd = narrow(
        scalars, relayed_shards(down_near, inner_width // PARTS // 2, active), active, normal_one, vec, upstream
    )
    swap = (lambda value: swap_dp(value, 1)) if direct else (lambda value: value)
    order = Order()
    order.mark(second_grad)
    down_got = swap(down_send)
    out_pieces = from_sequences(layer_low, order)
    inner_grad, up_sum, up_send, up_keep = inner_back(scalars, order.gate(second_grad), wd, slope, first_low)
    up_got = swap(up_send)
    order.mark(inner_grad)
    if direct:
        ((send, down_keep),) = fold(order.gate(scalars), [(down_keep, down_got, (2, 1, 2))])
        down_got = swap_dp(order.mark(send), 2)
    sum_one_grad, attended_grad, sums_one, out_send, out_keep = outer_back(
        order.gate(scalars), inner_grad, wu, sum_two_grad, normal_one, scale_one, vec, wo, attended
    )
    order.mark(attended_grad)
    if direct:
        ((send, up_keep),) = fold(order.gate(scalars), [(up_keep, up_got, (1, 2, 3))])
        up_got = swap_dp(order.mark(send), 4)
    out_got = swap(out_send)

    def attend(side):
        given = (query, keys, values, keys_other, values_other, attended, attended_grad, lse, segments)
        return order.mark(*attend_back(order.gate(scalars), *given, qblock, chunk, pairs, side))

    dq, dk, dv, *far = attend(0)
    if direct:
        (send, down_keep), (third, out_keep) = fold(
            order.gate(scalars), [(down_keep, down_got, (1, 1, 3)), (out_keep, out_got, (1, 2, 3))]
        )
        order.mark(send, third)
        down_got, out_got = swap_dp(send, 4), swap_dp(third, 4)
    layer_out = order.mark(both_sequences(order, out_pieces))
    one_low, one_high, one_keep, gradient, sums_first = qkv_back(
        0, order.gate(scalars), dq, dk, dv, *[swap_dp(x, 1) for x in order.gate(far)], ordered, w_qkv, sum_one_grad,
        sums_one, sums_two, up_sum
    )
    order.mark(gradient)
    one_got = (swap(one_low), swap(one_high))
    if direct:
        ((send, up_keep),) = fold(order.gate(scalars), [(up_keep, up_got, (1, 1, 2))])
        up_got = swap_dp(order.mark(send), 2)
    dq, dk, dv, *far = attend(1)
    if direct:
        send, ff_keep = merge(order.gate(scalars), [(down_keep, down_got), (up_keep, up_got)], share)
        ff_got = swap_seq(order.mark(send), 1)
        (send, one_keep), (other, out_keep) = fold(
            order.gate(scalars), [(one_keep, one_got, (2, 1, 2)), (out_keep, out_got, (1, 1, 2))]
        )
        order.mark(send, other)
        one_got, out_got = swap_dp(send, 2), swap_dp(other, 2)
    two_low, two_high, two_keep, gradient, _ = qkv_back(
        1, order.gate(scalars), dq, dk, dv, *[swap_dp(x, 1) for x in order.gate(far)], ordered, w_qkv, gradient, sums_first
    )
    order.mark(gradient)
    two_got = (swap(two_low), swap(two_high))
    in_pieces = from_sequences(gradient, order)
    if not direct:
        down_grad, up_grad = scatter_all(down_send, down_keep), scatter_all(up_send, up_keep)
        one, two = scatter_all(jnp.concatenate([one_low, one_high]), one_keep), scatter_all(jnp.concatenate([two_low, two_high]), two_keep)
        cut = width // 2
        query_grad, key_grad, value_grad = [
            jnp.concatenate([side[:, i * cut : (i + 1) * cut] for side in (one, two)], axis=1) for i in range(3)
        ]
        out_grad = scatter_all(out_send, out_keep)
        small, late = one[:, 3 * cut :].T, two[:, 3 * cut :].T
        up_bias_grad = lax.psum_scatter(up_sum[0], AXES, scatter_dimension=0, tiled=True)
    else:
        ((send, one_keep),) = fold(order.gate(scalars), [(one_keep, one_got, (1, 1, 3))])
        one_got = swap_dp(order.mark(send), 4)
        ((send, ff_keep),) = fold(order.gate(scalars), [(ff_keep, ff_got, (1, 1, 5))])
        ff_got = swap_seq(order.mark(send), 2)
        ((sent, two_keep),) = fold(order.gate(scalars), [(two_keep, two_got, (2, 1, 2, True))])
        two_got = tuple(swap_dp(x, 2) for x in order.mark(*sent))
        send, keep = merge(order.gate(scalars), [(one_keep, one_got), (out_keep, out_got)], share)
        got = swap_seq(order.mark(send), 1)
        ((send, two_keep),) = fold(order.gate(scalars), [(two_keep, two_got, (1, 1, 3))])
        two_got = swap_dp(order.mark(send), 4)
    input_grad = order.mark(both_sequences(order, in_pieces).astype(jnp.float32))
    if direct:
        ((send, keep),) = fold(order.gate(scalars), [(keep, got, (1, 1, 5))])
        got = swap_seq(order.mark(send), 2)
        send, two_keep = merge(order.gate(scalars), [(two_keep, two_got)], share)
        two_got = swap_seq(order.mark(send), 1)
        ((send, two_keep),) = fold(order.gate(scalars), [(two_keep, two_got, (1, 1, 5))])
        two_got = swap_seq(order.mark(send), 2)
        down_grad, up_grad = order.mark(*last_ff(order.gate(scalars), ff_keep, ff_got, width))
        query_grad, key_grad, value_grad, out_grad, small, late, line = last_qkv(
            order.gate(scalars), keep, got, two_keep, two_got, width
        )
        up_bias_grad = line[0, LANES - inner_width // devices :]
    ob, g1, s1 = [small[i, :share] for i in (0, 1, 2)]
    db, g2, s2 = [small[i, :share] for i in (8, 9, 10)]
    qb, vb = [late[i, :share] for i in (0, 1)]
    return (
        layer_out, input_grad, query_grad, qb, key_grad, value_grad, vb, out_grad, ob, g1, s1, up_grad, up_bias_grad, down_grad, db, g2, s2,
    )


def solution(mesh):
    wide, flat = P("dp", None), P("dp")
    in_specs = (
        P("dp", "seq", None), wide, wide, flat, wide, wide, flat, wide, flat, flat, flat, wide, flat, wide, flat,
        flat, flat, P("dp", "seq", None),
    )
    rows, cells = P(AXES, None), P(AXES)
    out_specs = (
        P("dp", "seq", None), P("dp", "seq", None), rows, cells, rows, rows, cells, rows, cells, cells, cells, rows,
        cells, rows, cells, cells, cells,
    )
    return jax.shard_map(per_device, mesh=mesh, in_specs=in_specs, out_specs=out_specs, check_vma=False)
```
